32 devices in a mesh: dp: 8 (over y, x, core), mp: 4 (over z).
Axes of the slice: x: 2, y: 2, z: 4, core: 2. Of those that a mesh axis runs over, the one named last changes fastest.
Arguments:
- text_states: bfloat16 [128, 40, 768], P(('dp', 'mp')), may hold values from -6 to 6
- patch_states: bfloat16 [128, 145, 1024], P(('dp', 'mp')), may hold values from -6 to 6
- patch_rows: int32 [128], P('dp'), may hold values from 50 to 145, as said below
- cotangent: bfloat16 [128, 40, 768], P(('dp', 'mp')), may hold values from -6 to 6
- w_attn: bfloat16 [3, 768, 768], P(None, None, 'mp'), may hold values from -0.21875 to 0.21875
- attn_bias: bfloat16 [2, 768], P(None, 'mp'), may hold values from -3 to 3
- w_attn_out: bfloat16 [768, 768], P('mp'), may hold values from -0.4375 to 0.4375
- w_query: bfloat16 [768, 768], P(None, 'mp'), may hold values from -0.21875 to 0.21875
- w_patch: bfloat16 [2, 1024, 768], P(None, None, 'mp'), may hold values from -0.1875 to 0.1875
- cross_bias: bfloat16 [2, 768], P(None, 'mp'), may hold values from -3 to 3
- w_cross_out: bfloat16 [768, 768], P('mp'), may hold values from -0.625 to 0.625
- w_hidden: bfloat16 [768, 3072], P(None, 'mp'), may hold values from -0.21875 to 0.21875
- hidden_bias: bfloat16 [3072], P('mp'), may hold values from -3 to 3
- w_output: bfloat16 [3072, 768], P('mp'), may hold values from -0.15625 to 0.15625
- out_bias: bfloat16 [3, 768], replicated, may hold values from -3 to 3
- norm_gain: bfloat16 [3, 768], replicated, may hold values from 0.5 to 1.5
- norm_shift: bfloat16 [3, 768], replicated, may hold values from -2 to 2
Outputs:
- layer_out: float32 [128, 40, 768], P(('dp', 'mp'))
- text_grad: float32 [128, 40, 768], P(('dp', 'mp'))
- patch_grad: float32 [128, 145, 1024], P(('dp', 'mp'))
- grad_attn: float32 [3, 768, 768], P(None, None, 'mp')
- grad_attn_bias: float32 [2, 768], P(None, 'mp')
- grad_attn_out: float32 [768, 768], P('mp')
- grad_query: float32 [768, 768], P(None, 'mp')
- grad_patch: float32 [2, 1024, 768], P(None, None, 'mp')
- grad_cross_bias: float32 [2, 768], P(None, 'mp')
- grad_cross_out: float32 [768, 768], P('mp')
- grad_hidden: float32 [768, 3072], P(None, 'mp')
- grad_hidden_bias: float32 [3072], P('mp')
- grad_output: float32 [3072, 768], P('mp')
- grad_out_bias: float32 [3, 768], replicated
- grad_gain: float32 [3, 768], replicated
- grad_shift: float32 [3, 768], replicated
The draws below stay inside these ranges and needn't reach their ends.
Inputs may be any that keep to these rules, and one draw needn't show every extreme that they name: `patch_rows`: each entry is 50 or 145.
All inputs are finite; a program needn't handle non-finite values.
Results may differ from the reference program's by a relative error of at most 0.019.
Values may be sent and summed in bfloat16 or wider, within the bound.
A program may use at most 128 MiB of HBM per device.

```python
import math
import jax
import jax.numpy as jnp
from jax import lax

D = 768
HEADS = 12
HEAD = 64
FF = 3072
PW = 1024
L = 40
P_SIZE = 145
SHORT_P = 50
GROUP = 16
ITEMS = 128


def draw_patch_rows(key, part):
    chosen = jax.random.randint(key, (ITEMS,), 0, 2)
    counts = jnp.where(chosen == 1, P_SIZE, SHORT_P).astype(jnp.int32)
    return counts.at[0].set(P_SIZE).at[1].set(SHORT_P)


def steps_of(key, extent, pieces, low, high):
    level = 1.0
    for dim, shards_of in pieces:
        draws = jax.random.uniform(jax.random.fold_in(jax.random.fold_in(key, 6), dim), (shards_of,), jnp.float32, low / len(pieces), high / len(pieces))
        level = level * jnp.repeat(jnp.exp(draws), extent[dim] // shards_of).reshape((-1,) + (1,) * (len(extent) - 1 - dim))
    return level


def noise(own_key, shape, deviation, limit, cuts=(), dtype=jnp.bfloat16):
    level = steps_of(own_key, shape, cuts, -0.22, 0.18) if cuts else 1.0
    array = jax.random.normal(own_key, shape, jnp.float32) * deviation * level
    return jnp.minimum(jnp.maximum(array, -limit), limit).astype(dtype)


def setup_inputs(seed: int = 0) -> dict:
    streams_of = jax.random.split(jax.random.key(seed), 18)
    text_states = noise(streams_of[0], (ITEMS, L, D), 1.0, 6.0, ((0, 32),))
    patch_states = noise(streams_of[1], (ITEMS, P_SIZE, PW), 1.0, 6.0, ((0, 32),))
    patch_rows = draw_patch_rows(jax.random.fold_in(streams_of[17], 71), 0)
    cotangent = noise(streams_of[3], (ITEMS, L, D), 1.0, 6.0, ((0, 32),))
    w_attn = noise(streams_of[4], (3, D, D), D ** -0.5, 0.21875, ((2, 4),))
    attn_bias = noise(streams_of[5], (2, D), 0.5, 3.0, ((1, 4),))
    w_attn_out = noise(streams_of[6], (D, D), (D // 4) ** -0.5, 0.4375, ((0, 4),))
    w_query = noise(streams_of[7], (D, D), D ** -0.5, 0.21875, ((1, 4),))
    w_patch = noise(streams_of[8], (2, PW, D), PW ** -0.5, 0.1875, ((2, 4),))
    cross_bias = noise(streams_of[9], (2, D), 0.5, 3.0, ((1, 4),))
    w_cross_out = noise(streams_of[10], (D, D), (D // 8) ** -0.5, 0.625, ((0, 4),))
    w_hidden = noise(streams_of[11], (D, FF), D ** -0.5, 0.21875, ((1, 4),))
    hidden_bias = noise(streams_of[12], (FF,), 0.5, 3.0, ((0, 4),))
    w_output = noise(streams_of[13], (FF, D), (FF // 2) ** -0.5, 0.15625, ((0, 4),))
    out_bias = noise(streams_of[14], (3, D), 0.5, 3.0)
    norm_gain = jnp.clip(1.0 + 0.1 * jax.random.normal(streams_of[15], (3, D), jnp.float32), 0.5, 1.5).astype(jnp.bfloat16)
    norm_shift = noise(streams_of[16], (3, D), 0.3, 2.0)
    return dict(text_states=text_states, patch_states=patch_states, patch_rows=patch_rows, cotangent=cotangent, w_attn=w_attn, attn_bias=attn_bias, w_attn_out=w_attn_out, w_query=w_query, w_patch=w_patch, cross_bias=cross_bias, w_cross_out=w_cross_out, w_hidden=w_hidden, hidden_bias=hidden_bias, w_output=w_output, out_bias=out_bias, norm_gain=norm_gain, norm_shift=norm_shift)


@jax.custom_vjp
def low(v):
    return lax.optimization_barrier(v.astype(jnp.bfloat16)).astype(jnp.float32)

@jax.custom_vjp
def low_back(v):
    return v

def low_keep(v):
    return (low(v), None)

def low_pass(kept, grad):
    return (grad,)

def back_keep(v):
    return (v, None)

def back_low(kept, grad):
    return (low(grad),)
low.defvjp(low_keep, low_pass)
low_back.defvjp(back_keep, back_low)
precise = lax.Precision.HIGHEST
epsilon = 1e-06

def round_both(value):
    return low(low_back(value))

def layer_norm(hidden_sum, gain, shift):
    row_mean = lax.optimization_barrier(jnp.mean(hidden_sum, -1, keepdims=True))
    centred = hidden_sum - row_mean
    variance = lax.optimization_barrier(jnp.mean(centred * centred, -1, keepdims=True))
    return centred * lax.rsqrt(variance + epsilon) * gain + shift

def attention(queries, key_part, values, valid):
    score_scale = 1.0 / math.sqrt(HEAD)
    head_q = queries.reshape(queries.shape[0], queries.shape[1], HEADS, HEAD)
    head_k = key_part.reshape(key_part.shape[0], key_part.shape[1], HEADS, HEAD)
    head_v = values.reshape(values.shape[0], values.shape[1], HEADS, HEAD)
    scores = low_back(jnp.einsum('bqhe,bkhe->bhqk', head_q, head_k, precision=precise) * score_scale)
    if valid is not None:
        scores = jnp.where(valid, scores, -1e+30)
    attn_prob = jax.nn.softmax(scores, axis=-1)
    mixed = jnp.einsum('bhqk,bkhe->bqhe', low(attn_prob), head_v, precision=precise)
    return round_both(mixed.reshape(queries.shape))

def cross_modal_layer(text_in, patch_in, valid, params):
    w_attn, attn_bias, w_attn_out, w_query, w_patch, cross_bias, w_cross_out, w_hidden, hidden_bias, w_output, out_bias, norm_gain, norm_shift = params
    projected = jnp.einsum('bld,tdc->tblc', text_in, w_attn, precision=precise)
    queries = round_both(projected[0] + attn_bias[0])
    key_part = round_both(projected[1])
    values = round_both(projected[2] + attn_bias[1])
    self_mixed = attention(queries, key_part, values, None)
    self_sum = low_back(jnp.einsum('blc,cd->bld', self_mixed, w_attn_out, precision=precise))
    first = low(layer_norm(text_in + self_sum + out_bias[0], norm_gain[0], norm_shift[0]))
    cross_q = round_both(jnp.einsum('bld,dc->blc', first, w_query, precision=precise) + cross_bias[0])
    patch_proj = jnp.einsum('bpc,tcd->tbpd', patch_in, w_patch, precision=precise)
    cross_k = round_both(patch_proj[0])
    cross_v = round_both(patch_proj[1] + cross_bias[1])
    cross_mixed = attention(cross_q, cross_k, cross_v, valid)
    cross_sum = low_back(jnp.einsum('blc,cd->bld', cross_mixed, w_cross_out, precision=precise))
    second = low(layer_norm(first + cross_sum + out_bias[1], norm_gain[1], norm_shift[1]))
    hidden_pre = low_back(jnp.einsum('bld,df->blf', second, w_hidden, precision=precise) + hidden_bias)
    hidden = low(jax.nn.gelu(hidden_pre, approximate=False))
    ffn_sum = low_back(jnp.einsum('blf,fd->bld', hidden, w_output, precision=precise))
    return layer_norm(second + ffn_sum + out_bias[2], norm_gain[2], norm_shift[2])

def reference(text_states, patch_states, patch_rows, cotangent, w_attn, attn_bias, w_attn_out, w_query, w_patch, cross_bias, w_cross_out, w_hidden, hidden_bias, w_output, out_bias, norm_gain, norm_shift):
    params = tuple((a.astype(jnp.float32) for a in (w_attn, attn_bias, w_attn_out, w_query, w_patch, cross_bias, w_cross_out, w_hidden, hidden_bias, w_output, out_bias, norm_gain, norm_shift)))
    blocks = ITEMS // GROUP
    text_blocks = text_states.reshape(blocks, GROUP, L, D)
    patch_blocks = patch_states.reshape(blocks, GROUP, P_SIZE, PW)
    row_blocks = patch_rows.reshape(blocks, GROUP)
    grad_blocks = cotangent.reshape(blocks, GROUP, L, D)

    def block_step(totals, inputs):
        text_in, patch_in, rows_in, grad_in = inputs
        positions = lax.broadcasted_iota(jnp.int32, (GROUP, P_SIZE), 1)
        valid = (positions < rows_in[:, None].astype(jnp.int32))[:, None, None, :]

        def forward(text_arg, patch_arg, param_arg):
            return cross_modal_layer(text_arg, patch_arg, valid, param_arg)
        result, pull = jax.vjp(forward, text_in.astype(jnp.float32), patch_in.astype(jnp.float32), params)
        text_back, patch_back, param_back = pull(grad_in.astype(jnp.float32))
        totals = jax.tree.map(lambda left, right: left + right, totals, param_back)
        return (totals, (result, text_back, patch_back))
    start_totals = jax.tree.map(lambda arr: jnp.zeros(arr.shape, jnp.float32), params)
    totals, (layer_out, text_grad, patch_grad) = lax.scan(block_step, start_totals, (text_blocks, patch_blocks, row_blocks, grad_blocks))
    return (layer_out.reshape(ITEMS, L, D), text_grad.reshape(ITEMS, L, D), patch_grad.reshape(ITEMS, P_SIZE, PW), totals[0], totals[1], totals[2], totals[3], totals[4], totals[5], totals[6], totals[7], totals[8], totals[9], totals[10], totals[11], totals[12])
```

```python
import math
import functools
import jax, jax.numpy as jnp
from jax import lax
from jax.experimental import pallas as pl
from jax.experimental.pallas import tpu as pltpu

from jax.sharding import PartitionSpec as P

MESH = pl.DeviceIdType.MESH

def bit_of(d, b):
    return lax.rem(lax.div(d, jnp.int32(2 ** b)), jnp.int32(2))

def flip(d, b):
    return d + (1 - 2 * bit_of(d, b)) * (2 ** b)

def when(cond, fn):
    if cond is True:
        fn()
    else:
        pl.when(cond)(fn)

class Gather:
    def __init__(self, src, dst, row0, rows, order, d, z, nz, sems, base):
        self.src, self.dst, self.row0, self.order = src, dst, row0, order
        self.d, self.z, self.nz = d, z, nz
        self.piece = rows // (2 ** len(order))
        self.zs, self.zr, self.ps, self.pr = sems
        self.base = base
        self.k = len(order)

    def win(self, s):
        w = jnp.int32(0)
        for i, b in enumerate(self.order):
            if i >= s:
                w = w + bit_of(self.d, b) * (2 ** i)
        size = self.piece * 2 ** s
        start = self.row0 + w * self.piece
        return pl.ds(pl.multiple_of(start, 16), size)

    def shard(self, dr, j):
        return self.z - j if dr == 0 else self.z + j

    def has(self, dr, j):
        return self.z >= j if dr == 0 else self.z + j < self.nz

    def zcopy(self, dr, j):
        t = self.shard(dr, j)
        rows = self.win(0)
        src = self.src.at[rows] if j == 0 else self.dst.at[t, rows]
        to = self.z + 1 if dr == 0 else self.z - 1
        return pltpu.make_async_remote_copy(src, self.dst.at[t, rows], self.zs.at[self.base, dr, j], self.zr.at[self.base, dr, j], device_id=(self.d, to), device_id_type=MESH)

    def zcan(self, dr, j):
        ahead = self.z + 1 < self.nz if dr == 0 else self.z >= 1
        return ahead if j == 0 else jnp.logical_and(ahead, self.has(dr, j))

    def pcopy(self, s, dr, j):
        t = self.shard(dr, j)
        rows = self.win(s)
        b = self.order[s]
        return pltpu.make_async_remote_copy(self.dst.at[t, rows], self.dst.at[t, rows], self.ps.at[self.base, s, dr, j - 1], self.pr.at[self.base, s, dr, j - 1], device_id=(flip(self.d, b), self.z), device_id_type=MESH)

    def events(self):
        return self.nz + self.k

    def event(self, e):
        nz, k = self.nz, self.k
        if e == 0:
            for dr in (0, 1):
                when(self.zcan(dr, 0), lambda: self.zcopy(dr, 0).start())
            return
        for s in range(k, -1, -1):
            j = e - s
            if not 1 <= j <= nz - 1:
                continue
            for dr in (0, 1):
                def go(dr=dr, j=j, s=s):
                    if s == 0:
                        self.zcopy(dr, j - 1).wait_recv()
                        if j <= nz - 2:
                            when(self.zcan(dr, j), lambda: self.zcopy(dr, j).start())
                    else:
                        self.pcopy(s - 1, dr, j).wait_recv()
                    if s < k:
                        self.pcopy(s, dr, j).start()
                when(self.has(dr, j), go)

    def finish(self):
        nz, k = self.nz, self.k
        for dr in (0, 1):
            for j in range(nz - 1):
                when(self.zcan(dr, j), lambda dr=dr, j=j: self.zcopy(dr, j).wait_send())
            for s in range(k):
                for j in range(1, nz):
                    when(self.has(dr, j), lambda dr=dr, j=j, s=s: self.pcopy(s, dr, j).wait_send())

def enter(d, z, nd, nz, bits):
    bar = pltpu.get_barrier_semaphore()
    for b in bits:
        pl.semaphore_signal(bar, inc=1, device_id=(flip(d, b), z), device_id_type=MESH)
    @pl.when(z + 1 < nz)
    def _():
        pl.semaphore_signal(bar, inc=1, device_id=(d, z + 1), device_id_type=MESH)
    @pl.when(z >= 1)
    def _():
        pl.semaphore_signal(bar, inc=1, device_id=(d, z - 1), device_id_type=MESH)
    last = nz - 1
    pl.semaphore_wait(bar, len(bits) + lax.div(z + last, jnp.int32(nz)) + lax.div(last - z + last, jnp.int32(nz)))

def gather_kernel(plan, nd, nz, bits, *refs):
    n = max(p[0] for p in plan) + 1
    ins, outs = refs[:n], refs[n:2 * n]
    own = refs[2 * n:3 * n]
    zs, zr, ps, pr, lsem = refs[3 * n:]
    d, z = lax.axis_index("dp"), lax.axis_index("mp")
    loads = [pltpu.make_async_copy(ins[i], own[i], lsem.at[i]) for i in range(n)]
    enter(d, z, nd, nz, bits)
    for c in loads:
        c.start()
    chunks = [Gather(ins[i], outs[i], r0, rows, order, d, z, nz, (zs, zr, ps, pr), c) for c, (i, r0, rows, order, _) in enumerate(plan)]
    last = max(g.events() + p[4] for g, p in zip(chunks, plan))
    for t in range(last):
        for g, p in zip(chunks, plan):
            if 0 <= t - p[4] < g.events():
                g.event(t - p[4])
        if t == 2:
            for c in loads:
                c.wait()
            stores = [pltpu.make_async_copy(own[i], outs[i].at[z], lsem.at[i]) for i in range(n)]
            for c in stores:
                c.start()
    for c in stores:
        c.wait()
    for g in chunks:
        g.finish()

def gather_weights(shards, plan, nd, nz, bits):
    n = len(shards)
    nc = len(plan)
    sem = pltpu.SemaphoreType.DMA
    return pl.pallas_call(
        functools.partial(gather_kernel, plan, nd, nz, bits),
        out_shape=tuple(jax.ShapeDtypeStruct((nz,) + a.shape, a.dtype) for a in shards),
        in_specs=[pl.BlockSpec(memory_space=pl.ANY)] * n,
        out_specs=tuple([pl.BlockSpec(memory_space=pl.ANY)] * n),
        scratch_shapes=[pltpu.VMEM(a.shape, a.dtype) for a in shards]
        + [sem((nc, 2, nz - 1)), sem((nc, 2, nz - 1)), sem((nc, 3, 2, nz - 1)), sem((nc, 3, 2, nz - 1)), sem((n,))],
        compiler_params=pltpu.CompilerParams(collective_id=0, has_side_effects=True),
    )(*shards)

class Reduce:
    def __init__(self, part, keep, halves, recvs, ups, downs, extra, result, row0, rows, order, d, z, nz, bits, sems, base):
        self.part, self.keep, self.core_in = part, keep, halves
        self.recvs, self.ups, self.downs, self.extra, self.result = recvs, ups, downs, extra, result
        self.row0, self.rows, self.order = row0, rows, order
        self.d, self.z, self.nz = d, z, nz
        self.bits = bits
        self.ss, self.rs = sems
        self.base = base
        self.slot = 0
        self.pending = []
        self.steps = []
        self.build()

    def remote(self, src, dst, to, cond=True):
        s = self.slot
        self.slot += 1
        copy = lambda: pltpu.make_async_remote_copy(src, dst, self.ss.at[self.base, s], self.rs.at[self.base, s], device_id=to, device_id_type=MESH)
        self.pending.append((cond, copy))
        return copy

    def build(self):
        d, z, nz = self.d, self.z, self.nz
        half = self.rows // 2
        cb = self.bits[0]
        mine = bit_of(d, cb)
        lo = pl.multiple_of(self.row0 + mine * half, 16)
        ot = pl.multiple_of(self.row0 + (1 - mine) * half, 16)
        send = self.remote(self.part.at[:, pl.ds(ot, half), :], self.core_in, (flip(d, cb), z))
        load = lambda: pltpu.make_async_copy(self.part.at[:, pl.ds(lo, half), :], self.keep, self.ss.at[self.base, self.slots_max - 1])
        def first():
            send().start()
            load().start()
        def arrive():
            load().wait()
            send().wait_recv()
            add_rows(self.keep, self.core_in, nz, half)
        self.steps.append(first)
        prev = arrive
        start, size, whole = jnp.int32(0), half, True
        taken = []
        for op in self.order:
            if op == "z":
                for h in range(nz):
                    self.steps.append(functools.partial(self.zhop, h, start, size, prev if h == 0 else None))
                self.zbase = self.slot
                self.slot += 2 * nz
                prev = None
                whole = False
                zprep = self.zcopies(start, size)
                self.zc = zprep
            else:
                size //= 2
                m = bit_of(d, op)
                keep0 = pl.multiple_of(start + m * size, 16)
                send0 = pl.multiple_of(start + (1 - m) * size, 16)
                buf = self.recvs[op]
                if whole:
                    src = self.keep.at[:, pl.ds(send0, size), :]
                    dst = buf
                else:
                    src = self.keep.at[z, pl.ds(send0, size), :]
                    dst = buf.at[0]
                cp = self.remote(src, dst, (flip(d, op), z))
                def step(prev=prev, cp=cp):
                    if prev is not None:
                        prev()
                    cp().start()
                self.steps.append(step)
                def prev(cp=cp, keep0=keep0, size=size, whole=whole, buf=buf):
                    cp().wait_recv()
                    if whole:
                        add_rows(self.keep.at[:, pl.ds(keep0, size), :], buf, nz, size)
                    else:
                        add_plain(self.keep.at[z, pl.ds(keep0, size), :], buf.at[0], size)
                taken.append(op)
                start = keep0
        for e, b in enumerate(self.bits[3:]):
            cp = self.remote(self.keep.at[z, pl.ds(start, size), :], self.extra.at[e], (flip(d, b), z))
            def step(prev=prev, cp=cp):
                if prev is not None:
                    prev()
                cp().start()
            self.steps.append(step)
            def prev(cp=cp, e=e, start=start, size=size):
                cp().wait_recv()
                cp().wait_send()
                add_plain(self.keep.at[z, pl.ds(start, size), :], self.extra.at[e], size)
            self.pending.pop()
        pos = pl.multiple_of(mine * half + start, 16)
        def place(prev=prev, pos=pos, start=start, size=size):
            if prev is not None:
                prev()
            copy_plain(self.result.at[pl.ds(pos, size), :], self.keep.at[z, pl.ds(start, size), :], size)
        prev = place
        for op in list(reversed(taken)) + [cb]:
            m = bit_of(d, op)
            win = self.result.at[pl.ds(pos, size), :]
            cp = self.remote(win, win, (flip(d, op), z))
            def step(prev=prev, cp=cp):
                prev()
                cp().start()
            self.steps.append(step)
            prev = lambda cp=cp: cp().wait_recv()
            pos = pl.multiple_of(pos - m * size, 16)
            size *= 2
        self.steps.append(prev)

    slots_max = 24

    def zcopies(self, start, size):
        out = {}
        d, z, nz = self.d, self.z, self.nz
        rows = pl.ds(start, size)
        for t in range(nz):
            su, sd = self.zbase + t, self.zbase + nz + t
            if t >= 1:
                out["u", t] = lambda t=t, s=su: pltpu.make_async_remote_copy(self.keep.at[t, rows, :], self.ups.at[t - 1], self.ss.at[self.base, s], self.rs.at[self.base, s], device_id=(d, z + 1), device_id_type=MESH)
                self.pending.append((z < t, out["u", t]))
            if t <= nz - 2:
                out["d", t] = lambda t=t, s=sd: pltpu.make_async_remote_copy(self.keep.at[t, rows, :], self.downs.at[t], self.ss.at[self.base, s], self.rs.at[self.base, s], device_id=(d, z - 1), device_id_type=MESH)
                self.pending.append((z > t, out["d", t]))
        return out

    def zhop(self, h, start, size, prev):
        z, nz = self.z, self.nz
        if prev is not None:
            prev()
        rows = pl.ds(start, size)
        @pl.when(z == h)
        def _():
            for t in range(nz - 1, h - 1, -1):
                if t == 0:
                    continue
                if h > 0:
                    self.zc["u", t]().wait_recv()
                    add_plain(self.keep.at[t, rows, :], self.ups.at[t - 1], size)
                if t > h:
                    self.zc["u", t]().start()
        me = nz - 1 - h
        @pl.when(z == me)
        def _():
            for t in range(0, me + 1):
                if t == nz - 1:
                    continue
                if h > 0:
                    self.zc["d", t]().wait_recv()
                    add_plain(self.keep.at[t, rows, :], self.downs.at[t], size)
                if t < me:
                    self.zc["d", t]().start()

    def finish(self):
        for cond, cp in self.pending:
            when(cond, lambda: cp().wait_send())

def add_plain(dst, src, rows):
    step = 16
    def body(i, c):
        r = pl.ds(pl.multiple_of(i * step, step), step)
        dst[r, :] = dst[r, :] + src[r, :]
        return c
    lax.fori_loop(0, rows // step, body, 0, unroll=min(4, rows // step))

def copy_plain(dst, src, rows):
    dst[...] = src[...]

def add_rows(dst, src, nz, rows):
    for t in range(nz):
        add_plain(dst.at[t], src.at[t], rows)

def reduce_kernel(plan, shapes, nz, bits, *refs):
    n = len(shapes)
    nc = len(plan)
    ins, outs = refs[:n], refs[n:2 * n]
    it = iter(refs[2 * n:])
    results = [next(it) for _ in range(n)]
    d, z = lax.axis_index("dp"), lax.axis_index("mp")
    bufs = []
    for _ in plan:
        keep, core_in = next(it), next(it)
        recvs = {b: next(it) for b in bits[1:3]}
        ups, downs = next(it), next(it)
        extra = next(it) if len(bits) > 3 else None
        bufs.append((keep, core_in, recvs, ups, downs, extra))
    ss, rs, lsem = it
    enter(d, z, None, nz, bits)
    chunks = []
    for c, (i, r0, rows, order, _) in enumerate(plan):
        chunks.append(Reduce(ins[i], *bufs[c], results[i].at[pl.ds(r0, rows), :], r0, rows, order, d, z, nz, bits, (ss, rs), c))
    last = max(len(c.steps) + p[4] for c, p in zip(chunks, plan))
    for t in range(last):
        for c, p in zip(chunks, plan):
            if 0 <= t - p[4] < len(c.steps):
                c.steps[t - p[4]]()
    stores = [pltpu.make_async_copy(results[i], outs[i], lsem.at[i]) for i in range(n)]
    for s in stores:
        s.start()
    for c in chunks:
        c.finish()
    for s in stores:
        s.wait()

def window_rows(rows, order, op):
    size = rows // 2
    for o in order:
        if o == "z":
            if op == "z":
                return size
        else:
            size //= 2
            if o == op:
                return size
    return size

def reduce_grads(parts, plan, nz, bits):
    sem = pltpu.SemaphoreType.DMA
    n, nc = len(parts), len(plan)
    shapes = [a.shape[1:] for a in parts]
    dt = parts[0].dtype
    scratch = [pltpu.VMEM(s, dt) for s in shapes]
    for i, r0, rows, order, _ in plan:
        C = shapes[i][1]
        scratch += [pltpu.VMEM((nz, rows // 2, C), dt)] * 2
        for b in bits[1:3]:
            lead = nz if order.index(b) < order.index("z") else 1
            scratch.append(pltpu.VMEM((lead, window_rows(rows, order, b), C), dt))
        scratch += [pltpu.VMEM((nz - 1, window_rows(rows, order, "z"), C), dt)] * 2
        if len(bits) > 3:
            scratch.append(pltpu.VMEM((len(bits) - 3, window_rows(rows, order, None), C), dt))
    return pl.pallas_call(
        functools.partial(reduce_kernel, plan, shapes, nz, bits),
        out_shape=tuple(jax.ShapeDtypeStruct(s, dt) for s in shapes),
        in_specs=[pl.BlockSpec(memory_space=pl.ANY)] * n,
        out_specs=tuple([pl.BlockSpec(memory_space=pl.ANY)] * n),
        scratch_shapes=scratch + [sem((nc, Reduce.slots_max)), sem((nc, Reduce.slots_max)), sem((n,))],
        compiler_params=pltpu.CompilerParams(collective_id=1, has_side_effects=True, vmem_limit_bytes=60 << 20),
    )(*parts)

HEAD = 64
epsilon = 1e-06

def norm_forward(hidden_sum, gain, shift):
    row_mean = jnp.mean(hidden_sum, -1, keepdims=True)
    centred = hidden_sum - row_mean
    inverse = lax.rsqrt(jnp.mean(centred * centred, -1, keepdims=True) + epsilon)
    normed = centred * inverse
    return (normed * gain.astype(jnp.float32) + shift.astype(jnp.float32), normed, inverse)

def norm_backward(grad_out, normed, inverse, gain):
    scaled = grad_out * gain.astype(jnp.float32)
    grad_in = inverse * (scaled - jnp.mean(scaled, -1, keepdims=True) - normed * jnp.mean(scaled * normed, -1, keepdims=True))
    return (grad_in, jnp.sum(grad_out * normed, axis=(0, 1)), jnp.sum(grad_out, axis=(0, 1)))

def heads(flat):
    return flat.reshape(flat.shape[:-1] + (flat.shape[-1] // HEAD, HEAD))

def ein(form, *ops):
    return jnp.einsum(form, *ops, preferred_element_type=jnp.float32)

score_scale = 1.0 / math.sqrt(HEAD)

def probabilities(q, k, valid):
    scores = ein("ziqhe,zikhe->zihqk", heads(q), heads(k)) * score_scale
    if valid is not None:
        scores = jnp.where(valid, scores, -1e30)
    highest = jnp.max(scores, -1, keepdims=True)
    log_total = highest + jnp.log(jnp.sum(jnp.exp(scores - highest), -1, keepdims=True))
    return jnp.exp(scores - log_total)

def attend(prob, v, shape):
    mixed = ein("zihqk,zikhe->ziqhe", prob.astype(jnp.bfloat16), heads(v))
    return mixed.reshape(shape).astype(jnp.bfloat16)

def attend_backward(q, k, v, prob, grad_mixed):
    gm = heads(grad_mixed)
    grad_v = ein("zihqk,ziqhe->zikhe", prob.astype(jnp.bfloat16), gm)
    grad_prob = ein("ziqhe,zikhe->zihqk", gm, heads(v))
    delta = jnp.sum(prob * grad_prob, -1, keepdims=True)
    gs = (prob * (grad_prob - delta)).astype(jnp.bfloat16)
    gq = ein("zihqk,zikhe->ziqhe", gs, heads(k)) * score_scale
    gk = ein("zihqk,ziqhe->zikhe", gs, heads(q)) * score_scale
    return (gq.reshape(q.shape).astype(jnp.bfloat16), gk.reshape(k.shape).astype(jnp.bfloat16), grad_v.reshape(v.shape).astype(jnp.bfloat16))

def plane_bits(nd):
    return tuple(range(nd.bit_length() - 1))

def per_device(nd, nz, text_states, patch_states, patch_rows, cotangent, w_attn, attn_bias, w_attn_out, w_query, w_patch, cross_bias, w_cross_out, w_hidden, hidden_bias, w_output, out_bias, norm_gain, norm_shift):
    bf, f32 = jnp.bfloat16, jnp.float32
    bits = plane_bits(nd)
    z = lax.axis_index("mp")
    ni = text_states.shape[0]
    hw = w_query.shape[1]
    W_A = jnp.concatenate([w_attn[0], w_attn[1], w_attn[2], w_query], 1)
    W_B = jnp.concatenate([w_patch[0], w_patch[1]], 1)
    W_O = jnp.concatenate([w_attn_out, w_cross_out], 0)
    shards = (W_A, W_B, W_O, w_hidden, w_output)
    GA, GB, GO, GH, GW = gather_weights(shards, gather_plan(shards, bits), nd, nz, bits[:3])
    full_bias = lax.all_gather(jnp.concatenate([attn_bias.reshape(-1), cross_bias.reshape(-1), hidden_bias]).astype(f32), "mp", axis=0)
    ab = full_bias[:, :2 * hw].reshape(nz, 2, 1, 1, hw)
    cb = full_bias[:, 2 * hw:4 * hw].reshape(nz, 2, 1, 1, hw)
    hb = full_bias[:, 4 * hw:].reshape(nz, 1, 1, -1)
    bias_rows = out_bias.astype(f32)
    x = text_states
    proj = ein("ild,zdc->zilc", x, GA[..., :3 * hw])
    q = (proj[..., :hw] + ab[:, 0]).astype(bf)
    k = proj[..., hw:2 * hw].astype(bf)
    v = (proj[..., 2 * hw:] + ab[:, 1]).astype(bf)
    self_prob = probabilities(q, k, None)
    self_mixed = attend(self_prob, v, q.shape)
    self_sum = ein("zilc,zcd->ild", self_mixed, GO[:, :hw])
    first_norm, n0, i0 = norm_forward(x.astype(f32) + self_sum + bias_rows[0], norm_gain[0], norm_shift[0])
    first = first_norm.astype(bf)
    cq = (ein("ild,zdc->zilc", first, GA[..., 3 * hw:]) + cb[:, 0]).astype(bf)
    kv = ein("ipc,zcd->zipd", patch_states, GB)
    ck = kv[..., :hw].astype(bf)
    cv = (kv[..., hw:] + cb[:, 1]).astype(bf)
    rows = lax.dynamic_slice_in_dim(patch_rows, z * ni, ni)
    positions = lax.broadcasted_iota(jnp.int32, (ni, patch_states.shape[1]), 1)
    valid = (positions < rows[:, None])[None, :, None, None, :]
    cross_prob = probabilities(cq, ck, valid)
    cross_mixed = attend(cross_prob, cv, cq.shape)
    cross_sum = ein("zilc,zcd->ild", cross_mixed, GO[:, hw:])
    second_norm, n1, i1 = norm_forward(first.astype(f32) + cross_sum + bias_rows[1], norm_gain[1], norm_shift[1])
    second = second_norm.astype(bf)
    pre = ein("ild,zdf->zilf", second, GH) + hb
    act, pull = jax.vjp(lambda p: jax.nn.gelu(p, approximate=False), pre)
    hid = act.astype(bf)
    ffn_sum = ein("zilf,zfd->ild", hid, GW)
    layer_out, n2, i2 = norm_forward(second.astype(f32) + ffn_sum + bias_rows[2], norm_gain[2], norm_shift[2])
    grad_third, gain2, shift2 = norm_backward(cotangent.astype(f32), n2, i2, norm_gain[2])
    g3 = grad_third.astype(bf)
    dW = ein("zilf,ild->zfd", hid, g3).astype(bf)
    dpre = pull(ein("ild,zfd->zilf", g3, GW))[0].astype(bf)
    dH = ein("ild,zilf->zdf", second, dpre).astype(bf)
    dhb = jnp.sum(dpre, axis=(1, 2), dtype=f32)
    grad_second, gain1, shift1 = norm_backward(grad_third + ein("zilf,zdf->ild", dpre, GH), n1, i1, norm_gain[1])
    g2 = grad_second.astype(bf)
    dO2 = ein("zilc,ild->zcd", cross_mixed, g2).astype(bf)
    cmg = ein("ild,zcd->zilc", g2, GO[:, hw:]).astype(bf)
    dcq, dck, dcv = attend_backward(cq, ck, cv, cross_prob, cmg)
    dkv = jnp.concatenate([dck, dcv], -1)
    dB = ein("ipc,ziph->zch", patch_states, dkv).astype(bf)
    dcqb = jnp.sum(dcq, axis=(1, 2), dtype=f32)
    dcvb = jnp.sum(dcv, axis=(1, 2), dtype=f32)
    patch_grad = ein("ziph,zch->ipc", dkv, GB)
    grad_first, gain0, shift0 = norm_backward(grad_second + ein("zilc,zdc->ild", dcq, GA[..., 3 * hw:]), n0, i0, norm_gain[0])
    g1 = grad_first.astype(bf)
    dO1 = ein("zilc,ild->zcd", self_mixed, g1).astype(bf)
    smg = ein("ild,zcd->zilc", g1, GO[:, :hw]).astype(bf)
    dq, dk, dv = attend_backward(q, k, v, self_prob, smg)
    dqkv = jnp.concatenate([dq, dk, dv], -1)
    dA = jnp.concatenate([ein("ild,zilc->zdc", x, dqkv).astype(bf), ein("ild,zilc->zdc", first, dcq).astype(bf)], -1)
    dO = jnp.concatenate([dO1, dO2], 1)
    text_grad = grad_first + ein("zilc,zdc->ild", dqkv, GA[..., :3 * hw])
    small = jnp.concatenate([
        jnp.sum(grad_first, axis=(0, 1)), jnp.sum(grad_second, axis=(0, 1)), jnp.sum(grad_third, axis=(0, 1)),
        gain0, gain1, gain2, shift0, shift1, shift2,
        jnp.concatenate([jnp.sum(dq, axis=(1, 2), dtype=f32), jnp.sum(dv, axis=(1, 2), dtype=f32), dcqb, dcvb, dhb], 1).reshape(-1)])
    small = lax.psum(small, ("dp", "mp"))
    D = x.shape[-1]
    grads = (dA, dB, dO, dH, dW)
    RA, RB, RO, RH, RW = reduce_grads(grads, reduce_plan(shards, bits), nz, bits)
    RA, RB, RO, RH, RW = (r.astype(f32) for r in (RA, RB, RO, RH, RW))
    rep = small[:9 * D].reshape(3, 3, D)
    own = lax.dynamic_index_in_dim(small[9 * D:].reshape(nz, -1), z, 0, False)
    return (
        layer_out, text_grad, patch_grad,
        jnp.stack([RA[:, t * hw:(t + 1) * hw] for t in range(3)]),
        own[:2 * hw].reshape(2, hw), RO[:hw], RA[:, 3 * hw:],
        jnp.stack([RB[:, :hw], RB[:, hw:]]),
        own[2 * hw:4 * hw].reshape(2, hw), RO[hw:], RH, own[4 * hw:], RW,
        rep[0], rep[1], rep[2],
    )

def gather_plan(shards, bits):
    c, x, y = bits[:3]
    a, b, o, h, w = (s.shape[0] for s in shards)
    return ((0, 0, a, (x, y, c), 0), (1, 0, b, (y, x, c), 0), (2, 0, o, (x, c), 0), (3, 0, h, (y, x, c), 0), (4, 0, w, (y, c), 0))

def reduce_plan(shards, bits):
    c, x, y = bits[:3]
    a, b, o, h, w = (s.shape[0] for s in shards)
    return ((4, 0, w, (y, x, "z"), 0), (3, 0, h, (x, y, "z"), 1), (2, 0, o, ("z", x, y), 2), (1, 0, b, (y, x, "z"), 3), (0, 0, a, (x, y, "z"), 4))

def solution(mesh):
    nd, nz = mesh.shape["dp"], mesh.shape["mp"]
    rows = P(("dp", "mp"), None, None)
    return jax.shard_map(
        functools.partial(per_device, nd, nz),
        mesh=mesh,
        in_specs=(rows, rows, P("dp"), rows, P(None, None, "mp"), P(None, "mp"), P("mp", None), P(None, "mp"), P(None, None, "mp"), P(None, "mp"), P("mp", None), P(None, "mp"), P("mp"), P("mp", None), P(), P(), P()),
        out_specs=(rows, rows, rows, P(None, None, "mp"), P(None, "mp"), P("mp", None), P(None, "mp"), P(None, None, "mp"), P(None, "mp"), P("mp", None), P(None, "mp"), P("mp"), P("mp", None), P(), P(), P()),
        check_vma=False,
    )
```

```python
import functools
import math

import jax
import jax.numpy as jnp
from jax import lax
from jax.experimental import pallas as pl
from jax.experimental.pallas import tpu as pltpu
from jax.sharding import PartitionSpec as P

MESH = pl.DeviceIdType.MESH
HEAD = 64
LANES = 128
epsilon = 1e-06
score_scale = 1.0 / math.sqrt(HEAD)
bf16, f32 = jnp.bfloat16, jnp.float32


def bit_of(d, b):
    return lax.rem(lax.div(d, jnp.int32(2 ** b)), jnp.int32(2))


def flip(d, b):
    return d + (1 - 2 * bit_of(d, b)) * (2 ** b)


def when(cond, fn):
    if cond is True:
        fn()
    else:
        pl.when(cond)(fn)


class Gather:
    def __init__(self, src, dst, row0, rows, order, d, z, nz, sems, base):
        self.src, self.dst, self.row0, self.order = src, dst, row0, order
        self.d, self.z, self.nz = d, z, nz
        self.piece = rows // (2 ** len(order))
        self.zs, self.zr, self.ps, self.pr = sems
        self.base = base
        self.k = len(order)

    def win(self, s):
        w = jnp.int32(0)
        for i, b in enumerate(self.order):
            if i >= s:
                w = w + bit_of(self.d, b) * (2 ** i)
        size = self.piece * 2 ** s
        start = self.row0 + w * self.piece
        return pl.ds(pl.multiple_of(start, 16), size)

    def shard(self, dr, j):
        return self.z - j if dr == 0 else self.z + j

    def has(self, dr, j):
        return self.z >= j if dr == 0 else self.z + j < self.nz

    def zcopy(self, dr, j):
        t = self.shard(dr, j)
        rows = self.win(0)
        src = self.src.at[rows] if j == 0 else self.dst.at[t, rows]
        to = self.z + 1 if dr == 0 else self.z - 1
        return pltpu.make_async_remote_copy(src, self.dst.at[t, rows], self.zs.at[self.base, dr, j], self.zr.at[self.base, dr, j], device_id=(self.d, to), device_id_type=MESH)

    def zcan(self, dr, j):
        ahead = self.z + 1 < self.nz if dr == 0 else self.z >= 1
        return ahead if j == 0 else jnp.logical_and(ahead, self.has(dr, j))

    def pcopy(self, s, dr, j):
        t = self.shard(dr, j)
        rows = self.win(s)
        b = self.order[s]
        return pltpu.make_async_remote_copy(self.dst.at[t, rows], self.dst.at[t, rows], self.ps.at[self.base, s, dr, j - 1], self.pr.at[self.base, s, dr, j - 1], device_id=(flip(self.d, b), self.z), device_id_type=MESH)

    def events(self):
        return self.nz + self.k

    def event(self, e):
        nz, k = self.nz, self.k
        if e == 0:
            for dr in (0, 1):
                when(self.zcan(dr, 0), lambda: self.zcopy(dr, 0).start())
            return
        for s in range(k, -1, -1):
            j = e - s
            if not 1 <= j <= nz - 1:
                continue
            for dr in (0, 1):
                def go(dr=dr, j=j, s=s):
                    if s == 0:
                        self.zcopy(dr, j - 1).wait_recv()
                        if j <= nz - 2:
                            when(self.zcan(dr, j), lambda: self.zcopy(dr, j).start())
                    else:
                        self.pcopy(s - 1, dr, j).wait_recv()
                    if s < k:
                        self.pcopy(s, dr, j).start()
                when(self.has(dr, j), go)

    def finish(self):
        nz, k = self.nz, self.k
        for dr in (0, 1):
            for j in range(nz - 1):
                when(self.zcan(dr, j), lambda dr=dr, j=j: self.zcopy(dr, j).wait_send())
            for s in range(k):
                for j in range(1, nz):
                    when(self.has(dr, j), lambda dr=dr, j=j, s=s: self.pcopy(s, dr, j).wait_send())


def add_into(dst, src, rows):
    step = 32 if rows % 32 == 0 else 16

    def body(i, c):
        r = pl.ds(pl.multiple_of(i * step, step), step)
        dst[r, :] = dst[r, :] + src[r, :]
        return c
    lax.fori_loop(0, rows // step, body, 0)


def add_all(dst, src, count, rows):
    def body(t, c):
        add_into(dst.at[t], src.at[t], rows)
        return c
    lax.fori_loop(0, count, body, 0)


def op_rows(half, order, op):
    size = half
    for o in order:
        if o == "z":
            if op == "z":
                return size
        else:
            size //= 2
            if o == op:
                return size
    return size


class Reduce:
    slots_max = 20

    def __init__(self, keep, bufs, result, pos, half, order, d, z, nz, bits, sems, base):
        self.keep = keep
        self.recvs, self.ups, self.downs, self.extra = bufs
        self.result, self.pos, self.half, self.order = result, pos, half, order
        self.d, self.z, self.nz, self.bits = d, z, nz, bits
        self.ss, self.rs, self.ls = sems
        self.base = base
        self.slot = 0
        self.pending = []
        self.steps = []
        self.build()

    def copy(self, s, src, dst, to):
        return lambda: pltpu.make_async_remote_copy(src, dst, self.ss.at[self.base, s], self.rs.at[self.base, s], device_id=to, device_id_type=MESH)

    def remote(self, src, dst, to, keep=True):
        cp = self.copy(self.slot, src, dst, to)
        self.slot += 1
        if keep:
            self.pending.append((True, cp))
        return cp

    def build(self):
        d, z, nz = self.d, self.z, self.nz
        prev = None
        start, size, whole = jnp.int32(0), self.half, True
        taken = []

        def then(prev, cp):
            def step():
                if prev is not None:
                    prev()
                cp().start()
            self.steps.append(step)

        for op in self.order:
            if op == "z":
                self.zbase = self.slot
                self.slot += 2 * nz
                self.zc = self.zcopies(start, size)
                for h in range(nz):
                    self.steps.append(functools.partial(self.zhop, h, start, size, prev if h == 0 else None))
                prev, whole = None, False
                continue
            size //= 2
            m = bit_of(d, op)
            keep0 = pl.multiple_of(start + m * size, 16)
            send0 = pl.multiple_of(start + (1 - m) * size, 16)
            buf = self.recvs[op]
            if whole:
                cp = self.remote(self.keep.at[:, pl.ds(send0, size), :], buf, (flip(d, op), z))
            else:
                cp = self.remote(self.keep.at[z, pl.ds(send0, size), :], buf.at[0], (flip(d, op), z))
            then(prev, cp)

            def prev(cp=cp, keep0=keep0, size=size, whole=whole, buf=buf):
                cp().wait_recv()
                if whole:
                    add_all(self.keep.at[:, pl.ds(keep0, size), :], buf, nz, size)
                else:
                    add_into(self.keep.at[z, pl.ds(keep0, size), :], buf.at[0], size)
            taken.append(op)
            start = keep0
        for e, b in enumerate(self.bits[3:]):
            cp = self.remote(self.keep.at[z, pl.ds(start, size), :], self.extra.at[e], (flip(d, b), z), False)
            then(prev, cp)

            def prev(cp=cp, e=e, start=start, size=size):
                cp().wait_recv()
                cp().wait_send()
                add_into(self.keep.at[z, pl.ds(start, size), :], self.extra.at[e], size)
        pos = pl.multiple_of(self.pos + start, 16)
        own = lambda pos=pos, size=size: pltpu.make_async_copy(self.keep.at[z, pl.ds(start, size), :], self.result.at[pl.ds(pos, size), :], self.ls.at[self.base])

        def place(prev=prev, own=own):
            if prev is not None:
                prev()
            own().start()
        first = True
        for op in list(reversed(taken)) + [self.bits[0]]:
            win = self.result.at[pl.ds(pos, size), :]
            if first:
                cp = self.remote(self.keep.at[z, pl.ds(start, size), :], win, (flip(d, op), z))
            else:
                cp = self.remote(win, win, (flip(d, op), z))
            if first:
                def step(cp=cp):
                    place()
                    cp().start()
                self.steps.append(step)

                def prev(cp=cp):
                    cp().wait_recv()
                    own().wait()
                first = False
            else:
                then(prev, cp)
                prev = lambda cp=cp: cp().wait_recv()
            if op != self.bits[0]:
                pos = pl.multiple_of(pos - bit_of(d, op) * size, 16)
                size *= 2
        self.steps.append(prev)

    def zcopies(self, start, size):
        out = {}
        d, z, nz = self.d, self.z, self.nz
        rows = pl.ds(start, size)
        for t in range(nz):
            src = self.keep.at[t, rows, :]
            if t >= 1:
                out["u", t] = self.copy(self.zbase + t, src, self.ups.at[t - 1], (d, z + 1))
                self.pending.append((z < t, out["u", t]))
            if t <= nz - 2:
                out["d", t] = self.copy(self.zbase + nz + t, src, self.downs.at[t], (d, z - 1))
                self.pending.append((z > t, out["d", t]))
        return out

    def zhop(self, h, start, size, prev):
        z, nz = self.z, self.nz
        if prev is not None:
            prev()
        rows = pl.ds(start, size)

        @pl.when(z == h)
        def _():
            for t in range(nz - 1, max(h, 1) - 1, -1):
                if h > 0:
                    self.zc["u", t]().wait_recv()
                    add_into(self.keep.at[t, rows, :], self.ups.at[t - 1], size)
                if t > h:
                    self.zc["u", t]().start()
        me = nz - 1 - h

        @pl.when(z == me)
        def _():
            for t in range(0, min(me, nz - 2) + 1):
                if h > 0:
                    self.zc["d", t]().wait_recv()
                    add_into(self.keep.at[t, rows, :], self.downs.at[t], size)
                if t < me:
                    self.zc["d", t]().start()

    def finish(self):
        for cond, cp in self.pending:
            when(cond, lambda: cp().wait_send())


def enter(d, z, nz, bits):
    bar = pltpu.get_barrier_semaphore()
    for b in bits:
        pl.semaphore_signal(bar, inc=1, device_id=(flip(d, b), z), device_id_type=MESH)
    for o in range(1, nz):
        pl.semaphore_signal(bar, inc=1, device_id=(d, lax.rem(z + o, jnp.int32(nz))), device_id_type=MESH)
    pl.semaphore_wait(bar, len(bits) + nz - 1)


def dot(a, b):
    return lax.dot_general(a, b, (((1,), (0,)), ((), ())), preferred_element_type=f32)


def dot_nt(a, b):
    return lax.dot_general(a, b, (((1,), (1,)), ((), ())), preferred_element_type=f32)


def dot_tn(a, b):
    return lax.dot_general(a, b, (((0,), (0,)), ((), ())), preferred_element_type=f32)


def norm_forward(h, gain, shift):
    centred = h - jnp.mean(h, -1, keepdims=True)
    inverse = lax.rsqrt(jnp.mean(centred * centred, -1, keepdims=True) + epsilon)
    normed = centred * inverse
    return normed * gain + shift, normed, inverse


def norm_backward(grad, normed, inverse, gain):
    scaled = grad * gain
    return inverse * (scaled - jnp.mean(scaled, -1, keepdims=True) - normed * jnp.mean(scaled * normed, -1, keepdims=True))


def col_sum(v):
    return jnp.sum(v, axis=0, keepdims=True)


class Dims:
    pass


def layer_kernel(m, *refs):
    n_in, n_out = len(m.inputs), len(m.outputs)
    R = dict(zip(m.inputs + m.outputs + m.scratch, refs))
    g = Dims()
    for k, v in R.items():
        setattr(g, k, v)
    ni, L, T, D, nz, hp, nh, KP, NP = m.ni, m.L, m.T, m.D, m.nz, m.hp, m.nh, m.KP, m.NP
    d, z = lax.axis_index("dp"), lax.axis_index("mp")
    core = bit_of(d, m.bits[0])
    partner = flip(d, m.bits[0])

    def shard(o):
        t = z
        for b in range(nz.bit_length() - 1):
            t = t + lax.rem(lax.div(o, jnp.int32(2 ** b)), jnp.int32(2)) * (1 - 2 * bit_of(z, b)) * (2 ** b)
        return t

    g.DCQ = g.HD.at[:, :, 0:hp]
    g.DQ = g.DP.at[:, :, 0:m.QW]

    g.VG[z] = g.vown[...]
    enter(d, z, nz, m.bits)
    gsem = (g.zs, g.zr, g.ps, g.pr)
    own = {"A": g.A, "B": g.B, "O": g.O, "H": g.H, "W": g.W, "V": g.vown}
    far = {"A": g.GA, "B": g.GB, "O": g.GO, "H": g.GH, "W": g.GW, "V": g.VG}
    gathers = [Gather(own[k], far[k], r0, rows, order, d, z, nz, gsem, c) for c, (k, r0, rows, order, _) in enumerate(m.gather_plan)]
    queue = []
    for tick in range(64):
        for c, p in enumerate(m.gather_plan):
            e = tick - p[4]
            if 0 <= e < gathers[c].events():
                queue.append((c, e))

    def advance(stop):
        names = stop if isinstance(stop, str) else ""
        while queue:
            if names:
                if not any(m.gather_plan[c][0] in names for c, e in queue):
                    return
            c, e = queue.pop(0)
            gathers[c].event(e)

    def gather_some(k):
        for _ in range(k):
            if queue:
                c, e = queue.pop(0)
                gathers[c].event(e)

    pair_slot = [0]

    def pair(ref, rows):
        s = pair_slot[0]
        pair_slot[0] += 1
        return pltpu.make_async_remote_copy(ref.at[pl.ds(0, rows)], ref.at[pl.ds(rows, rows)], g.cs.at[s], g.cr.at[s], device_id=(partner, z), device_id_type=MESH)

    def fetch(buf, sem, slot, key, rows, o):
        dst = buf.at[slot, pl.ds(0, rows[1])] if buf.shape[1] != rows[1] else buf.at[slot]
        src = pl.ds(rows[0], rows[1])

        @pl.when(o == 0)
        def _():
            pltpu.make_async_copy(own[key].at[src], dst, sem.at[slot]).start()

        @pl.when(o != 0)
        def _():
            pltpu.make_async_copy(far[key].at[shard(o), src], dst, sem.at[slot]).start()

    def arrived(buf, sem, slot, key, rows):
        dst = buf.at[slot, pl.ds(0, rows[1])] if buf.shape[1] != rows[1] else buf.at[slot]
        pltpu.make_async_copy(own[key].at[pl.ds(rows[0], rows[1])], dst, sem.at[slot]).wait()

    def stream(blocks, body, between=None):
        for buf, sem, key, rows in blocks:
            fetch(buf, sem, 0, key, rows, 0)

        def step(o, c):
            slot = lax.rem(o, jnp.int32(2))

            @pl.when(o + 1 < nz)
            def _():
                for buf, sem, key, rows in blocks:
                    fetch(buf, sem, 1 - slot, key, rows, o + 1)
            for buf, sem, key, rows in blocks:
                arrived(buf, sem, slot, key, rows)
            body(o, slot)
            if between is not None:
                between(o)
            return c
        lax.fori_loop(0, nz, step, 0)

    lane = lax.broadcasted_iota(jnp.int32, (L, hp), 1)
    low = [lane // HEAD == h for h in range(nh)]
    high = [lane // HEAD == h + 1 for h in range(nh)]

    def stack(v, masks):
        return jnp.concatenate([jnp.where(k, v, 0.0) for k in masks], axis=0).astype(bf16)

    def unstack(v, masks):
        out = jnp.where(masks[0], v[0:L], 0.0)
        for h in range(1, nh):
            out = out + jnp.where(masks[h], v[h * L:(h + 1) * L], 0.0)
        return out

    def softmax(s):
        e = jnp.exp(s - jnp.max(s, -1, keepdims=True))
        return e / jnp.sum(e, -1, keepdims=True)

    for c, p in enumerate(m.gather_plan):
        if p[4] == 0:
            gathers[c].event(0)
    queue[:] = [q for q in queue if not (q[1] == 0 and m.gather_plan[q[0]][4] == 0)]
    for i in range(ni):
        g.XF[i * L:(i + 1) * L] = g.x[i].astype(f32)
        g.PT[i * KP:i * KP + NP] = g.patches[i]
        g.PT[i * KP + NP // 16 * 16:(i + 1) * KP] = jnp.concatenate([g.patches[i, NP // 16 * 16:NP].astype(f32), jnp.zeros((KP - NP, m.PW), f32)], 0).astype(bf16)
    g.X[0:T] = g.XF[...].astype(bf16)
    swaps = [pair(g.X, T), pair(g.PT, ni * KP)]
    for s in swaps:
        s.start()

    advance("AVO")
    g.ACC[...] = jnp.zeros((T, D), f32)

    def self_forward(o, slot):
        t = shard(o)
        bias = g.VG[t].astype(f32)[0:1, LANES:]
        qkv = (dot(g.X[0:T], g.SA[slot, :, LANES:]) + bias).astype(bf16)
        g.QKV[o] = qkv
        qf = qkv.astype(f32)
        outs = []
        for i in range(ni):
            r = slice(i * L, (i + 1) * L)
            qs = stack(qf[r, 0:hp], high)
            k_i = qf[r, 3 * LANES:3 * LANES + hp].astype(bf16)
            v_i = qf[r, 2 * LANES:2 * LANES + hp].astype(bf16)
            p = softmax(dot_nt(qs, k_i) * score_scale)
            g.PS[o * ni + i] = p
            outs.append(unstack(dot(p.astype(bf16), v_i), low))
        mixed = jnp.concatenate(outs, 0).astype(bf16)
        g.MX[0, o, 0:T] = mixed
        g.ACC[...] += dot(mixed, g.SO[slot])

    self_blocks = [(g.SA, g.sa, "A", (0, D)), (g.SO, g.so, "O", (0, hp))]
    stream(self_blocks, self_forward)

    def out_row(j):
        return g.ob[j:j + 1, :], g.gain[j:j + 1, :], g.shift[j:j + 1, :]

    ob, gn, sh = out_row(0)
    first, normed, inv = norm_forward(g.XF[...] + g.ACC[...] + ob, gn, sh)
    g.NM[0] = normed
    g.INV[0] = jnp.broadcast_to(inv, (T, LANES))
    g.F[0:T] = first.astype(bf16)
    advance("B")
    g.ACC[...] = jnp.zeros((T, D), f32)

    key_pos = lax.broadcasted_iota(jnp.int32, (nh * L, KP), 1)

    def cross_forward(o, slot):
        t = shard(o)
        vb = g.VG[t].astype(f32)
        cq = (dot(g.F[0:T], g.SA[slot, :, 0:hp]) + vb[0:1, 0:hp]).astype(bf16)
        g.CQ[o] = cq
        cqf = cq.astype(f32)
        kv = (dot(g.PT[0:ni * KP], g.SB[slot]) + vb[1:2, 0:m.BW]).astype(bf16)
        g.KV[o] = kv
        outs = []
        for i in range(ni):
            qs = stack(cqf[i * L:(i + 1) * L], low)
            kvi = g.KV[o, i * KP:(i + 1) * KP]
            s = dot_nt(qs, kvi[:, 0:hp]) * score_scale
            s = jnp.where(key_pos < g.rows[z * ni + i], s, -1e30)
            p = softmax(s)
            g.PC[o * ni + i] = p
            outs.append(unstack(dot(p.astype(bf16), kvi[:, LANES:LANES + hp]), high))
        mixed = jnp.concatenate(outs, 0).astype(bf16)
        g.MX[1, o, 0:T] = mixed
        g.ACC[...] += dot(mixed, g.SO[slot])

    cross_out = (g.SO, g.so, "O", (LANES, hp))
    cross_blocks = [(g.SA, g.sa, "A", (0, D)), (g.SB, g.sb, "B", (0, m.PW)), cross_out]
    stream(cross_blocks, cross_forward)
    ob, gn, sh = out_row(1)
    second, normed, inv = norm_forward(g.F[0:T].astype(f32) + g.ACC[...] + ob, gn, sh)
    g.NM[1] = normed
    g.INV[1] = jnp.broadcast_to(inv, (T, LANES))
    g.S2[0:T] = second.astype(bf16)
    advance("H")
    other = g.MX.at[1 - core]
    mix_swap = pltpu.make_async_remote_copy(other.at[:, pl.ds(0, T)], other.at[:, pl.ds(T, T)], g.cs.at[m.swaps - 1], g.cr.at[m.swaps - 1], device_id=(partner, z), device_id_type=MESH)
    mix_swap.start()
    swaps += [pair(g.F, T), pair(g.S2, T)]
    for s in swaps[2:4]:
        s.start()

    def hidden_forward(o, slot):
        t = shard(o)
        pre = dot(g.S2[0:T], g.SA[slot]) + g.VG[t].astype(f32)[2:3, :]
        cdf = 0.5 * (1.0 + lax.erf(pre * math.sqrt(0.5)))
        g.GP[o] = cdf + pre * jnp.exp(-0.5 * pre * pre) * (1.0 / math.sqrt(2.0 * math.pi))
        g.HD[o, 0:T] = (pre * cdf).astype(bf16)

    stream([(g.SA, g.sa, "H", (0, D))], hidden_forward)
    hid_swaps = [pair(g.HD.at[o], T) for o in range(nz)]
    for s in hid_swaps:
        s.start()
    advance("W")
    g.ACC[...] = jnp.zeros((T, D), f32)

    def output_forward(o, slot):
        g.ACC[...] += dot(g.HD[o, 0:T], g.SA[slot])

    stream([(g.SA, g.sa, "W", (0, m.FZ))], output_forward)
    ob, gn, sh = out_row(2)
    final, normed, inv = norm_forward(g.S2[0:T].astype(f32) + g.ACC[...] + ob, gn, sh)
    g.layer_out[...] = final.reshape(ni, L, D)

    for i in range(ni):
        g.ACC[i * L:(i + 1) * L] = g.cot[i].astype(f32)
    cot = g.ACC[...]
    g.SM[...] = jnp.zeros(g.SM.shape, f32)

    def record(j, grad_in, grad_out, normed):
        g.SM[j:j + 1] = col_sum(grad_in)
        g.SM[3 + j:4 + j] = col_sum(grad_out * normed)
        g.SM[6 + j:7 + j] = col_sum(grad_out)

    third = norm_backward(cot, normed, inv, gn)
    record(2, third, cot, normed)
    g.G3[0:T] = third.astype(bf16)
    swap3 = pair(g.G3, T)
    swap3.start()

    rsem = (g.ss, g.rs, g.ls)
    results = {"A": g.RA, "B": g.RB, "O": g.RO, "H": g.RH, "W": g.RW}
    chunks = []
    for c, (k, h0, half, order) in enumerate(m.reduce_plan):
        recvs = {b: R[f"rv{c}_{b}"] for b in m.bits[1:3]}
        bufs = (recvs, R[f"up{c}"], R[f"dn{c}"], R.get(f"ex{c}"))
        whole = m.rows[k] // 2
        chunks.append(Reduce(R[f"kp{c}"], bufs, results[k], core * whole + h0, half, order, d, z, nz, m.bits, rsem, c))
    active = []

    def launch(k):
        for c, p in enumerate(m.reduce_plan):
            if p[0] == k:
                active.append(list(chunks[c].steps))
        pump(1)

    def pump(times):
        for _ in range(times):
            for steps in active:
                if steps:
                    steps.pop(0)()

    def plan_of(k):
        return [(c, p[1], p[2]) for c, p in enumerate(m.reduce_plan) if p[0] == k]

    def half_columns(whole, h0, half):
        return pl.ds(pl.multiple_of(core * whole + h0, LANES), half)

    swap3.wait_recv()
    for s in hid_swaps:
        s.wait_recv()

    def job_w(o, c):
        t = shard(o)
        for ch, h0, half in plan_of("W"):
            R[f"kp{ch}"][t] = dot_tn(g.HD[o, :, half_columns(m.FZ // 2, h0, half)], g.G3[...]).astype(bf16)
        return c
    lax.fori_loop(0, nz, job_w, 0)
    for s in hid_swaps:
        s.wait_send()
    launch("W")

    g.ACC[...] = third

    def hidden_backward(o, slot):
        t = shard(o)
        pre = (dot_nt(g.G3[0:T], g.SA[slot]) * g.GP[o]).astype(bf16)
        g.DP[o, 0:T] = pre
        g.SM[pl.ds(9 + t, 1)] = col_sum(pre.astype(f32))
        pltpu.make_async_remote_copy(g.DP.at[o, pl.ds(0, T)], g.DP.at[o, pl.ds(T, T)], g.ds.at[0, o], g.dr.at[0, o], device_id=(partner, z), device_id_type=MESH).start()
        g.ACC[...] += dot_nt(pre, g.SH[slot])

    stream([(g.SA, g.sa, "W", (0, m.FZ)), (g.SH, g.sh, "H", (0, D))], hidden_backward)

    def loop_wait(ref, rows, kind):
        for o in range(nz):
            cp = pltpu.make_async_remote_copy(ref.at[o, pl.ds(0, rows)], ref.at[o, pl.ds(rows, rows)], g.ds.at[kind, o], g.dr.at[kind, o], device_id=(partner, z), device_id_type=MESH)
            cp.wait()

    def loop_send(ref, rows, kind, o):
        pltpu.make_async_remote_copy(ref.at[o, pl.ds(0, rows)], ref.at[o, pl.ds(rows, rows)], g.ds.at[kind, o], g.dr.at[kind, o], device_id=(partner, z), device_id_type=MESH).start()

    gn = g.gain[1:2, :]
    normed, inv = g.NM[1], g.INV[1][:, 0:1]
    grad = g.ACC[...]
    secondg = norm_backward(grad, normed, inv, gn)
    record(1, secondg, grad, normed)
    g.G12[1, 0:T] = secondg.astype(bf16)
    swap2 = pair(g.G12.at[1], T)
    swap2.start()
    pump(1)
    loop_wait(g.DP, T, 0)
    swaps[3].wait_recv()

    def job_h(o, c):
        t = shard(o)
        for ch, h0, half in plan_of("H"):
            R[f"kp{ch}"][t] = dot_tn(g.S2[:, half_columns(D // 2, h0, half)], g.DP[o]).astype(bf16)
        return c
    lax.fori_loop(0, nz, job_h, 0)
    launch("H")

    g.ACC[...] = secondg
    g.patch_grad[...] = jnp.zeros(g.patch_grad.shape, f32)

    def backward_unit(qs, k_i, v_i, p, ms, masks):
        grad_v = dot_tn(p.astype(bf16), ms)
        grad_p = dot_nt(ms, v_i)
        gs = (p * (grad_p - jnp.sum(p * grad_p, -1, keepdims=True))).astype(bf16)
        grad_q = unstack(dot(gs, k_i), masks) * score_scale
        grad_k = dot_tn(gs, qs) * score_scale
        return grad_q, grad_k.astype(bf16).astype(f32), grad_v.astype(bf16).astype(f32)

    def cross_backward(o, slot):
        t = shard(o)
        gm = dot_nt(g.G12[1, 0:T], g.SO[slot]).astype(bf16).astype(f32)
        cqf = g.CQ[o].astype(f32)
        grads = []
        for i in range(ni):
            r = slice(i * L, (i + 1) * L)
            kvi = g.KV[o, i * KP:(i + 1) * KP]
            gq, gk, gv = backward_unit(stack(cqf[r], low), kvi[:, 0:hp], kvi[:, LANES:LANES + hp], g.PC[o * ni + i], stack(gm[r], high), low)
            grads.append(gq)
            g.DKV[o, i * KP:(i + 1) * KP] = jnp.concatenate([gk[:, 0:LANES], gk[:, LANES:] + gv[:, 0:LANES], gv[:, LANES:]], 1).astype(bf16)
        dcq = jnp.concatenate(grads, 0).astype(bf16)
        g.DCQ[o, 0:T] = dcq
        loop_send(g.DCQ, T, 1, o)
        loop_send(g.DKV, ni * KP, 2, o)
        dkv = g.DKV[o, 0:ni * KP]
        g.SM[pl.ds(9 + nz + t, 1), 0:hp] = col_sum(dcq.astype(f32))
        g.SM[pl.ds(9 + 2 * nz + t, 1), 0:m.BW] = col_sum(dkv.astype(f32))
        g.ACC[...] += dot_nt(dcq, g.SA[slot, :, 0:hp])
        for i in range(ni):
            g.patch_grad[i] += dot_nt(g.DKV[o, i * KP:(i + 1) * KP], g.SB[slot])[0:NP]

    def between(o):
        @pl.when(o == 1)
        def _():
            pump(1)

        @pl.when(o == 3)
        def _():
            pump(1)
    stream(cross_blocks, cross_backward, between)
    gn = g.gain[0:1, :]
    normed, inv = g.NM[0], g.INV[0][:, 0:1]
    grad = g.ACC[...]
    firstg = norm_backward(grad, normed, inv, gn)
    record(0, firstg, grad, normed)
    g.G12[0, 0:T] = firstg.astype(bf16)
    swap1 = pair(g.G12.at[0], T)
    swap1.start()
    pump(1)
    loop_wait(g.DCQ, T, 1)
    loop_wait(g.DKV, ni * KP, 2)
    swaps[1].wait_recv()

    def job_b(o, c):
        t = shard(o)
        for ch, h0, half in plan_of("B"):
            R[f"kp{ch}"][t] = dot_tn(g.PT[:, half_columns(m.PW // 2, h0, half)], g.DKV[o]).astype(bf16)
        return c
    lax.fori_loop(0, nz, job_b, 0)
    launch("B")

    g.ACC[...] = firstg

    def self_backward(o, slot):
        t = shard(o)
        gm = dot_nt(g.G12[0, 0:T], g.SO[slot]).astype(bf16).astype(f32)
        qf = g.QKV[o].astype(f32)
        gqs, gks, gvs = [], [], []
        for i in range(ni):
            r = slice(i * L, (i + 1) * L)
            k_i = qf[r, 3 * LANES:3 * LANES + hp].astype(bf16)
            v_i = qf[r, 2 * LANES:2 * LANES + hp].astype(bf16)
            gq, gk, gv = backward_unit(stack(qf[r, 0:hp], high), k_i, v_i, g.PS[o * ni + i], stack(gm[r], low), high)
            gqs.append(gq)
            gks.append(gk)
            gvs.append(gv)
        gq, gk, gv = (jnp.concatenate(v, 0) for v in (gqs, gks, gvs))
        dq = jnp.concatenate([gq, gv[:, 0:LANES], gv[:, LANES:] + gk[:, 0:LANES], gk[:, LANES:]], 1).astype(bf16)
        g.DQ[o, 0:T] = dq
        loop_send(g.DQ, T, 3, o)
        g.SM[pl.ds(9 + 3 * nz + t, 1), 0:m.QW] = col_sum(dq.astype(f32))
        g.ACC[...] += dot_nt(dq, g.SA[slot, :, LANES:])

    stream(self_blocks, self_backward, between)
    g.text_grad[...] = g.ACC[...].reshape(ni, L, D)
    pump(1)
    loop_wait(g.DQ, T, 3)
    swap1.wait_recv()
    swap2.wait_recv()
    for s in swaps[0:1] + swaps[2:3] + [mix_swap]:
        s.wait_recv()

    def job_o(o, c):
        t = shard(o)
        g.TMP[...] = dot_tn(g.MX[core, o], g.G12[core])
        for ch, h0, half in plan_of("O"):
            R[f"kp{ch}"][t] = g.TMP[pl.ds(pl.multiple_of(core * HEAD + h0, 16), half)].astype(bf16)
        return c
    lax.fori_loop(0, nz, job_o, 0)
    launch("O")

    def job_a(o, c):
        t = shard(o)
        for ch, h0, half in plan_of("A"):
            cols = half_columns(D // 2, h0, half)
            kp = R[f"kp{ch}"]
            left = dot_tn(g.F[:, cols], g.DCQ[o])
            right = dot_tn(g.X[:, cols], g.DQ[o])
            kp[t, :, 0:LANES] = left[:, 0:LANES].astype(bf16)
            kp[t, :, LANES:hp] = (left[:, LANES:] + right[:, 0:LANES]).astype(bf16)
            kp[t, :, hp:] = right[:, LANES:].astype(bf16)
        return c
    lax.fori_loop(0, nz, job_a, 0)
    launch("A")

    sends = []
    for i, b in enumerate(m.bits):
        cp = pltpu.make_async_remote_copy(g.SM, g.SR.at[i], g.ms.at[i], g.mr.at[i], device_id=(flip(d, b), z), device_id_type=MESH)
        cp.start()
        pump(1)
        cp.wait()
        g.SM[...] += g.SR[i]
    g.SZ[z] = g.SM[...]
    nb = len(m.bits)
    for o in range(1, nz):
        to = lax.rem(z + o, jnp.int32(nz))
        cp = pltpu.make_async_remote_copy(g.SM, g.SZ.at[z], g.ms.at[nb + o], g.zm.at[z], device_id=(d, to), device_id_type=MESH)
        cp.start()
        sends.append(cp)
    pump(1)
    for o in range(1, nz):
        frm = lax.rem(z + o, jnp.int32(nz))
        pltpu.make_async_remote_copy(g.SM, g.SZ.at[frm], g.ms.at[nb + o], g.zm.at[frm], device_id=(d, frm), device_id_type=MESH).wait_recv()
    total = g.SZ[0]
    for t in range(1, nz):
        total = total + g.SZ[t]
    g.small[...] = total
    while any(active):
        pump(1)

    for cp in sends + swaps + [swap1, swap2, swap3, mix_swap]:
        cp.wait_send()
    for q in gathers:
        q.finish()
    for c in chunks:
        c.finish()


def gather_plan(rows, bits):
    c, x, y = bits[:3]
    a, b, o, h, w = (rows[k] for k in "ABOHW")
    return (
        ("V", 0, 16, (), 0), ("A", 0, a, (x, y, c), 0), ("O", 0, o, (x, c), 1), ("B", 0, b, (y, x, c), 1), ("H", 0, h, (y, x, c), 2), ("W", 0, w, (y, c), 2),
    )


def reduce_plan(rows, bits):
    c, x, y = bits[:3]
    plan = []
    for k in "WHBOA":
        half = rows[k] // 2
        orders = [(y, x, "z"), (x, "z", y), ("z", y, x)]
        unit = 64 if k == "O" else LANES
        n = half // unit
        cuts = [n * (i + 1) // 3 - n * i // 3 for i in range(3)]
        h0 = 0
        for cut, order in zip(cuts, orders):
            plan.append((k, h0, cut * unit, order))
            h0 += cut * unit
    return tuple(plan)


def run_layer(m, nd, shards, vown, x, patches, rows, cot, ob, gain, shift):
    nz = m.nz
    ni, L, D = x.shape
    T = ni * L
    m.ni, m.L, m.D, m.T = ni, L, D, T
    m.NP, m.PW = patches.shape[1:]
    m.KP = (m.NP + 15) // 16 * 16
    hw = D // nz
    m.nh = hw // HEAD
    m.hp = (hw + HEAD + LANES - 1) // LANES * LANES
    hp, KP, PW = m.hp, m.KP, m.PW
    A, B, O, H, W = shards
    m.BW, m.QW, m.FZ = B.shape[1], D - LANES, W.shape[0]
    FZ = m.FZ
    m.rows = {k: s.shape[0] for k, s in zip("ABOHW", shards)}
    lanes = {k: s.shape[1] for k, s in zip("ABOHW", shards)}
    m.gather_plan = gather_plan(m.rows, m.bits)
    m.reduce_plan = reduce_plan(m.rows, m.bits)
    m.swaps = nz + 9
    V, sem = pltpu.VMEM, pltpu.SemaphoreType.DMA
    nc, ng = len(m.reduce_plan), len(m.gather_plan)
    nb = len(m.bits)
    sums = (9 + 4 * nz + 7) // 8 * 8
    scratch = dict(
        VG=V((nz, 16, D), bf16), XF=V((T, D), f32), X=V((2 * T, D), bf16), PT=V((2 * ni * KP, PW), bf16),
        SA=V((2, D, D), bf16), SH=V((2, D, D), bf16), SB=V((2, PW, m.BW), bf16), SO=V((2, hp, D), bf16),
        ACC=V((T, D), f32), QKV=V((nz, T, m.QW), bf16), PS=V((nz * ni, m.nh * L, L), f32), MX=V((2, nz, 2 * T, hp), bf16),
        NM=V((2, T, D), f32), INV=V((2, T, LANES), f32), F=V((2 * T, D), bf16), S2=V((2 * T, D), bf16),
        CQ=V((nz, T, hp), bf16), KV=V((nz, ni * KP, m.BW), bf16), PC=V((nz * ni, m.nh * L, KP), f32),
        GP=V((nz, T, FZ), f32), HD=V((nz, 2 * T, FZ), bf16), SM=V((sums, D), f32), G3=V((2 * T, D), bf16), DP=V((nz, 2 * T, FZ), bf16),
        G12=V((2, 2 * T, D), bf16), DKV=V((nz, 2 * ni * KP, m.BW), bf16),
        TMP=V((hp, D), f32), SR=V((nb, sums, D), f32), SZ=V((nz, sums, D), f32),
        zs=sem((ng, 2, nz)), zr=sem((ng, 2, nz)), ps=sem((ng, 3, 2, nz)), pr=sem((ng, 3, 2, nz)),
        cs=sem((m.swaps,)), cr=sem((m.swaps,)), ds=sem((4, nz)), dr=sem((4, nz)),
        sa=sem((2,)), sh=sem((2,)), sb=sem((2,)), so=sem((2,)),
        ss=sem((nc, Reduce.slots_max)), rs=sem((nc, Reduce.slots_max)), ls=sem((nc,)), ms=sem((nb + nz,)), mr=sem((nb,)), zm=sem((nz,)),
    )
    for c, (k, h0, half, order) in enumerate(m.reduce_plan):
        C = lanes[k]
        scratch[f"kp{c}"] = V((nz, half, C), bf16)
        for b in m.bits[1:3]:
            lead = nz if order.index(b) < order.index("z") else 1
            scratch[f"rv{c}_{b}"] = V((lead, op_rows(half, order, b), C), bf16)
        for n in ("up", "dn"):
            scratch[f"{n}{c}"] = V((nz - 1, op_rows(half, order, "z"), C), bf16)
        if nb > 3:
            scratch[f"ex{c}"] = V((nb - 3, half // 4, C), bf16)
    S = jax.ShapeDtypeStruct
    hbm, vm, sm = (pl.BlockSpec(memory_space=s) for s in (pl.ANY, pltpu.VMEM, pltpu.SMEM))
    outs = dict(
        layer_out=(S((ni, L, D), f32), vm), text_grad=(S((ni, L, D), f32), vm), patch_grad=(S((ni, m.NP, PW), f32), vm), small=(S((sums, D), f32), vm),
        **{"R" + k: (S(s.shape, bf16), hbm) for k, s in zip("ABOHW", shards)},
        **{"G" + k: (S((nz,) + s.shape, bf16), hbm) for k, s in zip("ABOHW", shards)},
    )
    ins = dict(x=(x, vm), patches=(patches, vm), rows=(rows, sm), cot=(cot, vm), A=(A, hbm), B=(B, hbm), O=(O, hbm), H=(H, hbm), W=(W, hbm),
               vown=(vown, vm), ob=(ob, vm), gain=(gain, vm), shift=(shift, vm))
    m.inputs, m.outputs, m.scratch = list(ins), list(outs), list(scratch)
    res = pl.pallas_call(
        functools.partial(layer_kernel, m),
        out_shape=tuple(o[0] for o in outs.values()),
        in_specs=[i[1] for i in ins.values()],
        out_specs=tuple(o[1] for o in outs.values()),
        scratch_shapes=list(scratch.values()),
        compiler_params=pltpu.CompilerParams(collective_id=0, has_side_effects=True, vmem_limit_bytes=67043328),
        name="layer",
    )(*[i[0] for i in ins.values()])
    return dict(zip(outs, res))


def per_device(nd, nz, text_states, patch_states, patch_rows, cotangent, w_attn, attn_bias, w_attn_out, w_query, w_patch, cross_bias, w_cross_out, w_hidden, hidden_bias, w_output, out_bias, norm_gain, norm_shift):
    m = Dims()
    m.nz, m.bits = nz, tuple(range(nd.bit_length() - 1))
    z = lax.axis_index("mp")
    hw = w_query.shape[1]
    D = text_states.shape[-1]
    A = jnp.concatenate([w_query, w_attn[0], w_attn[2], w_attn[1]], 1)
    B = jnp.concatenate([w_patch[0], w_patch[1]], 1)
    O = jnp.concatenate([w_attn_out, w_cross_out], 0)
    zero = jnp.zeros((hw,), bf16)
    vown = jnp.stack([
        jnp.concatenate([cross_bias[0], attn_bias[0], attn_bias[1], zero]),
        jnp.pad(jnp.concatenate([zero, cross_bias[1]]), (0, D - 2 * hw)), hidden_bias])
    vown = jnp.pad(vown, ((0, 13), (0, 0)))
    r = run_layer(m, nd, (A, B, O, w_hidden, w_output), vown, text_states, patch_states, patch_rows, cotangent, out_bias.astype(f32), norm_gain.astype(f32), norm_shift.astype(f32))
    RA, RB, RO, RH, RW = (r["R" + k].astype(f32) for k in "ABOHW")
    small = r["small"]
    pick = lambda base: lax.dynamic_slice_in_dim(small, base + z, 1, 0)[0]
    cq, kv, qv = pick(9 + nz), pick(9 + 2 * nz), pick(9 + 3 * nz)
    at = hw - LANES
    part = lambda a, i: a[:, i * hw:(i + 1) * hw]
    return (
        r["layer_out"], r["text_grad"], r["patch_grad"],
        jnp.stack([part(RA, 1), part(RA, 3), part(RA, 2)]),
        jnp.stack([qv[at:at + hw], qv[at + hw:at + 2 * hw]]),
        RO[:hw], part(RA, 0), jnp.stack([part(RB, 0), part(RB, 1)]),
        jnp.stack([cq[:hw], kv[hw:2 * hw]]), RO[hw:], RH, pick(9), RW,
        small[0:3], small[3:6], small[6:9],
    )


def solution(mesh):
    nd, nz = mesh.shape["dp"], mesh.shape["mp"]
    rows = P(("dp", "mp"), None, None)
    return jax.shard_map(
        functools.partial(per_device, nd, nz),
        mesh=mesh,
        in_specs=(rows, rows, P("dp"), rows, P(None, None, "mp"), P(None, "mp"), P("mp", None), P(None, "mp"), P(None, None, "mp"), P(None, "mp"), P("mp", None), P(None, "mp"), P("mp"), P("mp", None), P(), P(), P()),
        out_specs=(rows, rows, rows, P(None, None, "mp"), P(None, "mp"), P("mp", None), P(None, "mp"), P(None, None, "mp"), P(None, "mp"), P("mp", None), P(None, "mp"), P("mp"), P("mp", None), P(), P(), P()),
        check_vma=False,
    )
```

```python
import functools
import math

import jax
import jax.numpy as jnp
from jax import lax
from jax.experimental import pallas as pl
from jax.experimental.pallas import tpu as pltpu
from jax.sharding import PartitionSpec as P

MESH = pl.DeviceIdType.MESH
HEAD = 64
LANES = 128
epsilon = 1e-06
DEV = set()
score_scale = 1.0 / math.sqrt(HEAD)
bf16, f32 = jnp.bfloat16, jnp.float32


def bit_of(d, b):
    return lax.rem(lax.div(d, jnp.int32(2 ** b)), jnp.int32(2))


def flip(d, b):
    return d + (1 - 2 * bit_of(d, b)) * (2 ** b)


def when(cond, fn):
    if cond is True:
        fn()
    else:
        pl.when(cond)(fn)


class Gather:
    def __init__(self, src, dst, row0, rows, order, pos, sems, base):
        self.src, self.dst, self.row0, self.order, self.pos = src, dst, row0, order, pos
        self.piece = rows // (2 ** len(order))
        self.zs, self.zr, self.ps, self.pr = sems
        self.base = base
        self.k = len(order)

    def win(self, s):
        w = jnp.int32(0)
        for i, b in enumerate(self.order):
            if i >= s:
                w = w + bit_of(self.pos.d, b) * (2 ** i)
        return pl.ds(pl.multiple_of(self.row0 + w * self.piece, 16), self.piece * 2 ** s)

    def shard(self, dr, j):
        return self.pos.z + j * (2 * dr - 1) * self.pos.sign

    def zcopy(self, dr, j):
        p = self.pos
        t, rows = self.shard(dr, j), self.win(0)
        src = self.src.at[rows] if j == 0 else self.dst.at[t, rows]
        real = dr + p.upper - 2 * dr * p.upper
        return pltpu.make_async_remote_copy(src, self.dst.at[t, rows], self.zs.at[self.base, real, j], self.zr.at[self.base, real, j], device_id=(p.d, p.z + (1 - 2 * dr) * p.sign), device_id_type=MESH)

    def pcopy(self, s, dr, j):
        p = self.pos
        part = self.dst.at[self.shard(dr, j), self.win(s)]
        return pltpu.make_async_remote_copy(part, part, self.ps.at[self.base, s, dr, j - 1], self.pr.at[self.base, s, dr, j - 1], device_id=(flip(p.d, self.order[s]), p.z), device_id_type=MESH)

    @staticmethod
    def has(cls, nz, dr, j):
        return cls >= j if dr == 0 else cls + j < nz

    @staticmethod
    def ahead(cls, dr):
        return dr == 0 or cls >= 1

    def item(self, cls, nz, st, dr, j):
        if st == -1:
            self.zcopy(dr, 0).start()
            return
        if st == 0:
            self.zcopy(dr, j - 1).wait_recv()
            if j <= nz - 2 and self.ahead(cls, dr):
                self.zcopy(dr, j).start()
        else:
            self.pcopy(st - 1, dr, j).wait_recv()
        if st < self.k:
            self.pcopy(st, dr, j).start()

    def finish(self, cls, nz):
        for dr in (0, 1):
            for j in range(nz - 1):
                if self.ahead(cls, dr) and self.has(cls, nz, dr, j):
                    self.zcopy(dr, j).wait_send()
            for s in range(self.k):
                for j in range(1, nz):
                    if self.has(cls, nz, dr, j):
                        self.pcopy(s, dr, j).wait_send()


def add_into(dst, src, rows):
    step = 32 if rows % 32 == 0 else 16

    def body(i, c):
        r = pl.ds(pl.multiple_of(i * step, step), step)
        dst[r, :] = dst[r, :] + src[r, :]
        return c
    lax.fori_loop(0, rows // step, body, 0)


def add_all(dst, src, count, rows):
    def body(t, c):
        add_into(dst.at[t], src.at[t], rows)
        return c
    lax.fori_loop(0, count, body, 0)


def op_rows(half, order, op):
    size = half
    for o in order:
        if o == "z":
            if op == "z":
                return size
        else:
            size //= 2
            if o == op:
                return size
    return size


class Reduce:
    def __init__(self, keep, recvs, line, extra, result, row, half, order, pos, nz, bits, sems, base):
        self.keep, self.recvs, self.line, self.extra = keep, recvs, line, extra
        self.result, self.row, self.half, self.order = result, row, half, order
        self.pos, self.nz, self.bits = pos, nz, bits
        self.ss, self.rs, self.ls = sems
        self.base = base
        self.slot = 2 * nz
        self.pending = []
        self.steps = []
        self.build()

    def copy(self, s, src, dst, to):
        return lambda: pltpu.make_async_remote_copy(src, dst, self.ss.at[self.base, s], self.rs.at[self.base, s], device_id=to, device_id_type=MESH)

    def remote(self, src, dst, b, keep=True):
        cp = self.copy(self.slot, src, dst, (flip(self.pos.d, b), self.pos.z))
        self.slot += 1
        if keep:
            self.pending.append(cp)
        return cp

    def build(self):
        d, z, nz = self.pos.d, self.pos.z, self.nz
        prev = lambda: None
        start, size, whole = jnp.int32(0), self.half, True
        taken = []

        def then(prev, cp):
            def step():
                prev()
                cp().start()
            self.steps.append(step)

        for op in self.order:
            if op == "z":
                self.rows = pl.ds(start, size)
                self.size = size
                self.steps.append(prev)
                prev, whole = (lambda: None), False
                continue
            size //= 2
            m = bit_of(d, op)
            keep0 = pl.multiple_of(start + m * size, 16)
            send0 = pl.multiple_of(start + (1 - m) * size, 16)
            buf = self.recvs[op]
            if whole:
                cp = self.remote(self.keep.at[:, pl.ds(send0, size), :], buf, op)
            else:
                cp = self.remote(self.keep.at[z, pl.ds(send0, size), :], buf.at[0], op)
            then(prev, cp)

            def prev(cp=cp, keep0=keep0, size=size, whole=whole, buf=buf):
                cp().wait_recv()
                if whole:
                    add_all(self.keep.at[:, pl.ds(keep0, size), :], buf, nz, size)
                else:
                    add_into(self.keep.at[z, pl.ds(keep0, size), :], buf.at[0], size)
            taken.append(op)
            start = keep0
        for e, b in enumerate(self.bits[3:]):
            cp = self.remote(self.keep.at[z, pl.ds(start, size), :], self.extra.at[e], b, False)

            def prev(before=prev, cp=cp, e=e, start=start, size=size):
                before()
                cp().start()
                cp().wait()
                add_into(self.keep.at[z, pl.ds(start, size), :], self.extra.at[e], size)
        at = pl.multiple_of(self.row + start, 16)
        total = self.keep.at[z, pl.ds(start, size), :]
        win = self.result.at[pl.ds(at, size), :]
        own = lambda win=win: pltpu.make_async_copy(total, win, self.ls.at[self.base])
        op = taken[-1]
        cp = self.remote(total, win, op)

        def step(prev=prev, cp=cp):
            prev()
            own().start()
            cp().start()
        self.steps.append(step)

        def prev(cp=cp):
            cp().wait_recv()
            own().wait()
        for nxt in taken[-2::-1] + [self.bits[0]]:
            at = pl.multiple_of(at - bit_of(d, op) * size, 16)
            size *= 2
            op = nxt
            win = self.result.at[pl.ds(at, size), :]
            cp = self.remote(win, win, op)
            then(prev, cp)
            prev = lambda cp=cp: cp().wait_recv()
        self.steps.append(prev)

    def hop(self, kind, i):
        p, nz = self.pos, self.nz
        far, near = nz - 1 - i, i
        if kind == 1:
            t = far * (1 - p.upper) + near * p.upper
            flow, to = p.upper, p.z + p.sign
        else:
            t = near * (1 - p.upper) + far * p.upper
            flow, to = 1 - p.upper, p.z - p.sign
        cell = self.keep.at[t, self.rows, :]
        land = self.line.at[flow, nz - 2 - i]
        s = flow * nz + i
        cp = lambda: pltpu.make_async_remote_copy(cell, land, self.ss.at[self.base, s], self.rs.at[self.base, s], device_id=(p.d, to), device_id_type=MESH)
        return cp, cell, land

    def sends(self, cls, kind):
        return self.nz - 1 - cls if kind == 1 else cls

    def along(self, cls, kind, i):
        if kind == 1 and cls == 0:
            for k in range(self.nz - 1):
                self.hop(1, k)[0]().start()
            return
        cp, cell, land = self.hop(kind, i)
        cp().wait_recv()
        add_into(cell, land, self.size)
        if i < self.sends(cls, kind):
            cp().start()

    def finish(self, cls):
        for cp in self.pending:
            cp().wait_send()
        for kind in (1, 2):
            for i in range(self.sends(cls, kind)):
                self.hop(kind, i)[0]().wait_send()


def enter(d, z, nz, bits):
    bar = pltpu.get_barrier_semaphore()
    for b in bits:
        pl.semaphore_signal(bar, inc=1, device_id=(flip(d, b), z), device_id_type=MESH)
    for o in range(1, nz):
        pl.semaphore_signal(bar, inc=1, device_id=(d, lax.rem(z + o, jnp.int32(nz))), device_id_type=MESH)
    pl.semaphore_wait(bar, len(bits) + nz - 1)


def dot(a, b):
    return lax.dot_general(a, b, (((1,), (0,)), ((), ())), preferred_element_type=f32)


def dot_nt(a, b):
    return lax.dot_general(a, b, (((1,), (1,)), ((), ())), preferred_element_type=f32)


def dot_tn(a, b):
    return lax.dot_general(a, b, (((0,), (0,)), ((), ())), preferred_element_type=f32)


def norm_forward(h, gain, shift):
    centred = h - jnp.mean(h, -1, keepdims=True)
    inverse = lax.rsqrt(jnp.mean(centred * centred, -1, keepdims=True) + epsilon)
    normed = centred * inverse
    return normed * gain + shift, normed, inverse


def norm_backward(grad, normed, inverse, gain):
    scaled = grad * gain
    return inverse * (scaled - jnp.mean(scaled, -1, keepdims=True) - normed * jnp.mean(scaled * normed, -1, keepdims=True))


def col_sum(v):
    return jnp.sum(v, axis=0, keepdims=True)


class Dims:
    pass


def layer_kernel(m, *refs):
    n_in, n_out = len(m.inputs), len(m.outputs)
    R = dict(zip(m.inputs + m.outputs + m.scratch, refs))
    g = Dims()
    for k, v in R.items():
        setattr(g, k, v)
    ni, L, T, D, nz, hp, nh, KP, NP = m.ni, m.L, m.T, m.D, m.nz, m.hp, m.nh, m.KP, m.NP
    d, z = lax.axis_index("dp"), lax.axis_index("mp")
    core = bit_of(d, m.bits[0])
    partner = flip(d, m.bits[0])

    def shard(o):
        t = z
        for b in range(nz.bit_length() - 1):
            t = t + lax.rem(lax.div(o, jnp.int32(2 ** b)), jnp.int32(2)) * (1 - 2 * bit_of(z, b)) * (2 ** b)
        return t

    g.DCQ = g.HD.at[:, :, 0:hp]
    g.DQ = g.DP.at[:, :, 0:m.QW]

    pos = Dims()
    pos.d, pos.z = d, z
    pos.upper = lax.div(2 * z, jnp.int32(nz))
    pos.sign = 1 - 2 * pos.upper
    kind = z * (1 - pos.upper) + (nz - 1 - z) * pos.upper
    classes = range(nz // 2)

    g.VG[z] = g.vown[...]
    enter(d, z, nz, m.bits)
    gsem = (g.zs, g.zr, g.ps, g.pr)
    own = {"A": g.A, "B": g.B, "O": g.O, "H": g.H, "W": g.W, "V": g.vown}
    far = {"A": g.GA, "B": g.GB, "O": g.GO, "H": g.GH, "W": g.GW, "V": g.VG}
    gathers = [Gather(own[k], far[k], r0, rows, order, pos, gsem, c) for c, (k, r0, rows, order) in enumerate(m.gather_plan)]
    calls = [0, 0]

    def gather_steps():
        at = calls[0]
        calls[0] += 1
        if "nog" in DEV:
            return
        for cls in classes:
            todo = m.gather_steps[cls][at]
            if todo:
                @pl.when(kind == cls)
                def _():
                    for c, st, dr, j in todo:
                        gathers[c].item(cls, nz, st, dr, j)

    def reduce_steps():
        at = calls[1]
        calls[1] += 1
        if "nor" in DEV:
            return
        for cls in classes:
            todo = m.reduce_steps[cls][at]
            if todo:
                @pl.when(kind == cls)
                def _():
                    for c, what in todo:
                        i = progress[cls, c, what]
                        progress[cls, c, what] += 1
                        if what == 0:
                            chunks[c].steps[i]()
                        else:
                            chunks[c].along(cls, what, i)

    def after_each(steps):
        def between(o):
            for q in range(nz - 1):
                pl.when(o == q)(lambda: steps())
        return between

    def finish_gather():
        if "nog" not in DEV:
            for cls in classes:
                @pl.when(kind == cls)
                def _():
                    for q in gathers:
                        q.finish(cls, nz)

    pair_slot = [0]

    def pair(ref, rows):
        s = pair_slot[0]
        pair_slot[0] += 1
        return pltpu.make_async_remote_copy(ref.at[pl.ds(0, rows)], ref.at[pl.ds(rows, rows)], g.cs.at[s], g.cr.at[s], device_id=(partner, z), device_id_type=MESH)

    def place(block, slot):
        buf, sem, key, rows, cols = block
        return buf.at[slot, pl.ds(0, rows[1]), pl.ds(*cols)], sem.at[slot]

    def fetch(block, slot, o):
        buf, sem, key, rows, cols = block
        dst, done = place(block, slot)
        r, c = pl.ds(*rows), pl.ds(*cols)

        def mine():
            pltpu.make_async_copy(own[key].at[r, c], dst, done).start()

        def other():
            pltpu.make_async_copy(far[key].at[shard(o), r, c], dst, done).start()
        if isinstance(o, int):
            mine()
        else:
            pl.when(o == 0)(mine)
            pl.when(o != 0)(other)

    def arrived(block, slot):
        buf, sem, key, rows, cols = block
        dst, done = place(block, slot)
        pltpu.make_async_copy(own[key].at[pl.ds(*rows), pl.ds(*cols)], dst, done).wait()

    def stream(blocks, body, between, ahead):
        def step(o, c):
            slot = lax.rem(o, jnp.int32(2))

            @pl.when(o + 1 < nz)
            def _():
                for b in blocks:
                    fetch(b, 1 - slot, o + 1)

            @pl.when(o + 1 == nz)
            def _():
                for b in ahead:
                    fetch(b, 0, 0)
            for b in blocks:
                arrived(b, slot)
            body(o, slot)
            between(o)
            return c
        lax.fori_loop(0, nz, step, 0)

    FZ, PW, BW = m.FZ, m.PW, m.BW
    self_blocks = [(g.SA, g.sa, "A", (0, D), (LANES, D - LANES)), (g.SO, g.so, "O", (0, hp), (0, D))]
    cross_blocks = [(g.SA, g.sa, "A", (0, D), (0, hp)), (g.SB, g.sb, "B", (0, PW), (0, BW)), (g.SO, g.so, "O", (LANES, hp), (0, D))]
    hidden_blocks = [(g.SA, g.sa, "H", (0, D), (0, FZ))]
    output_blocks = [(g.SA, g.sa, "W", (0, FZ), (0, D))]
    back_blocks = output_blocks + [(g.SH, g.sh, "H", (0, D), (0, FZ))]
    self_back = [(g.SA, g.sa, "A", (0, D), (LANES, D - LANES)), (g.SO, g.so, "O", (0, hp), (0, D))]
    for b in self_blocks:
        fetch(b, 0, 0)

    lane = lax.broadcasted_iota(jnp.int32, (L, hp), 1)
    low = [lane // HEAD == h for h in range(nh)]
    high = [lane // HEAD == h + 1 for h in range(nh)]

    def stack(v, masks):
        return jnp.concatenate([jnp.where(k, v, 0.0) for k in masks], axis=0).astype(bf16)

    def unstack(v, masks):
        out = jnp.where(masks[0], v[0:L], 0.0)
        for h in range(1, nh):
            out = out + jnp.where(masks[h], v[h * L:(h + 1) * L], 0.0)
        return out

    def softmax(s):
        e = jnp.exp(s - jnp.max(s, -1, keepdims=True))
        return e / jnp.sum(e, -1, keepdims=True)

    for i in range(ni):
        g.XF[i * L:(i + 1) * L] = g.x[i].astype(f32)
        g.PT[i * KP:i * KP + NP] = g.patches[i]
        g.PT[i * KP + NP // 16 * 16:(i + 1) * KP] = jnp.concatenate([g.patches[i, NP // 16 * 16:NP].astype(f32), jnp.zeros((KP - NP, m.PW), f32)], 0).astype(bf16)
    g.X[0:T] = g.XF[...].astype(bf16)
    swaps = [pair(g.X, T), pair(g.PT, ni * KP)]
    for s in swaps:
        s.start()

    g.ACC[...] = jnp.zeros((T, D), f32)
    gather_steps()

    def self_forward(o, slot):
        t = shard(o)
        bias = g.VG[t].astype(f32)[0:1, LANES:]
        qkv = (dot(g.X[0:T], g.SA[slot, :, LANES:]) + bias).astype(bf16)
        g.QKV[o] = qkv
        qf = qkv.astype(f32)
        outs = []
        for i in range(ni):
            r = slice(i * L, (i + 1) * L)
            qs = stack(qf[r, 0:hp], high)
            k_i = qf[r, 3 * LANES:3 * LANES + hp].astype(bf16)
            v_i = qf[r, 2 * LANES:2 * LANES + hp].astype(bf16)
            p = softmax(dot_nt(qs, k_i) * score_scale)
            g.PS[o * ni + i] = p
            outs.append(unstack(dot(p.astype(bf16), v_i), low))
        mixed = jnp.concatenate(outs, 0).astype(bf16)
        g.MX[0, o, 0:T] = mixed
        g.ACC[...] += dot(mixed, g.SO[slot])

    stream(self_blocks, self_forward, after_each(gather_steps), cross_blocks)

    def out_row(j):
        return g.ob[j:j + 1, :], g.gain[j:j + 1, :], g.shift[j:j + 1, :]

    ob, gn, sh = out_row(0)
    first, normed, inv = norm_forward(g.XF[...] + g.ACC[...] + ob, gn, sh)
    g.NM[0] = normed
    g.INV[0] = jnp.broadcast_to(inv, (T, LANES))
    g.F[0:T] = first.astype(bf16)
    g.ACC[...] = jnp.zeros((T, D), f32)
    gather_steps()

    key_pos = lax.broadcasted_iota(jnp.int32, (nh * L, KP), 1)

    def cross_forward(o, slot):
        t = shard(o)
        vb = g.VG[t].astype(f32)
        cq = (dot(g.F[0:T], g.SA[slot, :, 0:hp]) + vb[0:1, 0:hp]).astype(bf16)
        g.CQ[o] = cq
        cqf = cq.astype(f32)
        kv = (dot(g.PT[0:ni * KP], g.SB[slot]) + vb[1:2, 0:m.BW]).astype(bf16)
        g.KV[o] = kv
        outs = []
        for i in range(ni):
            qs = stack(cqf[i * L:(i + 1) * L], low)
            kvi = g.KV[o, i * KP:(i + 1) * KP]
            s = dot_nt(qs, kvi[:, 0:hp]) * score_scale
            s = jnp.where(key_pos < g.rows[z * ni + i], s, -1e30)
            p = softmax(s)
            g.PC[o * ni + i] = p
            outs.append(unstack(dot(p.astype(bf16), kvi[:, LANES:LANES + hp]), high))
        mixed = jnp.concatenate(outs, 0).astype(bf16)
        g.MX[1, o, 0:T] = mixed
        g.ACC[...] += dot(mixed, g.SO[slot])

    stream(cross_blocks, cross_forward, after_each(gather_steps), hidden_blocks)
    ob, gn, sh = out_row(1)
    second, normed, inv = norm_forward(g.F[0:T].astype(f32) + g.ACC[...] + ob, gn, sh)
    g.NM[1] = normed
    g.INV[1] = jnp.broadcast_to(inv, (T, LANES))
    g.S2[0:T] = second.astype(bf16)
    gather_steps()
    other = g.MX.at[1 - core]
    mix_swap = pltpu.make_async_remote_copy(other.at[:, pl.ds(0, T)], other.at[:, pl.ds(T, T)], g.cs.at[m.swaps - 1], g.cr.at[m.swaps - 1], device_id=(partner, z), device_id_type=MESH)
    mix_swap.start()
    swaps += [pair(g.F, T), pair(g.S2, T)]
    for s in swaps[2:4]:
        s.start()

    def hidden_forward(o, slot):
        t = shard(o)
        pre = dot(g.S2[0:T], g.SA[slot]) + g.VG[t].astype(f32)[2:3, :]
        cdf = 0.5 * (1.0 + lax.erf(pre * math.sqrt(0.5)))
        g.GP[o] = cdf + pre * jnp.exp(-0.5 * pre * pre) * (1.0 / math.sqrt(2.0 * math.pi))
        g.HD[o, 0:T] = (pre * cdf).astype(bf16)

    stream(hidden_blocks, hidden_forward, after_each(gather_steps), output_blocks)
    hid_swaps = [pair(g.HD.at[o], T) for o in range(nz)]
    for s in hid_swaps:
        s.start()
    g.ACC[...] = jnp.zeros((T, D), f32)
    gather_steps()

    def output_forward(o, slot):
        g.ACC[...] += dot(g.HD[o, 0:T], g.SA[slot])

    stream(output_blocks, output_forward, after_each(gather_steps), back_blocks)
    gather_steps()
    ob, gn, sh = out_row(2)
    final, normed, inv = norm_forward(g.S2[0:T].astype(f32) + g.ACC[...] + ob, gn, sh)
    g.layer_out[...] = final.reshape(ni, L, D)

    if "fwd" in DEV:
        for cp in swaps + hid_swaps + [mix_swap]:
            cp.wait()
        finish_gather()
        return
    for i in range(ni):
        g.ACC[i * L:(i + 1) * L] = g.cot[i].astype(f32)
    cot = g.ACC[...]
    g.SM[...] = jnp.zeros(g.SM.shape, f32)

    def record(j, grad_in, grad_out, normed):
        g.SM[j:j + 1] = col_sum(grad_in)
        g.SM[3 + j:4 + j] = col_sum(grad_out * normed)
        g.SM[6 + j:7 + j] = col_sum(grad_out)

    third = norm_backward(cot, normed, inv, gn)
    record(2, third, cot, normed)
    g.G3[0:T] = third.astype(bf16)
    swap3 = pair(g.G3, T)
    swap3.start()

    rsem = (g.ss, g.rs, g.ls)
    results = {"A": g.RA, "B": g.RB, "O": g.RO, "H": g.RH, "W": g.RW}
    chunks = []
    progress = {}
    for c, (k, h0, half, order) in enumerate(m.reduce_plan):
        recvs = {b: R[f"rv{c}_{b}"] for b in m.bits[1:3]}
        whole = m.rows[k] // 2
        chunks.append(Reduce(R[f"kp{c}"], recvs, R[f"ln{c}"], R.get(f"ex{c}"), results[k], core * whole + h0, half, order, pos, nz, m.bits, rsem, c))
        for cls in classes:
            for what in range(3):
                progress[cls, c, what] = 0

    def half_columns(whole):
        return pl.ds(pl.multiple_of(core * whole, LANES), whole)

    def deal(k, t, value):
        for c, p in enumerate(m.reduce_plan):
            if p[0] == k:
                R[f"kp{c}"][t] = value[p[1]:p[1] + p[2]].astype(bf16)

    reduce_steps()

    swap3.wait_recv()
    for s in hid_swaps:
        s.wait_recv()
    reduce_steps()

    def job_w(o, c):
        t = shard(o)
        deal("W", t, dot_tn(g.HD[o, :, half_columns(m.FZ // 2)], g.G3[...]))
        return c
    if "skip_job_w" not in DEV:
        lax.fori_loop(0, nz, job_w, 0)
    for s in hid_swaps:
        s.wait_send()
    reduce_steps()
    g.ACC[...] = third

    def loop_send(ref, rows, kind, o):
        pltpu.make_async_remote_copy(ref.at[o, pl.ds(0, rows)], ref.at[o, pl.ds(rows, rows)], g.ds.at[kind, o], g.dr.at[kind, o], device_id=(partner, z), device_id_type=MESH).start()

    def hidden_backward(o, slot):
        t = shard(o)
        pre = (dot_nt(g.G3[0:T], g.SA[slot]) * g.GP[o]).astype(bf16)
        g.DP[o, 0:T] = pre
        g.SM[pl.ds(9 + t, 1)] = col_sum(pre.astype(f32))
        loop_send(g.DP, T, 0, o)
        g.ACC[...] += dot_nt(pre, g.SH[slot])

    stream(back_blocks, hidden_backward, after_each(reduce_steps), cross_blocks)
    reduce_steps()

    def loop_wait(ref, rows, kind):
        for o in range(nz):
            cp = pltpu.make_async_remote_copy(ref.at[o, pl.ds(0, rows)], ref.at[o, pl.ds(rows, rows)], g.ds.at[kind, o], g.dr.at[kind, o], device_id=(partner, z), device_id_type=MESH)
            cp.wait()

    gn = g.gain[1:2, :]
    normed, inv = g.NM[1], g.INV[1][:, 0:1]
    grad = g.ACC[...]
    secondg = norm_backward(grad, normed, inv, gn)
    record(1, secondg, grad, normed)
    g.G12[1, 0:T] = secondg.astype(bf16)
    swap2 = pair(g.G12.at[1], T)
    swap2.start()
    reduce_steps()
    loop_wait(g.DP, T, 0)
    swaps[3].wait_recv()

    def job_h(o, c):
        t = shard(o)
        deal("H", t, dot_tn(g.S2[:, half_columns(D // 2)], g.DP[o]))
        return c
    if "skip_job_h" not in DEV:
        lax.fori_loop(0, nz, job_h, 0)
    reduce_steps()

    g.ACC[...] = secondg
    g.patch_grad[...] = jnp.zeros(g.patch_grad.shape, f32)

    def backward_unit(qs, k_i, v_i, p, ms, masks):
        grad_v = dot_tn(p.astype(bf16), ms)
        grad_p = dot_nt(ms, v_i)
        gs = (p * (grad_p - jnp.sum(p * grad_p, -1, keepdims=True))).astype(bf16)
        grad_q = unstack(dot(gs, k_i), masks) * score_scale
        grad_k = dot_tn(gs, qs) * score_scale
        return grad_q, grad_k.astype(bf16).astype(f32), grad_v.astype(bf16).astype(f32)

    def cross_backward(o, slot):
        t = shard(o)
        gm = dot_nt(g.G12[1, 0:T], g.SO[slot]).astype(bf16).astype(f32)
        cqf = g.CQ[o].astype(f32)
        grads = []
        for i in range(ni):
            r = slice(i * L, (i + 1) * L)
            kvi = g.KV[o, i * KP:(i + 1) * KP]
            gq, gk, gv = backward_unit(stack(cqf[r], low), kvi[:, 0:hp], kvi[:, LANES:LANES + hp], g.PC[o * ni + i], stack(gm[r], high), low)
            grads.append(gq)
            g.DKV[o, i * KP:(i + 1) * KP] = jnp.concatenate([gk[:, 0:LANES], gk[:, LANES:] + gv[:, 0:LANES], gv[:, LANES:]], 1).astype(bf16)
        dcq = jnp.concatenate(grads, 0).astype(bf16)
        g.DCQ[o, 0:T] = dcq
        loop_send(g.DCQ, T, 1, o)
        loop_send(g.DKV, ni * KP, 2, o)
        dkv = g.DKV[o, 0:ni * KP]
        g.SM[pl.ds(9 + nz + t, 1), 0:hp] = col_sum(dcq.astype(f32))
        g.SM[pl.ds(9 + 2 * nz + t, 1), 0:m.BW] = col_sum(dkv.astype(f32))
        g.ACC[...] += dot_nt(dcq, g.SA[slot, :, 0:hp])
        for i in range(ni):
            g.patch_grad[i] += dot_nt(g.DKV[o, i * KP:(i + 1) * KP], g.SB[slot])[0:NP]

    stream(cross_blocks, cross_backward, after_each(reduce_steps), self_blocks)
    reduce_steps()
    gn = g.gain[0:1, :]
    normed, inv = g.NM[0], g.INV[0][:, 0:1]
    grad = g.ACC[...]
    firstg = norm_backward(grad, normed, inv, gn)
    record(0, firstg, grad, normed)
    g.G12[0, 0:T] = firstg.astype(bf16)
    swap1 = pair(g.G12.at[0], T)
    swap1.start()
    reduce_steps()
    loop_wait(g.DCQ, T, 1)
    loop_wait(g.DKV, ni * KP, 2)
    swaps[1].wait_recv()

    def job_b(o, c):
        t = shard(o)
        deal("B", t, dot_tn(g.PT[:, half_columns(m.PW // 2)], g.DKV[o]))
        return c
    if "skip_job_b" not in DEV:
        lax.fori_loop(0, nz, job_b, 0)
    reduce_steps()

    g.ACC[...] = firstg

    def self_backward(o, slot):
        t = shard(o)
        gm = dot_nt(g.G12[0, 0:T], g.SO[slot]).astype(bf16).astype(f32)
        qf = g.QKV[o].astype(f32)
        gqs, gks, gvs = [], [], []
        for i in range(ni):
            r = slice(i * L, (i + 1) * L)
            k_i = qf[r, 3 * LANES:3 * LANES + hp].astype(bf16)
            v_i = qf[r, 2 * LANES:2 * LANES + hp].astype(bf16)
            gq, gk, gv = backward_unit(stack(qf[r, 0:hp], high), k_i, v_i, g.PS[o * ni + i], stack(gm[r], low), high)
            gqs.append(gq)
            gks.append(gk)
            gvs.append(gv)
        gq, gk, gv = (jnp.concatenate(v, 0) for v in (gqs, gks, gvs))
        dq = jnp.concatenate([gq, gv[:, 0:LANES], gv[:, LANES:] + gk[:, 0:LANES], gk[:, LANES:]], 1).astype(bf16)
        g.DQ[o, 0:T] = dq
        loop_send(g.DQ, T, 3, o)
        g.SM[pl.ds(9 + 3 * nz + t, 1), 0:m.QW] = col_sum(dq.astype(f32))
        g.ACC[...] += dot_nt(dq, g.SA[slot, :, LANES:])

    stream(self_blocks, self_backward, after_each(reduce_steps), [])
    g.text_grad[...] = g.ACC[...].reshape(ni, L, D)
    reduce_steps()
    loop_wait(g.DQ, T, 3)
    swap1.wait_recv()
    swap2.wait_recv()
    for s in swaps[0:1] + swaps[2:3] + [mix_swap]:
        s.wait_recv()

    def job_o(o, c):
        t = shard(o)
        g.TMP[...] = dot_tn(g.MX[core, o], g.G12[core])
        deal("O", t, g.TMP[pl.ds(pl.multiple_of(core * HEAD, 16), m.rows["O"] // 2)])
        return c
    if "skip_job_o" not in DEV:
        lax.fori_loop(0, nz, job_o, 0)
    reduce_steps()

    def job_a(o, c):
        t = shard(o)
        cols = half_columns(D // 2)
        left = dot_tn(g.F[:, cols], g.DCQ[o])
        right = dot_tn(g.X[:, cols], g.DQ[o])
        deal("A", t, jnp.concatenate([left[:, 0:LANES], left[:, LANES:] + right[:, 0:LANES], right[:, LANES:]], 1))
        return c
    if "skip_job_a" not in DEV:
        lax.fori_loop(0, nz, job_a, 0)
    reduce_steps()

    sends = []
    for i, b in enumerate(m.bits):
        cp = pltpu.make_async_remote_copy(g.SM, g.SR.at[i], g.ms.at[i], g.mr.at[i], device_id=(flip(d, b), z), device_id_type=MESH)
        cp.start()
        if i < 3:
            reduce_steps()
        cp.wait()
        g.SM[...] += g.SR[i]
    g.SZ[z] = g.SM[...]
    nb = len(m.bits)
    for o in range(1, nz):
        to = lax.rem(z + o, jnp.int32(nz))
        cp = pltpu.make_async_remote_copy(g.SM, g.SZ.at[z], g.ms.at[nb + o], g.zm.at[z], device_id=(d, to), device_id_type=MESH)
        cp.start()
        sends.append(cp)
    reduce_steps()
    reduce_steps()
    for o in range(1, nz):
        frm = lax.rem(z + o, jnp.int32(nz))
        pltpu.make_async_remote_copy(g.SM, g.SZ.at[frm], g.ms.at[nb + o], g.zm.at[frm], device_id=(d, frm), device_id_type=MESH).wait_recv()
    total = g.SZ[0]
    for t in range(1, nz):
        total = total + g.SZ[t]
    g.small[...] = total
    assert calls == [len(m.gather_steps[0]), len(m.reduce_steps[0])], calls

    for cp in sends + swaps + [swap1, swap2, swap3, mix_swap]:
        cp.wait_send()
    finish_gather()
    if "nor" not in DEV:
        for cls in classes:
            @pl.when(kind == cls)
            def _():
                for c in chunks:
                    c.finish(cls)


GATHER_PLAN = (("V", 0, 16, ""), ("O", 0, 384, "xyc"), ("W", 0, 256, "xc"), ("A", 384, 384, "yxc"), ("B", 0, 256, "xc"), ("A", 0, 384, "xyc"), ("B", 640, 384,
    "xc"), ("H", 0, 768, "xyc"), ("B", 256, 384, "yc"), ("W", 256, 256, "xyc"), ("W", 512, 256, "xc"))
GATHER_ORDER = ((0, 40, 120, 200, 13, 53, 133, 213, 61, 14, 141, 54, 160, 221, 134, 69, 214, 15, 149, 77, 55, 320, 280, 62, 229, 240, 157, 173, 222, 142, 135, 237,
    63, 215, 181, 174, 70, 189, 78, 150, 293, 230, 223, 333, 158, 143, 182, 238, 175, 190, 253, 71, 301, 334, 79, 360, 231, 400, 151, 294, 183, 341, 239,
    254, 159, -1, 261, 349, 335, 191, -1, 302, 295, 269, 80, -1, 309, 262, 255, 342, 373, -1, 343, 413, 317, 303, 270, 374, 350, 351, 263, 381, 414, 271,
    -1, 310, 375, 421, 382, 93, -1, 318, 422, 415, -1, 383, 101, 94, 429, 430, 311, -1, 389, 109, 95, 423, 319, -1, 102, 397, -1, 390, 431, -1, 391, 110,
    103, -1, 398, 399, 111, -1, -1, -1, -1), (0, 4, 40, 44, 120, 124, 200, 204, 9, 13, 49, 53, 129, 133, 209, 213, 57, 14, 61, 137, 54, 160, 164, 217,
    141, 134, 221, 169, 214, 173, 65, 320, 280, 284, 324, 145, 174, 73, 240, 244, 69, 62, 153, 329, 333, 77, 225, 149, 177, 289, 293, 142, 233, 222, 157,
    249, 253, 185, 181, 334, 229, 182, 189, 237, 190, 294, 297, 70, 254, 337, 78, 345, 301, 341, 360, 364, 400, 404, 349, 369, 230, 150, 373, 257, 342,
    238, 409, 413, 158, -1, 265, 261, 350, 374, 80, 84, -1, 302, 269, 414, -1, 305, 262, 377, 381, 89, 93, -1, 417, 313, 270, -1, 309, 382, 94, 425, 421,
    -1, 317, 422, -1, 310, 97, 429, 430, -1, 318, 385, 101, 102, -1, 389, 105, -1, 393, 109, 110, -1, 397, 390, -1, 398, -1, -1, -1, -1))
REDUCE_PLAN = (("W", 128, "xzy"), ("W", 128, "yxz"), ("W", 128, "zyx"), ("H", 192, "xyz"), ("H", 64, "yxz"), ("H", 128, "yxz"), ("B", 320, "zxy"), ("B", 192,
    "yxz"), ("O", 64, "xyz"), ("O", 64, "yzx"), ("O", 64, "xzy"), ("A", 128, "yxz"), ("A", 128, "yxz"), ("A", 128, "xzy"))
REDUCE_ORDER = ((-1, -1, 3, 6, 7, 0, -1, -1, -1, -1, -1, -1, 9, 12, 15, -1, -1, 3, 0, 1, -1, 12, -1, -1, -1, 18, 19, 21, -1, 9, 8, 6, 15, -1, -1, 3, 4, 2, 0, -1, 21,
    12, 13, -1, 30, 27, 24, -1, 39, 33, 36, 15, 16, -1, 21, 22, 9, 10, 6, -1, 0, -1, 30, 31, -1, 27, 28, 20, 18, 24, -1, 5, 3, 14, 12, 33, 17, 15, 39, 40,
    23, 21, 6, 18, 3, 12, 11, 9, 36, 0, 32, 30, 33, 34, 24, 25, 29, 27, 15, 18, 21, 6, 3, 12, 3, 12, 9, 30, 36, 37, 41, 39, 15, 0, 27, 18, 35, 33, 15, 0,
    21, 26, 24, 9, 21, 27, 6, 30, 9, 39, 6, 38, 18, 36, 24, 33, 27, 18, 30, 39, 27, 36, 30, 24, 33, 24, 39, 33, 36, 39, 36), (-1, -1, 3, 6, 0, -1, -1, -1,
    -1, -1, -1, 9, 12, 7, 15, -1, 3, 7, 0, -1, -1, 12, 7, 8, -1, 8, 6, 1, 1, -1, -1, 18, 21, 9, 1, 2, 15, -1, 6, 2, 0, -1, 3, 19, -1, 12, -1, 21, -1, 19,
    30, 27, 6, 24, 15, -1, 39, 20, 21, 9, 33, 0, 36, -1, 19, 4, -1, 20, 18, 30, 13, 13, 27, 13, 4, 4, 5, 6, 16, -1, 14, 14, 12, 24, 5, 3, 22, 16, 16, -1,
    22, 22, 17, 23, -1, 10, 10, 23, 21, 33, 0, 17, 15, 10, 31, 39, 11, 31, 31, 11, 9, 18, 28, 32, 12, 28, 32, 30, 3, 28, 21, 36, 29, 29, 40, 27, 6, 6, 40,
    33, 24, 9, 41, 40, 0, 18, 34, 15, 41, 39, 12, 34, 0, 30, 34, 12, 25, 35, 25, 3, 25, 35, 33, 36, 27, 26, 21, 3, 37, 26, 24, 18, 37, 21, 37, 9, 38, 15,
    33, 38, 39, 27, 9, 36, 30, 15, 24, 18, 33, 36, 39, 18, 30, 33, 27, 24, 30, 27, 24, 36, 39, 36, 39))


def unpack(orders, decode):
    out = []
    for order in orders:
        parts = [[]]
        for code in order:
            if code < 0:
                parts.append([])
            else:
                parts[-1].append(decode(code))
        out.append(parts)
    return out


def gather_code(code):
    return code // 40, code // 8 % 5 - 1, code // 4 % 2, code % 4


def reduce_code(code):
    return code // 3, code % 3


def plans(m):
    link = dict(zip("cxy", m.bits[:3]), z="z")
    m.gather_plan = [(k, r0, rows, tuple(link[o] for o in order)) for k, r0, rows, order in GATHER_PLAN]
    m.gather_steps = unpack(GATHER_ORDER, gather_code)
    m.reduce_plan = []
    at = {}
    for k, half, order in REDUCE_PLAN:
        h0 = at.get(k, 0)
        at[k] = h0 + half
        m.reduce_plan.append((k, h0, half, tuple(link[o] for o in order)))
    m.reduce_steps = unpack(REDUCE_ORDER, reduce_code)
    assert all(at[k] * 2 == m.rows[k] for k in at) and m.nz == 4


def run_layer(m, nd, shards, vown, x, patches, rows, cot, ob, gain, shift):
    nz = m.nz
    ni, L, D = x.shape
    T = ni * L
    m.ni, m.L, m.D, m.T = ni, L, D, T
    m.NP, m.PW = patches.shape[1:]
    m.KP = (m.NP + 15) // 16 * 16
    hw = D // nz
    m.nh = hw // HEAD
    m.hp = (hw + HEAD + LANES - 1) // LANES * LANES
    hp, KP, PW = m.hp, m.KP, m.PW
    A, B, O, H, W = shards
    m.BW, m.QW, m.FZ = B.shape[1], D - LANES, W.shape[0]
    FZ = m.FZ
    m.rows = {k: s.shape[0] for k, s in zip("ABOHW", shards)}
    lanes = {k: s.shape[1] for k, s in zip("ABOHW", shards)}
    plans(m)
    m.swaps = nz + 9
    V, sem = pltpu.VMEM, pltpu.SemaphoreType.DMA
    nc, ng = len(m.reduce_plan), len(m.gather_plan)
    nb = len(m.bits)
    sums = (9 + 4 * nz + 7) // 8 * 8
    scratch = dict(
        VG=V((nz, 16, D), bf16), XF=V((T, D), f32), X=V((2 * T, D), bf16), PT=V((2 * ni * KP, PW), bf16),
        SA=V((2, D, D), bf16), SH=V((2, D, D), bf16), SB=V((2, PW, m.BW), bf16), SO=V((2, hp, D), bf16),
        ACC=V((T, D), f32), QKV=V((nz, T, m.QW), bf16), PS=V((nz * ni, m.nh * L, L), f32), MX=V((2, nz, 2 * T, hp), bf16),
        NM=V((2, T, D), f32), INV=V((2, T, LANES), f32), F=V((2 * T, D), bf16), S2=V((2 * T, D), bf16),
        CQ=V((nz, T, hp), bf16), KV=V((nz, ni * KP, m.BW), bf16), PC=V((nz * ni, m.nh * L, KP), f32),
        GP=V((nz, T, FZ), f32), HD=V((nz, 2 * T, FZ), bf16), SM=V((sums, D), f32), G3=V((2 * T, D), bf16), DP=V((nz, 2 * T, FZ), bf16),
        G12=V((2, 2 * T, D), bf16), DKV=V((nz, 2 * ni * KP, m.BW), bf16),
        TMP=V((hp, D), f32), SR=V((nb, sums, D), f32), SZ=V((nz, sums, D), f32),
        zs=sem((ng, 2, nz)), zr=sem((ng, 2, nz)), ps=sem((ng, 3, 2, nz)), pr=sem((ng, 3, 2, nz)),
        cs=sem((m.swaps,)), cr=sem((m.swaps,)), ds=sem((4, nz)), dr=sem((4, nz)),
        sa=sem((2,)), sh=sem((2,)), sb=sem((2,)), so=sem((2,)),
        ss=sem((nc, 2 * nz + 5 + nb)), rs=sem((nc, 2 * nz + 5 + nb)), ls=sem((nc,)), ms=sem((nb + nz,)), mr=sem((nb,)), zm=sem((nz,)),
    )
    for c, (k, h0, half, order) in enumerate(m.reduce_plan):
        C = lanes[k]
        scratch[f"kp{c}"] = V((nz, half, C), bf16)
        for b in m.bits[1:3]:
            lead = nz if order.index(b) < order.index("z") else 1
            scratch[f"rv{c}_{b}"] = V((lead, op_rows(half, order, b), C), bf16)
        scratch[f"ln{c}"] = V((2, nz - 1, op_rows(half, order, "z"), C), bf16)
        if nb > 3:
            scratch[f"ex{c}"] = V((nb - 3, half // 4, C), bf16)
    S = jax.ShapeDtypeStruct
    hbm, vm, sm = (pl.BlockSpec(memory_space=s) for s in (pl.ANY, pltpu.VMEM, pltpu.SMEM))
    outs = dict(
        layer_out=(S((ni, L, D), f32), vm), text_grad=(S((ni, L, D), f32), vm), patch_grad=(S((ni, m.NP, PW), f32), vm), small=(S((sums, D), f32), vm),
        **{"R" + k: (S(s.shape, bf16), hbm) for k, s in zip("ABOHW", shards)},
        **{"G" + k: (S((nz,) + s.shape, bf16), hbm) for k, s in zip("ABOHW", shards)},
    )
    ins = dict(x=(x, vm), patches=(patches, vm), rows=(rows, sm), cot=(cot, vm), A=(A, hbm), B=(B, hbm), O=(O, hbm), H=(H, hbm), W=(W, hbm),
               vown=(vown, vm), ob=(ob, vm), gain=(gain, vm), shift=(shift, vm))
    m.inputs, m.outputs, m.scratch = list(ins), list(outs), list(scratch)
    res = pl.pallas_call(
        functools.partial(layer_kernel, m),
        out_shape=tuple(o[0] for o in outs.values()),
        in_specs=[i[1] for i in ins.values()],
        out_specs=tuple(o[1] for o in outs.values()),
        scratch_shapes=list(scratch.values()),
        compiler_params=pltpu.CompilerParams(collective_id=0, has_side_effects=True, vmem_limit_bytes=67043328),
        name="layer",
    )(*[i[0] for i in ins.values()])
    return dict(zip(outs, res))


def per_device(nd, nz, text_states, patch_states, patch_rows, cotangent, w_attn, attn_bias, w_attn_out, w_query, w_patch, cross_bias, w_cross_out, w_hidden, hidden_bias, w_output, out_bias, norm_gain, norm_shift):
    m = Dims()
    m.nz, m.bits = nz, tuple(range(nd.bit_length() - 1))
    z = lax.axis_index("mp")
    hw = w_query.shape[1]
    D = text_states.shape[-1]
    A = jnp.concatenate([w_query, w_attn[0], w_attn[2], w_attn[1]], 1)
    B = jnp.concatenate([w_patch[0], w_patch[1]], 1)
    O = jnp.concatenate([w_attn_out, w_cross_out], 0)
    zero = jnp.zeros((hw,), bf16)
    vown = jnp.stack([
        jnp.concatenate([cross_bias[0], attn_bias[0], attn_bias[1], zero]),
        jnp.pad(jnp.concatenate([zero, cross_bias[1]]), (0, D - 2 * hw)), hidden_bias])
    vown = jnp.pad(vown, ((0, 13), (0, 0)))
    r = run_layer(m, nd, (A, B, O, w_hidden, w_output), vown, text_states, patch_states, patch_rows, cotangent, out_bias.astype(f32), norm_gain.astype(f32), norm_shift.astype(f32))
    RA, RB, RO, RH, RW = (r["R" + k].astype(f32) for k in "ABOHW")
    small = r["small"]
    pick = lambda base: lax.dynamic_slice_in_dim(small, base + z, 1, 0)[0]
    cq, kv, qv = pick(9 + nz), pick(9 + 2 * nz), pick(9 + 3 * nz)
    at = hw - LANES
    part = lambda a, i: a[:, i * hw:(i + 1) * hw]
    return (
        r["layer_out"], r["text_grad"], r["patch_grad"],
        jnp.stack([part(RA, 1), part(RA, 3), part(RA, 2)]),
        jnp.stack([qv[at:at + hw], qv[at + hw:at + 2 * hw]]),
        RO[:hw], part(RA, 0), jnp.stack([part(RB, 0), part(RB, 1)]),
        jnp.stack([cq[:hw], kv[hw:2 * hw]]), RO[hw:], RH, pick(9), RW,
        small[0:3], small[3:6], small[6:9],
    )


def solution(mesh):
    nd, nz = mesh.shape["dp"], mesh.shape["mp"]
    rows = P(("dp", "mp"), None, None)
    return jax.shard_map(
        functools.partial(per_device, nd, nz),
        mesh=mesh,
        in_specs=(rows, rows, P("dp"), rows, P(None, None, "mp"), P(None, "mp"), P("mp", None), P(None, "mp"), P(None, None, "mp"), P(None, "mp"), P("mp", None), P(None, "mp"), P("mp"), P("mp", None), P(), P(), P()),
        out_specs=(rows, rows, rows, P(None, None, "mp"), P(None, "mp"), P("mp", None), P(None, "mp"), P(None, None, "mp"), P(None, "mp"), P("mp", None), P(None, "mp"), P("mp"), P("mp", None), P(), P(), P()),
        check_vma=False,
    )
```

```python
import functools
import math

import jax
import jax.numpy as jnp
from jax import lax
from jax.experimental import pallas as pl
from jax.experimental.pallas import tpu as pltpu
from jax.sharding import PartitionSpec as P

MESH = pl.DeviceIdType.MESH
HEAD = 64
LANES = 128
epsilon = 1e-06
score_scale = 1.0 / math.sqrt(HEAD)
bf16, f32 = jnp.bfloat16, jnp.float32


def bit_of(d, b):
    return lax.rem(lax.div(d, jnp.int32(2 ** b)), jnp.int32(2))


def flip(d, b):
    return d + (1 - 2 * bit_of(d, b)) * (2 ** b)


def when(cond, fn):
    if cond is True:
        fn()
    else:
        pl.when(cond)(fn)


class Gather:
    def __init__(self, src, dst, row0, rows, order, pos, sems, base):
        self.src, self.dst, self.row0, self.order, self.pos = src, dst, row0, order, pos
        self.piece = rows // (2 ** len(order))
        self.zs, self.zr, self.ps, self.pr = sems
        self.base = base
        self.k = len(order)

    def win(self, s):
        w = jnp.int32(0)
        for i, b in enumerate(self.order):
            if i >= s:
                w = w + bit_of(self.pos.d, b) * (2 ** i)
        return pl.ds(pl.multiple_of(self.row0 + w * self.piece, 16), self.piece * 2 ** s)

    def shard(self, dr, j):
        return self.pos.z + j * (2 * dr - 1) * self.pos.sign

    def zcopy(self, dr, j):
        p = self.pos
        t, rows = self.shard(dr, j), self.win(0)
        src = self.src.at[rows] if j == 0 else self.dst.at[t, rows]
        real = dr + p.upper - 2 * dr * p.upper
        return pltpu.make_async_remote_copy(src, self.dst.at[t, rows], self.zs.at[self.base, real, j], self.zr.at[self.base, real, j], device_id=(p.d, p.z + (1 - 2 * dr) * p.sign), device_id_type=MESH)

    def pcopy(self, s, dr, j):
        p = self.pos
        part = self.dst.at[self.shard(dr, j), self.win(s)]
        return pltpu.make_async_remote_copy(part, part, self.ps.at[self.base, s, dr, j - 1], self.pr.at[self.base, s, dr, j - 1], device_id=(flip(p.d, self.order[s]), p.z), device_id_type=MESH)

    @staticmethod
    def has(cls, nz, dr, j):
        return cls >= j if dr == 0 else cls + j < nz

    @staticmethod
    def ahead(cls, dr):
        return dr == 0 or cls >= 1

    def item(self, cls, nz, st, dr, j):
        if st == -1:
            self.zcopy(dr, 0).start()
            return
        if st == 0:
            self.zcopy(dr, j - 1).wait_recv()
            if j <= nz - 2 and self.ahead(cls, dr):
                self.zcopy(dr, j).start()
        else:
            self.pcopy(st - 1, dr, j).wait_recv()
        if st < self.k:
            self.pcopy(st, dr, j).start()

    def finish(self, cls, nz):
        for dr in (0, 1):
            for j in range(nz - 1):
                if self.ahead(cls, dr) and self.has(cls, nz, dr, j):
                    self.zcopy(dr, j).wait_send()
            for s in range(self.k):
                for j in range(1, nz):
                    if self.has(cls, nz, dr, j):
                        self.pcopy(s, dr, j).wait_send()


def add_into(dst, src, rows):
    step = 32 if rows % 32 == 0 else 16

    def body(i, c):
        r = pl.ds(pl.multiple_of(i * step, step), step)
        dst[r, :] = dst[r, :] + src[r, :]
        return c
    lax.fori_loop(0, rows // step, body, 0)


def add_all(dst, src, count, rows):
    def body(t, c):
        add_into(dst.at[t], src.at[t], rows)
        return c
    lax.fori_loop(0, count, body, 0)


def op_rows(half, order, op):
    size = half
    for o in order:
        if o == "z":
            if op == "z":
                return size
        else:
            size //= 2
            if o == op:
                return size
    return size


class Reduce:
    def __init__(self, keep, recvs, line, extra, result, row, half, order, pos, nz, bits, sems, base):
        self.keep, self.recvs, self.line, self.extra = keep, recvs, line, extra
        self.result, self.row, self.half, self.order = result, row, half, order
        self.pos, self.nz, self.bits = pos, nz, bits
        self.ss, self.rs, self.ls = sems
        self.base = base
        self.slot = 2 * nz
        self.pending = []
        self.steps = []
        self.build()

    def copy(self, s, src, dst, to):
        return lambda: pltpu.make_async_remote_copy(src, dst, self.ss.at[self.base, s], self.rs.at[self.base, s], device_id=to, device_id_type=MESH)

    def remote(self, src, dst, b, keep=True):
        cp = self.copy(self.slot, src, dst, (flip(self.pos.d, b), self.pos.z))
        self.slot += 1
        if keep:
            self.pending.append(cp)
        return cp

    def build(self):
        d, z, nz = self.pos.d, self.pos.z, self.nz
        prev = lambda: None
        start, size, whole = jnp.int32(0), self.half, True
        taken = []

        def then(prev, cp):
            def step():
                prev()
                cp().start()
            self.steps.append(step)

        for op in self.order:
            if op == "z":
                self.rows = pl.ds(start, size)
                self.size = size
                self.steps.append(prev)
                prev, whole = (lambda: None), False
                continue
            size //= 2
            m = bit_of(d, op)
            keep0 = pl.multiple_of(start + m * size, 16)
            send0 = pl.multiple_of(start + (1 - m) * size, 16)
            buf = self.recvs[op]
            if whole:
                cp = self.remote(self.keep.at[:, pl.ds(send0, size), :], buf, op)
            else:
                cp = self.remote(self.keep.at[z, pl.ds(send0, size), :], buf.at[0], op)
            then(prev, cp)

            def prev(cp=cp, keep0=keep0, size=size, whole=whole, buf=buf):
                cp().wait_recv()
                if whole:
                    add_all(self.keep.at[:, pl.ds(keep0, size), :], buf, nz, size)
                else:
                    add_into(self.keep.at[z, pl.ds(keep0, size), :], buf.at[0], size)
            taken.append(op)
            start = keep0
        for e, b in enumerate(self.bits[3:]):
            cp = self.remote(self.keep.at[z, pl.ds(start, size), :], self.extra.at[e], b, False)

            def prev(before=prev, cp=cp, e=e, start=start, size=size):
                before()
                cp().start()
                cp().wait()
                add_into(self.keep.at[z, pl.ds(start, size), :], self.extra.at[e], size)
        at = pl.multiple_of(self.row + start, 16)
        total = self.keep.at[z, pl.ds(start, size), :]
        win = self.result.at[pl.ds(at, size), :]
        own = lambda win=win: pltpu.make_async_copy(total, win, self.ls.at[self.base])
        op = taken[-1]
        cp = self.remote(total, win, op)

        def step(prev=prev, cp=cp):
            prev()
            own().start()
            cp().start()
        self.steps.append(step)

        def prev(cp=cp):
            cp().wait_recv()
            own().wait()
        for nxt in taken[-2::-1] + [self.bits[0]]:
            at = pl.multiple_of(at - bit_of(d, op) * size, 16)
            size *= 2
            op = nxt
            win = self.result.at[pl.ds(at, size), :]
            cp = self.remote(win, win, op)
            then(prev, cp)
            prev = lambda cp=cp: cp().wait_recv()
        self.steps.append(prev)

    def hop(self, kind, i):
        p, nz = self.pos, self.nz
        far, near = nz - 1 - i, i
        if kind == 1:
            t = far * (1 - p.upper) + near * p.upper
            flow, to = p.upper, p.z + p.sign
        else:
            t = near * (1 - p.upper) + far * p.upper
            flow, to = 1 - p.upper, p.z - p.sign
        cell = self.keep.at[t, self.rows, :]
        land = self.line.at[flow, nz - 2 - i]
        s = flow * nz + i
        cp = lambda: pltpu.make_async_remote_copy(cell, land, self.ss.at[self.base, s], self.rs.at[self.base, s], device_id=(p.d, to), device_id_type=MESH)
        return cp, cell, land

    def sends(self, cls, kind):
        return self.nz - 1 - cls if kind == 1 else cls

    def along(self, cls, kind, i):
        if kind == 1 and cls == 0:
            for k in range(self.nz - 1):
                self.hop(1, k)[0]().start()
            return
        cp, cell, land = self.hop(kind, i)
        cp().wait_recv()
        add_into(cell, land, self.size)
        if i < self.sends(cls, kind):
            cp().start()

    def finish(self, cls):
        for cp in self.pending:
            cp().wait_send()
        for kind in (1, 2):
            for i in range(self.sends(cls, kind)):
                self.hop(kind, i)[0]().wait_send()


def enter(d, z, nz, bits):
    bar = pltpu.get_barrier_semaphore()
    for b in bits:
        pl.semaphore_signal(bar, inc=1, device_id=(flip(d, b), z), device_id_type=MESH)
    for o in range(1, nz):
        pl.semaphore_signal(bar, inc=1, device_id=(d, lax.rem(z + o, jnp.int32(nz))), device_id_type=MESH)
    pl.semaphore_wait(bar, len(bits) + nz - 1)


def dot(a, b):
    return lax.dot_general(a, b, (((1,), (0,)), ((), ())), preferred_element_type=f32)


def dot_nt(a, b):
    return lax.dot_general(a, b, (((1,), (1,)), ((), ())), preferred_element_type=f32)


def dot_tn(a, b):
    return lax.dot_general(a, b, (((0,), (0,)), ((), ())), preferred_element_type=f32)


def norm_forward(h, gain, shift):
    centred = h - jnp.mean(h, -1, keepdims=True)
    inverse = lax.rsqrt(jnp.mean(centred * centred, -1, keepdims=True) + epsilon)
    normed = centred * inverse
    return normed * gain + shift, normed, inverse


def norm_backward(grad, normed, inverse, gain):
    scaled = grad * gain
    return inverse * (scaled - jnp.mean(scaled, -1, keepdims=True) - normed * jnp.mean(scaled * normed, -1, keepdims=True))


def col_sum(v):
    return jnp.sum(v, axis=0, keepdims=True)


def nth_shard(z, nz, o):
    t = z
    for b in range(nz.bit_length() - 1):
        t = t + lax.rem(lax.div(o, jnp.int32(2 ** b)), jnp.int32(2)) * (1 - 2 * bit_of(z, b)) * (2 ** b)
    return t


class Dims:
    pass


def layer_kernel(m, *refs):
    n_in, n_out = len(m.inputs), len(m.outputs)
    R = dict(zip(m.inputs + m.outputs + m.scratch, refs))
    g = Dims()
    for k, v in R.items():
        setattr(g, k, v)
    ni, L, T, D, nz, hp, nh, KP, NP = m.ni, m.L, m.T, m.D, m.nz, m.hp, m.nh, m.KP, m.NP
    d, z = lax.axis_index("dp"), lax.axis_index("mp")
    core = bit_of(d, m.bits[0])
    partner = flip(d, m.bits[0])

    shard = functools.partial(nth_shard, z, nz)

    g.DCQ = g.HD.at[:, :, 0:hp]
    g.DQ = g.DP.at[:, :, 0:m.QW]
    g.KV = g.DKV.at[:, 0:ni * KP]

    pos = Dims()
    pos.d, pos.z = d, z
    pos.upper = lax.div(2 * z, jnp.int32(nz))
    pos.sign = 1 - 2 * pos.upper
    kind = z * (1 - pos.upper) + (nz - 1 - z) * pos.upper
    classes = range(nz // 2)

    hw = m.hw
    joins = [(g.wq, g.AO.at[pl.ds(0, hw)]), (g.wa.at[0], g.AO.at[pl.ds(hw, hw)]), (g.wa.at[2], g.AO.at[pl.ds(2 * hw, hw)]), (g.wa.at[1], g.AO.at[pl.ds(3 * hw, hw)]),
             (g.wp.at[0], g.BO.at[pl.ds(0, hw)]), (g.wp.at[1], g.BO.at[pl.ds(hw, hw)]), (g.wao, g.OO.at[pl.ds(0, hw)]), (g.wco, g.OO.at[pl.ds(hw, hw)])]
    joins = [pltpu.make_async_copy(a, b, g.js.at[i]) for i, (a, b) in enumerate(joins)]
    for cp in joins:
        cp.start()
    g.TMP[0:16, 0:D] = jnp.zeros((16, D), f32)
    ab, cb = g.ab[...].astype(f32), g.cb[...].astype(f32)
    g.TMP[0:1, 0:hw] = cb[0:1]
    g.TMP[0:1, hw:2 * hw] = ab[0:1]
    g.TMP[0:1, 2 * hw:3 * hw] = ab[1:2]
    g.TMP[1:2, hw:2 * hw] = cb[1:2]
    g.TMP[2:3, 0:D] = g.hb[...].astype(f32).reshape(1, D)
    g.VO[...] = g.TMP[0:16, 0:D].astype(bf16)
    g.VG[z] = g.VO[...]
    enter(d, z, nz, m.bits)
    for cp in joins:
        cp.wait()
    gsem = (g.zs, g.zr, g.ps, g.pr)
    own = {"A": g.AO, "B": g.BO, "O": g.OO, "H": g.H, "W": g.W, "V": g.VO}
    far = {"A": g.GA, "B": g.GB, "O": g.GO, "H": g.GH, "W": g.GW, "V": g.VG}
    gathers = [Gather(own[k], far[k], r0, rows, order, pos, gsem, c) for c, (k, r0, rows, order) in enumerate(m.gather_plan)]
    calls = [0, 0]

    def gather_steps():
        at = calls[0]
        calls[0] += 1
        for cls in classes:
            todo = m.gather_steps[cls][at]
            if todo:
                @pl.when(kind == cls)
                def _():
                    for c, st, dr, j in todo:
                        gathers[c].item(cls, nz, st, dr, j)

    nb = len(m.bits)

    def small_copy(i):
        return pltpu.make_async_remote_copy(g.SM, g.SR.at[i], g.ms.at[i], g.mr.at[i], device_id=(flip(d, m.bits[i]), z), device_id_type=MESH)

    def small_spread(o, frm):
        to = lax.rem(z + o, jnp.int32(nz))
        return pltpu.make_async_remote_copy(g.SM, g.SZ.at[frm(to)], g.ms.at[nb + o], g.zm.at[frm(to)], device_id=(d, to), device_id_type=MESH)

    def small_step(i):
        if i > 0 and i < 4:
            small_copy(i - 1).wait()
            g.SM[...] += g.SR[i - 1]
        if i < 3:
            small_copy(i).start()
        elif i == 3:
            for e in range(3, nb):
                small_copy(e).start()
                small_copy(e).wait()
                g.SM[...] += g.SR[e]
            g.SZ[z] = g.SM[...]
            for o in range(1, nz):
                small_spread(o, lambda to: z).start()
        elif i == 5:
            for o in range(1, nz):
                small_spread(o, lambda to: to).wait_recv()
            total = g.SZ[0]
            for t in range(1, nz):
                total = total + g.SZ[t]
            g.small[...] = total

    def reduce_steps():
        at = calls[1]
        calls[1] += 1
        for cls in classes:
            todo = m.reduce_steps[cls][at]
            if todo:
                @pl.when(kind == cls)
                def _():
                    for c, what in todo:
                        i = progress[cls, c, what]
                        progress[cls, c, what] += 1
                        if c == len(chunks):
                            small_step(i)
                        elif what == 0:
                            chunks[c].steps[i]()
                        else:
                            chunks[c].along(cls, what, i)

    def after_each(steps):
        def between(o):
            for q in range(nz - 1):
                pl.when(o == q)(lambda: steps())
        return between

    def finish_gather():
        for cls in classes:
            @pl.when(kind == cls)
            def _():
                for q in gathers:
                    q.finish(cls, nz)

    pair_slot = [0]

    def pair(ref, rows):
        s = pair_slot[0]
        pair_slot[0] += 1
        return pltpu.make_async_remote_copy(ref.at[pl.ds(0, rows)], ref.at[pl.ds(rows, rows)], g.cs.at[s], g.cr.at[s], device_id=(partner, z), device_id_type=MESH)

    def place(block, slot):
        buf, sem, key, rows, cols = block
        return buf.at[slot, pl.ds(0, rows[1]), pl.ds(*cols)], sem.at[slot]

    def fetch(block, slot, o):
        buf, sem, key, rows, cols = block
        dst, done = place(block, slot)
        r, c = pl.ds(*rows), pl.ds(*cols)

        def mine():
            pltpu.make_async_copy(own[key].at[r, c], dst, done).start()

        def other():
            pltpu.make_async_copy(far[key].at[shard(o), r, c], dst, done).start()
        if isinstance(o, int):
            mine()
        else:
            pl.when(o == 0)(mine)
            pl.when(o != 0)(other)

    def arrived(block, slot):
        buf, sem, key, rows, cols = block
        dst, done = place(block, slot)
        pltpu.make_async_copy(own[key].at[pl.ds(*rows), pl.ds(*cols)], dst, done).wait()

    def stream(blocks, body, between, ahead, refill=()):
        def step(o, c):
            if blocks:
                @pl.when(o + 1 < nz)
                def _():
                    for b in blocks:
                        fetch(b, slot_of(b, o + 1), o + 1)
            if ahead:
                @pl.when(o + 1 == nz)
                def _():
                    for b in ahead:
                        fetch(b, 0, 0)
            for b in blocks:
                arrived(b, slot_of(b, o))
            body(o, lax.rem(o, jnp.int32(2)))
            for b in refill:
                fetch(b, o, o)
            between(o)
            return c
        lax.fori_loop(0, nz, step, 0)

    def slot_of(block, o):
        return lax.rem(o, jnp.int32(block[0].shape[0]))

    FZ, PW, BW = m.FZ, m.PW, m.BW
    self_blocks = [(g.SA, g.sa, "A", (LANES, D - LANES), (0, D)), (g.SO, g.so, "O", (0, hp), (0, D))]
    cross_blocks = [(g.SA, g.sa, "A", (0, hp), (0, D)), (g.SB, g.sb, "B", (0, BW), (0, PW)), (g.SO, g.so, "O", (LANES, hp), (0, D))]
    hidden_blocks = [(g.SA, g.sa, "H", (0, D), (0, FZ))]
    output_blocks = [(g.SA, g.sa, "W", (0, FZ), (0, D))]
    back_blocks = [(g.SH, g.sh, "H", (0, D), (0, FZ))]
    cross_back = [cross_blocks[0], cross_blocks[2]]
    for b in self_blocks:
        fetch(b, 0, 0)

    lane = lax.broadcasted_iota(jnp.int32, (L, hp), 1)
    low = [lane // HEAD == h for h in range(nh)]
    high = [lane // HEAD == h + 1 for h in range(nh)]

    def stack(v, masks):
        return jnp.concatenate([jnp.where(k, v, 0.0) for k in masks], axis=0).astype(bf16)

    def unstack(v, masks):
        out = jnp.where(masks[0], v[0:L], 0.0)
        for h in range(1, nh):
            out = out + jnp.where(masks[h], v[h * L:(h + 1) * L], 0.0)
        return out

    def softmax(s):
        e = jnp.exp(s - jnp.max(s, -1, keepdims=True))
        return e / jnp.sum(e, -1, keepdims=True)

    for i in range(ni):
        g.XF[i * L:(i + 1) * L] = g.x[i].astype(f32)
        mine = jnp.concatenate([g.patches[:, i, :].astype(f32), jnp.zeros((KP - NP, m.PW), f32)], 0)
        g.PT[i * KP:(i + 1) * KP] = mine.astype(bf16)
    g.X[0:T] = g.XF[...].astype(bf16)
    swaps = [pair(g.X, T), pair(g.PT, ni * KP)]
    for s in swaps:
        s.start()

    g.ACC[...] = jnp.zeros((T, D), f32)
    gather_steps()

    def self_forward(o, slot):
        t = shard(o)
        bias = g.VG[t].astype(f32)[0:1, LANES:]
        qkv = (dot_nt(g.X[0:T], g.SA[o, 0:m.QW]) + bias).astype(bf16)
        g.QKV[o] = qkv
        qf = qkv.astype(f32)
        outs = []
        for i in range(ni):
            r = slice(i * L, (i + 1) * L)
            qs = stack(qf[r, 0:hp], high)
            k_i = qf[r, 3 * LANES:3 * LANES + hp].astype(bf16)
            v_i = qf[r, 2 * LANES:2 * LANES + hp].astype(bf16)
            p = softmax(dot_nt(qs, k_i) * score_scale)
            g.PS[o * ni + i] = p
            outs.append(unstack(dot(p.astype(bf16), v_i), low))
        mixed = jnp.concatenate(outs, 0).astype(bf16)
        g.MX[0, o, 0:T] = mixed
        g.ACC[...] += dot(mixed, g.SO[o])

    stream(self_blocks, self_forward, after_each(gather_steps), cross_blocks)

    def out_row(j):
        return tuple(v[...].astype(f32)[j:j + 1, :] for v in (g.ob, g.gain, g.shift))

    ob, gn, sh = out_row(0)
    first, normed, inv = norm_forward(g.XF[...] + g.ACC[...] + ob, gn, sh)
    g.NM[0] = normed
    g.INV[0] = jnp.broadcast_to(inv, (T, LANES))
    g.F[0:T] = first.astype(bf16)
    g.ACC[...] = jnp.zeros((T, D), f32)
    gather_steps()

    key_pos = lax.broadcasted_iota(jnp.int32, (nh * L, KP), 1)

    def cross_forward(o, slot):
        t = shard(o)
        vb = g.VG[t].astype(f32)
        cq = (dot_nt(g.F[0:T], g.SA[o, 0:hp]) + vb[0:1, 0:hp]).astype(bf16)
        g.CQ[o] = cq
        cqf = cq.astype(f32)
        kv = (dot_nt(g.PT[0:ni * KP], g.SB[slot]) + vb[1:2, 0:m.BW]).astype(bf16)
        g.KV[o] = kv
        outs = []
        for i in range(ni):
            qs = stack(cqf[i * L:(i + 1) * L], low)
            kvi = g.KV[o, i * KP:(i + 1) * KP]
            s = dot_nt(qs, kvi[:, 0:hp]) * score_scale
            s = jnp.where(key_pos < g.rows[z * ni + i], s, -1e30)
            p = softmax(s)
            g.PC[o * ni + i] = p
            outs.append(unstack(dot(p.astype(bf16), kvi[:, LANES:LANES + hp]), high))
        mixed = jnp.concatenate(outs, 0).astype(bf16)
        g.MX[1, o, 0:T] = mixed
        g.ACC[...] += dot(mixed, g.SO[o])

    stream(cross_blocks, cross_forward, after_each(gather_steps), hidden_blocks)
    ob, gn, sh = out_row(1)
    second, normed, inv = norm_forward(g.F[0:T].astype(f32) + g.ACC[...] + ob, gn, sh)
    g.NM[1] = normed
    g.INV[1] = jnp.broadcast_to(inv, (T, LANES))
    g.S2[0:T] = second.astype(bf16)
    gather_steps()
    other = g.MX.at[1 - core]
    mix_swap = pltpu.make_async_remote_copy(other.at[:, pl.ds(0, T)], other.at[:, pl.ds(T, T)], g.cs.at[m.swaps - 1], g.cr.at[m.swaps - 1], device_id=(partner, z), device_id_type=MESH)
    mix_swap.start()
    swaps += [pair(g.F, T), pair(g.S2, T)]
    for s in swaps[2:4]:
        s.start()

    def hidden_forward(o, slot):
        t = shard(o)
        pre = dot(g.S2[0:T], g.SA[o]) + g.VG[t].astype(f32)[2:3, :]
        cdf = 0.5 * (1.0 + lax.erf(pre * math.sqrt(0.5)))
        g.GP[o] = cdf + pre * jnp.exp(-0.5 * pre * pre) * (1.0 / math.sqrt(2.0 * math.pi))
        g.HD[o, 0:T] = (pre * cdf).astype(bf16)

    stream(hidden_blocks, hidden_forward, after_each(gather_steps), output_blocks)
    hid_swaps = [pair(g.HD.at[o], T) for o in range(nz)]
    for s in hid_swaps:
        s.start()
    g.ACC[...] = jnp.zeros((T, D), f32)
    gather_steps()

    def output_forward(o, slot):
        g.ACC[...] += dot(g.HD[o, 0:T], g.SA[o])

    stream(output_blocks, output_forward, after_each(gather_steps), back_blocks)
    gather_steps()
    ob, gn, sh = out_row(2)
    final, normed, inv = norm_forward(g.S2[0:T].astype(f32) + g.ACC[...] + ob, gn, sh)
    g.FO[...] = final.reshape(ni, L, D)
    layer_store = pltpu.make_async_copy(g.FO, g.layer_out, g.js.at[8])
    layer_store.start()

    for i in range(ni):
        g.ACC[i * L:(i + 1) * L] = g.cot[i].astype(f32)
    cot = g.ACC[...]
    g.SM[...] = jnp.zeros(g.SM.shape, f32)

    def record(j, grad_in, grad_out, normed):
        g.SM[j:j + 1] = col_sum(grad_in)
        g.SM[3 + j:4 + j] = col_sum(grad_out * normed)
        g.SM[6 + j:7 + j] = col_sum(grad_out)

    third = norm_backward(cot, normed, inv, gn)
    record(2, third, cot, normed)
    g.G3[0:T] = third.astype(bf16)
    swap3 = pair(g.G3, T)
    swap3.start()

    rsem = (g.ss, g.rs, g.ls)
    results = {"A": g.RA, "B": g.RB, "O": g.RO, "H": g.RH, "W": g.RW}
    chunks = []
    progress = {}
    for c, (k, h0, half, order) in enumerate(m.reduce_plan):
        recvs = {b: R[f"rv{c}_{b}"] for b in m.bits[1:3]}
        whole = m.rows[k] // 2
        chunks.append(Reduce(R[f"kp{c}"], recvs, R[f"ln{c}"], R.get(f"ex{c}"), results[k], core * whole + h0, half, order, pos, nz, m.bits, rsem, c))
    for cls in classes:
        for c in range(len(chunks) + 1):
            for what in range(3):
                progress[cls, c, what] = 0

    def half_columns(apart, count=None):
        return pl.ds(pl.multiple_of(core * apart, LANES), count or apart)

    def deal(k, t, value):
        for c, p in enumerate(m.reduce_plan):
            if p[0] == k:
                R[f"kp{c}"][t] = value[p[1]:p[1] + p[2]].astype(bf16)

    reduce_steps()

    swap3.wait_recv()
    for s in hid_swaps:
        s.wait_recv()
    reduce_steps()

    def job_w(o, c):
        t = shard(o)
        deal("W", t, dot_tn(g.HD[o, :, half_columns(m.FZ // 2)], g.G3[...]))
        return c
    lax.fori_loop(0, nz, job_w, 0)
    for s in hid_swaps:
        s.wait_send()
    reduce_steps()
    g.ACC[...] = third

    def loop_send(ref, rows, kind, o):
        pltpu.make_async_remote_copy(ref.at[o, pl.ds(0, rows)], ref.at[o, pl.ds(rows, rows)], g.ds.at[kind, o], g.dr.at[kind, o], device_id=(partner, z), device_id_type=MESH).start()

    def hidden_backward(o, slot):
        t = shard(o)
        pre = (dot_nt(g.G3[0:T], g.SA[o]) * g.GP[o]).astype(bf16)
        g.DP[o, 0:T] = pre
        g.SM[pl.ds(9 + t, 1)] = col_sum(pre.astype(f32))
        loop_send(g.DP, T, 0, o)
        g.ACC[...] += dot_nt(pre, g.SH[slot])

    stream(back_blocks, hidden_backward, after_each(reduce_steps), [], cross_back)
    reduce_steps()

    def loop_wait(ref, rows, kind):
        for o in range(nz):
            cp = pltpu.make_async_remote_copy(ref.at[o, pl.ds(0, rows)], ref.at[o, pl.ds(rows, rows)], g.ds.at[kind, o], g.dr.at[kind, o], device_id=(partner, z), device_id_type=MESH)
            cp.wait()

    gn = out_row(1)[1]
    normed, inv = g.NM[1], g.INV[1][:, 0:1]
    grad = g.ACC[...]
    secondg = norm_backward(grad, normed, inv, gn)
    record(1, secondg, grad, normed)
    g.G12[1, 0:T] = secondg.astype(bf16)
    swap2 = pair(g.G12.at[1], T)
    swap2.start()
    reduce_steps()
    loop_wait(g.DP, T, 0)
    swaps[3].wait_recv()

    def job_h(o, c):
        t = shard(o)
        deal("H", t, dot_tn(g.S2[:, half_columns(D // 2)], g.DP[o]))
        return c
    lax.fori_loop(0, nz, job_h, 0)
    reduce_steps()

    g.ACC[...] = secondg

    def backward_unit(qs, k_i, v_i, p, ms, masks):
        grad_v = dot_tn(p.astype(bf16), ms)
        grad_p = dot_nt(ms, v_i)
        gs = (p * (grad_p - jnp.sum(p * grad_p, -1, keepdims=True))).astype(bf16)
        grad_q = unstack(dot(gs, k_i), masks) * score_scale
        grad_k = dot_tn(gs, qs) * score_scale
        return grad_q, grad_k.astype(bf16).astype(f32), grad_v.astype(bf16).astype(f32)

    def cross_backward(o, slot):
        t = shard(o)
        for b in cross_back:
            arrived(b, o)
        gm = dot_nt(g.G12[1, 0:T], g.SO[o]).astype(bf16).astype(f32)
        cqf = g.CQ[o].astype(f32)
        grads = []
        for i in range(ni):
            r = slice(i * L, (i + 1) * L)
            kvi = g.KV[o, i * KP:(i + 1) * KP]
            gq, gk, gv = backward_unit(stack(cqf[r], low), kvi[:, 0:hp], kvi[:, LANES:LANES + hp], g.PC[o * ni + i], stack(gm[r], high), low)
            grads.append(gq)
            g.DKV[o, i * KP:(i + 1) * KP] = jnp.concatenate([gk[:, 0:LANES], gk[:, LANES:] + gv[:, 0:LANES], gv[:, LANES:]], 1).astype(bf16)
        dcq = jnp.concatenate(grads, 0).astype(bf16)
        g.DCQ[o, 0:T] = dcq
        loop_send(g.DCQ, T, 1, o)
        loop_send(g.DKV, ni * KP, 2, o)
        dkv = g.DKV[o, 0:ni * KP]
        g.SM[pl.ds(9 + nz + t, 1), 0:hp] = col_sum(dcq.astype(f32))
        g.SM[pl.ds(9 + 2 * nz + t, 1), 0:m.BW] = col_sum(dkv.astype(f32))
        g.ACC[...] += dot(dcq, g.SA[o, 0:hp])
        pltpu.make_async_copy(g.DKV.at[o, pl.ds(0, ni * KP)], g.DK.at[o], g.dk.at[o]).start()

    stream([], cross_backward, after_each(reduce_steps), [], self_blocks)
    reduce_steps()
    gn = out_row(0)[1]
    normed, inv = g.NM[0], g.INV[0][:, 0:1]
    grad = g.ACC[...]
    firstg = norm_backward(grad, normed, inv, gn)
    record(0, firstg, grad, normed)
    g.G12[0, 0:T] = firstg.astype(bf16)
    swap1 = pair(g.G12.at[0], T)
    swap1.start()
    reduce_steps()
    loop_wait(g.DCQ, T, 1)
    loop_wait(g.DKV, ni * KP, 2)
    swaps[1].wait_recv()

    def job_b(o, c):
        t = shard(o)
        g.TMP[...] = dot_tn(g.DKV[o, :, half_columns(LANES, hp)], g.PT[...])
        deal("B", t, g.TMP[pl.ds(pl.multiple_of(core * HEAD, 16), BW // 2)])
        return c
    lax.fori_loop(0, nz, job_b, 0)
    reduce_steps()

    g.ACC[...] = firstg

    def self_backward(o, slot):
        t = shard(o)
        for b in self_blocks:
            arrived(b, o)
        gm = dot_nt(g.G12[0, 0:T], g.SO[o]).astype(bf16).astype(f32)
        qf = g.QKV[o].astype(f32)
        gqs, gks, gvs = [], [], []
        for i in range(ni):
            r = slice(i * L, (i + 1) * L)
            k_i = qf[r, 3 * LANES:3 * LANES + hp].astype(bf16)
            v_i = qf[r, 2 * LANES:2 * LANES + hp].astype(bf16)
            gq, gk, gv = backward_unit(stack(qf[r, 0:hp], high), k_i, v_i, g.PS[o * ni + i], stack(gm[r], low), high)
            gqs.append(gq)
            gks.append(gk)
            gvs.append(gv)
        gq, gk, gv = (jnp.concatenate(v, 0) for v in (gqs, gks, gvs))
        dq = jnp.concatenate([gq, gv[:, 0:LANES], gv[:, LANES:] + gk[:, 0:LANES], gk[:, LANES:]], 1).astype(bf16)
        g.DQ[o, 0:T] = dq
        loop_send(g.DQ, T, 3, o)
        g.SM[pl.ds(9 + 3 * nz + t, 1), 0:m.QW] = col_sum(dq.astype(f32))
        g.ACC[...] += dot(dq, g.SA[o, 0:m.QW])

    stream([], self_backward, after_each(reduce_steps), [])
    layer_store.wait()
    g.FO[...] = g.ACC[...].reshape(ni, L, D)
    text_store = pltpu.make_async_copy(g.FO, g.text_grad, g.js.at[8])
    text_store.start()
    reduce_steps()
    loop_wait(g.DQ, T, 3)
    swap1.wait_recv()
    swap2.wait_recv()
    for s in swaps[0:1] + swaps[2:3] + [mix_swap]:
        s.wait_recv()

    def job_o(o, c):
        t = shard(o)
        g.TMP[:, 0:D] = dot_tn(g.MX[core, o], g.G12[core])
        deal("O", t, g.TMP[pl.ds(pl.multiple_of(core * HEAD, 16), hw), 0:D])
        return c
    lax.fori_loop(0, nz, job_o, 0)
    reduce_steps()

    def job_a(o, c):
        t = shard(o)

        @pl.when(core == 0)
        def _():
            left = dot_tn(g.DCQ[o], g.F[...])
            right = dot_tn(g.DQ[o, :, 0:hp], g.X[...])
            deal("A", t, jnp.concatenate([left[0:LANES], left[LANES:] + right[0:LANES], right[LANES:]], 0))

        @pl.when(core == 1)
        def _():
            deal("A", t, dot_tn(g.DQ[o, :, hp:], g.X[...]))
        return c
    lax.fori_loop(0, nz, job_a, 0)
    reduce_steps()

    reduce_steps()
    assert calls == [len(m.gather_steps[0]), len(m.reduce_steps[0])], calls
    assert all(sum(len(p) for p in m.reduce_steps[cls]) == sum(progress[cls, c, w] for c in range(len(chunks) + 1) for w in range(3)) for cls in classes)

    sends = [small_spread(o, lambda to: z) for o in range(1, nz)]
    for cp in sends + swaps + [swap1, swap2, swap3, mix_swap]:
        cp.wait_send()
    for o in range(nz):
        pltpu.make_async_copy(g.DKV.at[o, pl.ds(0, ni * KP)], g.DK.at[o], g.dk.at[o]).wait()
    text_store.wait()
    finish_gather()
    for cls in classes:
        @pl.when(kind == cls)
        def _():
            for c in chunks:
                c.finish(cls)


GATHER_PLAN = (("V", 0, 16, ""), ("A", 0, 256, "yxc"), ("A", 256, 256, "yxc"), ("A", 512, 256, "xyc"), ("B", 0, 384, "xc"), ("O", 0, 384, "xyc"), ("H", 0, 256,
    "yxc"), ("H", 256, 256, "yc"), ("H", 512, 256, "xyc"), ("W", 512, 256, "xc"), ("W", 256, 256, "xyc"), ("W", 0, 256, "yc"))
GATHER_ORDER = ((0, 80, 120, 40, 200, 400, 13, 93, 133, 53, 101, 213, 141, 413, 61, 14, 94, 109, 134, 149, 221, 117, 54, 102, 421, 157, 214, 414, 69, 160, 15, 142,
    95, 77, 229, 135, 320, 62, 110, 55, 237, -1, 118, 222, 215, 429, 422, 415, 143, 150, 240, 280, 103, 437, 158, 70, 63, 173, 223, 78, 333, 423, 230,
    111, 238, -1, 119, 71, 430, 151, 334, 174, 253, 79, 438, 159, 231, 293, 181, 360, 341, 440, 239, -1, 431, 342, 189, 175, 261, -1, 439, 335, 182, 254,
    301, -1, 349, 350, 190, 262, 183, 255, 309, 294, -1, 453, 357, 358, 343, 191, 269, 263, 295, -1, 373, 277, 270, 302, -1, 461, 454, 278, 374, 271, 351,
    310, -1, 469, 359, 381, 375, 279, 303, -1, 455, 382, 462, 389, 311, -1, 390, -1, 470, 383, -1, 463, -1, 391, 471, -1, -1), (0, 4, 80, 84, 120, 124,
    40, 44, 200, 204, 400, 404, 9, 13, 89, 93, 129, 133, 49, 53, 97, 209, 213, 101, 137, 409, 413, 141, 57, 14, 61, 94, 105, 134, 145, 54, 217, 113, 153,
    214, 149, 221, 414, 102, 160, 164, 157, 109, 62, 417, 117, 320, 421, 324, 225, 65, 233, 169, 173, 73, -1, 142, 69, 229, 425, 329, 333, 222, 240, 244,
    280, 249, 284, 422, 77, 429, 237, 174, 433, 289, 110, 437, 334, 150, 253, 118, 70, 158, 293, 230, 78, 254, 257, 238, -1, 430, 177, 294, -1, 440, 444,
    438, 360, 185, 364, 181, 261, 297, -1, 337, 341, 189, 369, 262, 305, 301, -1, 449, 453, 182, 345, 373, 309, 302, 342, 374, 190, 349, -1, 457, 454,
    353, 357, 265, 269, 310, -1, 465, 461, 377, 273, 277, -1, 469, 462, 350, 385, 270, 381, -1, 470, 358, 382, 278, -1, 389, -1, 390, -1, -1, -1, -1, -1))
REDUCE_PLAN = (("W", 128, "zyx"), ("W", 128, "yxz"), ("W", 128, "xyz"), ("H", 128, "xyz"), ("H", 128, "zxy"), ("H", 128, "yxz"), ("B", 64, "xyz"), ("B", 128,
    "yzx"), ("O", 64, "xyz"), ("O", 64, "zyx"), ("O", 64, "zxy"), ("A", 128, "yxz"), ("A", 128, "yxz"), ("A", 128, "xzy"))
REDUCE_ORDER = ((-1, -1, 0, 1, 6, 3, -1, -1, -1, -1, -1, -1, 15, 9, 12, 13, -1, 6, 3, -1, -1, -1, 2, 0, 15, 9, -1, -1, 0, 18, 6, 7, 3, 4, 21, -1, 0, 15, 16, -1, 9,
    10, -1, -1, 0, 18, 14, 12, 8, 6, -1, 27, 28, 24, 30, 31, -1, 39, 33, 36, 5, 0, 3, 21, 22, 12, 17, 15, -1, 0, 42, 24, 18, 19, 42, 6, 11, 9, 39, 40, 29,
    27, 3, 33, 15, 32, 42, 30, 6, 6, 36, 33, 34, 12, 30, 23, 21, 24, 25, 20, 18, 9, 27, 36, 37, 3, 21, 3, 15, 9, 27, 41, 39, 15, 42, 21, 9, 27, 12, 30,
    35, 33, 18, 39, 26, 24, 12, 33, 21, 12, 38, 36, 27, 18, 30, 21, 27, 39, 42, 18, 24, 36, 42, 30, 33, 30, 39, 33, 36, 24, 39, 36, 24), (-1, -1, 0, 6, 3,
    -1, -1, -1, -1, -1, 1, -1, 15, 9, 12, -1, 1, 6, 3, 2, -1, 1, -1, 2, 0, 13, -1, 15, 9, -1, 6, 3, 13, -1, 0, 18, 21, 15, 13, 14, -1, 0, 7, 7, 7, 9, 14,
    12, -1, 8, 4, 4, 4, 8, 6, -1, 0, 18, 5, 16, 16, 16, 5, 3, 10, -1, 17, 21, 3, 10, 17, 6, 15, 10, 12, -1, 0, 11, 11, 9, 27, 28, 28, 24, 30, -1, 39, 0,
    33, 18, 6, 36, 3, 15, 28, 29, 31, 12, -1, 6, 42, 9, 3, 29, 27, 24, 31, 42, 31, 32, 32, 30, 22, 22, 33, 39, 23, 22, 9, 19, 19, 9, 23, 19, 42, 21, 20,
    30, 20, 18, 40, 36, 40, 33, 15, 41, 40, 21, 12, 34, 15, 27, 41, 39, 34, 34, 24, 35, 25, 25, 36, 25, 35, 33, 37, 42, 21, 30, 26, 37, 26, 18, 24, 37,
    39, 12, 38, 27, 38, 33, 36, 12, 21, 18, 30, 27, 24, 21, 36, 39, 18, 42, 30, 42, 33, 24, 30, 27, 33, 24, 39, 27, 36, 39, 36))


def unpack(orders, decode):
    out = []
    for order in orders:
        parts = [[]]
        for code in order:
            if code < 0:
                parts.append([])
            else:
                parts[-1].append(decode(code))
        out.append(parts)
    return out


def gather_code(code):
    return code // 40, code // 8 % 5 - 1, code // 4 % 2, code % 4


def reduce_code(code):
    return code // 3, code % 3


def plans(m):
    link = dict(zip("cxy", m.bits[:3]), z="z")
    m.gather_plan = [(k, r0, rows, tuple(link[o] for o in order)) for k, r0, rows, order in GATHER_PLAN]
    m.gather_steps = unpack(GATHER_ORDER, gather_code)
    m.reduce_plan = []
    at = {}
    for k, half, order in REDUCE_PLAN:
        h0 = at.get(k, 0)
        at[k] = h0 + half
        m.reduce_plan.append((k, h0, half, tuple(link[o] for o in order)))
    m.reduce_steps = unpack(REDUCE_ORDER, reduce_code)
    assert all(at[k] * 2 == m.rows[k] for k in at) and m.nz == 4


def run_layer(m, x, patches, rows, cot, wa, ab, wao, wq, wp, cb, wco, H, hb, W, ob, gain, shift):
    nz = m.nz
    ni, L, D = x.shape
    T = ni * L
    m.ni, m.L, m.D, m.T = ni, L, D, T
    m.NP, m.PW = patches.shape[1:]
    by_patch = jnp.swapaxes(patches, 0, 1)
    m.KP = (m.NP + 15) // 16 * 16
    hw = m.hw = D // nz
    m.nh = hw // HEAD
    m.hp = (hw + HEAD + LANES - 1) // LANES * LANES
    hp, KP, PW = m.hp, m.KP, m.PW
    m.BW, m.QW, m.FZ = 2 * hw, D - LANES, W.shape[0]
    FZ, BW = m.FZ, m.BW
    m.rows = dict(A=D, B=BW, O=2 * hw, H=D, W=FZ)
    lanes = dict(A=D, B=PW, O=D, H=FZ, W=D)
    plans(m)
    m.swaps = nz + 9
    V, sem = pltpu.VMEM, pltpu.SemaphoreType.DMA
    nc, ng = len(m.reduce_plan), len(m.gather_plan)
    nb = len(m.bits)
    sums = (9 + 4 * nz + 7) // 8 * 8
    scratch = dict(
        VG=V((nz, 16, D), bf16), XF=V((T, D), f32), X=V((2 * T, D), bf16), PT=V((2 * ni * KP, PW), bf16),
        SA=V((nz, D, D), bf16), SH=V((2, D, D), bf16), SB=V((2, BW, PW), bf16), SO=V((nz, hp, D), bf16),
        ACC=V((T, D), f32), QKV=V((nz, T, m.QW), bf16), PS=V((nz * ni, m.nh * L, L), f32), MX=V((2, nz, 2 * T, hp), bf16),
        NM=V((2, T, D), f32), INV=V((2, T, LANES), f32), F=V((2 * T, D), bf16), S2=V((2 * T, D), bf16),
        CQ=V((nz, T, hp), bf16), PC=V((nz * ni, m.nh * L, KP), f32),
        GP=V((nz, T, FZ), f32), HD=V((nz, 2 * T, FZ), bf16), SM=V((sums, D), f32), G3=V((2 * T, D), bf16), DP=V((nz, 2 * T, FZ), bf16),
        G12=V((2, 2 * T, D), bf16), DKV=V((nz, 2 * ni * KP, m.BW), bf16),
        TMP=V((hp, PW), f32), FO=V((ni, L, D), f32), AO=V((D, D), bf16), BO=V((BW, PW), bf16), OO=V((2 * hw, D), bf16), VO=V((16, D), bf16), SR=V((nb, sums, D), f32), SZ=V((nz, sums, D), f32),
        zs=sem((ng, 2, nz)), zr=sem((ng, 2, nz)), ps=sem((ng, 3, 2, nz)), pr=sem((ng, 3, 2, nz)),
        cs=sem((m.swaps,)), cr=sem((m.swaps,)), ds=sem((4, nz)), dr=sem((4, nz)),
        dk=sem((nz,)), js=sem((9,)), sa=sem((nz,)), sh=sem((2,)), sb=sem((2,)), so=sem((nz,)),
        ss=sem((nc, 2 * nz + 5 + nb)), rs=sem((nc, 2 * nz + 5 + nb)), ls=sem((nc,)), ms=sem((nb + nz,)), mr=sem((nb,)), zm=sem((nz,)),
    )
    for c, (k, h0, half, order) in enumerate(m.reduce_plan):
        C = lanes[k]
        scratch[f"kp{c}"] = V((nz, half, C), bf16)
        for b in m.bits[1:3]:
            lead = nz if order.index(b) < order.index("z") else 1
            scratch[f"rv{c}_{b}"] = V((lead, op_rows(half, order, b), C), bf16)
        scratch[f"ln{c}"] = V((2, nz - 1, op_rows(half, order, "z"), C), bf16)
        if nb > 3:
            scratch[f"ex{c}"] = V((nb - 3, half // 4, C), bf16)
    S = jax.ShapeDtypeStruct
    hbm, vm, sm = (pl.BlockSpec(memory_space=s) for s in (pl.ANY, pltpu.VMEM, pltpu.SMEM))
    outs = dict(
        layer_out=(S((ni, L, D), f32), hbm), text_grad=(S((ni, L, D), f32), hbm), DK=(S((nz, ni * KP, m.BW), bf16), hbm), small=(S((sums, D), f32), vm),
        **{"R" + k: (S((m.rows[k], lanes[k]), bf16), hbm) for k in "ABOHW"},
        **{"G" + k: (S((nz, m.rows[k], lanes[k]), bf16), hbm) for k in "ABOHW"},
    )
    turn = lambda a: jnp.swapaxes(a, -1, -2)
    ins = dict(x=(x, vm), patches=(by_patch, vm), rows=(rows, sm), cot=(cot, vm), wa=(turn(wa), hbm), ab=(ab, vm), wao=(wao, hbm), wq=(turn(wq), hbm), wp=(turn(wp), hbm),
               cb=(cb, vm), wco=(wco, hbm), H=(H, hbm), hb=(hb, vm), W=(W, hbm), ob=(ob, vm), gain=(gain, vm), shift=(shift, vm))
    m.inputs, m.outputs, m.scratch = list(ins), list(outs), list(scratch)
    res = pl.pallas_call(
        functools.partial(layer_kernel, m),
        out_shape=tuple(o[0] for o in outs.values()),
        in_specs=[i[1] for i in ins.values()],
        out_specs=tuple(o[1] for o in outs.values()),
        scratch_shapes=list(scratch.values()),
        compiler_params=pltpu.CompilerParams(collective_id=0, has_side_effects=True, vmem_limit_bytes=67043328),
        name="layer",
    )(*[i[0] for i in ins.values()])
    return dict(zip(outs, res))


finish_ins = ("RA", "RB", "RO", "RH", "RW", "layer_out", "text_grad", "DK", "GB", "wp", "small")
finish_outs = ("layer_out_", "text_grad_", "patch_grad", "attn", "attn_bias", "attn_out", "query", "patch", "cross_bias", "cross_out", "hidden", "hidden_bias", "output", "out_bias", "gain", "shift")


def finish_kernel(m, names, *refs):
    g = Dims()
    for k, v in zip(names, refs):
        setattr(g, k, v)
    nz, hw, ni, KP, NP = m.nz, m.hw, m.ni, m.KP, m.NP
    z = lax.axis_index("mp")
    loads = {}

    def load(name, src, dst):
        cp = pltpu.make_async_copy(src, dst, g.isem.at[len(loads)])
        cp.start()
        loads[name] = cp
    load("W", g.RW, g.vW)
    load("H", g.RH, g.vH)
    load("DK", g.DK, g.vD)
    for j in range(2):
        load(f"B0{j}", g.wp.at[j], g.vB.at[0, pl.ds(j * hw, hw)])
    for o in range(1, nz):
        load(f"B{o}", g.GB.at[nth_shard(z, nz, jnp.int32(o))], g.vB.at[o])
    load("lo", g.layer_out, g.vL)
    load("tg", g.text_grad, g.vT)
    load("B", g.RB, g.vP)
    load("O", g.RO, g.vO)
    load("A", g.RA, g.vA)
    stores = []

    def store(src, dst):
        cp = pltpu.make_async_copy(src, dst, g.osem.at[len(stores)])
        cp.start()
        stores.append(cp)

    def widen(src, dst, row0=0):
        step = HEAD

        def body(i, c):
            r = pl.multiple_of(i * step, step)
            dst[pl.ds(r, step), :] = src[pl.ds(row0 + r, step), :].astype(f32)
            return c
        lax.fori_loop(0, dst.shape[0] // step, body, 0)

    loads["W"].wait()
    widen(g.vW, g.fW)
    store(g.fW, g.output)
    loads["H"].wait()
    widen(g.vH, g.fH)
    store(g.fH, g.hidden)
    loads["DK"].wait()
    for k in ["B00", "B01"] + [f"B{o}" for o in range(1, nz)]:
        loads[k].wait()
    for i in range(ni):
        total = dot(g.vD[0, i * KP:(i + 1) * KP], g.vB[0])
        for o in range(1, nz):
            total = total + dot(g.vD[o, i * KP:(i + 1) * KP], g.vB[o])
        g.fG[:, i, :] = total[0:NP]
    store(g.fG, g.patch_grad)
    loads["lo"].wait()
    store(g.vL, g.layer_out_)
    loads["tg"].wait()
    store(g.vT, g.text_grad_)
    loads["B"].wait()
    for j in range(2):
        widen(g.vP, g.fP.at[j], j * hw)
    store(g.fP, g.patch)
    loads["O"].wait()
    widen(g.vO, g.fO)
    store(g.fO.at[pl.ds(0, hw)], g.attn_out)
    store(g.fO.at[pl.ds(hw, hw)], g.cross_out)
    loads["A"].wait()
    widen(g.vA, g.fQ)
    for j, part in ((0, 1), (1, 3), (2, 2)):
        widen(g.vA, g.fA.at[j], part * hw)
    store(g.fQ, g.query)
    store(g.fA, g.attn)
    row = lambda k: g.small[pl.ds(9 + k * nz + z, 1), :]
    qv = row(3)[:, 0:5 * LANES]
    at = hw - LANES
    g.attn_bias[0:1] = qv[:, at:at + hw]
    g.attn_bias[1:2] = qv[:, at + hw:at + 2 * hw]
    g.cross_bias[0:1] = row(1)[:, 0:hw]
    g.cross_bias[1:2] = row(2)[:, hw:2 * hw]
    g.hidden_bias[...] = row(0).reshape(m.FZ)
    g.out_bias[...] = g.small[0:3, :]
    g.gain[...] = g.small[3:6, :]
    g.shift[...] = g.small[6:9, :]
    for cp in stores:
        cp.wait()


def finish(m, r, wp):
    nz, ni, L, D, PW, FZ, BW, KP, NP = m.nz, m.ni, m.L, m.D, m.PW, m.FZ, m.BW, m.KP, m.NP
    hw = m.hw = D // nz
    S, V, sem = jax.ShapeDtypeStruct, pltpu.VMEM, pltpu.SemaphoreType.DMA
    hbm, vm = pl.BlockSpec(memory_space=pl.ANY), pl.BlockSpec(memory_space=pltpu.VMEM)
    shapes = ((ni, L, D), (ni, L, D), (NP, ni, PW), (3, hw, D), (2, hw), (hw, D), (hw, D), (2, hw, PW), (2, hw), (hw, D), (D, FZ), (FZ,), (FZ, D), (3, D), (3, D), (3, D))
    small = {"attn_bias", "cross_bias", "hidden_bias", "out_bias", "gain", "shift"}
    scratch = dict(
        vW=V((FZ, D), bf16), vH=V((D, FZ), bf16), vD=V((nz, ni * KP, BW), bf16), vB=V((nz, BW, PW), bf16), vL=V((ni, L, D), f32), vT=V((ni, L, D), f32),
        vP=V((BW, PW), bf16), vO=V((2 * hw, D), bf16), vA=V((D, D), bf16), fW=V((FZ, D), f32), fH=V((D, FZ), f32), fG=V((NP, ni, PW), f32),
        fP=V((2, hw, PW), f32), fO=V((2 * hw, D), f32), fQ=V((hw, D), f32), fA=V((3, hw, D), f32), isem=sem((9 + nz,)), osem=sem((9 + ni,)),
    )
    ins = [r[k] if k != "wp" else jnp.swapaxes(wp, -1, -2) for k in finish_ins]
    return pl.pallas_call(
        functools.partial(finish_kernel, m, finish_ins + finish_outs + tuple(scratch)),
        out_shape=tuple(S(s, f32) for s in shapes),
        in_specs=[vm if k == "small" else hbm for k in finish_ins],
        out_specs=tuple(vm if k in small else hbm for k in finish_outs),
        scratch_shapes=list(scratch.values()),
        compiler_params=pltpu.CompilerParams(vmem_limit_bytes=56 << 20),
        name="finish",
    )(*ins)


def per_device(nd, nz, text_states, patch_states, patch_rows, cotangent, w_attn, attn_bias, w_attn_out, w_query, w_patch, cross_bias, w_cross_out, w_hidden, hidden_bias, w_output, out_bias, norm_gain, norm_shift):
    m = Dims()
    m.nz, m.bits = nz, tuple(range(nd.bit_length() - 1))
    r = run_layer(m, text_states, patch_states, patch_rows, cotangent, w_attn, attn_bias, w_attn_out, w_query, w_patch, cross_bias, w_cross_out, w_hidden, hidden_bias, w_output, out_bias, norm_gain, norm_shift)
    outs = list(finish(m, r, w_patch))
    for k in ("attn", "query", "patch"):
        at = finish_outs.index(k)
        outs[at] = jnp.swapaxes(outs[at], -1, -2)
    at = finish_outs.index("patch_grad")
    outs[at] = jnp.swapaxes(outs[at], 0, 1)
    return tuple(outs)


def solution(mesh):
    nd, nz = mesh.shape["dp"], mesh.shape["mp"]
    rows = P(("dp", "mp"), None, None)
    return jax.shard_map(
        functools.partial(per_device, nd, nz),
        mesh=mesh,
        in_specs=(rows, rows, P("dp"), rows, P(None, None, "mp"), P(None, "mp"), P("mp", None), P(None, "mp"), P(None, None, "mp"), P(None, "mp"), P("mp", None), P(None, "mp"), P("mp"), P("mp", None), P(), P(), P()),
        out_specs=(rows, rows, rows, P(None, None, "mp"), P(None, "mp"), P("mp", None), P(None, "mp"), P(None, None, "mp"), P(None, "mp"), P("mp", None), P(None, "mp"), P("mp"), P("mp", None), P(), P(), P()),
        check_vma=False,
    )
```

```python
import functools
import math

import jax
import jax.numpy as jnp
from jax import lax
from jax.experimental import pallas as pl
from jax.experimental.pallas import tpu as pltpu
from jax.sharding import PartitionSpec as P

MESH = pl.DeviceIdType.MESH
HEAD = 64
LANES = 128
epsilon = 1e-06
score_scale = 1.0 / math.sqrt(HEAD)
bf16, f32 = jnp.bfloat16, jnp.float32


def bit_of(d, b):
    return lax.rem(lax.div(d, jnp.int32(2 ** b)), jnp.int32(2))


def flip(d, b):
    return d + (1 - 2 * bit_of(d, b)) * (2 ** b)


def when(cond, fn):
    if cond is True:
        fn()
    else:
        pl.when(cond)(fn)


class Gather:
    def __init__(self, src, dst, row0, rows, order, pos, nz, sems, base):
        self.nz = nz
        self.src, self.dst, self.row0, self.order, self.pos = src, dst, row0, order, pos
        self.piece = rows // (2 ** len(order))
        self.zs, self.zr, self.ps, self.pr = sems
        self.base = base
        self.k = len(order)

    def win(self, s):
        w = jnp.int32(0)
        for i, b in enumerate(self.order):
            if i >= s:
                w = w + bit_of(self.pos.d, b) * (2 ** i)
        return pl.ds(pl.multiple_of(self.row0 + w * self.piece, 16), self.piece * 2 ** s)

    def shard(self, dr, j):
        return self.pos.z + j * (2 * dr - 1) * self.pos.sign

    def cell(self, t, at):
        return lax.rem(t - at - 1 + self.nz, jnp.int32(self.nz))

    def zcopy(self, dr, j):
        p = self.pos
        t, rows = self.shard(dr, j), self.win(0)
        src = self.src.at[rows] if j == 0 else self.dst.at[t, rows]
        to = p.z + (1 - 2 * dr) * p.sign
        s = dr if j == 0 else 2 + self.cell(t, p.z)
        return pltpu.make_async_remote_copy(src, self.dst.at[t, rows], self.zs.at[self.base, s], self.zr.at[self.base, self.cell(t, to)], device_id=(p.d, to), device_id_type=MESH)

    def zwait(self, dr, j):
        p = self.pos
        t = self.shard(dr, j)
        part = self.dst.at[t, self.win(0)]
        pltpu.make_async_remote_copy(part, part, self.zs.at[self.base, 0], self.zr.at[self.base, self.cell(t, p.z)], device_id=(p.d, p.z - (1 - 2 * dr) * p.sign), device_id_type=MESH).wait_recv()

    def pcopy(self, s, dr, j):
        p = self.pos
        t = self.shard(dr, j)
        part = self.dst.at[t, self.win(s)]
        c = self.cell(t, p.z)
        return pltpu.make_async_remote_copy(part, part, self.ps.at[self.base, c], self.pr.at[self.base, s, c], device_id=(flip(p.d, self.order[s]), p.z), device_id_type=MESH)

    @staticmethod
    def has(cls, nz, dr, j):
        return cls >= j if dr == 0 else cls + j < nz

    @staticmethod
    def ahead(cls, dr):
        return dr == 0 or cls >= 1

    def item(self, cls, nz, st, dr, j):
        if st == -1:
            self.zcopy(dr, 0).start()
            return
        if st == 0:
            self.zwait(dr, j)
            if j <= nz - 2 and self.ahead(cls, dr):
                self.zcopy(dr, j).start()
        else:
            self.pcopy(st - 1, dr, j).wait()
        if st < self.k:
            self.pcopy(st, dr, j).start()

    def finish(self, cls, nz):
        for dr in (0, 1):
            for j in range(nz - 1):
                if self.ahead(cls, dr) and self.has(cls, nz, dr, j):
                    self.zcopy(dr, j).wait_send()


def add_into(dst, src, rows):
    step = 32 if rows % 32 == 0 else 16

    def body(i, c):
        r = pl.ds(pl.multiple_of(i * step, step), step)
        dst[r, :] = dst[r, :] + src[r, :]
        return c
    lax.fori_loop(0, rows // step, body, 0)


def add_all(dst, src, count, rows):
    def body(t, c):
        add_into(dst.at[t], src.at[t], rows)
        return c
    lax.fori_loop(0, count, body, 0)


def op_rows(half, order, op):
    size = half
    for o in order:
        if o == "z":
            if op == "z":
                return size
        else:
            size //= 2
            if o == op:
                return size
    return size


class Reduce:
    def __init__(self, keep, recvs, line, extra, result, row, half, order, pos, nz, bits, sems, base):
        self.keep, self.recvs, self.line, self.extra = keep, recvs, line, extra
        self.result, self.row, self.half, self.order = result, row, half, order
        self.pos, self.nz, self.bits = pos, nz, bits
        self.ss, self.rs, self.ls = sems
        self.base = base
        self.slot = 0
        self.last = None
        self.steps = []
        self.build()

    def remote(self, src, dst, b):
        r = self.slot
        self.slot += 1
        cp = lambda: pltpu.make_async_remote_copy(src, dst, self.ss.at[self.base, 0], self.rs.at[self.base, r], device_id=(flip(self.pos.d, b), self.pos.z), device_id_type=MESH)
        before, self.last = self.last, cp

        def start():
            if before is not None:
                before().wait_send()
            cp().start()
        return cp, start

    def build(self):
        d, z, nz = self.pos.d, self.pos.z, self.nz
        prev = lambda: None
        start, size, whole = jnp.int32(0), self.half, True
        taken = []

        def then(prev, start):
            def step():
                prev()
                start()
            self.steps.append(step)

        for op in self.order:
            if op == "z":
                self.rows = pl.ds(start, size)
                self.size = size
                self.steps.append(prev)
                prev, whole = (lambda: None), False
                continue
            size //= 2
            m = bit_of(d, op)
            keep0 = pl.multiple_of(start + m * size, 16)
            send0 = pl.multiple_of(start + (1 - m) * size, 16)
            buf = self.recvs[op]
            if whole:
                cp, leave = self.remote(self.keep.at[:, pl.ds(send0, size), :], buf, op)
            else:
                cp, leave = self.remote(self.keep.at[z, pl.ds(send0, size), :], buf.at[0], op)
            then(prev, leave)

            def prev(cp=cp, keep0=keep0, size=size, whole=whole, buf=buf):
                cp().wait_recv()
                if whole:
                    add_all(self.keep.at[:, pl.ds(keep0, size), :], buf, nz, size)
                else:
                    add_into(self.keep.at[z, pl.ds(keep0, size), :], buf.at[0], size)
            taken.append(op)
            start = keep0
        for e, b in enumerate(self.bits[3:]):
            cp, leave = self.remote(self.keep.at[z, pl.ds(start, size), :], self.extra.at[e], b)

            def prev(before=prev, cp=cp, leave=leave, e=e, start=start, size=size):
                before()
                leave()
                cp().wait_recv()
                cp().wait_send()
                add_into(self.keep.at[z, pl.ds(start, size), :], self.extra.at[e], size)
        at = pl.multiple_of(self.row + start, 16)
        total = self.keep.at[z, pl.ds(start, size), :]
        win = self.result.at[pl.ds(at, size), :]
        own = lambda win=win: pltpu.make_async_copy(total, win, self.ls.at[self.base])
        op = taken[-1]
        cp, leave = self.remote(total, win, op)

        def step(prev=prev, leave=leave):
            prev()
            own().start()
            leave()
        self.steps.append(step)

        def prev(cp=cp):
            cp().wait_recv()
            own().wait()
        for nxt in taken[-2::-1] + [self.bits[0]]:
            at = pl.multiple_of(at - bit_of(d, op) * size, 16)
            size *= 2
            op = nxt
            win = self.result.at[pl.ds(at, size), :]
            cp, leave = self.remote(win, win, op)
            then(prev, leave)
            prev = lambda cp=cp: cp().wait_recv()
        self.steps.append(prev)

    def hop(self, cls, kind, i, arriving):
        p, nz = self.pos, self.nz
        far, near = nz - 1 - i, i
        if kind == 1:
            t, way = far * (1 - p.upper) + near * p.upper, p.sign
        else:
            t, way = near * (1 - p.upper) + far * p.upper, -p.sign
        cell = self.keep.at[t, self.rows, :]
        s = 1 + (i if kind == 1 else nz - 1 - cls + i)
        first = kind == 1 and (arriving or cls < nz // 2 - 1)
        r = i if first else nz - 1 + i
        to = p.z - way if arriving else p.z + way
        land = self.line.at[r]
        cp = pltpu.make_async_remote_copy(cell, land, self.ss.at[self.base, s], self.rs.at[self.base, 5 + len(self.bits) - 3 + r], device_id=(p.d, to), device_id_type=MESH)
        return cp, cell, land

    def sends(self, cls, kind):
        return self.nz - 1 - cls if kind == 1 else cls

    def along(self, cls, kind, i):
        if kind == 1 and cls == 0:
            for k in range(self.nz - 1):
                self.hop(cls, 1, k, False)[0].start()
            return
        cp, cell, land = self.hop(cls, kind, i, True)
        cp.wait_recv()
        add_into(cell, land, self.size)
        if i < self.sends(cls, kind):
            self.hop(cls, kind, i, False)[0].start()

    def finish(self, cls):
        self.last().wait_send()
        for kind in (1, 2):
            for i in range(self.sends(cls, kind)):
                self.hop(cls, kind, i, False)[0].wait_send()


def enter(d, z, nz, bits):
    bar = pltpu.get_barrier_semaphore()
    for b in bits:
        pl.semaphore_signal(bar, inc=1, device_id=(flip(d, b), z), device_id_type=MESH)
    for o in range(1, nz):
        pl.semaphore_signal(bar, inc=1, device_id=(d, lax.rem(z + o, jnp.int32(nz))), device_id_type=MESH)
    pl.semaphore_wait(bar, len(bits) + nz - 1)


def dot(a, b):
    return lax.dot_general(a, b, (((1,), (0,)), ((), ())), preferred_element_type=f32)


def dot_nt(a, b):
    return lax.dot_general(a, b, (((1,), (1,)), ((), ())), preferred_element_type=f32)


def dot_tn(a, b):
    return lax.dot_general(a, b, (((0,), (0,)), ((), ())), preferred_element_type=f32)


def norm_forward(h, gain, shift):
    centred = h - jnp.mean(h, -1, keepdims=True)
    inverse = lax.rsqrt(jnp.mean(centred * centred, -1, keepdims=True) + epsilon)
    normed = centred * inverse
    return normed * gain + shift, normed, inverse


def norm_backward(grad, normed, inverse, gain):
    scaled = grad * gain
    return inverse * (scaled - jnp.mean(scaled, -1, keepdims=True) - normed * jnp.mean(scaled * normed, -1, keepdims=True))


def col_sum(v):
    return jnp.sum(v, axis=0, keepdims=True)


def nth_shard(z, nz, o):
    t = z
    for b in range(nz.bit_length() - 1):
        t = t + lax.rem(lax.div(o, jnp.int32(2 ** b)), jnp.int32(2)) * (1 - 2 * bit_of(z, b)) * (2 ** b)
    return t


class Dims:
    pass


def layer_kernel(m, *refs):
    n_in, n_out = len(m.inputs), len(m.outputs)
    R = dict(zip(m.inputs + m.outputs + m.scratch, refs))
    g = Dims()
    for k, v in R.items():
        setattr(g, k, v)
    ni, L, T, D, nz, hp, nh, KP, NP = m.ni, m.L, m.T, m.D, m.nz, m.hp, m.nh, m.KP, m.NP
    d, z = lax.axis_index("dp"), lax.axis_index("mp")
    core = bit_of(d, m.bits[0])
    partner = flip(d, m.bits[0])

    shard = functools.partial(nth_shard, z, nz)

    g.DCQ = g.HD.at[:, :, 0:hp]
    g.DQ = g.DP.at[:, :, 0:m.QW]
    g.KV = g.DKV.at[:, 0:ni * KP]

    pos = Dims()
    pos.d, pos.z = d, z
    pos.upper = lax.div(2 * z, jnp.int32(nz))
    pos.sign = 1 - 2 * pos.upper
    kind = z * (1 - pos.upper) + (nz - 1 - z) * pos.upper
    classes = range(nz // 2)

    hw = m.hw
    joins = [(g.wq, g.AO.at[pl.ds(0, hw)]), (g.wa.at[0], g.AO.at[pl.ds(hw, hw)]), (g.wa.at[2], g.AO.at[pl.ds(2 * hw, hw)]), (g.wa.at[1], g.AO.at[pl.ds(3 * hw, hw)]),
             (g.wp.at[0], g.BO.at[pl.ds(0, hw)]), (g.wp.at[1], g.BO.at[pl.ds(hw, hw)]), (g.wao, g.OO.at[pl.ds(0, hw)]), (g.wco, g.OO.at[pl.ds(hw, hw)])]
    joins = [pltpu.make_async_copy(a, b, g.js.at[i]) for i, (a, b) in enumerate(joins)]
    for cp in joins:
        cp.start()
    g.TMP[0:16, 0:D] = jnp.zeros((16, D), f32)
    ab, cb = g.ab[...].astype(f32), g.cb[...].astype(f32)
    g.TMP[0:1, 0:hw] = cb[0:1]
    g.TMP[0:1, hw:2 * hw] = ab[0:1]
    g.TMP[0:1, 2 * hw:3 * hw] = ab[1:2]
    g.TMP[1:2, hw:2 * hw] = cb[1:2]
    g.TMP[2:3, 0:D] = g.hb[...].astype(f32).reshape(1, D)
    g.VO[...] = g.TMP[0:16, 0:D].astype(bf16)
    g.VG[z] = g.VO[...]
    enter(d, z, nz, m.bits)
    for cp in joins:
        cp.wait()
    gsem = (g.zs, g.zr, g.ps, g.pr)
    own = {"A": g.AO, "B": g.BO, "O": g.OO, "H": g.H, "W": g.W, "V": g.VO}
    far = {"A": g.GA, "B": g.GB, "O": g.GO, "H": g.GH, "W": g.GW, "V": g.VG}
    gathers = [Gather(own[k], far[k], r0, rows, order, pos, nz, gsem, c) for c, (k, r0, rows, order) in enumerate(m.gather_plan)]
    calls = [0, 0]

    def gather_steps():
        at = calls[0]
        calls[0] += 1
        for cls in classes:
            todo = m.gather_steps[cls][at]
            if todo:
                @pl.when(kind == cls)
                def _():
                    for c, st, dr, j in todo:
                        gathers[c].item(cls, nz, st, dr, j)

    nb = len(m.bits)

    def small_copy(i):
        return pltpu.make_async_remote_copy(g.SM, g.SR.at[i], g.ms.at[i], g.mr.at[i], device_id=(flip(d, m.bits[i]), z), device_id_type=MESH)

    def small_spread(o, frm):
        to = lax.rem(z + o, jnp.int32(nz))
        return pltpu.make_async_remote_copy(g.SM, g.SZ.at[frm(to)], g.ms.at[nb + o], g.zm.at[frm(to)], device_id=(d, to), device_id_type=MESH)

    def small_step(i):
        if i > 0 and i < 4:
            small_copy(i - 1).wait()
            g.SM[...] += g.SR[i - 1]
        if i < 3:
            small_copy(i).start()
        elif i == 3:
            for e in range(3, nb):
                small_copy(e).start()
                small_copy(e).wait()
                g.SM[...] += g.SR[e]
            g.SZ[z] = g.SM[...]
            for o in range(1, nz):
                small_spread(o, lambda to: z).start()
        elif i == 5:
            for o in range(1, nz):
                small_spread(o, lambda to: to).wait_recv()
            total = g.SZ[0]
            for t in range(1, nz):
                total = total + g.SZ[t]
            g.small[...] = total

    def reduce_steps():
        at = calls[1]
        calls[1] += 1
        for cls in classes:
            todo = m.reduce_steps[cls][at]
            if todo:
                @pl.when(kind == cls)
                def _():
                    for c, what in todo:
                        i = progress[cls, c, what]
                        progress[cls, c, what] += 1
                        if c == len(chunks):
                            small_step(i)
                        elif what == 0:
                            chunks[c].steps[i]()
                        else:
                            chunks[c].along(cls, what, i)

    def after_each(steps):
        def between(o):
            for q in range(nz - 1):
                pl.when(o == q)(lambda: steps())
        return between

    def finish_gather():
        for cls in classes:
            @pl.when(kind == cls)
            def _():
                for q in gathers:
                    q.finish(cls, nz)

    pair_slot = [0]

    def pair(ref, rows):
        s = pair_slot[0]
        pair_slot[0] += 1
        return pltpu.make_async_remote_copy(ref.at[pl.ds(0, rows)], ref.at[pl.ds(rows, rows)], g.cs.at[s], g.cr.at[s], device_id=(partner, z), device_id_type=MESH)

    def place(block, slot):
        buf, sem, key, rows, cols = block
        return buf.at[slot, pl.ds(0, rows[1]), pl.ds(*cols)], sem.at[slot]

    def fetch(block, slot, o):
        buf, sem, key, rows, cols = block
        dst, done = place(block, slot)
        r, c = pl.ds(*rows), pl.ds(*cols)

        def mine():
            pltpu.make_async_copy(own[key].at[r, c], dst, done).start()

        def other():
            pltpu.make_async_copy(far[key].at[shard(o), r, c], dst, done).start()
        if isinstance(o, int):
            mine() if o == 0 else other()
        else:
            pl.when(o == 0)(mine)
            pl.when(o != 0)(other)

    def arrived(block, slot):
        buf, sem, key, rows, cols = block
        dst, done = place(block, slot)
        pltpu.make_async_copy(own[key].at[pl.ds(*rows), pl.ds(*cols)], dst, done).wait()

    def stream(blocks, body, between, ahead, refill=()):
        def step(o, c):
            if blocks:
                @pl.when(o + 1 < nz)
                def _():
                    for b in blocks:
                        fetch(b, slot_of(b, o + 1), o + 1)
            if ahead:
                @pl.when(o + 1 == nz)
                def _():
                    for b in ahead:
                        fetch(b, 0, 0)
            for b in blocks:
                arrived(b, slot_of(b, o))
            body(o, lax.rem(o, jnp.int32(2)))
            for b in refill:
                fetch(b, o, o)
            between(o)
            return c
        lax.fori_loop(0, nz, step, 0)

    def slot_of(block, o):
        return lax.rem(o, jnp.int32(block[0].shape[0]))

    FZ, PW, BW = m.FZ, m.PW, m.BW
    self_blocks = [(g.SA, g.sa, "A", (LANES, D - LANES), (0, D)), (g.SO, g.so, "O", (0, hp), (0, D))]
    cross_blocks = [(g.SA, g.sa, "A", (0, hp), (0, D)), (g.SB, g.sb, "B", (0, BW), (0, PW)), (g.SO, g.so, "O", (LANES, hp), (0, D))]
    hidden_blocks = [(g.SA, g.sa, "H", (0, D), (0, FZ))]
    output_blocks = [(g.SA, g.sa, "W", (0, FZ), (0, D))]
    back_blocks = [(g.SH, g.sh, "H", (0, D), (0, FZ))]
    cross_back = [cross_blocks[0], cross_blocks[2]]
    for b in self_blocks:
        fetch(b, 0, 0)

    lane = lax.broadcasted_iota(jnp.int32, (L, hp), 1)
    low = [lane // HEAD == h for h in range(nh)]
    high = [lane // HEAD == h + 1 for h in range(nh)]

    def stack(v, masks):
        return jnp.concatenate([jnp.where(k, v, 0.0) for k in masks], axis=0).astype(bf16)

    def unstack(v, masks):
        out = jnp.where(masks[0], v[0:L], 0.0)
        for h in range(1, nh):
            out = out + jnp.where(masks[h], v[h * L:(h + 1) * L], 0.0)
        return out

    def softmax(s):
        e = jnp.exp(s - jnp.max(s, -1, keepdims=True))
        return e / jnp.sum(e, -1, keepdims=True)

    gather_steps()
    for i in range(ni):
        g.ACC[i * L:(i + 1) * L] = g.x[i].astype(f32)
        mine = jnp.concatenate([g.patches[:, i, :].astype(f32), jnp.zeros((KP - NP, m.PW), f32)], 0)
        g.PT[i * KP:(i + 1) * KP] = mine.astype(bf16)
    g.X[0:T] = g.ACC[...].astype(bf16)
    swaps = [pair(g.X, T), pair(g.PT, ni * KP)]
    for s in swaps:
        s.start()

    g.ACC[...] = jnp.zeros((T, D), f32)
    gather_steps()

    def self_forward(o, slot):
        t = shard(o)
        bias = g.VG[t].astype(f32)[0:1, LANES:]
        qkv = (dot_nt(g.X[0:T], g.SA[o, 0:m.QW]) + bias).astype(bf16)
        g.QKV[o] = qkv
        qf = qkv.astype(f32)
        outs = []
        for i in range(ni):
            r = slice(i * L, (i + 1) * L)
            qs = stack(qf[r, 0:hp], high)
            k_i = qf[r, 3 * LANES:3 * LANES + hp].astype(bf16)
            v_i = qf[r, 2 * LANES:2 * LANES + hp].astype(bf16)
            p = softmax(dot_nt(qs, k_i) * score_scale)
            g.PS[o * ni + i] = p
            outs.append(unstack(dot(p.astype(bf16), v_i), low))
        mixed = jnp.concatenate(outs, 0).astype(bf16)
        g.MX[0, o, 0:T] = mixed
        g.ACC[...] += dot(mixed, g.SO[o])

    stream(self_blocks, self_forward, after_each(gather_steps), cross_blocks)

    def out_row(j):
        return tuple(v[...].astype(f32)[j:j + 1, :] for v in (g.ob, g.gain, g.shift))

    ob, gn, sh = out_row(0)
    first, normed, inv = norm_forward(g.X[0:T].astype(f32) + g.ACC[...] + ob, gn, sh)
    g.NM[0] = normed
    g.INV[...] = jnp.broadcast_to(inv, (T, LANES))
    g.F[0:T] = first.astype(bf16)
    g.ACC[...] = jnp.zeros((T, D), f32)
    gather_steps()

    key_pos = lax.broadcasted_iota(jnp.int32, (nh * L, KP), 1)

    def cross_forward(o, slot):
        t = shard(o)
        vb = g.VG[t].astype(f32)
        cq = (dot_nt(g.F[0:T], g.SA[o, 0:hp]) + vb[0:1, 0:hp]).astype(bf16)
        g.CQ[o] = cq
        cqf = cq.astype(f32)
        kv = (dot_nt(g.PT[0:ni * KP], g.SB[slot]) + vb[1:2, 0:m.BW]).astype(bf16)
        g.KV[o] = kv
        outs = []
        for i in range(ni):
            qs = stack(cqf[i * L:(i + 1) * L], low)
            kvi = g.KV[o, i * KP:(i + 1) * KP]
            s = dot_nt(qs, kvi[:, 0:hp]) * score_scale
            s = jnp.where(key_pos < g.rows[z * ni + i], s, -1e30)
            p = softmax(s)
            g.PC[o * ni + i] = p
            outs.append(unstack(dot(p.astype(bf16), kvi[:, LANES:LANES + hp]), high))
        mixed = jnp.concatenate(outs, 0).astype(bf16)
        g.MX[1, o, 0:T] = mixed
        g.ACC[...] += dot(mixed, g.SO[o])

    stream(cross_blocks, cross_forward, after_each(gather_steps), hidden_blocks)
    ob, gn, sh = out_row(1)
    second, normed, inv = norm_forward(g.F[0:T].astype(f32) + g.ACC[...] + ob, gn, sh)
    g.NM[1] = normed
    g.INV[:, HEAD:] = jnp.broadcast_to(inv, (T, LANES - HEAD))
    g.S2[0:T] = second.astype(bf16)
    gather_steps()
    other = g.MX.at[1 - core]
    mix_swap = pltpu.make_async_remote_copy(other.at[:, pl.ds(0, T)], other.at[:, pl.ds(T, T)], g.cs.at[m.swaps - 1], g.cr.at[m.swaps - 1], device_id=(partner, z), device_id_type=MESH)
    mix_swap.start()
    swaps += [pair(g.F, T), pair(g.S2, T)]
    for s in swaps[2:4]:
        s.start()

    def hidden_forward(o, slot):
        t = shard(o)
        pre = dot(g.S2[0:T], g.SA[o]) + g.VG[t].astype(f32)[2:3, :]
        cdf = 0.5 * (1.0 + lax.erf(pre * math.sqrt(0.5)))
        g.GP[o] = cdf + pre * jnp.exp(-0.5 * pre * pre) * (1.0 / math.sqrt(2.0 * math.pi))
        g.HD[o, 0:T] = (pre * cdf).astype(bf16)

    stream(hidden_blocks, hidden_forward, after_each(gather_steps), output_blocks)
    hid_swaps = [pair(g.HD.at[o], T) for o in range(nz)]
    for s in hid_swaps:
        s.start()
    g.ACC[...] = jnp.zeros((T, D), f32)
    gather_steps()

    def output_forward(o, slot):
        g.ACC[...] += dot(g.HD[o, 0:T], g.SA[o])

    stream(output_blocks, output_forward, after_each(gather_steps), back_blocks)
    gather_steps()
    ob, gn, sh = out_row(2)
    final, normed, inv = norm_forward(g.S2[0:T].astype(f32) + g.ACC[...] + ob, gn, sh)
    g.FO[...] = final.reshape(ni, L, D)
    layer_store = pltpu.make_async_copy(g.FO, g.layer_out, g.js.at[8])
    layer_store.start()

    for i in range(ni):
        g.ACC[i * L:(i + 1) * L] = g.cot[i].astype(f32)
    cot = g.ACC[...]
    g.SM[...] = jnp.zeros(g.SM.shape, f32)

    def record(j, grad_in, grad_out, normed):
        g.SM[j:j + 1] = col_sum(grad_in)
        g.SM[3 + j:4 + j] = col_sum(grad_out * normed)
        g.SM[6 + j:7 + j] = col_sum(grad_out)

    third = norm_backward(cot, normed, inv, gn)
    record(2, third, cot, normed)
    g.G3[0:T] = third.astype(bf16)
    swap3 = pair(g.G3, T)
    swap3.start()

    rsem = (g.ss, g.rs, g.ls)
    results = {"A": g.RA, "B": g.RB, "O": g.RO, "H": g.RH, "W": g.RW}
    chunks = []
    progress = {}
    for c, (k, h0, half, order) in enumerate(m.reduce_plan):
        recvs = {b: R[f"rv{c}_{b}"] for b in m.bits[1:3]}
        whole = m.rows[k] // 2
        chunks.append(Reduce(R[f"kp{c}"], recvs, R[f"ln{c}"], R.get(f"ex{c}"), results[k], core * whole + h0, half, order, pos, nz, m.bits, rsem, c))
    for cls in classes:
        for c in range(len(chunks) + 1):
            for what in range(3):
                progress[cls, c, what] = 0

    def half_columns(apart, count=None):
        return pl.ds(pl.multiple_of(core * apart, LANES), count or apart)

    def deal(k, t, value):
        for c, p in enumerate(m.reduce_plan):
            if p[0] == k:
                R[f"kp{c}"][t] = value[p[1]:p[1] + p[2]].astype(bf16)

    reduce_steps()

    swap3.wait_recv()
    for s in hid_swaps:
        s.wait_recv()
    reduce_steps()

    def job_w(o, c):
        t = shard(o)
        deal("W", t, dot_tn(g.HD[o, :, half_columns(m.FZ // 2)], g.G3[...]))
        return c
    lax.fori_loop(0, nz, job_w, 0)
    for s in hid_swaps:
        s.wait_send()
    reduce_steps()
    g.ACC[...] = third

    def loop_send(ref, rows, kind, o):
        pltpu.make_async_remote_copy(ref.at[o, pl.ds(0, rows)], ref.at[o, pl.ds(rows, rows)], g.ds.at[kind, o], g.dr.at[kind, o], device_id=(partner, z), device_id_type=MESH).start()

    def hidden_backward(o, slot):
        t = shard(o)
        pre = (dot_nt(g.G3[0:T], g.SA[o]) * g.GP[o]).astype(bf16)
        g.DP[o, 0:T] = pre
        g.SM[pl.ds(9 + t, 1)] = col_sum(pre.astype(f32))
        loop_send(g.DP, T, 0, o)
        g.ACC[...] += dot_nt(pre, g.SH[slot])

    stream(back_blocks, hidden_backward, after_each(reduce_steps), [], cross_back)
    reduce_steps()

    def loop_wait(ref, rows, kind):
        for o in range(nz):
            cp = pltpu.make_async_remote_copy(ref.at[o, pl.ds(0, rows)], ref.at[o, pl.ds(rows, rows)], g.ds.at[kind, o], g.dr.at[kind, o], device_id=(partner, z), device_id_type=MESH)
            cp.wait()

    gn = out_row(1)[1]
    normed, inv = g.NM[1], g.INV[:, HEAD:HEAD + 1]
    grad = g.ACC[...]
    secondg = norm_backward(grad, normed, inv, gn)
    record(1, secondg, grad, normed)
    g.G12[1, 0:T] = secondg.astype(bf16)
    swap2 = pair(g.G12.at[1], T)
    swap2.start()
    reduce_steps()
    loop_wait(g.DP, T, 0)
    swaps[3].wait_recv()

    def job_h(o, c):
        t = shard(o)
        deal("H", t, dot_tn(g.S2[:, half_columns(D // 2)], g.DP[o]))
        return c
    lax.fori_loop(0, nz, job_h, 0)
    reduce_steps()

    g.ACC[...] = secondg

    def backward_unit(qs, k_i, v_i, p, ms, masks):
        grad_v = dot_tn(p.astype(bf16), ms)
        grad_p = dot_nt(ms, v_i)
        gs = (p * (grad_p - jnp.sum(p * grad_p, -1, keepdims=True))).astype(bf16)
        grad_q = unstack(dot(gs, k_i), masks) * score_scale
        grad_k = dot_tn(gs, qs) * score_scale
        return grad_q, grad_k.astype(bf16).astype(f32), grad_v.astype(bf16).astype(f32)

    def cross_backward(o, slot):
        t = shard(o)
        for b in cross_back:
            arrived(b, o)
        gm = dot_nt(g.G12[1, 0:T], g.SO[o]).astype(bf16).astype(f32)
        cqf = g.CQ[o].astype(f32)
        grads = []
        for i in range(ni):
            r = slice(i * L, (i + 1) * L)
            kvi = g.KV[o, i * KP:(i + 1) * KP]
            gq, gk, gv = backward_unit(stack(cqf[r], low), kvi[:, 0:hp], kvi[:, LANES:LANES + hp], g.PC[o * ni + i], stack(gm[r], high), low)
            grads.append(gq)
            g.DKV[o, i * KP:(i + 1) * KP] = jnp.concatenate([gk[:, 0:LANES], gk[:, LANES:] + gv[:, 0:LANES], gv[:, LANES:]], 1).astype(bf16)
        dcq = jnp.concatenate(grads, 0).astype(bf16)
        g.DCQ[o, 0:T] = dcq
        loop_send(g.DCQ, T, 1, o)
        loop_send(g.DKV, ni * KP, 2, o)
        dkv = g.DKV[o, 0:ni * KP]
        g.SM[pl.ds(9 + nz + t, 1), 0:hp] = col_sum(dcq.astype(f32))
        g.SM[pl.ds(9 + 2 * nz + t, 1), 0:m.BW] = col_sum(dkv.astype(f32))
        g.ACC[...] += dot(dcq, g.SA[o, 0:hp])

    stream([], cross_backward, after_each(reduce_steps), [], self_blocks)
    reduce_steps()
    gn = out_row(0)[1]
    normed, inv = g.NM[0], g.INV[:, 0:1]
    grad = g.ACC[...]
    firstg = norm_backward(grad, normed, inv, gn)
    record(0, firstg, grad, normed)
    g.G12[0, 0:T] = firstg.astype(bf16)
    swap1 = pair(g.G12.at[0], T)
    swap1.start()
    reduce_steps()
    loop_wait(g.DCQ, T, 1)
    loop_wait(g.DKV, ni * KP, 2)
    swaps[1].wait_recv()

    def job_b(o, c):
        t = shard(o)
        g.TMP[...] = dot_tn(g.DKV[o, :, half_columns(LANES, hp)], g.PT[...])
        deal("B", t, g.TMP[pl.ds(pl.multiple_of(core * HEAD, 16), BW // 2)])
        return c
    lax.fori_loop(0, nz, job_b, 0)
    for o in range(2):
        fetch(cross_blocks[1], o, o)
    reduce_steps()

    g.ACC[...] = firstg

    def self_backward(o, slot):
        t = shard(o)
        for b in self_blocks:
            arrived(b, o)
        gm = dot_nt(g.G12[0, 0:T], g.SO[o]).astype(bf16).astype(f32)
        qf = g.QKV[o].astype(f32)
        gqs, gks, gvs = [], [], []
        for i in range(ni):
            r = slice(i * L, (i + 1) * L)
            k_i = qf[r, 3 * LANES:3 * LANES + hp].astype(bf16)
            v_i = qf[r, 2 * LANES:2 * LANES + hp].astype(bf16)
            gq, gk, gv = backward_unit(stack(qf[r, 0:hp], high), k_i, v_i, g.PS[o * ni + i], stack(gm[r], low), high)
            gqs.append(gq)
            gks.append(gk)
            gvs.append(gv)
        gq, gk, gv = (jnp.concatenate(v, 0) for v in (gqs, gks, gvs))
        dq = jnp.concatenate([gq, gv[:, 0:LANES], gv[:, LANES:] + gk[:, 0:LANES], gk[:, LANES:]], 1).astype(bf16)
        g.DQ[o, 0:T] = dq
        loop_send(g.DQ, T, 3, o)
        g.SM[pl.ds(9 + 3 * nz + t, 1), 0:m.QW] = col_sum(dq.astype(f32))
        g.ACC[...] += dot(dq, g.SA[o, 0:m.QW])

    stream([], self_backward, after_each(reduce_steps), [])
    layer_store.wait()
    g.FO[...] = g.ACC[...].reshape(ni, L, D)
    text_store = pltpu.make_async_copy(g.FO, g.text_grad, g.js.at[8])
    text_store.start()
    reduce_steps()
    loop_wait(g.DQ, T, 3)
    swap1.wait_recv()
    swap2.wait_recv()
    for s in swaps[0:1] + swaps[2:3] + [mix_swap]:
        s.wait_recv()

    def job_o(o, c):
        t = shard(o)
        g.TMP[:, 0:D] = dot_tn(g.MX[core, o], g.G12[core])
        deal("O", t, g.TMP[pl.ds(pl.multiple_of(core * HEAD, 16), hw), 0:D])
        return c
    lax.fori_loop(0, nz, job_o, 0)
    reduce_steps()

    def job_a(o, c):
        t = shard(o)

        @pl.when(core == 0)
        def _():
            left = dot_tn(g.DCQ[o], g.F[...])
            right = dot_tn(g.DQ[o, :, 0:hp], g.X[...])
            deal("A", t, jnp.concatenate([left[0:LANES], left[LANES:] + right[0:LANES], right[LANES:]], 0))

        @pl.when(core == 1)
        def _():
            deal("A", t, dot_tn(g.DQ[o, :, hp:], g.X[...]))
        return c
    lax.fori_loop(0, nz, job_a, 0)
    reduce_steps()

    reduce_steps()
    for part in range(nz // 2):
        for slot in range(2):
            arrived(cross_blocks[1], slot)
        for i in range(ni):
            r = pl.ds(i * KP, KP)
            total = (dot(g.DKV[2 * part, r], g.SB[0]) + dot(g.DKV[2 * part + 1, r], g.SB[1]))[0:NP]
            g.PG[:, i, :] = total if part == 0 else g.PG[:, i, :] + total
            if i == ni - 1 and part < nz // 2 - 1:
                for slot in range(2):
                    fetch(cross_blocks[1], slot, 2 * part + 2 + slot)
            if i == ni - 1 and part == nz // 2 - 1:
                patch_store = pltpu.make_async_copy(g.PG, g.patch_out, g.js.at[9])
                patch_store.start()
            if i % 2 == 1:
                reduce_steps()
    assert calls == [len(m.gather_steps[0]), len(m.reduce_steps[0])], calls
    assert all(sum(len(p) for p in m.reduce_steps[cls]) == sum(progress[cls, c, w] for c in range(len(chunks) + 1) for w in range(3)) for cls in classes)

    sends = [small_spread(o, lambda to: z) for o in range(1, nz)]
    for cp in sends + swaps + [swap1, swap2, swap3, mix_swap]:
        cp.wait_send()
    text_store.wait()
    patch_store.wait()
    finish_gather()
    for cls in classes:
        @pl.when(kind == cls)
        def _():
            for c in chunks:
                c.finish(cls)


GATHER_PLAN = (("V", 0, 16, ""), ("H", 256, 256, "yxc"), ("A", 256, 256, "yxc"), ("A", 512, 256, "yc"), ("O", 0, 384, "yxc"), ("B", 0, 128, "yxc"), ("B", 128, 256,
    "yc"), ("H", 0, 256, "xc"), ("A", 0, 256, "yxc"), ("H", 512, 256, "xyc"), ("W", 0, 256, "xc"), ("W", 256, 256, "xyc"), ("W", 512, 256, "yc"))
GATHER_ORDER = ((0, 320, 160, 80, -1, 13, 360, 93, 333, 373, 101, 173, 120, 14, 341, 381, 94, 334, 200, 181, 374, 109, 174, 117, 389, 349, 102, 133, 397, 342, 15,
    357, 189, 335, 182, 382, 240, 40, 175, 197, 213, 141, 110, 440, 95, 343, 149, -1, 390, 375, 118, 134, 350, 214, 183, 221, 398, 190, 358, 103, 135,
    280, 198, 351, 480, 142, 383, 222, 253, 359, 150, 215, -1, 143, 53, 191, 453, 391, 229, 151, 199, 254, 399, 400, 111, 237, 54, 261, 223, 230, 454,
    119, -1, 269, 238, 61, 293, 461, -1, 262, 231, 255, 62, 462, -1, 270, 239, 69, 55, 301, 469, 455, 493, 263, -1, 77, 271, 70, 309, 294, 63, 477, 470,
    463, 494, -1, 78, 413, 478, 501, -1, 302, 71, 295, 471, 414, 509, 502, -1, 79, 421, 310, 479, 510, 303, 495, 415, -1, 429, 311, 422, -1, -1, 430, 423,
    503, -1, -1, 431, 511, -1, -1), (0, 4, 320, 80, 84, 324, 360, 364, 160, 164, -1, 9, 13, 93, 329, 333, 169, 373, 89, 369, 173, 120, 124, 14, 101, 381,
    334, 337, 341, 377, 174, 200, 204, 94, 177, 129, 109, 374, 97, 209, 117, 181, 345, 133, 213, 353, 389, 349, 134, 240, 244, 342, 397, 214, 40, 357, 44,
    440, 385, 185, 444, 382, 182, 393, 193, 102, 249, 253, 105, 49, 53, 137, 449, 113, 453, 217, 145, 189, 280, 284, -1, 254, 221, 141, 350, 54, 197, 454,
    480, 142, 289, 484, 222, 149, 358, 190, 293, 150, 489, 390, 198, 110, 493, 400, 398, 404, 457, 118, -1, 257, 225, 294, 461, -1, 265, 261, 233, 229,
    57, 409, 61, 413, 462, 494, -1, 269, 237, 262, 230, 297, -1, 270, 238, 62, 414, 305, 301, 302, 497, -1, 65, 309, 310, 465, 505, 501, 417, -1, 73, 69,
    425, 473, 469, 509, -1, 77, 421, 477, 470, 502, 70, -1, 429, 78, 422, 478, 510, -1, 430, -1, -1, -1, -1, -1, -1))
REDUCE_PLAN = (("W", 128, "xyz"), ("W", 128, "yxz"), ("W", 128, "zyx"), ("H", 128, "zyx"), ("H", 128, "xyz"), ("H", 128, "xzy"), ("B", 128, "yzx"), ("B", 64,
    "xyz"), ("O", 64, "yzx"), ("O", 64, "xyz"), ("O", 64, "zxy"), ("A", 64, "xyz"), ("A", 64, "yxz"), ("A", 64, "zxy"), ("A", 64, "yzx"), ("A", 64,
    "xyz"), ("A", 64, "xyz"))
REDUCE_ORDER = ((-1, -1, 6, 7, 0, 3, -1, -1, -1, -1, -1, -1, 12, 9, 10, 15, -1, 0, 3, -1, -1, -1, 0, 1, 12, -1, 8, 6, -1, 18, 21, 12, 13, -1, 6, 15, 16, -1, 3, 4,
    -1, -1, 2, 0, 21, 11, 9, 6, -1, 30, 31, 0, 18, 6, 19, 24, 27, 14, 12, -1, 48, 36, 0, 39, 40, 45, 33, 21, 22, 42, 9, 0, 6, 17, 15, 5, 3, -1, 51, -1, 6,
    51, 27, -1, 24, 25, 12, -1, 48, -1, 36, 32, 30, 45, 42, 43, 33, 15, 9, 3, 20, 18, 27, 28, 51, 48, 49, 12, 45, 46, 41, 39, 12, 36, 37, 33, 34, 23, 30,
    21, 15, 9, 26, 24, 18, 3, 39, 3, 51, 30, 44, 42, 15, 21, 24, 29, 27, 15, 18, 9, 42, 50, 48, 39, 30, 21, 27, 9, 24, 47, 45, 42, 21, 38, 30, 36, 18, 48,
    27, 51, 39, 30, 35, 33, 18, 24, 27, 36, 45, 24, 48, 42, 33, 39, 48, 42, 36, 45, 39, 51, 36, 33, 45, 33), (-1, -1, 6, 0, 3, -1, -1, -1, -1, -1, 7, -1,
    12, 9, 15, -1, 7, 0, 3, -1, 7, 8, -1, -1, 8, 6, 0, 12, 10, -1, 10, -1, 6, 18, 21, 10, 1, 12, 11, 15, 1, -1, 1, 13, 13, 2, 6, 3, 13, 11, 2, 0, 9, -1,
    14, 14, 12, 16, 16, -1, 6, 21, 16, 18, 4, 17, 4, 0, -1, 4, 9, 5, 12, 17, 15, 5, 3, 0, -1, 30, 31, 31, 6, 0, 31, 24, 27, 12, 21, 9, 6, -1, 48, 32, 36,
    39, 45, 19, 33, 42, 32, 30, 19, 12, 24, 27, 3, 15, -1, 51, 9, -1, 19, 51, 20, -1, 36, 40, 48, -1, 40, 20, 18, -1, 40, 22, 41, 45, 22, 22, 42, 27, 25,
    41, 39, 23, 25, 3, 23, 21, 25, 15, 33, 26, 43, 3, 30, 43, 26, 24, 9, 43, 51, 28, 28, 44, 48, 28, 9, 49, 44, 42, 49, 36, 49, 29, 45, 46, 18, 46, 21,
    50, 46, 39, 50, 48, 37, 37, 29, 37, 47, 33, 30, 47, 45, 34, 34, 34, 24, 38, 27, 38, 36, 51, 39, 18, 42, 48, 35, 30, 15, 35, 45, 33, 21, 24, 27, 39,
    36, 51, 42, 15, 21, 48, 30, 18, 48, 33, 45, 30, 24, 27, 18, 45, 36, 39, 24, 51, 27, 42, 33, 36, 39, 42, 33))


def unpack(orders, decode):
    out = []
    for order in orders:
        parts = [[]]
        for code in order:
            if code < 0:
                parts.append([])
            else:
                parts[-1].append(decode(code))
        out.append(parts)
    return out


def gather_code(code):
    return code // 40, code // 8 % 5 - 1, code // 4 % 2, code % 4


def reduce_code(code):
    return code // 3, code % 3


def plans(m):
    link = dict(zip("cxy", m.bits[:3]), z="z")
    m.gather_plan = [(k, r0, rows, tuple(link[o] for o in order)) for k, r0, rows, order in GATHER_PLAN]
    m.gather_steps = unpack(GATHER_ORDER, gather_code)
    m.reduce_plan = []
    at = {}
    for k, half, order in REDUCE_PLAN:
        h0 = at.get(k, 0)
        at[k] = h0 + half
        m.reduce_plan.append((k, h0, half, tuple(link[o] for o in order)))
    m.reduce_steps = unpack(REDUCE_ORDER, reduce_code)
    assert all(at[k] * 2 == m.rows[k] for k in at) and m.nz == 4


def run_layer(m, x, patches, rows, cot, wa, ab, wao, wq, wp, cb, wco, H, hb, W, ob, gain, shift):
    nz = m.nz
    ni, L, D = x.shape
    T = ni * L
    m.ni, m.L, m.D, m.T = ni, L, D, T
    m.NP, m.PW = patches.shape[1:]
    by_patch = jnp.swapaxes(patches, 0, 1)
    m.KP = (m.NP + 15) // 16 * 16
    hw = m.hw = D // nz
    m.nh = hw // HEAD
    m.hp = (hw + HEAD + LANES - 1) // LANES * LANES
    hp, KP, PW = m.hp, m.KP, m.PW
    m.BW, m.QW, m.FZ = 2 * hw, D - LANES, W.shape[0]
    FZ, BW = m.FZ, m.BW
    m.rows = dict(A=D, B=BW, O=2 * hw, H=D, W=FZ)
    lanes = dict(A=D, B=PW, O=D, H=FZ, W=D)
    plans(m)
    m.swaps = nz + 9
    V, sem = pltpu.VMEM, pltpu.SemaphoreType.DMA
    nc, ng = len(m.reduce_plan), len(m.gather_plan)
    nb = len(m.bits)
    sums = (9 + 4 * nz + 7) // 8 * 8
    scratch = dict(
        VG=V((nz, 16, D), bf16), X=V((2 * T, D), bf16), PT=V((2 * ni * KP, PW), bf16),
        SA=V((nz, D, D), bf16), SH=V((2, D, D), bf16), SB=V((2, BW, PW), bf16), SO=V((nz, hp, D), bf16),
        ACC=V((T, D), f32), QKV=V((nz, T, m.QW), bf16), PS=V((nz * ni, m.nh * L, L), f32), MX=V((2, nz, 2 * T, hp), bf16),
        NM=V((2, T, D), f32), INV=V((T, LANES), f32), F=V((2 * T, D), bf16), S2=V((2 * T, D), bf16),
        CQ=V((nz, T, hp), bf16), PC=V((nz * ni, m.nh * L, KP), f32),
        GP=V((nz, T, FZ), f32), HD=V((nz, 2 * T, FZ), bf16), SM=V((sums, D), f32), G3=V((2 * T, D), bf16), DP=V((nz, 2 * T, FZ), bf16),
        G12=V((2, 2 * T, D), bf16), DKV=V((nz, 2 * ni * KP, m.BW), bf16),
        TMP=V((hp, PW), f32), FO=V((ni, L, D), f32), PG=V((m.NP, ni, PW), f32), AO=V((D, D), bf16), BO=V((BW, PW), bf16), OO=V((2 * hw, D), bf16), VO=V((16, D), bf16), SR=V((nb, sums, D), f32), SZ=V((nz, sums, D), f32),
        zs=sem((ng, nz + 1)), zr=sem((ng, nz - 1)), ps=sem((ng, nz - 1)), pr=sem((ng, 3, nz - 1)),
        cs=sem((m.swaps,)), cr=sem((m.swaps,)), ds=sem((4, nz)), dr=sem((4, nz)),
        js=sem((10,)), sa=sem((nz,)), sh=sem((2,)), sb=sem((2,)), so=sem((nz,)),
        ss=sem((nc, nz)), rs=sem((nc, 5 + nb - 3 + nz - 1 + nz // 2)), ls=sem((nc,)), ms=sem((nb + nz,)), mr=sem((nb,)), zm=sem((nz,)),
    )
    for c, (k, h0, half, order) in enumerate(m.reduce_plan):
        C = lanes[k]
        scratch[f"kp{c}"] = V((nz, half, C), bf16)
        for b in m.bits[1:3]:
            lead = nz if order.index(b) < order.index("z") else 1
            scratch[f"rv{c}_{b}"] = V((lead, op_rows(half, order, b), C), bf16)
        scratch[f"ln{c}"] = V((nz - 1 + nz // 2, op_rows(half, order, "z"), C), bf16)
        if nb > 3:
            scratch[f"ex{c}"] = V((nb - 3, half // 4, C), bf16)
    S = jax.ShapeDtypeStruct
    hbm, vm, sm = (pl.BlockSpec(memory_space=s) for s in (pl.ANY, pltpu.VMEM, pltpu.SMEM))
    outs = dict(
        layer_out=(S((ni, L, D), f32), hbm), text_grad=(S((ni, L, D), f32), hbm), patch_out=(S((m.NP, ni, PW), f32), hbm), small=(S((sums, D), f32), vm),
        **{"R" + k: (S((m.rows[k], lanes[k]), bf16), hbm) for k in "ABOHW"},
        **{"G" + k: (S((nz, m.rows[k], lanes[k]), bf16), hbm) for k in "ABOHW"},
    )
    turn = lambda a: jnp.swapaxes(a, -1, -2)
    ins = dict(x=(x, vm), patches=(by_patch, vm), rows=(rows, sm), cot=(cot, vm), wa=(turn(wa), hbm), ab=(ab, vm), wao=(wao, hbm), wq=(turn(wq), hbm), wp=(turn(wp), hbm),
               cb=(cb, vm), wco=(wco, hbm), H=(H, hbm), hb=(hb, vm), W=(W, hbm), ob=(ob, vm), gain=(gain, vm), shift=(shift, vm))
    m.inputs, m.outputs, m.scratch = list(ins), list(outs), list(scratch)
    res = pl.pallas_call(
        functools.partial(layer_kernel, m),
        out_shape=tuple(o[0] for o in outs.values()),
        in_specs=[i[1] for i in ins.values()],
        out_specs=tuple(o[1] for o in outs.values()),
        scratch_shapes=list(scratch.values()),
        compiler_params=pltpu.CompilerParams(collective_id=0, has_side_effects=True, vmem_limit_bytes=67043328),
        name="layer",
    )(*[i[0] for i in ins.values()])
    return dict(zip(outs, res))


finish_ins = ("RA", "RB", "RO", "RH", "RW", "layer_out", "text_grad", "patch_out", "small")
finish_outs = ("layer_out_", "text_grad_", "patch_grad", "attn", "attn_bias", "attn_out", "query", "patch", "cross_bias", "cross_out", "hidden", "hidden_bias", "output", "out_bias", "gain", "shift")


def finish_kernel(m, names, *refs):
    g = Dims()
    for k, v in zip(names, refs):
        setattr(g, k, v)
    nz, hw, ni, KP, NP = m.nz, m.hw, m.ni, m.KP, m.NP
    z = lax.axis_index("mp")
    loads = {}

    def load(name, src, dst):
        cp = pltpu.make_async_copy(src, dst, g.isem.at[len(loads)])
        cp.start()
        loads[name] = cp
    load("W", g.RW, g.vW)
    load("H", g.RH, g.vH)
    load("pg", g.patch_out, g.fG)
    load("lo", g.layer_out, g.vL)
    load("tg", g.text_grad, g.vT)
    load("B", g.RB, g.vP)
    load("O", g.RO, g.vO)
    load("A", g.RA, g.vA)
    stores = []

    def store(src, dst):
        cp = pltpu.make_async_copy(src, dst, g.osem.at[len(stores)])
        cp.start()
        stores.append(cp)

    def widen(src, dst, row0=0):
        step = HEAD

        def body(i, c):
            r = pl.multiple_of(i * step, step)
            dst[pl.ds(r, step), :] = src[pl.ds(row0 + r, step), :].astype(f32)
            return c
        lax.fori_loop(0, dst.shape[0] // step, body, 0)

    loads["W"].wait()
    widen(g.vW, g.fW)
    store(g.fW, g.output)
    loads["H"].wait()
    widen(g.vH, g.fH)
    store(g.fH, g.hidden)
    loads["pg"].wait()
    store(g.fG, g.patch_grad)
    loads["lo"].wait()
    store(g.vL, g.layer_out_)
    loads["tg"].wait()
    store(g.vT, g.text_grad_)
    loads["B"].wait()
    for j in range(2):
        widen(g.vP, g.fP.at[j], j * hw)
    store(g.fP, g.patch)
    loads["O"].wait()
    widen(g.vO, g.fO)
    store(g.fO.at[pl.ds(0, hw)], g.attn_out)
    store(g.fO.at[pl.ds(hw, hw)], g.cross_out)
    loads["A"].wait()
    widen(g.vA, g.fQ)
    for j, part in ((0, 1), (1, 3), (2, 2)):
        widen(g.vA, g.fA.at[j], part * hw)
    store(g.fQ, g.query)
    store(g.fA, g.attn)
    row = lambda k: g.small[pl.ds(9 + k * nz + z, 1), :]
    qv = row(3)[:, 0:5 * LANES]
    at = hw - LANES
    g.attn_bias[0:1] = qv[:, at:at + hw]
    g.attn_bias[1:2] = qv[:, at + hw:at + 2 * hw]
    g.cross_bias[0:1] = row(1)[:, 0:hw]
    g.cross_bias[1:2] = row(2)[:, hw:2 * hw]
    g.hidden_bias[...] = row(0).reshape(m.FZ)
    g.out_bias[...] = g.small[0:3, :]
    g.gain[...] = g.small[3:6, :]
    g.shift[...] = g.small[6:9, :]
    for cp in stores:
        cp.wait()


def finish(m, r):
    nz, ni, L, D, PW, FZ, BW, KP, NP = m.nz, m.ni, m.L, m.D, m.PW, m.FZ, m.BW, m.KP, m.NP
    hw = m.hw = D // nz
    S, V, sem = jax.ShapeDtypeStruct, pltpu.VMEM, pltpu.SemaphoreType.DMA
    hbm, vm = pl.BlockSpec(memory_space=pl.ANY), pl.BlockSpec(memory_space=pltpu.VMEM)
    shapes = ((ni, L, D), (ni, L, D), (NP, ni, PW), (3, hw, D), (2, hw), (hw, D), (hw, D), (2, hw, PW), (2, hw), (hw, D), (D, FZ), (FZ,), (FZ, D), (3, D), (3, D), (3, D))
    small = {"attn_bias", "cross_bias", "hidden_bias", "out_bias", "gain", "shift"}
    scratch = dict(
        vW=V((FZ, D), bf16), vH=V((D, FZ), bf16), vL=V((ni, L, D), f32), vT=V((ni, L, D), f32),
        vP=V((BW, PW), bf16), vO=V((2 * hw, D), bf16), vA=V((D, D), bf16), fW=V((FZ, D), f32), fH=V((D, FZ), f32), fG=V((NP, ni, PW), f32),
        fP=V((2, hw, PW), f32), fO=V((2 * hw, D), f32), fQ=V((hw, D), f32), fA=V((3, hw, D), f32), isem=sem((8,)), osem=sem((11,)),
    )
    ins = [r[k] for k in finish_ins]
    return pl.pallas_call(
        functools.partial(finish_kernel, m, finish_ins + finish_outs + tuple(scratch)),
        out_shape=tuple(S(s, f32) for s in shapes),
        in_specs=[vm if k == "small" else hbm for k in finish_ins],
        out_specs=tuple(vm if k in small else hbm for k in finish_outs),
        scratch_shapes=list(scratch.values()),
        compiler_params=pltpu.CompilerParams(vmem_limit_bytes=56 << 20),
        name="finish",
    )(*ins)


def per_device(nd, nz, text_states, patch_states, patch_rows, cotangent, w_attn, attn_bias, w_attn_out, w_query, w_patch, cross_bias, w_cross_out, w_hidden, hidden_bias, w_output, out_bias, norm_gain, norm_shift):
    m = Dims()
    m.nz, m.bits = nz, tuple(range(nd.bit_length() - 1))
    r = run_layer(m, text_states, patch_states, patch_rows, cotangent, w_attn, attn_bias, w_attn_out, w_query, w_patch, cross_bias, w_cross_out, w_hidden, hidden_bias, w_output, out_bias, norm_gain, norm_shift)
    outs = list(finish(m, r))
    for k in ("attn", "query", "patch"):
        at = finish_outs.index(k)
        outs[at] = jnp.swapaxes(outs[at], -1, -2)
    at = finish_outs.index("patch_grad")
    outs[at] = jnp.swapaxes(outs[at], 0, 1)
    return tuple(outs)


def solution(mesh):
    nd, nz = mesh.shape["dp"], mesh.shape["mp"]
    rows = P(("dp", "mp"), None, None)
    return jax.shard_map(
        functools.partial(per_device, nd, nz),
        mesh=mesh,
        in_specs=(rows, rows, P("dp"), rows, P(None, None, "mp"), P(None, "mp"), P("mp", None), P(None, "mp"), P(None, None, "mp"), P(None, "mp"), P("mp", None), P(None, "mp"), P("mp"), P("mp", None), P(), P(), P()),
        out_specs=(rows, rows, rows, P(None, None, "mp"), P(None, "mp"), P("mp", None), P(None, "mp"), P(None, None, "mp"), P(None, "mp"), P("mp", None), P(None, "mp"), P("mp"), P("mp", None), P(), P(), P()),
        check_vma=False,
    )
```

```python
import functools
import math

import jax
import jax.numpy as jnp
from jax import lax
from jax.experimental import pallas as pl
from jax.experimental.pallas import tpu as pltpu
from jax.sharding import PartitionSpec as P

MESH = pl.DeviceIdType.MESH
HEAD = 64
LANES = 128
epsilon = 1e-06
score_scale = 1.0 / math.sqrt(HEAD)
bf16, f32 = jnp.bfloat16, jnp.float32


def bit_of(d, b):
    return lax.rem(lax.div(d, jnp.int32(2 ** b)), jnp.int32(2))


def flip(d, b):
    return d + (1 - 2 * bit_of(d, b)) * (2 ** b)


def when(cond, fn):
    if cond is True:
        fn()
    else:
        pl.when(cond)(fn)


class Gather:
    def __init__(self, src, dst, row0, rows, order, pos, nz, sems, base):
        self.nz = nz
        self.src, self.dst, self.row0, self.order, self.pos = src, dst, row0, order, pos
        self.piece = rows // (2 ** len(order))
        self.zs, self.zr, self.pr = sems
        self.rbase, self.base = base, base * 2 * nz
        self.k = len(order)

    def win(self, s):
        w = jnp.int32(0)
        for i, b in enumerate(self.order):
            if i >= s:
                w = w + bit_of(self.pos.d, b) * (2 ** i)
        return pl.ds(pl.multiple_of(self.row0 + w * self.piece, 16), self.piece * 2 ** s)

    def shard(self, dr, j):
        return self.pos.z + j * (2 * dr - 1) * self.pos.sign

    def cell(self, t, at):
        return lax.rem(t - at - 1 + self.nz, jnp.int32(self.nz))

    def zcopy(self, dr, j):
        p = self.pos
        t, rows = self.shard(dr, j), self.win(0)
        src = self.src.at[rows] if j == 0 else self.dst.at[t, rows]
        to = p.z + (1 - 2 * dr) * p.sign
        s = self.base + (dr if j == 0 else 2 + self.cell(t, p.z))
        return pltpu.make_async_remote_copy(src, self.dst.at[t, rows], self.zs.at[s], self.zr.at[self.rbase, self.cell(t, to)], device_id=(p.d, to), device_id_type=MESH)

    def zwait(self, dr, j):
        p = self.pos
        t = self.shard(dr, j)
        part = self.dst.at[t, self.win(0)]
        pltpu.make_async_remote_copy(part, part, self.zs.at[self.base], self.zr.at[self.rbase, self.cell(t, p.z)], device_id=(p.d, p.z - (1 - 2 * dr) * p.sign), device_id_type=MESH).wait_recv()

    def pcopy(self, s, dr, j):
        p = self.pos
        t = self.shard(dr, j)
        part = self.dst.at[t, self.win(s)]
        c = self.cell(t, p.z)
        return pltpu.make_async_remote_copy(part, part, self.zs.at[self.base + self.nz + 1 + c], self.pr.at[self.rbase, s, c], device_id=(flip(p.d, self.order[s]), p.z), device_id_type=MESH)

    @staticmethod
    def has(cls, nz, dr, j):
        return cls >= j if dr == 0 else cls + j < nz

    @staticmethod
    def ahead(cls, dr):
        return dr == 0 or cls >= 1

    def item(self, cls, nz, st, dr, j):
        if st == -1:
            self.zcopy(dr, 0).start()
            return
        if st == 0:
            self.zwait(dr, j)
            if j <= nz - 2 and self.ahead(cls, dr):
                self.zcopy(dr, j).start()
        else:
            self.pcopy(st - 1, dr, j).wait()
        if st < self.k:
            self.pcopy(st, dr, j).start()

    def finish(self, cls, nz):
        for dr in (0, 1):
            for j in range(nz - 1):
                if self.ahead(cls, dr) and self.has(cls, nz, dr, j):
                    self.zcopy(dr, j).wait_send()


def add_into(dst, src, rows):
    step = 32 if rows % 32 == 0 else 16

    def body(i, c):
        r = pl.ds(pl.multiple_of(i * step, step), step)
        dst[r, :] = dst[r, :] + src[r, :]
        return c
    lax.fori_loop(0, rows // step, body, 0)


def add_all(dst, src, count, rows):
    def body(t, c):
        add_into(dst.at[t], src.at[t], rows)
        return c
    lax.fori_loop(0, count, body, 0)


def op_rows(half, order, op):
    size = half
    for o in order:
        if o == "z":
            if op == "z":
                return size
        else:
            size //= 2
            if o == op:
                return size
    return size


class Reduce:
    def __init__(self, keep, recvs, line, extra, result, row, half, order, pos, nz, bits, sems, base):
        self.keep, self.recvs, self.line, self.extra = keep, recvs, line, extra
        self.result, self.row, self.half, self.order = result, row, half, order
        self.pos, self.nz, self.bits = pos, nz, bits
        self.ss, self.rs, self.ls = sems
        self.base = base
        self.slot = 0
        self.last = None
        self.steps = []
        self.build()

    def remote(self, src, dst, b):
        r = self.slot
        self.slot += 1
        cp = lambda: pltpu.make_async_remote_copy(src, dst, self.ss.at[self.base * self.nz], self.rs.at[self.base, r], device_id=(flip(self.pos.d, b), self.pos.z), device_id_type=MESH)
        before, self.last = self.last, cp

        def start():
            if before is not None:
                before().wait_send()
            cp().start()
        return cp, start

    def build(self):
        d, z, nz = self.pos.d, self.pos.z, self.nz
        prev = lambda: None
        start, size, whole = jnp.int32(0), self.half, True
        taken = []

        def then(prev, start):
            def step():
                prev()
                start()
            self.steps.append(step)

        for op in self.order:
            if op == "z":
                self.rows = pl.ds(start, size)
                self.size = size
                self.steps.append(prev)
                prev, whole = (lambda: None), False
                continue
            size //= 2
            m = bit_of(d, op)
            keep0 = pl.multiple_of(start + m * size, 16)
            send0 = pl.multiple_of(start + (1 - m) * size, 16)
            buf = self.recvs[op]
            if whole:
                cp, leave = self.remote(self.keep.at[:, pl.ds(send0, size), :], buf, op)
            else:
                cp, leave = self.remote(self.keep.at[z, pl.ds(send0, size), :], buf.at[0], op)
            then(prev, leave)

            def prev(cp=cp, keep0=keep0, size=size, whole=whole, buf=buf):
                cp().wait_recv()
                if whole:
                    add_all(self.keep.at[:, pl.ds(keep0, size), :], buf, nz, size)
                else:
                    add_into(self.keep.at[z, pl.ds(keep0, size), :], buf.at[0], size)
            taken.append(op)
            start = keep0
        for e, b in enumerate(self.bits[3:]):
            cp, leave = self.remote(self.keep.at[z, pl.ds(start, size), :], self.extra.at[e], b)

            def prev(before=prev, cp=cp, leave=leave, e=e, start=start, size=size):
                before()
                leave()
                cp().wait_recv()
                cp().wait_send()
                add_into(self.keep.at[z, pl.ds(start, size), :], self.extra.at[e], size)
        at = pl.multiple_of(self.row + start, 16)
        total = self.keep.at[z, pl.ds(start, size), :]
        win = self.result.at[pl.ds(at, size), :]
        own = lambda win=win: pltpu.make_async_copy(total, win, self.ls.at[self.base])
        op = taken[-1]
        cp, leave = self.remote(total, win, op)

        def step(prev=prev, leave=leave):
            prev()
            own().start()
            leave()
        self.steps.append(step)

        def prev(cp=cp):
            cp().wait_recv()
            own().wait()
        for nxt in taken[-2::-1] + [self.bits[0]]:
            at = pl.multiple_of(at - bit_of(d, op) * size, 16)
            size *= 2
            op = nxt
            win = self.result.at[pl.ds(at, size), :]
            cp, leave = self.remote(win, win, op)
            then(prev, leave)
            prev = lambda cp=cp: cp().wait_recv()
        self.steps.append(prev)

    def hop(self, cls, kind, i, arriving):
        p, nz = self.pos, self.nz
        far, near = nz - 1 - i, i
        if kind == 1:
            t, way = far * (1 - p.upper) + near * p.upper, p.sign
        else:
            t, way = near * (1 - p.upper) + far * p.upper, -p.sign
        cell = self.keep.at[t, self.rows, :]
        s = 1 + (i if kind == 1 else nz - 1 - cls + i)
        first = kind == 1 and (arriving or cls < nz // 2 - 1)
        r = i if first else nz - 1 + i
        to = p.z - way if arriving else p.z + way
        land = self.line.at[r]
        cp = pltpu.make_async_remote_copy(cell, land, self.ss.at[self.base * self.nz + s], self.rs.at[self.base, 5 + len(self.bits) - 3 + r], device_id=(p.d, to), device_id_type=MESH)
        return cp, cell, land

    def sends(self, cls, kind):
        return self.nz - 1 - cls if kind == 1 else cls

    def along(self, cls, kind, i):
        if kind == 1 and cls == 0:
            for k in range(self.nz - 1):
                self.hop(cls, 1, k, False)[0].start()
            return
        cp, cell, land = self.hop(cls, kind, i, True)
        cp.wait_recv()
        add_into(cell, land, self.size)
        if i < self.sends(cls, kind):
            self.hop(cls, kind, i, False)[0].start()

    def finish(self, cls):
        self.last().wait_send()
        for kind in (1, 2):
            for i in range(self.sends(cls, kind)):
                self.hop(cls, kind, i, False)[0].wait_send()


def enter(d, z, nz, bits):
    bar = pltpu.get_barrier_semaphore()
    for b in bits:
        pl.semaphore_signal(bar, inc=1, device_id=(flip(d, b), z), device_id_type=MESH)
    @pl.when(z + 1 < nz)
    def _():
        pl.semaphore_signal(bar, inc=1, device_id=(d, z + 1), device_id_type=MESH)

    @pl.when(z >= 1)
    def _():
        pl.semaphore_signal(bar, inc=1, device_id=(d, z - 1), device_id_type=MESH)
    last = nz - 1
    pl.semaphore_wait(bar, len(bits) + lax.div(z + last, jnp.int32(nz)) + lax.div(last - z + last, jnp.int32(nz)))


def dot(a, b):
    return lax.dot_general(a, b, (((1,), (0,)), ((), ())), preferred_element_type=f32)


def dot_nt(a, b):
    return lax.dot_general(a, b, (((1,), (1,)), ((), ())), preferred_element_type=f32)


def dot_tn(a, b):
    return lax.dot_general(a, b, (((0,), (0,)), ((), ())), preferred_element_type=f32)


def norm_forward(h, gain, shift):
    centred = h - jnp.mean(h, -1, keepdims=True)
    inverse = lax.rsqrt(jnp.mean(centred * centred, -1, keepdims=True) + epsilon)
    normed = centred * inverse
    return normed * gain + shift, normed, inverse


def norm_backward(grad, normed, inverse, gain):
    scaled = grad * gain
    return inverse * (scaled - jnp.mean(scaled, -1, keepdims=True) - normed * jnp.mean(scaled * normed, -1, keepdims=True))


def col_sum(v):
    return jnp.sum(v, axis=0, keepdims=True)


def nth_shard(z, nz, o):
    t = z
    for b in range(nz.bit_length() - 1):
        t = t + lax.rem(lax.div(o, jnp.int32(2 ** b)), jnp.int32(2)) * (1 - 2 * bit_of(z, b)) * (2 ** b)
    return t


class Dims:
    pass


def layer_kernel(m, *refs):
    n_in, n_out = len(m.inputs), len(m.outputs)
    R = dict(zip(m.inputs + m.outputs + m.scratch, refs))
    g = Dims()
    for k, v in R.items():
        setattr(g, k, v)
    ni, L, T, D, nz, hp, nh, KP, NP = m.ni, m.L, m.T, m.D, m.nz, m.hp, m.nh, m.KP, m.NP
    d, z = lax.axis_index("dp"), lax.axis_index("mp")
    core = bit_of(d, m.bits[0])
    partner = flip(d, m.bits[0])

    shard = functools.partial(nth_shard, z, nz)

    g.DCQ = g.HD.at[:, :, 0:hp]
    g.DQ = g.DP.at[:, :, 0:m.QW]
    g.KV = g.DKV.at[:, 0:ni * KP]

    pos = Dims()
    pos.d, pos.z = d, z
    pos.upper = lax.div(2 * z, jnp.int32(nz))
    pos.sign = 1 - 2 * pos.upper
    kind = z * (1 - pos.upper) + (nz - 1 - z) * pos.upper
    classes = range(nz // 2)

    hw = m.hw
    joins = [(g.wq, g.AO.at[pl.ds(0, hw)]), (g.wa.at[0], g.AO.at[pl.ds(hw, hw)]), (g.wa.at[2], g.AO.at[pl.ds(2 * hw, hw)]), (g.wa.at[1], g.AO.at[pl.ds(3 * hw, hw)]),
             (g.wp.at[0], g.BO.at[pl.ds(0, hw)]), (g.wp.at[1], g.BO.at[pl.ds(hw, hw)]), (g.wao, g.OO.at[pl.ds(0, hw)]), (g.wco, g.OO.at[pl.ds(hw, hw)])]
    joins = [pltpu.make_async_copy(a, b, g.js.at[i]) for i, (a, b) in enumerate(joins)]
    for cp in joins:
        cp.start()
    loads = [pltpu.make_async_copy(a, b, g.js.at[10 + i]) for i, (a, b) in enumerate(((g.x, g.XV), (g.patches, g.PV)))]
    for cp in loads:
        cp.start()
    g.TMP[0:16, 0:D] = jnp.zeros((16, D), f32)
    ab, cb = g.ab[...].astype(f32), g.cb[...].astype(f32)
    g.TMP[0:1, 0:hw] = cb[0:1]
    g.TMP[0:1, hw:2 * hw] = ab[0:1]
    g.TMP[0:1, 2 * hw:3 * hw] = ab[1:2]
    g.TMP[1:2, hw:2 * hw] = cb[1:2]
    g.TMP[2:3, 0:D] = g.hb[...].astype(f32).reshape(1, D)
    g.VO[...] = g.TMP[0:16, 0:D].astype(bf16)
    g.VG[z] = g.VO[...]
    enter(d, z, nz, m.bits)
    for cp in joins:
        cp.wait()
    gsem = (g.out, g.zr, g.pr)
    own = {"A": g.AO, "B": g.BO, "O": g.OO, "H": g.H, "W": g.W, "V": g.VO}
    far = {"A": g.GA, "B": g.GB, "O": g.GO, "H": g.GH, "W": g.GW, "V": g.VG}
    gathers = [Gather(own[k], far[k], r0, rows, order, pos, nz, gsem, c) for c, (k, r0, rows, order) in enumerate(m.gather_plan)]
    calls = [0, 0]

    def gather_steps():
        at = calls[0]
        calls[0] += 1
        for cls in classes:
            todo = m.gather_steps[cls][at]
            if todo:
                @pl.when(kind == cls)
                def _():
                    for c, st, dr, j in todo:
                        gathers[c].item(cls, nz, st, dr, j)

    nb = len(m.bits)

    def small_copy(i):
        return pltpu.make_async_remote_copy(g.SM, g.SR.at[i], g.ms.at[i], g.mr.at[i], device_id=(flip(d, m.bits[i]), z), device_id_type=MESH)

    def small_spread(o, frm):
        to = lax.rem(z + o, jnp.int32(nz))
        return pltpu.make_async_remote_copy(g.SM, g.SZ.at[frm(to)], g.ms.at[nb + o], g.zm.at[frm(to)], device_id=(d, to), device_id_type=MESH)

    small_store = lambda: pltpu.make_async_copy(g.SM, g.small, g.js.at[13])

    def small_step(i):
        if i > 0 and i < 4:
            small_copy(i - 1).wait()
            g.SM[...] += g.SR[i - 1]
        if i < 3:
            small_copy(i).start()
        elif i == 3:
            for e in range(3, nb):
                small_copy(e).start()
                small_copy(e).wait()
                g.SM[...] += g.SR[e]
            g.SZ[z] = g.SM[...]
            for o in range(1, nz):
                small_spread(o, lambda to: z).start()
        elif i == 5:
            for o in range(1, nz):
                small_spread(o, lambda to: to).wait_recv()
            for o in range(1, nz):
                small_spread(o, lambda to: z).wait_send()
            total = g.SZ[0]
            for t in range(1, nz):
                total = total + g.SZ[t]
            g.SM[...] = total
            small_store().start()

    def reduce_steps():
        at = calls[1]
        calls[1] += 1
        for cls in classes:
            todo = m.reduce_steps[cls][at]
            if todo:
                @pl.when(kind == cls)
                def _():
                    for c, what in todo:
                        i = progress[cls, c, what]
                        progress[cls, c, what] += 1
                        if c == len(chunks):
                            small_step(i)
                        elif what == 0:
                            chunks[c].steps[i]()
                        else:
                            chunks[c].along(cls, what, i)

    def after_each(steps):
        def between(o):
            for q in range(nz - 1):
                pl.when(o == q)(lambda: steps())
        return between

    def finish_gather():
        for cls in classes:
            @pl.when(kind == cls)
            def _():
                for q in gathers:
                    q.finish(cls, nz)

    pair_slot = [0]

    def pair(ref, rows):
        s = pair_slot[0]
        pair_slot[0] += 1
        return pltpu.make_async_remote_copy(ref.at[pl.ds(0, rows)], ref.at[pl.ds(rows, rows)], g.cs.at[s], g.cr.at[s], device_id=(partner, z), device_id_type=MESH)

    def place(block, slot):
        buf, sem, key, rows, cols = block
        return buf.at[slot, pl.ds(0, rows[1]), pl.ds(*cols)], sem.at[slot]

    def fetch(block, slot, o):
        buf, sem, key, rows, cols = block
        dst, done = place(block, slot)
        r, c = pl.ds(*rows), pl.ds(*cols)

        def mine():
            pltpu.make_async_copy(own[key].at[r, c], dst, done).start()

        def other():
            pltpu.make_async_copy(far[key].at[shard(o), r, c], dst, done).start()
        if isinstance(o, int):
            mine() if o == 0 else other()
        else:
            pl.when(o == 0)(mine)
            pl.when(o != 0)(other)

    def arrived(block, slot):
        buf, sem, key, rows, cols = block
        dst, done = place(block, slot)
        pltpu.make_async_copy(own[key].at[pl.ds(*rows), pl.ds(*cols)], dst, done).wait()

    def stream(blocks, body, between, ahead, refill=()):
        def step(o, c):
            if blocks:
                @pl.when(o + 1 < nz)
                def _():
                    for b in blocks:
                        fetch(b, slot_of(b, o + 1), o + 1)
            if ahead:
                @pl.when(o + 1 == nz)
                def _():
                    for b in ahead:
                        fetch(b, 0, 0)
            for b in blocks:
                arrived(b, slot_of(b, o))
            body(o, lax.rem(o, jnp.int32(2)))
            for b in refill:
                fetch(b, o, o)
            between(o)
            return c
        lax.fori_loop(0, nz, step, 0)

    def slot_of(block, o):
        return lax.rem(o, jnp.int32(block[0].shape[0]))

    FZ, PW, BW = m.FZ, m.PW, m.BW
    self_blocks = [(g.SA, g.sa, "A", (LANES, D - LANES), (0, D)), (g.SO, g.so, "O", (0, hp), (0, D))]
    cross_blocks = [(g.SA, g.sa, "A", (0, hp), (0, D)), (g.SB, g.sb, "B", (0, BW), (0, PW)), (g.SO, g.so, "O", (LANES, hp), (0, D))]
    hidden_blocks = [(g.SA, g.sa, "H", (0, D), (0, FZ))]
    output_blocks = [(g.SA, g.sa, "W", (0, FZ), (0, D))]
    back_blocks = [(g.SH, g.sh, "H", (0, D), (0, FZ))]
    cross_back = [cross_blocks[0], cross_blocks[2]]
    for b in self_blocks:
        fetch(b, 0, 0)

    lane = lax.broadcasted_iota(jnp.int32, (L, hp), 1)
    low = [lane // HEAD == h for h in range(nh)]
    high = [lane // HEAD == h + 1 for h in range(nh)]

    def stack(v, masks):
        return jnp.concatenate([jnp.where(k, v, 0.0) for k in masks], axis=0).astype(bf16)

    def unstack(v, masks):
        out = jnp.where(masks[0], v[0:L], 0.0)
        for h in range(1, nh):
            out = out + jnp.where(masks[h], v[h * L:(h + 1) * L], 0.0)
        return out

    def softmax(s):
        e = jnp.exp(s - jnp.max(s, -1, keepdims=True))
        return e / jnp.sum(e, -1, keepdims=True)

    gather_steps()
    for cp in loads:
        cp.wait()
    for i in range(ni):
        g.ACC[i * L:(i + 1) * L] = g.XV[i].astype(f32)
        mine = jnp.concatenate([g.PV[:, i, :].astype(f32), jnp.zeros((KP - NP, m.PW), f32)], 0)
        g.PT[i * KP:(i + 1) * KP] = mine.astype(bf16)
    g.X[0:T] = g.ACC[...].astype(bf16)
    cot_load = pltpu.make_async_copy(g.cot, g.XV, g.js.at[12])
    cot_load.start()
    swaps = [pair(g.X, T), pair(g.PT, ni * KP)]
    for s in swaps:
        s.start()

    g.ACC[...] = jnp.zeros((T, D), f32)
    gather_steps()

    def self_forward(o, slot):
        t = shard(o)
        bias = g.VG[t].astype(f32)[0:1, LANES:]
        qkv = (dot_nt(g.X[0:T], g.SA[o, 0:m.QW]) + bias).astype(bf16)
        g.QKV[o] = qkv
        qf = qkv.astype(f32)
        outs = []
        for i in range(ni):
            r = slice(i * L, (i + 1) * L)
            qs = stack(qf[r, 0:hp], high)
            k_i = qf[r, 3 * LANES:3 * LANES + hp].astype(bf16)
            v_i = qf[r, 2 * LANES:2 * LANES + hp].astype(bf16)
            p = softmax(dot_nt(qs, k_i) * score_scale)
            g.PS[o * ni + i] = p
            outs.append(unstack(dot(p.astype(bf16), v_i), low))
        mixed = jnp.concatenate(outs, 0).astype(bf16)
        g.MX[0, o, 0:T] = mixed
        g.ACC[...] += dot(mixed, g.SO[o])

    stream(self_blocks, self_forward, after_each(gather_steps), cross_blocks)

    def out_row(j):
        return tuple(v[...].astype(f32)[j:j + 1, :] for v in (g.ob, g.gain, g.shift))

    ob, gn, sh = out_row(0)
    first, normed, inv = norm_forward(g.X[0:T].astype(f32) + g.ACC[...] + ob, gn, sh)
    g.NM[0] = normed
    g.INV[...] = jnp.broadcast_to(inv, (T, LANES))
    g.F[0:T] = first.astype(bf16)
    g.ACC[...] = jnp.zeros((T, D), f32)
    gather_steps()

    key_pos = lax.broadcasted_iota(jnp.int32, (nh * L, KP), 1)

    def cross_forward(o, slot):
        t = shard(o)
        vb = g.VG[t].astype(f32)
        cq = (dot_nt(g.F[0:T], g.SA[o, 0:hp]) + vb[0:1, 0:hp]).astype(bf16)
        g.CQ[o] = cq
        cqf = cq.astype(f32)
        kv = (dot_nt(g.PT[0:ni * KP], g.SB[slot]) + vb[1:2, 0:m.BW]).astype(bf16)
        g.KV[o] = kv
        outs = []
        for i in range(ni):
            qs = stack(cqf[i * L:(i + 1) * L], low)
            kvi = g.KV[o, i * KP:(i + 1) * KP]
            s = dot_nt(qs, kvi[:, 0:hp]) * score_scale
            s = jnp.where(key_pos < g.rows[z * ni + i], s, -1e30)
            p = softmax(s)
            g.PC[o * ni + i] = p
            outs.append(unstack(dot(p.astype(bf16), kvi[:, LANES:LANES + hp]), high))
        mixed = jnp.concatenate(outs, 0).astype(bf16)
        g.MX[1, o, 0:T] = mixed
        g.ACC[...] += dot(mixed, g.SO[o])

    stream(cross_blocks, cross_forward, after_each(gather_steps), hidden_blocks)
    ob, gn, sh = out_row(1)
    second, normed, inv = norm_forward(g.F[0:T].astype(f32) + g.ACC[...] + ob, gn, sh)
    g.NM[1] = normed
    g.INV[:, HEAD:] = jnp.broadcast_to(inv, (T, LANES - HEAD))
    g.S2[0:T] = second.astype(bf16)
    gather_steps()
    other = g.MX.at[1 - core]
    mix_swap = pltpu.make_async_remote_copy(other.at[:, pl.ds(0, T)], other.at[:, pl.ds(T, T)], g.cs.at[m.swaps - 1], g.cr.at[m.swaps - 1], device_id=(partner, z), device_id_type=MESH)
    mix_swap.start()
    swaps += [pair(g.F, T), pair(g.S2, T)]
    for s in swaps[2:4]:
        s.start()

    def hidden_forward(o, slot):
        t = shard(o)
        pre = dot(g.S2[0:T], g.SA[o]) + g.VG[t].astype(f32)[2:3, :]
        cdf = 0.5 * (1.0 + lax.erf(pre * math.sqrt(0.5)))
        g.GP[o] = cdf + pre * jnp.exp(-0.5 * pre * pre) * (1.0 / math.sqrt(2.0 * math.pi))
        g.HD[o, 0:T] = (pre * cdf).astype(bf16)

    stream(hidden_blocks, hidden_forward, after_each(gather_steps), output_blocks)
    hid_swaps = [pair(g.HD.at[o], T) for o in range(nz)]
    for s in hid_swaps:
        s.start()
    g.ACC[...] = jnp.zeros((T, D), f32)
    gather_steps()

    def output_forward(o, slot):
        g.ACC[...] += dot(g.HD[o, 0:T], g.SA[o])

    stream(output_blocks, output_forward, after_each(gather_steps), back_blocks)
    gather_steps()
    ob, gn, sh = out_row(2)
    final, normed, inv = norm_forward(g.S2[0:T].astype(f32) + g.ACC[...] + ob, gn, sh)
    g.TMP[0:T, 0:D] = final
    layer_store = pltpu.make_async_copy(g.TMP.at[pl.ds(0, T), pl.ds(0, D)], g.layer_out, g.js.at[8])
    layer_store.start()

    cot_load.wait()
    for i in range(ni):
        g.ACC[i * L:(i + 1) * L] = g.XV[i].astype(f32)
    cot = g.ACC[...]
    g.SM[...] = jnp.zeros(g.SM.shape, f32)

    def record(j, grad_in, grad_out, normed):
        g.SM[j:j + 1] = col_sum(grad_in)
        g.SM[3 + j:4 + j] = col_sum(grad_out * normed)
        g.SM[6 + j:7 + j] = col_sum(grad_out)

    third = norm_backward(cot, normed, inv, gn)
    record(2, third, cot, normed)
    g.G3[0:T] = third.astype(bf16)
    swap3 = pair(g.G3, T)
    swap3.start()

    finish_gather()
    rsem = (g.out, g.rs, g.ls)
    results = {"A": g.RA, "B": g.RB, "O": g.RO, "H": g.RH, "W": g.RW}
    chunks = []
    progress = {}
    for c, (k, h0, half, order) in enumerate(m.reduce_plan):
        recvs = {b: R[f"rv{c}_{b}"] for b in m.bits[1:3]}
        whole = m.rows[k] // 2
        chunks.append(Reduce(R[f"kp{c}"], recvs, R[f"ln{c}"], R.get(f"ex{c}"), results[k], core * whole + h0, half, order, pos, nz, m.bits, rsem, c))
    for cls in classes:
        for c in range(len(chunks) + 1):
            for what in range(3):
                progress[cls, c, what] = 0

    def half_columns(apart, count=None):
        return pl.ds(pl.multiple_of(core * apart, LANES), count or apart)

    def deal(k, t, value):
        for c, p in enumerate(m.reduce_plan):
            if p[0] == k:
                R[f"kp{c}"][t] = value[p[1]:p[1] + p[2]].astype(bf16)

    reduce_steps()

    swap3.wait_recv()
    for s in hid_swaps:
        s.wait_recv()
    reduce_steps()

    def job_w(o, c):
        t = shard(o)
        deal("W", t, dot_tn(g.HD[o, :, half_columns(m.FZ // 2)], g.G3[...]))
        return c
    lax.fori_loop(0, nz, job_w, 0)
    for s in hid_swaps:
        s.wait_send()
    reduce_steps()
    g.ACC[...] = third

    def loop_send(ref, rows, kind, o):
        pltpu.make_async_remote_copy(ref.at[o, pl.ds(0, rows)], ref.at[o, pl.ds(rows, rows)], g.ds.at[kind, o], g.dr.at[kind, o], device_id=(partner, z), device_id_type=MESH).start()

    def hidden_backward(o, slot):
        t = shard(o)
        pre = (dot_nt(g.G3[0:T], g.SA[o]) * g.GP[o]).astype(bf16)
        g.DP[o, 0:T] = pre
        g.SM[pl.ds(9 + t, 1)] = col_sum(pre.astype(f32))
        loop_send(g.DP, T, 0, o)
        g.ACC[...] += dot_nt(pre, g.SH[slot])

    stream(back_blocks, hidden_backward, after_each(reduce_steps), [], cross_back)
    reduce_steps()

    def loop_wait(ref, rows, kind):
        for o in range(nz):
            cp = pltpu.make_async_remote_copy(ref.at[o, pl.ds(0, rows)], ref.at[o, pl.ds(rows, rows)], g.ds.at[kind, o], g.dr.at[kind, o], device_id=(partner, z), device_id_type=MESH)
            cp.wait()

    gn = out_row(1)[1]
    normed, inv = g.NM[1], g.INV[:, HEAD:HEAD + 1]
    grad = g.ACC[...]
    secondg = norm_backward(grad, normed, inv, gn)
    record(1, secondg, grad, normed)
    g.G12[1, 0:T] = secondg.astype(bf16)
    swap2 = pair(g.G12.at[1], T)
    swap2.start()
    reduce_steps()
    loop_wait(g.DP, T, 0)
    swaps[3].wait_recv()

    def job_h(o, c):
        t = shard(o)
        deal("H", t, dot_tn(g.S2[:, half_columns(D // 2)], g.DP[o]))
        return c
    lax.fori_loop(0, nz, job_h, 0)
    reduce_steps()

    g.ACC[...] = secondg

    def backward_unit(qs, k_i, v_i, p, ms, masks):
        grad_v = dot_tn(p.astype(bf16), ms)
        grad_p = dot_nt(ms, v_i)
        gs = (p * (grad_p - jnp.sum(p * grad_p, -1, keepdims=True))).astype(bf16)
        grad_q = unstack(dot(gs, k_i), masks) * score_scale
        grad_k = dot_tn(gs, qs) * score_scale
        return grad_q, grad_k.astype(bf16).astype(f32), grad_v.astype(bf16).astype(f32)

    def cross_backward(o, slot):
        t = shard(o)
        for b in cross_back:
            arrived(b, o)
        gm = dot_nt(g.G12[1, 0:T], g.SO[o]).astype(bf16).astype(f32)
        cqf = g.CQ[o].astype(f32)
        grads = []
        for i in range(ni):
            r = slice(i * L, (i + 1) * L)
            kvi = g.KV[o, i * KP:(i + 1) * KP]
            gq, gk, gv = backward_unit(stack(cqf[r], low), kvi[:, 0:hp], kvi[:, LANES:LANES + hp], g.PC[o * ni + i], stack(gm[r], high), low)
            grads.append(gq)
            g.DKV[o, i * KP:(i + 1) * KP] = jnp.concatenate([gk[:, 0:LANES], gk[:, LANES:] + gv[:, 0:LANES], gv[:, LANES:]], 1).astype(bf16)
        dcq = jnp.concatenate(grads, 0).astype(bf16)
        g.DCQ[o, 0:T] = dcq
        loop_send(g.DCQ, T, 1, o)
        loop_send(g.DKV, ni * KP, 2, o)
        dkv = g.DKV[o, 0:ni * KP]
        g.SM[pl.ds(9 + nz + t, 1), BW:BW + hp] = col_sum(dcq.astype(f32))
        g.SM[pl.ds(9 + nz + t, 1), 0:BW] = col_sum(dkv.astype(f32))
        g.ACC[...] += dot(dcq, g.SA[o, 0:hp])

    stream([], cross_backward, after_each(reduce_steps), [], self_blocks)
    reduce_steps()
    gn = out_row(0)[1]
    normed, inv = g.NM[0], g.INV[:, 0:1]
    grad = g.ACC[...]
    firstg = norm_backward(grad, normed, inv, gn)
    record(0, firstg, grad, normed)
    g.G12[0, 0:T] = firstg.astype(bf16)
    swap1 = pair(g.G12.at[0], T)
    swap1.start()
    reduce_steps()
    loop_wait(g.DCQ, T, 1)
    loop_wait(g.DKV, ni * KP, 2)
    swaps[1].wait_recv()

    layer_store.wait()

    def job_b(o, c):
        t = shard(o)
        g.TMP[...] = dot_tn(g.DKV[o, :, half_columns(LANES, hp)], g.PT[...])
        deal("B", t, g.TMP[pl.ds(pl.multiple_of(core * HEAD, 16), BW // 2)])
        return c
    lax.fori_loop(0, nz, job_b, 0)
    for o in range(2):
        fetch(cross_blocks[1], o, o)
    reduce_steps()

    g.ACC[...] = firstg

    def self_backward(o, slot):
        t = shard(o)
        for b in self_blocks:
            arrived(b, o)
        gm = dot_nt(g.G12[0, 0:T], g.SO[o]).astype(bf16).astype(f32)
        qf = g.QKV[o].astype(f32)
        gqs, gks, gvs = [], [], []
        for i in range(ni):
            r = slice(i * L, (i + 1) * L)
            k_i = qf[r, 3 * LANES:3 * LANES + hp].astype(bf16)
            v_i = qf[r, 2 * LANES:2 * LANES + hp].astype(bf16)
            gq, gk, gv = backward_unit(stack(qf[r, 0:hp], high), k_i, v_i, g.PS[o * ni + i], stack(gm[r], low), high)
            gqs.append(gq)
            gks.append(gk)
            gvs.append(gv)
        gq, gk, gv = (jnp.concatenate(v, 0) for v in (gqs, gks, gvs))
        dq = jnp.concatenate([gq, gv[:, 0:LANES], gv[:, LANES:] + gk[:, 0:LANES], gk[:, LANES:]], 1).astype(bf16)
        g.DQ[o, 0:T] = dq
        loop_send(g.DQ, T, 3, o)
        g.SM[pl.ds(9 + 2 * nz + t, 1), 0:m.QW] = col_sum(dq.astype(f32))
        g.ACC[...] += dot(dq, g.SA[o, 0:m.QW])

    stream([], self_backward, after_each(reduce_steps), [])
    text_store = pltpu.make_async_copy(g.ACC, g.text_grad, g.js.at[8])
    text_store.start()
    reduce_steps()
    loop_wait(g.DQ, T, 3)
    swap1.wait_recv()
    swap2.wait_recv()
    for s in swaps[0:1] + swaps[2:3] + [mix_swap]:
        s.wait_recv()

    def job_o(o, c):
        t = shard(o)
        g.TMP[:, 0:D] = dot_tn(g.MX[core, o], g.G12[core])
        deal("O", t, g.TMP[pl.ds(pl.multiple_of(core * HEAD, 16), hw), 0:D])
        return c
    lax.fori_loop(0, nz, job_o, 0)
    reduce_steps()

    def job_a(o, c):
        t = shard(o)

        @pl.when(core == 0)
        def _():
            left = dot_tn(g.DCQ[o], g.F[...])
            right = dot_tn(g.DQ[o, :, 0:hp], g.X[...])
            deal("A", t, jnp.concatenate([left[0:LANES], left[LANES:] + right[0:LANES], right[LANES:]], 0))

        @pl.when(core == 1)
        def _():
            deal("A", t, dot_tn(g.DQ[o, :, hp:], g.X[...]))
        return c
    lax.fori_loop(0, nz, job_a, 0)
    reduce_steps()

    reduce_steps()
    for part in range(nz // 2):
        for slot in range(2):
            arrived(cross_blocks[1], slot)
        for i in range(ni):
            r = pl.ds(i * KP, KP)
            total = (dot(g.DKV[2 * part, r], g.SB[0]) + dot(g.DKV[2 * part + 1, r], g.SB[1]))[0:NP]
            g.PG[:, i, :] = total if part == 0 else g.PG[:, i, :] + total
            if i == ni - 1 and part < nz // 2 - 1:
                for slot in range(2):
                    fetch(cross_blocks[1], slot, 2 * part + 2 + slot)
            if i == ni - 1 and part == nz // 2 - 1:
                patch_store = pltpu.make_async_copy(g.PG, g.patch_out, g.js.at[9])
                patch_store.start()
            if i % 2 == 1:
                reduce_steps()
    assert calls == [len(m.gather_steps[0]), len(m.reduce_steps[0])], calls
    assert all(sum(len(p) for p in m.reduce_steps[cls]) == sum(progress[cls, c, w] for c in range(len(chunks) + 1) for w in range(3)) for cls in classes)

    for cp in swaps + [swap1, swap2, swap3, mix_swap]:
        cp.wait_send()
    text_store.wait()
    patch_store.wait()
    small_store().wait()
    for cls in classes:
        @pl.when(kind == cls)
        def _():
            for c in chunks:
                c.finish(cls)


GATHER_PLAN = (("V", 0, 16, ""), ("A", 0, 256, "yxc"), ("W", 0, 512, "yc"), ("O", 0, 384, "yxc"), ("H", 0, 384, "yxc"), ("A", 256, 256, "xyc"), ("A", 512, 256,
    "yc"), ("H", 384, 384, "yxc"), ("W", 512, 256, "yc"), ("B", 0, 384, "yxc"))
GATHER_ORDER = ((0, 40, 200, 120, -1, 13, 53, 213, 133, 61, 14, 360, 221, 54, 214, 141, 134, 69, 15, 229, 222, 77, 240, 62, 373, 237, 55, 142, 149, 215, 230, 135,
    157, 70, 160, 238, 381, 374, 78, 63, 150, 253, 143, 223, 280, 158, 375, 382, 254, 261, 389, 320, 173, 269, -1, 397, 71, 231, 383, 80, 255, 293, 151,
    79, 239, 262, 174, 159, 181, 270, 175, -1, 390, 333, 263, 301, 294, 398, 271, -1, 295, 391, 182, 183, -1, 399, 341, 93, 189, -1, 309, 302, 303, 349,
    334, 197, -1, 317, 101, 94, 190, -1, 342, 335, 109, 198, 191, -1, 310, 350, 95, 199, 102, -1, 318, 311, 343, 110, -1, 319, -1, 351, 103, -1, -1, 111,
    -1, -1, -1), (0, 4, 40, 44, 200, 204, 120, 124, -1, 9, 13, 49, 53, 209, 213, 129, 133, 14, 360, 364, 57, 54, 217, 61, 214, 221, 137, 134, 369, 65,
    141, 373, 240, 62, 244, 73, 69, 222, 225, 374, 77, 233, 249, 229, 253, 160, 164, 145, 142, 237, 153, 377, 254, 169, 149, 280, 284, 173, 381, 157, 70,
    174, 230, 78, 289, 320, 324, 293, 150, 238, 382, 158, 294, 80, 84, 257, 329, 385, 333, 265, 261, -1, 393, 269, 262, 389, 177, 93, 270, -1, 397, 334,
    89, 181, 182, -1, 297, 390, -1, 301, 185, 398, -1, 302, 337, 94, 193, 189, -1, 345, 341, 197, 190, -1, 305, 349, 101, 198, -1, 313, 342, 309, 109, -1,
    317, 350, 310, 97, 318, -1, 105, -1, 102, -1, -1, 110, -1, -1, -1))
REDUCE_PLAN = (("W", 128, "xyz"), ("W", 128, "yxz"), ("W", 128, "zyx"), ("H", 128, "zyx"), ("H", 128, "xyz"), ("H", 128, "xzy"), ("B", 128, "yzx"), ("B", 64,
    "xyz"), ("O", 64, "yzx"), ("O", 64, "xyz"), ("O", 64, "zxy"), ("A", 64, "xyz"), ("A", 64, "yxz"), ("A", 64, "zxy"), ("A", 64, "yzx"), ("A", 64,
    "xyz"), ("A", 64, "xyz"))
REDUCE_ORDER = ((-1, -1, 6, 7, 0, 3, -1, -1, -1, -1, -1, -1, 12, 9, 10, 15, -1, 0, 3, -1, -1, -1, 0, 1, 12, -1, 8, 6, -1, 18, 21, 12, 13, -1, 6, 15, 16, -1, 3, 4,
    -1, -1, 2, 0, 21, 11, 9, 6, -1, 30, 31, 0, 18, 6, 19, 24, 27, 14, 12, -1, 48, 36, 0, 39, 40, 45, 33, 21, 22, 42, 9, 0, 6, 17, 15, 5, 3, -1, 51, -1, 6,
    51, 27, -1, 24, 25, 12, -1, 48, -1, 36, 32, 30, 45, 42, 43, 33, 15, 9, 3, 20, 18, 27, 28, 51, 48, 49, 12, 45, 46, 41, 39, 12, 36, 37, 33, 34, 23, 30,
    21, 15, 9, 26, 24, 18, 3, 39, 3, 51, 30, 44, 42, 15, 21, 24, 29, 27, 15, 18, 9, 42, 50, 48, 39, 30, 21, 27, 9, 24, 47, 45, 42, 21, 38, 30, 36, 18, 48,
    27, 51, 39, 30, 35, 33, 18, 24, 27, 36, 45, 24, 48, 42, 33, 39, 48, 42, 36, 45, 39, 51, 36, 33, 45, 33), (-1, -1, 6, 0, 3, -1, -1, -1, -1, -1, 7, -1,
    12, 9, 15, -1, 7, 0, 3, -1, 7, 8, -1, -1, 8, 6, 0, 12, 10, -1, 10, -1, 6, 18, 21, 10, 1, 12, 11, 15, 1, -1, 1, 13, 13, 2, 6, 3, 13, 11, 2, 0, 9, -1,
    14, 14, 12, 16, 16, -1, 6, 21, 16, 18, 4, 17, 4, 0, -1, 4, 9, 5, 12, 17, 15, 5, 3, 0, -1, 30, 31, 31, 6, 0, 31, 24, 27, 12, 21, 9, 6, -1, 48, 32, 36,
    39, 45, 19, 33, 42, 32, 30, 19, 12, 24, 27, 3, 15, -1, 51, 9, -1, 19, 51, 20, -1, 36, 40, 48, -1, 40, 20, 18, -1, 40, 22, 41, 45, 22, 22, 42, 27, 25,
    41, 39, 23, 25, 3, 23, 21, 25, 15, 33, 26, 43, 3, 30, 43, 26, 24, 9, 43, 51, 28, 28, 44, 48, 28, 9, 49, 44, 42, 49, 36, 49, 29, 45, 46, 18, 46, 21,
    50, 46, 39, 50, 48, 37, 37, 29, 37, 47, 33, 30, 47, 45, 34, 34, 34, 24, 38, 27, 38, 36, 51, 39, 18, 42, 48, 35, 30, 15, 35, 45, 33, 21, 24, 27, 39,
    36, 51, 42, 15, 21, 48, 30, 18, 48, 33, 45, 30, 24, 27, 18, 45, 36, 39, 24, 51, 27, 42, 33, 36, 39, 42, 33))


def unpack(orders, decode):
    out = []
    for order in orders:
        parts = [[]]
        for code in order:
            if code < 0:
                parts.append([])
            else:
                parts[-1].append(decode(code))
        out.append(parts)
    return out


def gather_code(code):
    return code // 40, code // 8 % 5 - 1, code // 4 % 2, code % 4


def reduce_code(code):
    return code // 3, code % 3


def plans(m):
    link = dict(zip("cxy", m.bits[:3]), z="z")
    m.gather_plan = [(k, r0, rows, tuple(link[o] for o in order)) for k, r0, rows, order in GATHER_PLAN]
    m.gather_steps = unpack(GATHER_ORDER, gather_code)
    m.reduce_plan = []
    at = {}
    for k, half, order in REDUCE_PLAN:
        h0 = at.get(k, 0)
        at[k] = h0 + half
        m.reduce_plan.append((k, h0, half, tuple(link[o] for o in order)))
    m.reduce_steps = unpack(REDUCE_ORDER, reduce_code)
    assert all(at[k] * 2 == m.rows[k] for k in at) and m.nz == 4


def run_layer(m, x, patches, rows, cot, wa, ab, wao, wq, wp, cb, wco, H, hb, W, ob, gain, shift):
    nz = m.nz
    ni, L, D = x.shape
    T = ni * L
    m.ni, m.L, m.D, m.T = ni, L, D, T
    m.NP, m.PW = patches.shape[1:]
    by_patch = jnp.swapaxes(patches, 0, 1)
    m.KP = (m.NP + 15) // 16 * 16
    hw = m.hw = D // nz
    m.nh = hw // HEAD
    m.hp = (hw + HEAD + LANES - 1) // LANES * LANES
    hp, KP, PW = m.hp, m.KP, m.PW
    m.BW, m.QW, m.FZ = 2 * hw, D - LANES, W.shape[0]
    FZ, BW = m.FZ, m.BW
    m.rows = dict(A=D, B=BW, O=2 * hw, H=D, W=FZ)
    lanes = dict(A=D, B=PW, O=D, H=FZ, W=D)
    plans(m)
    m.swaps = nz + 9
    V, sem = pltpu.VMEM, pltpu.SemaphoreType.DMA
    nc, ng = len(m.reduce_plan), len(m.gather_plan)
    nb = len(m.bits)
    sums = (9 + 3 * nz + 7) // 8 * 8
    scratch = dict(
        VG=V((nz, 16, D), bf16), X=V((2 * T, D), bf16), PT=V((2 * ni * KP, PW), bf16),
        SA=V((nz, D, D), bf16), SH=V((2, D, D), bf16), SB=V((2, BW, PW), bf16), SO=V((nz, hp, D), bf16),
        ACC=V((T, D), f32), QKV=V((nz, T, m.QW), bf16), PS=V((nz * ni, m.nh * L, L), f32), MX=V((2, nz, 2 * T, hp), bf16),
        NM=V((2, T, D), f32), INV=V((T, LANES), f32), F=V((2 * T, D), bf16), S2=V((2 * T, D), bf16),
        CQ=V((nz, T, hp), bf16), PC=V((nz * ni, m.nh * L, KP), f32),
        GP=V((nz, T, FZ), f32), HD=V((nz, 2 * T, FZ), bf16), SM=V((sums, D), f32), G3=V((2 * T, D), bf16), DP=V((nz, 2 * T, FZ), bf16),
        G12=V((2, 2 * T, D), bf16), DKV=V((nz, 2 * ni * KP, m.BW), bf16),
        TMP=V((hp, PW), f32), XV=V(x.shape, bf16), PV=V(by_patch.shape, bf16), PG=V((m.NP, ni, PW), f32), AO=V((D, D), bf16), BO=V((BW, PW), bf16), OO=V((2 * hw, D), bf16), VO=V((16, D), bf16), SR=V((nb, sums, D), f32), SZ=V((nz, sums, D), f32),
        out=sem((max(2 * nz * ng, nz * nc),)), zr=sem((ng, nz - 1)), pr=sem((ng, 3, nz - 1)),
        cs=sem((m.swaps,)), cr=sem((m.swaps,)), ds=sem((4, nz)), dr=sem((4, nz)),
        js=sem((14,)), sa=sem((nz,)), sh=sem((2,)), sb=sem((2,)), so=sem((nz,)),
        rs=sem((nc, 5 + nb - 3 + nz - 1 + nz // 2)), ls=sem((nc,)), ms=sem((nb + nz,)), mr=sem((nb,)), zm=sem((nz,)),
    )
    for c, (k, h0, half, order) in enumerate(m.reduce_plan):
        C = lanes[k]
        scratch[f"kp{c}"] = V((nz, half, C), bf16)
        for b in m.bits[1:3]:
            lead = nz if order.index(b) < order.index("z") else 1
            scratch[f"rv{c}_{b}"] = V((lead, op_rows(half, order, b), C), bf16)
        scratch[f"ln{c}"] = V((nz - 1 + nz // 2, op_rows(half, order, "z"), C), bf16)
        if nb > 3:
            scratch[f"ex{c}"] = V((nb - 3, half // 4, C), bf16)
    S = jax.ShapeDtypeStruct
    hbm, vm, sm = (pl.BlockSpec(memory_space=s) for s in (pl.ANY, pltpu.VMEM, pltpu.SMEM))
    outs = dict(
        layer_out=(S((T, D), f32), hbm), text_grad=(S((T, D), f32), hbm), patch_out=(S((m.NP, ni, PW), f32), hbm), small=(S((sums, D), f32), hbm),
        **{"R" + k: (S((m.rows[k], lanes[k]), bf16), hbm) for k in "ABOHW"},
        **{"G" + k: (S((nz, m.rows[k], lanes[k]), bf16), hbm) for k in "ABOHW"},
    )
    turn = lambda a: jnp.swapaxes(a, -1, -2)
    ins = dict(x=(x, hbm), patches=(by_patch, hbm), rows=(rows, sm), cot=(cot, hbm), wa=(turn(wa), hbm), ab=(ab, vm), wao=(wao, hbm), wq=(turn(wq), hbm), wp=(turn(wp), hbm),
               cb=(cb, vm), wco=(wco, hbm), H=(H, hbm), hb=(hb, vm), W=(W, hbm), ob=(ob, vm), gain=(gain, vm), shift=(shift, vm))
    m.inputs, m.outputs, m.scratch = list(ins), list(outs), list(scratch)
    res = pl.pallas_call(
        functools.partial(layer_kernel, m),
        out_shape=tuple(o[0] for o in outs.values()),
        in_specs=[i[1] for i in ins.values()],
        out_specs=tuple(o[1] for o in outs.values()),
        scratch_shapes=list(scratch.values()),
        compiler_params=pltpu.CompilerParams(collective_id=0, has_side_effects=True, vmem_limit_bytes=67043328),
        name="layer",
    )(*[i[0] for i in ins.values()])
    return dict(zip(outs, res))


finish_ins = ("RA", "RB", "RO", "RH", "RW", "layer_out", "text_grad", "patch_out", "small")
finish_outs = ("layer_out_", "text_grad_", "patch_grad", "attn", "attn_bias", "attn_out", "query", "patch", "cross_bias", "cross_out", "hidden", "hidden_bias", "output", "out_bias", "gain", "shift")


def finish_kernel(m, names, *refs):
    g = Dims()
    for k, v in zip(names, refs):
        setattr(g, k, v)
    nz, hw, ni, KP, NP = m.nz, m.hw, m.ni, m.KP, m.NP
    z = lax.axis_index("mp")
    loads = {}

    def load(name, src, dst):
        cp = pltpu.make_async_copy(src, dst, g.isem.at[len(loads)])
        cp.start()
        loads[name] = cp
    load("W", g.RW, g.vW)
    load("H", g.RH, g.vH)
    load("pg", g.patch_out, g.fG)
    load("lo", g.layer_out, g.vL)
    load("tg", g.text_grad, g.vT)
    load("B", g.RB, g.vP)
    load("O", g.RO, g.vO)
    load("A", g.RA, g.vA)
    stores = []

    def store(src, dst):
        cp = pltpu.make_async_copy(src, dst, g.osem.at[len(stores)])
        cp.start()
        stores.append(cp)

    def widen(src, dst, row0=0):
        step = HEAD

        def body(i, c):
            r = pl.multiple_of(i * step, step)
            dst[pl.ds(r, step), :] = src[pl.ds(row0 + r, step), :].astype(f32)
            return c
        lax.fori_loop(0, dst.shape[0] // step, body, 0)

    loads["W"].wait()
    widen(g.vW, g.fW)
    store(g.fW, g.output)
    loads["H"].wait()
    widen(g.vH, g.fH)
    store(g.fH, g.hidden)
    loads["pg"].wait()
    store(g.fG, g.patch_grad)
    loads["lo"].wait()
    store(g.vL, g.layer_out_)
    loads["tg"].wait()
    store(g.vT, g.text_grad_)
    loads["B"].wait()
    for j in range(2):
        widen(g.vP, g.fP.at[j], j * hw)
    store(g.fP, g.patch)
    loads["O"].wait()
    widen(g.vO, g.fO)
    store(g.fO.at[pl.ds(0, hw)], g.attn_out)
    store(g.fO.at[pl.ds(hw, hw)], g.cross_out)
    loads["A"].wait()
    widen(g.vA, g.fQ)
    for j, part in ((0, 1), (1, 3), (2, 2)):
        widen(g.vA, g.fA.at[j], part * hw)
    store(g.fQ, g.query)
    store(g.fA, g.attn)
    row = lambda k: g.small[pl.ds(9 + k * nz + z, 1), :]
    qv = row(2)[:, 0:5 * LANES]
    at = hw - LANES
    g.attn_bias[0:1] = qv[:, at:at + hw]
    g.attn_bias[1:2] = qv[:, at + hw:at + 2 * hw]
    g.cross_bias[0:1] = row(1)[:, 2 * hw:3 * hw]
    g.cross_bias[1:2] = row(1)[:, hw:2 * hw]
    g.hidden_bias[...] = row(0).reshape(m.FZ)
    g.out_bias[...] = g.small[0:3, :]
    g.gain[...] = g.small[3:6, :]
    g.shift[...] = g.small[6:9, :]
    for cp in stores:
        cp.wait()


def finish(m, r):
    nz, ni, L, D, PW, FZ, BW, KP, NP = m.nz, m.ni, m.L, m.D, m.PW, m.FZ, m.BW, m.KP, m.NP
    hw = m.hw = D // nz
    S, V, sem = jax.ShapeDtypeStruct, pltpu.VMEM, pltpu.SemaphoreType.DMA
    hbm, vm = pl.BlockSpec(memory_space=pl.ANY), pl.BlockSpec(memory_space=pltpu.VMEM)
    shapes = ((m.T, D), (m.T, D), (NP, ni, PW), (3, hw, D), (2, hw), (hw, D), (hw, D), (2, hw, PW), (2, hw), (hw, D), (D, FZ), (FZ,), (FZ, D), (3, D), (3, D), (3, D))
    small = {"attn_bias", "cross_bias", "hidden_bias", "out_bias", "gain", "shift"}
    scratch = dict(
        vW=V((FZ, D), bf16), vH=V((D, FZ), bf16), vL=V((m.T, D), f32), vT=V((m.T, D), f32),
        vP=V((BW, PW), bf16), vO=V((2 * hw, D), bf16), vA=V((D, D), bf16), fW=V((FZ, D), f32), fH=V((D, FZ), f32), fG=V((NP, ni, PW), f32),
        fP=V((2, hw, PW), f32), fO=V((2 * hw, D), f32), fQ=V((hw, D), f32), fA=V((3, hw, D), f32), isem=sem((8,)), osem=sem((11,)),
    )
    ins = [r[k] for k in finish_ins]
    return pl.pallas_call(
        functools.partial(finish_kernel, m, finish_ins + finish_outs + tuple(scratch)),
        out_shape=tuple(S(s, f32) for s in shapes),
        in_specs=[vm if k == "small" else hbm for k in finish_ins],
        out_specs=tuple(vm if k in small else hbm for k in finish_outs),
        scratch_shapes=list(scratch.values()),
        compiler_params=pltpu.CompilerParams(vmem_limit_bytes=56 << 20),
        name="finish",
    )(*ins)


def per_device(nd, nz, text_states, patch_states, patch_rows, cotangent, w_attn, attn_bias, w_attn_out, w_query, w_patch, cross_bias, w_cross_out, w_hidden, hidden_bias, w_output, out_bias, norm_gain, norm_shift):
    m = Dims()
    m.nz, m.bits = nz, tuple(range(nd.bit_length() - 1))
    r = run_layer(m, text_states, patch_states, patch_rows, cotangent, w_attn, attn_bias, w_attn_out, w_query, w_patch, cross_bias, w_cross_out, w_hidden, hidden_bias, w_output, out_bias, norm_gain, norm_shift)
    outs = list(finish(m, r))
    for k in ("attn", "query", "patch"):
        at = finish_outs.index(k)
        outs[at] = jnp.swapaxes(outs[at], -1, -2)
    for at in range(2):
        outs[at] = outs[at].reshape(text_states.shape)
    at = finish_outs.index("patch_grad")
    outs[at] = jnp.swapaxes(outs[at], 0, 1)
    return tuple(outs)


def solution(mesh):
    nd, nz = mesh.shape["dp"], mesh.shape["mp"]
    rows = P(("dp", "mp"), None, None)
    return jax.shard_map(
        functools.partial(per_device, nd, nz),
        mesh=mesh,
        in_specs=(rows, rows, P("dp"), rows, P(None, None, "mp"), P(None, "mp"), P("mp", None), P(None, "mp"), P(None, None, "mp"), P(None, "mp"), P("mp", None), P(None, "mp"), P("mp"), P("mp", None), P(), P(), P()),
        out_specs=(rows, rows, rows, P(None, None, "mp"), P(None, "mp"), P("mp", None), P(None, "mp"), P(None, None, "mp"), P(None, "mp"), P("mp", None), P(None, "mp"), P("mp"), P("mp", None), P(), P(), P()),
        check_vma=False,
    )
```

```python
import functools
import math

import jax
import jax.numpy as jnp
from jax import lax
from jax.experimental import pallas as pl
from jax.experimental.pallas import tpu as pltpu
from jax.sharding import PartitionSpec as P

MESH = pl.DeviceIdType.MESH
HEAD = 64
LANES = 128
epsilon = 1e-06
score_scale = 1.0 / math.sqrt(HEAD)
bf16, f32 = jnp.bfloat16, jnp.float32


def bit_of(d, b):
    return lax.rem(lax.div(d, jnp.int32(2 ** b)), jnp.int32(2))


def flip(d, b):
    return d + (1 - 2 * bit_of(d, b)) * (2 ** b)


def when(cond, fn):
    if cond is True:
        fn()
    else:
        pl.when(cond)(fn)


class Gather:
    def __init__(self, src, dst, row0, rows, order, pos, nz, sems, base, pbase):
        self.nz, self.pbase = nz, pbase
        self.src, self.dst, self.row0, self.order, self.pos = src, dst, row0, order, pos
        self.piece = rows // (2 ** len(order))
        self.zs, self.zr, self.pr = sems
        self.rbase, self.base = base, base * 2 * nz
        self.k = len(order)

    def win(self, s):
        w = jnp.int32(0)
        for i, b in enumerate(self.order):
            if i >= s:
                w = w + bit_of(self.pos.d, b) * (2 ** i)
        return pl.ds(pl.multiple_of(self.row0 + w * self.piece, 16), self.piece * 2 ** s)

    def shard(self, dr, j):
        return self.pos.z + j * (2 * dr - 1) * self.pos.sign

    def cell(self, t, at):
        return lax.rem(t - at - 1 + self.nz, jnp.int32(self.nz))

    def zcopy(self, dr, j):
        p = self.pos
        t, rows = self.shard(dr, j), self.win(0)
        src = self.src.at[rows] if j == 0 else self.dst.at[t, rows]
        to = p.z + (1 - 2 * dr) * p.sign
        s = self.base + (dr if j == 0 else 2 + self.cell(t, p.z))
        return pltpu.make_async_remote_copy(src, self.dst.at[t, rows], self.zs.at[s], self.zr.at[self.rbase, self.cell(t, to)], device_id=(p.d, to), device_id_type=MESH)

    def zwait(self, dr, j):
        p = self.pos
        t = self.shard(dr, j)
        part = self.dst.at[t, self.win(0)]
        pltpu.make_async_remote_copy(part, part, self.zs.at[self.base], self.zr.at[self.rbase, self.cell(t, p.z)], device_id=(p.d, p.z - (1 - 2 * dr) * p.sign), device_id_type=MESH).wait_recv()

    def pcopy(self, s, dr, j):
        p = self.pos
        t = self.shard(dr, j)
        part = self.dst.at[t, self.win(s)]
        c = self.cell(t, p.z)
        return pltpu.make_async_remote_copy(part, part, self.zs.at[self.base + self.nz + 1 + c], self.pr.at[self.pbase + s * (self.nz - 1) + c], device_id=(flip(p.d, self.order[s]), p.z), device_id_type=MESH)

    @staticmethod
    def has(cls, nz, dr, j):
        return cls >= j if dr == 0 else cls + j < nz

    @staticmethod
    def ahead(cls, dr):
        return dr == 0 or cls >= 1

    def item(self, cls, nz, st, dr, j):
        if st == -1:
            self.zcopy(dr, 0).start()
            return
        if st == 0:
            self.zwait(dr, j)
            if j <= nz - 2 and self.ahead(cls, dr):
                self.zcopy(dr, j).start()
        else:
            self.pcopy(st - 1, dr, j).wait()
        if st < self.k:
            self.pcopy(st, dr, j).start()

    def finish(self, cls, nz):
        for dr in (0, 1):
            for j in range(nz - 1):
                if self.ahead(cls, dr) and self.has(cls, nz, dr, j):
                    self.zcopy(dr, j).wait_send()


def add_into(dst, src, rows):
    step = 32 if rows % 32 == 0 else 16

    def body(i, c):
        r = pl.ds(pl.multiple_of(i * step, step), step)
        dst[r, :] = dst[r, :] + src[r, :]
        return c
    lax.fori_loop(0, rows // step, body, 0)


def add_all(dst, src, count, rows):
    def body(t, c):
        add_into(dst.at[t], src.at[t], rows)
        return c
    lax.fori_loop(0, count, body, 0)


def op_rows(half, order, op):
    size = half
    for o in order:
        if o == "z":
            if op == "z":
                return size
        else:
            size //= 2
            if o == op:
                return size
    return size


class Reduce:
    def __init__(self, keep, recvs, line, extra, result, row, half, order, pos, nz, bits, sems, base):
        self.keep, self.recvs, self.line, self.extra = keep, recvs, line, extra
        self.result, self.row, self.half, self.order = result, row, half, order
        self.pos, self.nz, self.bits = pos, nz, bits
        self.ss, self.rs, self.ls = sems
        self.base = base
        self.slot = 0
        self.last = None
        self.steps = []
        self.build()

    def remote(self, src, dst, b):
        r = self.slot
        self.slot += 1
        cp = lambda: pltpu.make_async_remote_copy(src, dst, self.ss.at[self.base * self.nz], self.rs.at[self.base, r], device_id=(flip(self.pos.d, b), self.pos.z), device_id_type=MESH)
        before, self.last = self.last, cp

        def start():
            if before is not None:
                before().wait_send()
            cp().start()
        return cp, start

    def build(self):
        d, z, nz = self.pos.d, self.pos.z, self.nz
        prev = lambda: None
        start, size, whole = jnp.int32(0), self.half, True
        taken = []

        def then(prev, start):
            def step():
                prev()
                start()
            self.steps.append(step)

        for op in self.order:
            if op == "z":
                self.rows = pl.ds(start, size)
                self.size = size
                self.steps.append(prev)
                prev, whole = (lambda: None), False
                continue
            size //= 2
            m = bit_of(d, op)
            keep0 = pl.multiple_of(start + m * size, 16)
            send0 = pl.multiple_of(start + (1 - m) * size, 16)
            buf = self.recvs[op]
            if whole:
                cp, leave = self.remote(self.keep.at[:, pl.ds(send0, size), :], buf, op)
            else:
                cp, leave = self.remote(self.keep.at[z, pl.ds(send0, size), :], buf.at[0], op)
            then(prev, leave)

            def prev(cp=cp, keep0=keep0, size=size, whole=whole, buf=buf):
                cp().wait_recv()
                if whole:
                    add_all(self.keep.at[:, pl.ds(keep0, size), :], buf, nz, size)
                else:
                    add_into(self.keep.at[z, pl.ds(keep0, size), :], buf.at[0], size)
            taken.append(op)
            start = keep0
        for e, b in enumerate(self.bits[3:]):
            cp, leave = self.remote(self.keep.at[z, pl.ds(start, size), :], self.extra.at[e], b)

            def prev(before=prev, cp=cp, leave=leave, e=e, start=start, size=size):
                before()
                leave()
                cp().wait_recv()
                cp().wait_send()
                add_into(self.keep.at[z, pl.ds(start, size), :], self.extra.at[e], size)
        at = pl.multiple_of(self.row + start, 16)
        total = self.keep.at[z, pl.ds(start, size), :]
        win = self.result.at[pl.ds(at, size), :]
        own = lambda win=win: pltpu.make_async_copy(total, win, self.ls.at[self.base])
        op = taken[-1]
        cp, leave = self.remote(total, win, op)

        def step(prev=prev, leave=leave):
            prev()
            own().start()
            leave()
        self.steps.append(step)

        def prev(cp=cp):
            cp().wait_recv()
            own().wait()
        for nxt in taken[-2::-1] + [self.bits[0]]:
            at = pl.multiple_of(at - bit_of(d, op) * size, 16)
            size *= 2
            op = nxt
            win = self.result.at[pl.ds(at, size), :]
            cp, leave = self.remote(win, win, op)
            then(prev, leave)
            prev = lambda cp=cp: cp().wait_recv()
        self.steps.append(prev)

    def hop(self, cls, kind, i, arriving):
        p, nz = self.pos, self.nz
        far, near = nz - 1 - i, i
        if kind == 1:
            t, way = far * (1 - p.upper) + near * p.upper, p.sign
        else:
            t, way = near * (1 - p.upper) + far * p.upper, -p.sign
        cell = self.keep.at[t, self.rows, :]
        s = 1 + (i if kind == 1 else nz - 1 - cls + i)
        first = kind == 1 and (arriving or cls < nz // 2 - 1)
        r = i if first else nz - 1 + i
        to = p.z - way if arriving else p.z + way
        land = self.line.at[r]
        cp = pltpu.make_async_remote_copy(cell, land, self.ss.at[self.base * self.nz + s], self.rs.at[self.base, 5 + len(self.bits) - 3 + r], device_id=(p.d, to), device_id_type=MESH)
        return cp, cell, land

    def sends(self, cls, kind):
        return self.nz - 1 - cls if kind == 1 else cls

    def along(self, cls, kind, i):
        if kind == 1 and cls == 0:
            for k in range(self.nz - 1):
                self.hop(cls, 1, k, False)[0].start()
            return
        cp, cell, land = self.hop(cls, kind, i, True)
        cp.wait_recv()
        add_into(cell, land, self.size)
        if i < self.sends(cls, kind):
            self.hop(cls, kind, i, False)[0].start()

    def finish(self, cls):
        self.last().wait_send()
        for kind in (1, 2):
            for i in range(self.sends(cls, kind)):
                self.hop(cls, kind, i, False)[0].wait_send()


def enter(d, z, nz, bits):
    bar = pltpu.get_barrier_semaphore()
    for b in bits:
        pl.semaphore_signal(bar, inc=1, device_id=(flip(d, b), z), device_id_type=MESH)
    @pl.when(z + 1 < nz)
    def _():
        pl.semaphore_signal(bar, inc=1, device_id=(d, z + 1), device_id_type=MESH)

    @pl.when(z >= 1)
    def _():
        pl.semaphore_signal(bar, inc=1, device_id=(d, z - 1), device_id_type=MESH)
    last = nz - 1
    pl.semaphore_wait(bar, len(bits) + lax.div(z + last, jnp.int32(nz)) + lax.div(last - z + last, jnp.int32(nz)))


def dot(a, b):
    return lax.dot_general(a, b, (((1,), (0,)), ((), ())), preferred_element_type=f32)


def dot_nt(a, b):
    return lax.dot_general(a, b, (((1,), (1,)), ((), ())), preferred_element_type=f32)


def dot_tn(a, b):
    return lax.dot_general(a, b, (((0,), (0,)), ((), ())), preferred_element_type=f32)


def norm_forward(h, gain, shift):
    centred = h - jnp.mean(h, -1, keepdims=True)
    inverse = lax.rsqrt(jnp.mean(centred * centred, -1, keepdims=True) + epsilon)
    normed = centred * inverse
    return normed * gain + shift, normed, inverse


def norm_backward(grad, normed, inverse, gain):
    scaled = grad * gain
    return inverse * (scaled - jnp.mean(scaled, -1, keepdims=True) - normed * jnp.mean(scaled * normed, -1, keepdims=True))


def col_sum(v):
    return jnp.sum(v, axis=0, keepdims=True)


def nth_shard(z, nz, o):
    t = z
    for b in range(nz.bit_length() - 1):
        t = t + lax.rem(lax.div(o, jnp.int32(2 ** b)), jnp.int32(2)) * (1 - 2 * bit_of(z, b)) * (2 ** b)
    return t


class Dims:
    pass


def layer_kernel(m, *refs):
    n_in, n_out = len(m.inputs), len(m.outputs)
    R = dict(zip(m.inputs + m.outputs + m.scratch, refs))
    g = Dims()
    for k, v in R.items():
        setattr(g, k, v)
    ni, L, T, D, nz, hp, nh, KP, NP = m.ni, m.L, m.T, m.D, m.nz, m.hp, m.nh, m.KP, m.NP
    d, z = lax.axis_index("dp"), lax.axis_index("mp")
    core = bit_of(d, m.bits[0])
    partner = flip(d, m.bits[0])

    shard = functools.partial(nth_shard, z, nz)

    g.DCQ = g.HD.at[:, :, 0:hp]
    g.DQ = g.DP.at[:, :, 0:m.QW]
    g.KV = g.DKV.at[:, 0:ni * KP]

    pos = Dims()
    pos.d, pos.z = d, z
    pos.upper = lax.div(2 * z, jnp.int32(nz))
    pos.sign = 1 - 2 * pos.upper
    kind = z * (1 - pos.upper) + (nz - 1 - z) * pos.upper
    classes = range(nz // 2)

    hw = m.hw
    joins = [(g.wq, g.AO.at[pl.ds(0, hw)]), (g.wa.at[0], g.AO.at[pl.ds(hw, hw)]), (g.wa.at[2], g.AO.at[pl.ds(2 * hw, hw)]), (g.wa.at[1], g.AO.at[pl.ds(3 * hw, hw)]),
             (g.wp.at[0], g.BO.at[pl.ds(0, hw)]), (g.wp.at[1], g.BO.at[pl.ds(hw, hw)]), (g.wao, g.OO.at[pl.ds(0, hw)]), (g.wco, g.OO.at[pl.ds(hw, hw)])]
    joins = [pltpu.make_async_copy(a, b, g.js.at[i]) for i, (a, b) in enumerate(joins)]
    for cp in joins:
        cp.start()
    loads = [pltpu.make_async_copy(a, b, g.js.at[10 + i]) for i, (a, b) in enumerate(((g.x, g.XV), (g.patches, g.PV)))]
    for cp in loads:
        cp.start()
    g.TMP[0:16, 0:D] = jnp.zeros((16, D), f32)
    ab, cb = g.ab[...].astype(f32), g.cb[...].astype(f32)
    g.TMP[0:1, 0:hw] = cb[0:1]
    g.TMP[0:1, hw:2 * hw] = ab[0:1]
    g.TMP[0:1, 2 * hw:3 * hw] = ab[1:2]
    g.TMP[1:2, hw:2 * hw] = cb[1:2]
    g.TMP[2:3, 0:D] = g.hb[...].astype(f32).reshape(1, D)
    g.VO[...] = g.TMP[0:16, 0:D].astype(bf16)
    g.VG[z] = g.VO[...]
    enter(d, z, nz, m.bits)
    for cp in joins:
        cp.wait()
    gsem = (g.out, g.zr, g.pr)
    own = {"A": g.AO, "B": g.BO, "O": g.OO, "H": g.H, "W": g.W, "V": g.VO}
    far = {"A": g.GA, "B": g.GB, "O": g.GO, "H": g.GH, "W": g.GW, "V": g.VG}
    gathers = [Gather(own[k], far[k], r0, rows, order, pos, nz, gsem, c, (nz - 1) * sum(len(q[3]) for q in m.gather_plan[:c])) for c, (k, r0, rows, order) in enumerate(m.gather_plan)]
    calls = [0, 0]

    def gather_steps():
        at = calls[0]
        calls[0] += 1
        for cls in classes:
            todo = m.gather_steps[cls][at]
            if todo:
                @pl.when(kind == cls)
                def _():
                    for c, st, dr, j in todo:
                        gathers[c].item(cls, nz, st, dr, j)

    nb = len(m.bits)

    def small_copy(i):
        return pltpu.make_async_remote_copy(g.SM, g.SR.at[i], g.ms.at[i], g.mr.at[i], device_id=(flip(d, m.bits[i]), z), device_id_type=MESH)

    def small_spread(o, frm):
        to = lax.rem(z + o, jnp.int32(nz))
        return pltpu.make_async_remote_copy(g.SM, g.SZ.at[frm(to)], g.ms.at[nb + o], g.zm.at[frm(to)], device_id=(d, to), device_id_type=MESH)

    small_store = lambda: pltpu.make_async_copy(g.SM, g.small, g.js.at[13])

    def small_step(i):
        if i > 0 and i < 4:
            small_copy(i - 1).wait()
            g.SM[...] += g.SR[i - 1]
        if i < 3:
            small_copy(i).start()
        elif i == 3:
            for e in range(3, nb):
                small_copy(e).start()
                small_copy(e).wait()
                g.SM[...] += g.SR[e]
            g.SZ[z] = g.SM[...]
            for o in range(1, nz):
                small_spread(o, lambda to: z).start()
        elif i == 5:
            for o in range(1, nz):
                small_spread(o, lambda to: to).wait_recv()
            for o in range(1, nz):
                small_spread(o, lambda to: z).wait_send()
            total = g.SZ[0]
            for t in range(1, nz):
                total = total + g.SZ[t]
            g.SM[...] = total
            small_store().start()

    def reduce_steps():
        at = calls[1]
        calls[1] += 1
        for cls in classes:
            todo = m.reduce_steps[cls][at]
            if todo:
                @pl.when(kind == cls)
                def _():
                    for c, what in todo:
                        i = progress[cls, c, what]
                        progress[cls, c, what] += 1
                        if c == len(chunks):
                            small_step(i)
                        elif what == 0:
                            chunks[c].steps[i]()
                        else:
                            chunks[c].along(cls, what, i)

    def after_each(steps):
        def between(o):
            for q in range(nz - 1):
                pl.when(o == q)(lambda: steps())
        return between

    def finish_gather():
        for cls in classes:
            @pl.when(kind == cls)
            def _():
                for q in gathers:
                    q.finish(cls, nz)

    pair_slot = [0]

    def pair(ref, rows):
        s = pair_slot[0]
        pair_slot[0] += 1
        return pltpu.make_async_remote_copy(ref.at[pl.ds(0, rows)], ref.at[pl.ds(rows, rows)], g.cs.at[s], g.cr.at[s], device_id=(partner, z), device_id_type=MESH)

    def place(block, slot):
        buf, sem, key, rows, cols = block
        return buf.at[slot, pl.ds(0, rows[1]), pl.ds(*cols)], sem.at[slot]

    def fetch(block, slot, o):
        buf, sem, key, rows, cols = block
        dst, done = place(block, slot)
        r, c = pl.ds(*rows), pl.ds(*cols)

        def mine():
            pltpu.make_async_copy(own[key].at[r, c], dst, done).start()

        def other():
            pltpu.make_async_copy(far[key].at[shard(o), r, c], dst, done).start()
        if isinstance(o, int):
            mine() if o == 0 else other()
        else:
            pl.when(o == 0)(mine)
            pl.when(o != 0)(other)

    def arrived(block, slot):
        buf, sem, key, rows, cols = block
        dst, done = place(block, slot)
        pltpu.make_async_copy(own[key].at[pl.ds(*rows), pl.ds(*cols)], dst, done).wait()

    def stream(blocks, body, between, ahead, refill=()):
        def step(o, c):
            if blocks:
                @pl.when(o + 1 < nz)
                def _():
                    for b in blocks:
                        fetch(b, slot_of(b, o + 1), o + 1)
            if ahead:
                @pl.when(o + 1 == nz)
                def _():
                    for b in ahead:
                        fetch(b, 0, 0)
            for b in blocks:
                arrived(b, slot_of(b, o))
            body(o, lax.rem(o, jnp.int32(2)))
            for b in refill:
                fetch(b, o, o)
            between(o)
            return c
        lax.fori_loop(0, nz, step, 0)

    def slot_of(block, o):
        return lax.rem(o, jnp.int32(block[0].shape[0]))

    FZ, PW, BW = m.FZ, m.PW, m.BW
    self_blocks = [(g.SA, g.sa, "A", (LANES, D - LANES), (0, D)), (g.SO, g.so, "O", (0, hp), (0, D))]
    cross_blocks = [(g.SA, g.sa, "A", (0, hp), (0, D)), (g.SB, g.sb, "B", (0, BW), (0, PW)), (g.SO, g.so, "O", (LANES, hp), (0, D))]
    hidden_blocks = [(g.SA, g.sa, "H", (0, D), (0, FZ))]
    output_blocks = [(g.SA, g.sa, "W", (0, FZ), (0, D))]
    back_blocks = [(g.SH, g.sh, "H", (0, D), (0, FZ))]
    cross_back = [cross_blocks[0], cross_blocks[2]]
    for b in self_blocks:
        fetch(b, 0, 0)

    lane = lax.broadcasted_iota(jnp.int32, (L, hp), 1)
    low = [lane // HEAD == h for h in range(nh)]
    high = [lane // HEAD == h + 1 for h in range(nh)]

    def stack(v, masks):
        return jnp.concatenate([jnp.where(k, v, 0.0) for k in masks], axis=0).astype(bf16)

    def unstack(v, masks):
        out = jnp.where(masks[0], v[0:L], 0.0)
        for h in range(1, nh):
            out = out + jnp.where(masks[h], v[h * L:(h + 1) * L], 0.0)
        return out

    def softmax(s):
        e = jnp.exp(s - jnp.max(s, -1, keepdims=True))
        return e / jnp.sum(e, -1, keepdims=True)

    gather_steps()
    for cp in loads:
        cp.wait()
    for i in range(ni):
        g.ACC[i * L:(i + 1) * L] = g.XV[i].astype(f32)
        mine = jnp.concatenate([g.PV[:, i, :].astype(f32), jnp.zeros((KP - NP, m.PW), f32)], 0)
        g.PT[i * KP:(i + 1) * KP] = mine.astype(bf16)
    g.X[0:T] = g.ACC[...].astype(bf16)
    cot_load = pltpu.make_async_copy(g.cot, g.XV, g.js.at[12])
    cot_load.start()
    swaps = [pair(g.X, T), pair(g.PT, ni * KP)]
    for s in swaps:
        s.start()

    g.ACC[...] = jnp.zeros((T, D), f32)
    gather_steps()

    def self_forward(o, slot):
        t = shard(o)
        bias = g.VG[t].astype(f32)[0:1, LANES:]
        qkv = (dot_nt(g.X[0:T], g.SA[o, 0:m.QW]) + bias).astype(bf16)
        g.QKV[o] = qkv
        qf = qkv.astype(f32)
        outs = []
        for i in range(ni):
            r = slice(i * L, (i + 1) * L)
            qs = stack(qf[r, 0:hp], high)
            k_i = qf[r, 3 * LANES:3 * LANES + hp].astype(bf16)
            v_i = qf[r, 2 * LANES:2 * LANES + hp].astype(bf16)
            p = softmax(dot_nt(qs, k_i) * score_scale)
            g.PS[o * ni + i] = p
            outs.append(unstack(dot(p.astype(bf16), v_i), low))
        mixed = jnp.concatenate(outs, 0).astype(bf16)
        g.MX[0, o, 0:T] = mixed
        g.ACC[...] += dot(mixed, g.SO[o])

    stream(self_blocks, self_forward, after_each(gather_steps), cross_blocks)

    def out_row(j):
        return tuple(v[...].astype(f32)[j:j + 1, :] for v in (g.ob, g.gain, g.shift))

    ob, gn, sh = out_row(0)
    first, normed, inv = norm_forward(g.X[0:T].astype(f32) + g.ACC[...] + ob, gn, sh)
    g.NM[0] = normed
    g.INV[...] = jnp.broadcast_to(inv, (T, LANES))
    g.F[0:T] = first.astype(bf16)
    g.ACC[...] = jnp.zeros((T, D), f32)
    gather_steps()

    key_pos = lax.broadcasted_iota(jnp.int32, (nh * L, KP), 1)

    def cross_forward(o, slot):
        t = shard(o)
        vb = g.VG[t].astype(f32)
        cq = (dot_nt(g.F[0:T], g.SA[o, 0:hp]) + vb[0:1, 0:hp]).astype(bf16)
        g.CQ[o] = cq
        cqf = cq.astype(f32)
        kv = (dot_nt(g.PT[0:ni * KP], g.SB[slot]) + vb[1:2, 0:m.BW]).astype(bf16)
        g.KV[o] = kv
        outs = []
        for i in range(ni):
            qs = stack(cqf[i * L:(i + 1) * L], low)
            kvi = g.KV[o, i * KP:(i + 1) * KP]
            s = dot_nt(qs, kvi[:, 0:hp]) * score_scale
            s = jnp.where(key_pos < g.rows[z * ni + i], s, -1e30)
            p = softmax(s)
            g.PC[o * ni + i] = p
            outs.append(unstack(dot(p.astype(bf16), kvi[:, LANES:LANES + hp]), high))
        mixed = jnp.concatenate(outs, 0).astype(bf16)
        g.MX[1, o, 0:T] = mixed
        g.ACC[...] += dot(mixed, g.SO[o])

    stream(cross_blocks, cross_forward, after_each(gather_steps), hidden_blocks)
    ob, gn, sh = out_row(1)
    second, normed, inv = norm_forward(g.F[0:T].astype(f32) + g.ACC[...] + ob, gn, sh)
    g.NM[1] = normed
    g.INV[:, HEAD:] = jnp.broadcast_to(inv, (T, LANES - HEAD))
    g.S2[0:T] = second.astype(bf16)
    gather_steps()
    other = g.MX.at[1 - core]
    mix_swap = pltpu.make_async_remote_copy(other.at[:, pl.ds(0, T)], other.at[:, pl.ds(T, T)], g.cs.at[m.swaps - 1], g.cr.at[m.swaps - 1], device_id=(partner, z), device_id_type=MESH)
    mix_swap.start()
    swaps += [pair(g.F, T), pair(g.S2, T)]
    for s in swaps[2:4]:
        s.start()

    def hidden_forward(o, slot):
        t = shard(o)
        pre = dot(g.S2[0:T], g.SA[o]) + g.VG[t].astype(f32)[2:3, :]
        cdf = 0.5 * (1.0 + lax.erf(pre * math.sqrt(0.5)))
        g.GP[o] = cdf + pre * jnp.exp(-0.5 * pre * pre) * (1.0 / math.sqrt(2.0 * math.pi))
        g.HD[o, 0:T] = (pre * cdf).astype(bf16)

    stream(hidden_blocks, hidden_forward, after_each(gather_steps), output_blocks)
    hid_swaps = [pair(g.HD.at[o], T) for o in range(nz)]
    for s in hid_swaps:
        s.start()
    g.ACC[...] = jnp.zeros((T, D), f32)
    gather_steps()

    def output_forward(o, slot):
        g.ACC[...] += dot(g.HD[o, 0:T], g.SA[o])

    stream(output_blocks, output_forward, after_each(gather_steps), back_blocks)
    gather_steps()
    ob, gn, sh = out_row(2)
    final, normed, inv = norm_forward(g.S2[0:T].astype(f32) + g.ACC[...] + ob, gn, sh)
    g.TMP[0:T, 0:D] = final
    layer_store = pltpu.make_async_copy(g.TMP.at[pl.ds(0, T), pl.ds(0, D)], g.layer_out, g.js.at[8])
    layer_store.start()

    cot_load.wait()
    for i in range(ni):
        g.ACC[i * L:(i + 1) * L] = g.XV[i].astype(f32)
    cot = g.ACC[...]
    g.SM[...] = jnp.zeros(g.SM.shape, f32)

    def record(j, grad_in, grad_out, normed):
        g.SM[j:j + 1] = col_sum(grad_in)
        g.SM[3 + j:4 + j] = col_sum(grad_out * normed)
        g.SM[6 + j:7 + j] = col_sum(grad_out)

    third = norm_backward(cot, normed, inv, gn)
    record(2, third, cot, normed)
    g.G3[0:T] = third.astype(bf16)
    swap3 = pair(g.G3, T)
    swap3.start()

    finish_gather()
    rsem = (g.out, g.rs, g.ls)
    results = {"A": g.RA, "B": g.RB, "O": g.RO, "H": g.RH, "W": g.RW}
    chunks = []
    progress = {}
    for c, (k, h0, half, order) in enumerate(m.reduce_plan):
        recvs = {b: R[f"rv{c}_{b}"] for b in m.bits[1:3]}
        whole = m.rows[k] // 2
        chunks.append(Reduce(R[f"kp{c}"], recvs, R[f"ln{c}"], R.get(f"ex{c}"), results[k], core * whole + h0, half, order, pos, nz, m.bits, rsem, c))
    for cls in classes:
        for c in range(len(chunks) + 1):
            for what in range(3):
                progress[cls, c, what] = 0

    def half_columns(apart, count=None):
        return pl.ds(pl.multiple_of(core * apart, LANES), count or apart)

    def deal(k, t, value):
        for c, p in enumerate(m.reduce_plan):
            if p[0] == k:
                R[f"kp{c}"][t] = value[p[1]:p[1] + p[2]].astype(bf16)

    reduce_steps()

    reduce_steps()
    cols = half_columns(m.FZ // 2)
    own_part = dot_tn(g.HD[0, 0:T, cols], g.G3[0:T])
    swap3.wait_recv()
    for s in hid_swaps:
        s.wait_recv()
    deal("W", shard(jnp.int32(0)), own_part + dot_tn(g.HD[0, T:, cols], g.G3[T:]))

    def job_w(o, c):
        t = shard(o)
        deal("W", t, dot_tn(g.HD[o, :, cols], g.G3[...]))
        return c
    lax.fori_loop(1, nz, job_w, 0)
    for s in hid_swaps:
        s.wait_send()
    reduce_steps()
    g.ACC[...] = third

    def loop_send(ref, rows, kind, o):
        pltpu.make_async_remote_copy(ref.at[o, pl.ds(0, rows)], ref.at[o, pl.ds(rows, rows)], g.ds.at[kind, o], g.dr.at[kind, o], device_id=(partner, z), device_id_type=MESH).start()

    def hidden_backward(o, slot):
        t = shard(o)
        pre = (dot_nt(g.G3[0:T], g.SA[o]) * g.GP[o]).astype(bf16)
        g.DP[o, 0:T] = pre
        g.SM[pl.ds(9 + t, 1)] = col_sum(pre.astype(f32))
        loop_send(g.DP, T, 0, o)
        g.ACC[...] += dot_nt(pre, g.SH[slot])

    stream(back_blocks, hidden_backward, after_each(reduce_steps), [], cross_back)
    reduce_steps()

    def loop_wait(ref, rows, kind):
        for o in range(nz):
            cp = pltpu.make_async_remote_copy(ref.at[o, pl.ds(0, rows)], ref.at[o, pl.ds(rows, rows)], g.ds.at[kind, o], g.dr.at[kind, o], device_id=(partner, z), device_id_type=MESH)
            cp.wait()

    gn = out_row(1)[1]
    normed, inv = g.NM[1], g.INV[:, HEAD:HEAD + 1]
    grad = g.ACC[...]
    secondg = norm_backward(grad, normed, inv, gn)
    record(1, secondg, grad, normed)
    g.G12[1, 0:T] = secondg.astype(bf16)
    swap2 = pair(g.G12.at[1], T)
    swap2.start()
    reduce_steps()
    loop_wait(g.DP, T, 0)
    swaps[3].wait_recv()

    def job_h(o, c):
        t = shard(o)
        deal("H", t, dot_tn(g.S2[:, half_columns(D // 2)], g.DP[o]))
        return c
    lax.fori_loop(0, nz, job_h, 0)
    reduce_steps()

    g.ACC[...] = secondg

    def backward_unit(qs, k_i, v_i, p, ms, masks):
        grad_v = dot_tn(p.astype(bf16), ms)
        grad_p = dot_nt(ms, v_i)
        gs = (p * (grad_p - jnp.sum(p * grad_p, -1, keepdims=True))).astype(bf16)
        grad_q = unstack(dot(gs, k_i), masks) * score_scale
        grad_k = dot_tn(gs, qs) * score_scale
        return grad_q, grad_k.astype(bf16).astype(f32), grad_v.astype(bf16).astype(f32)

    def cross_backward(o, slot):
        t = shard(o)
        for b in cross_back:
            arrived(b, o)
        gm = dot_nt(g.G12[1, 0:T], g.SO[o]).astype(bf16).astype(f32)
        cqf = g.CQ[o].astype(f32)
        grads = []
        for i in range(ni):
            r = slice(i * L, (i + 1) * L)
            kvi = g.KV[o, i * KP:(i + 1) * KP]
            gq, gk, gv = backward_unit(stack(cqf[r], low), kvi[:, 0:hp], kvi[:, LANES:LANES + hp], g.PC[o * ni + i], stack(gm[r], high), low)
            grads.append(gq)
            g.DKV[o, i * KP:(i + 1) * KP] = jnp.concatenate([gk[:, 0:LANES], gk[:, LANES:] + gv[:, 0:LANES], gv[:, LANES:]], 1).astype(bf16)
        dcq = jnp.concatenate(grads, 0).astype(bf16)
        g.DCQ[o, 0:T] = dcq
        loop_send(g.DCQ, T, 1, o)
        loop_send(g.DKV, ni * KP, 2, o)
        dkv = g.DKV[o, 0:ni * KP]
        g.SM[pl.ds(9 + nz + t, 1), BW:BW + hp] = col_sum(dcq.astype(f32))
        g.SM[pl.ds(9 + nz + t, 1), 0:BW] = col_sum(dkv.astype(f32))
        g.ACC[...] += dot(dcq, g.SA[o, 0:hp])

    stream([], cross_backward, after_each(reduce_steps), [], self_blocks)
    reduce_steps()
    gn = out_row(0)[1]
    normed, inv = g.NM[0], g.INV[:, 0:1]
    grad = g.ACC[...]
    firstg = norm_backward(grad, normed, inv, gn)
    record(0, firstg, grad, normed)
    g.G12[0, 0:T] = firstg.astype(bf16)
    swap1 = pair(g.G12.at[0], T)
    swap1.start()
    reduce_steps()
    loop_wait(g.DCQ, T, 1)
    loop_wait(g.DKV, ni * KP, 2)
    swaps[1].wait_recv()

    layer_store.wait()

    def job_b(o, c):
        t = shard(o)
        g.TMP[...] = dot_tn(g.DKV[o, :, half_columns(LANES, hp)], g.PT[...])
        deal("B", t, g.TMP[pl.ds(pl.multiple_of(core * HEAD, 16), BW // 2)])
        return c
    lax.fori_loop(0, nz, job_b, 0)
    for o in range(2):
        fetch(cross_blocks[1], o, o)
    reduce_steps()

    g.ACC[...] = firstg

    def self_backward(o, slot):
        t = shard(o)
        for b in self_blocks:
            arrived(b, o)
        gm = dot_nt(g.G12[0, 0:T], g.SO[o]).astype(bf16).astype(f32)
        qf = g.QKV[o].astype(f32)
        gqs, gks, gvs = [], [], []
        for i in range(ni):
            r = slice(i * L, (i + 1) * L)
            k_i = qf[r, 3 * LANES:3 * LANES + hp].astype(bf16)
            v_i = qf[r, 2 * LANES:2 * LANES + hp].astype(bf16)
            gq, gk, gv = backward_unit(stack(qf[r, 0:hp], high), k_i, v_i, g.PS[o * ni + i], stack(gm[r], low), high)
            gqs.append(gq)
            gks.append(gk)
            gvs.append(gv)
        gq, gk, gv = (jnp.concatenate(v, 0) for v in (gqs, gks, gvs))
        dq = jnp.concatenate([gq, gv[:, 0:LANES], gv[:, LANES:] + gk[:, 0:LANES], gk[:, LANES:]], 1).astype(bf16)
        g.DQ[o, 0:T] = dq
        loop_send(g.DQ, T, 3, o)
        g.SM[pl.ds(9 + 2 * nz + t, 1), 0:m.QW] = col_sum(dq.astype(f32))
        g.ACC[...] += dot(dq, g.SA[o, 0:m.QW])

    stream([], self_backward, after_each(reduce_steps), [])
    text_store = pltpu.make_async_copy(g.ACC, g.text_grad, g.js.at[8])
    text_store.start()
    reduce_steps()
    loop_wait(g.DQ, T, 3)
    swap1.wait_recv()
    swap2.wait_recv()
    for s in swaps[0:1] + swaps[2:3] + [mix_swap]:
        s.wait_recv()

    def job_o(o, c):
        t = shard(o)
        g.TMP[:, 0:D] = dot_tn(g.MX[core, o], g.G12[core])
        deal("O", t, g.TMP[pl.ds(pl.multiple_of(core * HEAD, 16), hw), 0:D])
        return c
    lax.fori_loop(0, nz, job_o, 0)
    reduce_steps()

    def job_a(o, c):
        t = shard(o)

        @pl.when(core == 0)
        def _():
            left = dot_tn(g.DCQ[o], g.F[...])
            right = dot_tn(g.DQ[o, :, 0:hp], g.X[...])
            deal("A", t, jnp.concatenate([left[0:LANES], left[LANES:] + right[0:LANES], right[LANES:]], 0))

        @pl.when(core == 1)
        def _():
            deal("A", t, dot_tn(g.DQ[o, :, hp:], g.X[...]))
        return c
    lax.fori_loop(0, nz, job_a, 0)
    reduce_steps()

    reduce_steps()
    for part in range(nz // 2):
        for slot in range(2):
            arrived(cross_blocks[1], slot)
        for i in range(ni):
            r = pl.ds(i * KP, KP)
            total = (dot(g.DKV[2 * part, r], g.SB[0]) + dot(g.DKV[2 * part + 1, r], g.SB[1]))[0:NP]
            g.PG[:, i, :] = total if part == 0 else g.PG[:, i, :] + total
            if i == ni - 1 and part < nz // 2 - 1:
                for slot in range(2):
                    fetch(cross_blocks[1], slot, 2 * part + 2 + slot)
            if i == ni - 1 and part == nz // 2 - 1:
                patch_store = pltpu.make_async_copy(g.PG, g.patch_out, g.js.at[9])
                patch_store.start()
            if i % 2 == 1:
                reduce_steps()
    assert calls == [len(m.gather_steps[0]), len(m.reduce_steps[0])], calls
    assert all(sum(len(p) for p in m.reduce_steps[cls]) == sum(progress[cls, c, w] for c in range(len(chunks) + 1) for w in range(3)) for cls in classes)

    for cp in swaps + [swap1, swap2, swap3, mix_swap]:
        cp.wait_send()
    text_store.wait()
    patch_store.wait()
    small_store().wait()
    for cls in classes:
        @pl.when(kind == cls)
        def _():
            for c in chunks:
                c.finish(cls)


GATHER_PLAN = (("V", 0, 16, ""), ("A", 0, 256, "yxc"), ("W", 0, 512, "yc"), ("O", 0, 384, "yxc"), ("H", 0, 384, "yxc"), ("A", 256, 256, "xyc"), ("A", 512, 256,
    "yc"), ("H", 384, 384, "yxc"), ("W", 512, 256, "yc"), ("B", 0, 384, "yxc"))
GATHER_ORDER = ((0, 40, 200, 120, -1, 13, 53, 213, 133, 61, 14, 360, 221, 54, 214, 141, 134, 69, 15, 229, 222, 77, 240, 62, 373, 237, 55, 142, 149, 215, 230, 135,
    157, 70, 160, 238, 381, 374, 78, 63, 150, 253, 143, 223, 280, 158, 375, 382, 254, 261, 389, 320, 173, 269, -1, 397, 71, 231, 383, 80, 255, 293, 151,
    79, 239, 262, 174, 159, 181, 270, 175, -1, 390, 333, 263, 301, 294, 398, 271, -1, 295, 391, 182, 183, -1, 399, 341, 93, 189, -1, 309, 302, 303, 349,
    334, 197, -1, 317, 101, 94, 190, -1, 342, 335, 109, 198, 191, -1, 310, 350, 95, 199, 102, -1, 318, 311, 343, 110, -1, 319, -1, 351, 103, -1, -1, 111,
    -1, -1, -1), (0, 4, 40, 44, 200, 204, 120, 124, -1, 9, 13, 49, 53, 209, 213, 129, 133, 14, 360, 364, 57, 54, 217, 61, 214, 221, 137, 134, 369, 65,
    141, 373, 240, 62, 244, 73, 69, 222, 225, 374, 77, 233, 249, 229, 253, 160, 164, 145, 142, 237, 153, 377, 254, 169, 149, 280, 284, 173, 381, 157, 70,
    174, 230, 78, 289, 320, 324, 293, 150, 238, 382, 158, 294, 80, 84, 257, 329, 385, 333, 265, 261, -1, 393, 269, 262, 389, 177, 93, 270, -1, 397, 334,
    89, 181, 182, -1, 297, 390, -1, 301, 185, 398, -1, 302, 337, 94, 193, 189, -1, 345, 341, 197, 190, -1, 305, 349, 101, 198, -1, 313, 342, 309, 109, -1,
    317, 350, 310, 97, 318, -1, 105, -1, 102, -1, -1, 110, -1, -1, -1))
REDUCE_PLAN = (("W", 128, "xyz"), ("W", 128, "yxz"), ("W", 128, "zyx"), ("H", 128, "zyx"), ("H", 128, "xyz"), ("H", 128, "xzy"), ("B", 128, "yzx"), ("B", 64,
    "xyz"), ("O", 64, "yzx"), ("O", 64, "xyz"), ("O", 64, "zxy"), ("A", 64, "xyz"), ("A", 64, "yxz"), ("A", 64, "zxy"), ("A", 64, "yzx"), ("A", 64,
    "xyz"), ("A", 64, "xyz"))
REDUCE_ORDER = ((-1, -1, 6, 7, 0, 3, -1, -1, -1, -1, -1, -1, 12, 9, 10, 15, -1, 0, 3, -1, -1, -1, 0, 1, 12, -1, 8, 6, -1, 18, 21, 12, 13, -1, 6, 15, 16, -1, 3, 4,
    -1, -1, 2, 0, 21, 11, 9, 6, -1, 30, 31, 0, 18, 6, 19, 24, 27, 14, 12, -1, 48, 36, 0, 39, 40, 45, 33, 21, 22, 42, 9, 0, 6, 17, 15, 5, 3, -1, 51, -1, 6,
    51, 27, -1, 24, 25, 12, -1, 48, -1, 36, 32, 30, 45, 42, 43, 33, 15, 9, 3, 20, 18, 27, 28, 51, 48, 49, 12, 45, 46, 41, 39, 12, 36, 37, 33, 34, 23, 30,
    21, 15, 9, 26, 24, 18, 3, 39, 3, 51, 30, 44, 42, 15, 21, 24, 29, 27, 15, 18, 9, 42, 50, 48, 39, 30, 21, 27, 9, 24, 47, 45, 42, 21, 38, 30, 36, 18, 48,
    27, 51, 39, 30, 35, 33, 18, 24, 27, 36, 45, 24, 48, 42, 33, 39, 48, 42, 36, 45, 39, 51, 36, 33, 45, 33), (-1, -1, 6, 0, 3, -1, -1, -1, -1, -1, 7, -1,
    12, 9, 15, -1, 7, 0, 3, -1, 7, 8, -1, -1, 8, 6, 0, 12, 10, -1, 10, -1, 6, 18, 21, 10, 1, 12, 11, 15, 1, -1, 1, 13, 13, 2, 6, 3, 13, 11, 2, 0, 9, -1,
    14, 14, 12, 16, 16, -1, 6, 21, 16, 18, 4, 17, 4, 0, -1, 4, 9, 5, 12, 17, 15, 5, 3, 0, -1, 30, 31, 31, 6, 0, 31, 24, 27, 12, 21, 9, 6, -1, 48, 32, 36,
    39, 45, 19, 33, 42, 32, 30, 19, 12, 24, 27, 3, 15, -1, 51, 9, -1, 19, 51, 20, -1, 36, 40, 48, -1, 40, 20, 18, -1, 40, 22, 41, 45, 22, 22, 42, 27, 25,
    41, 39, 23, 25, 3, 23, 21, 25, 15, 33, 26, 43, 3, 30, 43, 26, 24, 9, 43, 51, 28, 28, 44, 48, 28, 9, 49, 44, 42, 49, 36, 49, 29, 45, 46, 18, 46, 21,
    50, 46, 39, 50, 48, 37, 37, 29, 37, 47, 33, 30, 47, 45, 34, 34, 34, 24, 38, 27, 38, 36, 51, 39, 18, 42, 48, 35, 30, 15, 35, 45, 33, 21, 24, 27, 39,
    36, 51, 42, 15, 21, 48, 30, 18, 48, 33, 45, 30, 24, 27, 18, 45, 36, 39, 24, 51, 27, 42, 33, 36, 39, 42, 33))


def unpack(orders, decode):
    out = []
    for order in orders:
        parts = [[]]
        for code in order:
            if code < 0:
                parts.append([])
            else:
                parts[-1].append(decode(code))
        out.append(parts)
    return out


def gather_code(code):
    return code // 40, code // 8 % 5 - 1, code // 4 % 2, code % 4


def reduce_code(code):
    return code // 3, code % 3


def plans(m):
    link = dict(zip("cxy", m.bits[:3]), z="z")
    m.gather_plan = [(k, r0, rows, tuple(link[o] for o in order)) for k, r0, rows, order in GATHER_PLAN]
    m.gather_steps = unpack(GATHER_ORDER, gather_code)
    m.reduce_plan = []
    at = {}
    for k, half, order in REDUCE_PLAN:
        h0 = at.get(k, 0)
        at[k] = h0 + half
        m.reduce_plan.append((k, h0, half, tuple(link[o] for o in order)))
    m.reduce_steps = unpack(REDUCE_ORDER, reduce_code)
    assert all(at[k] * 2 == m.rows[k] for k in at) and m.nz == 4


def run_layer(m, x, patches, rows, cot, wa, ab, wao, wq, wp, cb, wco, H, hb, W, ob, gain, shift):
    nz = m.nz
    ni, L, D = x.shape
    T = ni * L
    m.ni, m.L, m.D, m.T = ni, L, D, T
    m.NP, m.PW = patches.shape[1:]
    by_patch = jnp.swapaxes(patches, 0, 1)
    m.KP = (m.NP + 15) // 16 * 16
    hw = m.hw = D // nz
    m.nh = hw // HEAD
    m.hp = (hw + HEAD + LANES - 1) // LANES * LANES
    hp, KP, PW = m.hp, m.KP, m.PW
    m.BW, m.QW, m.FZ = 2 * hw, D - LANES, W.shape[0]
    FZ, BW = m.FZ, m.BW
    m.rows = dict(A=D, B=BW, O=2 * hw, H=D, W=FZ)
    lanes = dict(A=D, B=PW, O=D, H=FZ, W=D)
    plans(m)
    m.swaps = nz + 9
    V, sem = pltpu.VMEM, pltpu.SemaphoreType.DMA
    nc, ng = len(m.reduce_plan), len(m.gather_plan)
    nb = len(m.bits)
    sums = (9 + 3 * nz + 7) // 8 * 8
    scratch = dict(
        VG=V((nz, 16, D), bf16), X=V((2 * T, D), bf16), PT=V((2 * ni * KP, PW), bf16),
        SA=V((nz, D, D), bf16), SH=V((2, D, D), bf16), SB=V((2, BW, PW), bf16), SO=V((nz, hp, D), bf16),
        ACC=V((T, D), f32), QKV=V((nz, T, m.QW), bf16), PS=V((nz * ni, m.nh * L, L), f32), MX=V((2, nz, 2 * T, hp), bf16),
        NM=V((2, T, D), f32), INV=V((T, LANES), f32), F=V((2 * T, D), bf16), S2=V((2 * T, D), bf16),
        CQ=V((nz, T, hp), bf16), PC=V((nz * ni, m.nh * L, KP), f32),
        GP=V((nz, T, FZ), f32), HD=V((nz, 2 * T, FZ), bf16), SM=V((sums, D), f32), G3=V((2 * T, D), bf16), DP=V((nz, 2 * T, FZ), bf16),
        G12=V((2, 2 * T, D), bf16), DKV=V((nz, 2 * ni * KP, m.BW), bf16),
        TMP=V((hp, PW), f32), XV=V(x.shape, bf16), PV=V(by_patch.shape, bf16), PG=V((m.NP, ni, PW), f32), AO=V((D, D), bf16), BO=V((BW, PW), bf16), OO=V((2 * hw, D), bf16), VO=V((16, D), bf16), SR=V((nb, sums, D), f32), SZ=V((nz, sums, D), f32),
        out=sem((max(2 * nz * ng, nz * nc),)), zr=sem((ng, nz - 1)), pr=sem(((nz - 1) * sum(len(q[3]) for q in m.gather_plan),)),
        cs=sem((m.swaps,)), cr=sem((m.swaps,)), ds=sem((4, nz)), dr=sem((4, nz)),
        js=sem((14,)), sa=sem((nz,)), sh=sem((2,)), sb=sem((2,)), so=sem((nz,)),
        rs=sem((nc, 5 + nb - 3 + nz - 1 + nz // 2)), ls=sem((nc,)), ms=sem((nb + nz,)), mr=sem((nb,)), zm=sem((nz,)),
    )
    for c, (k, h0, half, order) in enumerate(m.reduce_plan):
        C = lanes[k]
        scratch[f"kp{c}"] = V((nz, half, C), bf16)
        for b in m.bits[1:3]:
            lead = nz if order.index(b) < order.index("z") else 1
            scratch[f"rv{c}_{b}"] = V((lead, op_rows(half, order, b), C), bf16)
        scratch[f"ln{c}"] = V((nz - 1 + nz // 2, op_rows(half, order, "z"), C), bf16)
        if nb > 3:
            scratch[f"ex{c}"] = V((nb - 3, half // 4, C), bf16)
    S = jax.ShapeDtypeStruct
    hbm, vm, sm = (pl.BlockSpec(memory_space=s) for s in (pl.ANY, pltpu.VMEM, pltpu.SMEM))
    outs = dict(
        layer_out=(S((T, D), f32), hbm), text_grad=(S((T, D), f32), hbm), patch_out=(S((m.NP, ni, PW), f32), hbm), small=(S((sums, D), f32), hbm),
        **{"R" + k: (S((m.rows[k], lanes[k]), bf16), hbm) for k in "ABOHW"},
        **{"G" + k: (S((nz, m.rows[k], lanes[k]), bf16), hbm) for k in "ABOHW"},
    )
    turn = lambda a: jnp.swapaxes(a, -1, -2)
    ins = dict(x=(x, hbm), patches=(by_patch, hbm), rows=(rows, sm), cot=(cot, hbm), wa=(turn(wa), hbm), ab=(ab, vm), wao=(wao, hbm), wq=(turn(wq), hbm), wp=(turn(wp), hbm),
               cb=(cb, vm), wco=(wco, hbm), H=(H, hbm), hb=(hb, vm), W=(W, hbm), ob=(ob, vm), gain=(gain, vm), shift=(shift, vm))
    m.inputs, m.outputs, m.scratch = list(ins), list(outs), list(scratch)
    res = pl.pallas_call(
        functools.partial(layer_kernel, m),
        out_shape=tuple(o[0] for o in outs.values()),
        in_specs=[i[1] for i in ins.values()],
        out_specs=tuple(o[1] for o in outs.values()),
        scratch_shapes=list(scratch.values()),
        compiler_params=pltpu.CompilerParams(collective_id=0, has_side_effects=True, vmem_limit_bytes=67043328),
        name="layer",
    )(*[i[0] for i in ins.values()])
    return dict(zip(outs, res))


finish_ins = ("RA", "RB", "RO", "RH", "RW", "layer_out", "text_grad", "patch_out", "small")
finish_outs = ("layer_out_", "text_grad_", "patch_grad", "attn", "attn_bias", "attn_out", "query", "patch", "cross_bias", "cross_out", "hidden", "hidden_bias", "output", "out_bias", "gain", "shift")


def finish_kernel(m, names, *refs):
    g = Dims()
    for k, v in zip(names, refs):
        setattr(g, k, v)
    nz, hw, ni, KP, NP = m.nz, m.hw, m.ni, m.KP, m.NP
    z = lax.axis_index("mp")
    loads = {}

    def load(name, src, dst):
        cp = pltpu.make_async_copy(src, dst, g.isem.at[len(loads)])
        cp.start()
        loads[name] = cp
    load("W", g.RW, g.vW)
    load("H", g.RH, g.vH)
    load("pg", g.patch_out, g.fG)
    load("lo", g.layer_out, g.vL)
    load("tg", g.text_grad, g.vT)
    load("B", g.RB, g.vP)
    load("O", g.RO, g.vO)
    load("A", g.RA, g.vA)
    stores = []

    def store(src, dst):
        cp = pltpu.make_async_copy(src, dst, g.osem.at[len(stores)])
        cp.start()
        stores.append(cp)

    def widen(src, dst, row0=0):
        step = HEAD

        def body(i, c):
            r = pl.multiple_of(i * step, step)
            dst[pl.ds(r, step), :] = src[pl.ds(row0 + r, step), :].astype(f32)
            return c
        lax.fori_loop(0, dst.shape[0] // step, body, 0)

    loads["W"].wait()
    widen(g.vW, g.fW)
    store(g.fW, g.output)
    loads["H"].wait()
    widen(g.vH, g.fH)
    store(g.fH, g.hidden)
    loads["pg"].wait()
    store(g.fG, g.patch_grad)
    loads["lo"].wait()
    store(g.vL, g.layer_out_)
    loads["tg"].wait()
    store(g.vT, g.text_grad_)
    loads["B"].wait()
    for j in range(2):
        widen(g.vP, g.fP.at[j], j * hw)
    store(g.fP, g.patch)
    loads["O"].wait()
    widen(g.vO, g.fO)
    store(g.fO.at[pl.ds(0, hw)], g.attn_out)
    store(g.fO.at[pl.ds(hw, hw)], g.cross_out)
    loads["A"].wait()
    widen(g.vA, g.fQ)
    for j, part in ((0, 1), (1, 3), (2, 2)):
        widen(g.vA, g.fA.at[j], part * hw)
    store(g.fQ, g.query)
    store(g.fA, g.attn)
    row = lambda k: g.small[pl.ds(9 + k * nz + z, 1), :]
    qv = row(2)[:, 0:5 * LANES]
    at = hw - LANES
    g.attn_bias[0:1] = qv[:, at:at + hw]
    g.attn_bias[1:2] = qv[:, at + hw:at + 2 * hw]
    g.cross_bias[0:1] = row(1)[:, 2 * hw:3 * hw]
    g.cross_bias[1:2] = row(1)[:, hw:2 * hw]
    g.hidden_bias[...] = row(0).reshape(m.FZ)
    g.out_bias[...] = g.small[0:3, :]
    g.gain[...] = g.small[3:6, :]
    g.shift[...] = g.small[6:9, :]
    for cp in stores:
        cp.wait()


def finish(m, r):
    nz, ni, L, D, PW, FZ, BW, KP, NP = m.nz, m.ni, m.L, m.D, m.PW, m.FZ, m.BW, m.KP, m.NP
    hw = m.hw = D // nz
    S, V, sem = jax.ShapeDtypeStruct, pltpu.VMEM, pltpu.SemaphoreType.DMA
    hbm, vm = pl.BlockSpec(memory_space=pl.ANY), pl.BlockSpec(memory_space=pltpu.VMEM)
    shapes = ((m.T, D), (m.T, D), (NP, ni, PW), (3, hw, D), (2, hw), (hw, D), (hw, D), (2, hw, PW), (2, hw), (hw, D), (D, FZ), (FZ,), (FZ, D), (3, D), (3, D), (3, D))
    small = {"attn_bias", "cross_bias", "hidden_bias", "out_bias", "gain", "shift"}
    scratch = dict(
        vW=V((FZ, D), bf16), vH=V((D, FZ), bf16), vL=V((m.T, D), f32), vT=V((m.T, D), f32),
        vP=V((BW, PW), bf16), vO=V((2 * hw, D), bf16), vA=V((D, D), bf16), fW=V((FZ, D), f32), fH=V((D, FZ), f32), fG=V((NP, ni, PW), f32),
        fP=V((2, hw, PW), f32), fO=V((2 * hw, D), f32), fQ=V((hw, D), f32), fA=V((3, hw, D), f32), isem=sem((8,)), osem=sem((11,)),
    )
    ins = [r[k] for k in finish_ins]
    return pl.pallas_call(
        functools.partial(finish_kernel, m, finish_ins + finish_outs + tuple(scratch)),
        out_shape=tuple(S(s, f32) for s in shapes),
        in_specs=[vm if k == "small" else hbm for k in finish_ins],
        out_specs=tuple(vm if k in small else hbm for k in finish_outs),
        scratch_shapes=list(scratch.values()),
        compiler_params=pltpu.CompilerParams(vmem_limit_bytes=56 << 20),
        name="finish",
    )(*ins)


def per_device(nd, nz, text_states, patch_states, patch_rows, cotangent, w_attn, attn_bias, w_attn_out, w_query, w_patch, cross_bias, w_cross_out, w_hidden, hidden_bias, w_output, out_bias, norm_gain, norm_shift):
    m = Dims()
    m.nz, m.bits = nz, tuple(range(nd.bit_length() - 1))
    r = run_layer(m, text_states, patch_states, patch_rows, cotangent, w_attn, attn_bias, w_attn_out, w_query, w_patch, cross_bias, w_cross_out, w_hidden, hidden_bias, w_output, out_bias, norm_gain, norm_shift)
    outs = list(finish(m, r))
    for k in ("attn", "query", "patch"):
        at = finish_outs.index(k)
        outs[at] = jnp.swapaxes(outs[at], -1, -2)
    for at in range(2):
        outs[at] = outs[at].reshape(text_states.shape)
    at = finish_outs.index("patch_grad")
    outs[at] = jnp.swapaxes(outs[at], 0, 1)
    return tuple(outs)


def solution(mesh):
    nd, nz = mesh.shape["dp"], mesh.shape["mp"]
    rows = P(("dp", "mp"), None, None)
    return jax.shard_map(
        functools.partial(per_device, nd, nz),
        mesh=mesh,
        in_specs=(rows, rows, P("dp"), rows, P(None, None, "mp"), P(None, "mp"), P("mp", None), P(None, "mp"), P(None, None, "mp"), P(None, "mp"), P("mp", None), P(None, "mp"), P("mp"), P("mp", None), P(), P(), P()),
        out_specs=(rows, rows, rows, P(None, None, "mp"), P(None, "mp"), P("mp", None), P(None, "mp"), P(None, None, "mp"), P(None, "mp"), P("mp", None), P(None, "mp"), P("mp"), P("mp", None), P(), P(), P()),
        check_vma=False,
    )
```

```python
import functools
import math

import jax
import jax.numpy as jnp
from jax import lax
from jax.experimental import pallas as pl
from jax.experimental.pallas import tpu as pltpu
from jax.sharding import PartitionSpec as P

MESH = pl.DeviceIdType.MESH
HEAD = 64
LANES = 128
epsilon = 1e-06
score_scale = 1.0 / math.sqrt(HEAD)
bf16, f32 = jnp.bfloat16, jnp.float32


def bit_of(d, b):
    return lax.rem(lax.div(d, jnp.int32(2 ** b)), jnp.int32(2))


def flip(d, b):
    return d + (1 - 2 * bit_of(d, b)) * (2 ** b)


def when(cond, fn):
    if cond is True:
        fn()
    else:
        pl.when(cond)(fn)


class Gather:
    def __init__(self, src, dst, row0, rows, order, pos, nz, sems, base, pbase):
        self.nz, self.pbase = nz, pbase
        self.src, self.dst, self.row0, self.order, self.pos = src, dst, row0, order, pos
        self.piece = rows // (2 ** len(order))
        self.zs, self.zr, self.pr = sems
        self.rbase, self.base = base, base * 2 * nz
        self.k = len(order)

    def win(self, s):
        w = jnp.int32(0)
        for i, b in enumerate(self.order):
            if i >= s:
                w = w + bit_of(self.pos.d, b) * (2 ** i)
        return pl.ds(pl.multiple_of(self.row0 + w * self.piece, 16), self.piece * 2 ** s)

    def shard(self, dr, j):
        return self.pos.z + j * (2 * dr - 1) * self.pos.sign

    def cell(self, t, at):
        return lax.rem(t - at - 1 + self.nz, jnp.int32(self.nz))

    def zcopy(self, dr, j):
        p = self.pos
        t, rows = self.shard(dr, j), self.win(0)
        src = self.src.at[rows] if j == 0 else self.dst.at[t, rows]
        to = p.z + (1 - 2 * dr) * p.sign
        s = self.base + (dr if j == 0 else 2 + self.cell(t, p.z))
        return pltpu.make_async_remote_copy(src, self.dst.at[t, rows], self.zs.at[s], self.zr.at[self.rbase, self.cell(t, to)], device_id=(p.d, to), device_id_type=MESH)

    def zwait(self, dr, j):
        p = self.pos
        t = self.shard(dr, j)
        part = self.dst.at[t, self.win(0)]
        pltpu.make_async_remote_copy(part, part, self.zs.at[self.base], self.zr.at[self.rbase, self.cell(t, p.z)], device_id=(p.d, p.z - (1 - 2 * dr) * p.sign), device_id_type=MESH).wait_recv()

    def pcopy(self, s, dr, j):
        p = self.pos
        t = self.shard(dr, j)
        part = self.dst.at[t, self.win(s)]
        c = self.cell(t, p.z)
        return pltpu.make_async_remote_copy(part, part, self.zs.at[self.base + self.nz + 1 + c], self.pr.at[self.pbase + s * (self.nz - 1) + c], device_id=(flip(p.d, self.order[s]), p.z), device_id_type=MESH)

    @staticmethod
    def has(cls, nz, dr, j):
        return cls >= j if dr == 0 else cls + j < nz

    @staticmethod
    def ahead(cls, dr):
        return dr == 0 or cls >= 1

    def item(self, cls, nz, st, dr, j):
        if st == -1:
            self.zcopy(dr, 0).start()
            return
        if st == 0:
            self.zwait(dr, j)
            if j <= nz - 2 and self.ahead(cls, dr):
                self.zcopy(dr, j).start()
        else:
            self.pcopy(st - 1, dr, j).wait()
        if st < self.k:
            self.pcopy(st, dr, j).start()

    def finish(self, cls, nz):
        for dr in (0, 1):
            for j in range(nz - 1):
                if self.ahead(cls, dr) and self.has(cls, nz, dr, j):
                    self.zcopy(dr, j).wait_send()


def add_into(dst, src, rows):
    step = 32 if rows % 32 == 0 else 16

    def body(i, c):
        r = pl.ds(pl.multiple_of(i * step, step), step)
        dst[r, :] = dst[r, :] + src[r, :]
        return c
    lax.fori_loop(0, rows // step, body, 0)


def add_all(dst, src, count, rows):
    def body(t, c):
        add_into(dst.at[t], src.at[t], rows)
        return c
    lax.fori_loop(0, count, body, 0)


def op_rows(half, order, op):
    size = half
    for o in order:
        if o == "z":
            if op == "z":
                return size
        else:
            size //= 2
            if o == op:
                return size
    return size


class Reduce:
    def __init__(self, keep, recvs, line, extra, result, row, half, order, pos, nz, bits, sems, base):
        self.keep, self.recvs, self.line, self.extra = keep, recvs, line, extra
        self.result, self.row, self.half, self.order = result, row, half, order
        self.pos, self.nz, self.bits = pos, nz, bits
        self.ss, self.rs, self.ls = sems
        self.base = base
        self.slot = 0
        self.last = None
        self.steps = []
        self.build()

    def remote(self, src, dst, b):
        r = self.slot
        self.slot += 1
        cp = lambda: pltpu.make_async_remote_copy(src, dst, self.ss.at[self.base * self.nz], self.rs.at[self.base, r], device_id=(flip(self.pos.d, b), self.pos.z), device_id_type=MESH)
        before, self.last = self.last, cp

        def start():
            if before is not None:
                before().wait_send()
            cp().start()
        return cp, start

    def build(self):
        d, z, nz = self.pos.d, self.pos.z, self.nz
        prev = lambda: None
        start, size, whole = jnp.int32(0), self.half, True
        taken = []

        def then(prev, start):
            def step():
                prev()
                start()
            self.steps.append(step)

        for op in self.order:
            if op == "z":
                self.rows = pl.ds(start, size)
                self.size = size
                self.steps.append(prev)
                prev, whole = (lambda: None), False
                continue
            size //= 2
            m = bit_of(d, op)
            keep0 = pl.multiple_of(start + m * size, 16)
            send0 = pl.multiple_of(start + (1 - m) * size, 16)
            buf = self.recvs[op]
            if whole:
                cp, leave = self.remote(self.keep.at[:, pl.ds(send0, size), :], buf, op)
            else:
                cp, leave = self.remote(self.keep.at[z, pl.ds(send0, size), :], buf.at[0], op)
            then(prev, leave)

            def prev(cp=cp, keep0=keep0, size=size, whole=whole, buf=buf):
                cp().wait_recv()
                if whole:
                    add_all(self.keep.at[:, pl.ds(keep0, size), :], buf, nz, size)
                else:
                    add_into(self.keep.at[z, pl.ds(keep0, size), :], buf.at[0], size)
            taken.append(op)
            start = keep0
        for e, b in enumerate(self.bits[3:]):
            cp, leave = self.remote(self.keep.at[z, pl.ds(start, size), :], self.extra.at[e], b)

            def prev(before=prev, cp=cp, leave=leave, e=e, start=start, size=size):
                before()
                leave()
                cp().wait_recv()
                cp().wait_send()
                add_into(self.keep.at[z, pl.ds(start, size), :], self.extra.at[e], size)
        at = pl.multiple_of(self.row + start, 16)
        total = self.keep.at[z, pl.ds(start, size), :]
        win = self.result.at[pl.ds(at, size), :]
        own = lambda win=win: pltpu.make_async_copy(total, win, self.ls.at[self.base])
        op = taken[-1]
        cp, leave = self.remote(total, win, op)

        def step(prev=prev, leave=leave):
            prev()
            own().start()
            leave()
        self.steps.append(step)

        def prev(cp=cp):
            cp().wait_recv()
            own().wait()
        for nxt in taken[-2::-1] + [self.bits[0]]:
            at = pl.multiple_of(at - bit_of(d, op) * size, 16)
            size *= 2
            op = nxt
            win = self.result.at[pl.ds(at, size), :]
            cp, leave = self.remote(win, win, op)
            then(prev, leave)
            prev = lambda cp=cp: cp().wait_recv()
        self.steps.append(prev)

    def hop(self, cls, kind, i, arriving):
        p, nz = self.pos, self.nz
        far, near = nz - 1 - i, i
        if kind == 1:
            t, way = far * (1 - p.upper) + near * p.upper, p.sign
        else:
            t, way = near * (1 - p.upper) + far * p.upper, -p.sign
        cell = self.keep.at[t, self.rows, :]
        s = 1 + (i if kind == 1 else nz - 1 - cls + i)
        first = kind == 1 and (arriving or cls < nz // 2 - 1)
        r = i if first else nz - 1 + i
        to = p.z - way if arriving else p.z + way
        land = self.line.at[r]
        cp = pltpu.make_async_remote_copy(cell, land, self.ss.at[self.base * self.nz + s], self.rs.at[self.base, 5 + len(self.bits) - 3 + r], device_id=(p.d, to), device_id_type=MESH)
        return cp, cell, land

    def sends(self, cls, kind):
        return self.nz - 1 - cls if kind == 1 else cls

    def along(self, cls, kind, i):
        if kind == 1 and cls == 0:
            for k in range(self.nz - 1):
                self.hop(cls, 1, k, False)[0].start()
            return
        cp, cell, land = self.hop(cls, kind, i, True)
        cp.wait_recv()
        add_into(cell, land, self.size)
        if i < self.sends(cls, kind):
            self.hop(cls, kind, i, False)[0].start()

    def finish(self, cls):
        self.last().wait_send()
        for kind in (1, 2):
            for i in range(self.sends(cls, kind)):
                self.hop(cls, kind, i, False)[0].wait_send()


def enter(d, z, nz, bits):
    bar = pltpu.get_barrier_semaphore()
    for b in bits:
        pl.semaphore_signal(bar, inc=1, device_id=(flip(d, b), z), device_id_type=MESH)
    @pl.when(z + 1 < nz)
    def _():
        pl.semaphore_signal(bar, inc=1, device_id=(d, z + 1), device_id_type=MESH)

    @pl.when(z >= 1)
    def _():
        pl.semaphore_signal(bar, inc=1, device_id=(d, z - 1), device_id_type=MESH)
    last = nz - 1
    pl.semaphore_wait(bar, len(bits) + lax.div(z + last, jnp.int32(nz)) + lax.div(last - z + last, jnp.int32(nz)))


def dot(a, b):
    return lax.dot_general(a, b, (((1,), (0,)), ((), ())), preferred_element_type=f32)


def dot_nt(a, b):
    return lax.dot_general(a, b, (((1,), (1,)), ((), ())), preferred_element_type=f32)


def dot_tn(a, b):
    return lax.dot_general(a, b, (((0,), (0,)), ((), ())), preferred_element_type=f32)


def norm_forward(h, gain, shift):
    centred = h - jnp.mean(h, -1, keepdims=True)
    inverse = lax.rsqrt(jnp.mean(centred * centred, -1, keepdims=True) + epsilon)
    normed = centred * inverse
    return normed * gain + shift, normed, inverse


def norm_backward(grad, normed, inverse, gain):
    scaled = grad * gain
    return inverse * (scaled - jnp.mean(scaled, -1, keepdims=True) - normed * jnp.mean(scaled * normed, -1, keepdims=True))


def col_sum(v):
    return jnp.sum(v, axis=0, keepdims=True)


def nth_shard(z, nz, o):
    t = z
    for b in range(nz.bit_length() - 1):
        t = t + lax.rem(lax.div(o, jnp.int32(2 ** b)), jnp.int32(2)) * (1 - 2 * bit_of(z, b)) * (2 ** b)
    return t


class Dims:
    pass


def layer_kernel(m, *refs):
    n_in, n_out = len(m.inputs), len(m.outputs)
    R = dict(zip(m.inputs + m.outputs + m.scratch, refs))
    g = Dims()
    for k, v in R.items():
        setattr(g, k, v)
    ni, L, T, D, nz, hp, nh, KP, NP = m.ni, m.L, m.T, m.D, m.nz, m.hp, m.nh, m.KP, m.NP
    d, z = lax.axis_index("dp"), lax.axis_index("mp")
    core = bit_of(d, m.bits[0])
    partner = flip(d, m.bits[0])

    shard = functools.partial(nth_shard, z, nz)

    g.DCQ = g.HD.at[:, :, 0:hp]
    g.DQ = g.DP.at[:, :, 0:m.QW]
    g.KV = g.DKV.at[:, 0:ni * KP]

    pos = Dims()
    pos.d, pos.z = d, z
    pos.upper = lax.div(2 * z, jnp.int32(nz))
    pos.sign = 1 - 2 * pos.upper
    kind = z * (1 - pos.upper) + (nz - 1 - z) * pos.upper
    classes = range(nz // 2)

    hw = m.hw
    joins = [(g.wq, g.AO.at[pl.ds(0, hw)]), (g.wa.at[0], g.AO.at[pl.ds(hw, hw)]), (g.wa.at[2], g.AO.at[pl.ds(2 * hw, hw)]), (g.wa.at[1], g.AO.at[pl.ds(3 * hw, hw)]),
             (g.wp.at[0], g.BO.at[pl.ds(0, hw)]), (g.wp.at[1], g.BO.at[pl.ds(hw, hw)]), (g.wao, g.OO.at[pl.ds(0, hw)]), (g.wco, g.OO.at[pl.ds(hw, hw)])]
    joins = [pltpu.make_async_copy(a, b, g.js.at[i]) for i, (a, b) in enumerate(joins)]
    for cp in joins:
        cp.start()
    loads = [pltpu.make_async_copy(a, b, g.js.at[10 + i]) for i, (a, b) in enumerate(((g.x, g.XV), (g.patches, g.PV)))]
    for cp in loads:
        cp.start()
    g.TMP[0:16, 0:D] = jnp.zeros((16, D), f32)
    ab, cb = g.ab[...].astype(f32), g.cb[...].astype(f32)
    g.TMP[0:1, 0:hw] = cb[0:1]
    g.TMP[0:1, hw:2 * hw] = ab[0:1]
    g.TMP[0:1, 2 * hw:3 * hw] = ab[1:2]
    g.TMP[1:2, hw:2 * hw] = cb[1:2]
    g.TMP[2:3, 0:D] = g.hb[...].astype(f32).reshape(1, D)
    g.VO[...] = g.TMP[0:16, 0:D].astype(bf16)
    g.VG[z] = g.VO[...]
    enter(d, z, nz, m.bits)
    for cp in joins:
        cp.wait()
    gsem = (g.out, g.zr, g.pr)
    own = {"A": g.AO, "B": g.BO, "O": g.OO, "H": g.H, "W": g.W, "V": g.VO}
    far = {"A": g.GA, "B": g.GB, "O": g.GO, "H": g.GH, "W": g.GW, "V": g.VG}
    gathers = [Gather(own[k], far[k], r0, rows, order, pos, nz, gsem, c, (nz - 1) * sum(len(q[3]) for q in m.gather_plan[:c])) for c, (k, r0, rows, order) in enumerate(m.gather_plan)]
    calls = [0, 0]

    def gather_steps():
        at = calls[0]
        calls[0] += 1
        for cls in classes:
            todo = m.gather_steps[cls][at]
            if todo:
                @pl.when(kind == cls)
                def _():
                    for c, st, dr, j in todo:
                        gathers[c].item(cls, nz, st, dr, j)

    nb = len(m.bits)

    def small_copy(i):
        return pltpu.make_async_remote_copy(g.SM, g.SR.at[i], g.ms.at[i], g.mr.at[i], device_id=(flip(d, m.bits[i]), z), device_id_type=MESH)

    def small_spread(o, frm):
        to = lax.rem(z + o, jnp.int32(nz))
        return pltpu.make_async_remote_copy(g.SM, g.SZ.at[frm(to)], g.ms.at[nb + o], g.zm.at[frm(to)], device_id=(d, to), device_id_type=MESH)

    small_store = lambda: pltpu.make_async_copy(g.SM, g.small, g.js.at[13])

    def small_step(i):
        if i > 0 and i < 4:
            small_copy(i - 1).wait()
            g.SM[...] += g.SR[i - 1]
        if i < 3:
            small_copy(i).start()
        elif i == 3:
            for e in range(3, nb):
                small_copy(e).start()
                small_copy(e).wait()
                g.SM[...] += g.SR[e]
            g.SZ[z] = g.SM[...]
            for o in range(1, nz):
                small_spread(o, lambda to: z).start()
        elif i == 5:
            for o in range(1, nz):
                small_spread(o, lambda to: to).wait_recv()
            for o in range(1, nz):
                small_spread(o, lambda to: z).wait_send()
            total = g.SZ[0]
            for t in range(1, nz):
                total = total + g.SZ[t]
            g.SM[...] = total
            small_store().start()

    def reduce_steps():
        at = calls[1]
        calls[1] += 1
        for cls in classes:
            todo = m.reduce_steps[cls][at]
            if todo:
                @pl.when(kind == cls)
                def _():
                    for c, what in todo:
                        i = progress[cls, c, what]
                        progress[cls, c, what] += 1
                        if c == len(chunks):
                            small_step(i)
                        elif what == 0:
                            chunks[c].steps[i]()
                        else:
                            chunks[c].along(cls, what, i)

    def after_each(steps):
        def between(o):
            for q in range(nz - 1):
                pl.when(o == q)(lambda: steps())
        return between

    def finish_gather():
        for cls in classes:
            @pl.when(kind == cls)
            def _():
                for q in gathers:
                    q.finish(cls, nz)

    pair_slot = [0]

    def pair(ref, rows):
        s = pair_slot[0]
        pair_slot[0] += 1
        return pltpu.make_async_remote_copy(ref.at[pl.ds(0, rows)], ref.at[pl.ds(rows, rows)], g.cs.at[s], g.cr.at[s], device_id=(partner, z), device_id_type=MESH)

    def place(block, slot):
        buf, sem, key, rows, cols = block
        return buf.at[slot, pl.ds(0, rows[1]), pl.ds(*cols)], sem.at[slot]

    def fetch(block, slot, o):
        buf, sem, key, rows, cols = block
        dst, done = place(block, slot)
        r, c = pl.ds(*rows), pl.ds(*cols)

        def mine():
            pltpu.make_async_copy(own[key].at[r, c], dst, done).start()

        def other():
            pltpu.make_async_copy(far[key].at[shard(o), r, c], dst, done).start()
        if isinstance(o, int):
            mine() if o == 0 else other()
        else:
            pl.when(o == 0)(mine)
            pl.when(o != 0)(other)

    def arrived(block, slot):
        buf, sem, key, rows, cols = block
        dst, done = place(block, slot)
        pltpu.make_async_copy(own[key].at[pl.ds(*rows), pl.ds(*cols)], dst, done).wait()

    def stream(blocks, body, between, ahead, refill=()):
        def step(o, c):
            if blocks:
                @pl.when(o + 1 < nz)
                def _():
                    for b in blocks:
                        fetch(b, slot_of(b, o + 1), o + 1)
            if ahead:
                @pl.when(o + 1 == nz)
                def _():
                    for b in ahead:
                        fetch(b, 0, 0)
            for b in blocks:
                arrived(b, slot_of(b, o))
            body(o, lax.rem(o, jnp.int32(2)))
            for b in refill:
                fetch(b, o, o)
            between(o)
            return c
        lax.fori_loop(0, nz, step, 0)

    def slot_of(block, o):
        return lax.rem(o, jnp.int32(block[0].shape[0]))

    FZ, PW, BW = m.FZ, m.PW, m.BW
    self_blocks = [(g.SA, g.sa, "A", (LANES, D - LANES), (0, D)), (g.SO, g.so, "O", (0, hp), (0, D))]
    cross_blocks = [(g.SA, g.sa, "A", (0, hp), (0, D)), (g.SB, g.sb, "B", (0, BW), (0, PW)), (g.SO, g.so, "O", (LANES, hp), (0, D))]
    hidden_blocks = [(g.SA, g.sa, "H", (0, D), (0, FZ))]
    output_blocks = [(g.SA, g.sa, "W", (0, FZ), (0, D))]
    back_blocks = [(g.SH, g.sh, "H", (0, D), (0, FZ))]
    cross_back = [cross_blocks[0], cross_blocks[2]]
    for b in self_blocks:
        fetch(b, 0, 0)

    lane = lax.broadcasted_iota(jnp.int32, (L, hp), 1)
    low = [lane // HEAD == h for h in range(nh)]
    high = [lane // HEAD == h + 1 for h in range(nh)]

    def stack(v, masks):
        return jnp.concatenate([jnp.where(k, v, 0.0) for k in masks], axis=0).astype(bf16)

    def unstack(v, masks):
        out = jnp.where(masks[0], v[0:L], 0.0)
        for h in range(1, nh):
            out = out + jnp.where(masks[h], v[h * L:(h + 1) * L], 0.0)
        return out

    def softmax(s):
        e = jnp.exp(s - jnp.max(s, -1, keepdims=True))
        return e / jnp.sum(e, -1, keepdims=True)

    gather_steps()
    for cp in loads:
        cp.wait()
    for i in range(ni):
        g.ACC[i * L:(i + 1) * L] = g.XV[i].astype(f32)
        mine = jnp.concatenate([g.PV[:, i, :].astype(f32), jnp.zeros((KP - NP, m.PW), f32)], 0)
        g.PT[i * KP:(i + 1) * KP] = mine.astype(bf16)
    g.X[0:T] = g.ACC[...].astype(bf16)
    cot_load = pltpu.make_async_copy(g.cot, g.XV, g.js.at[12])
    cot_load.start()
    swaps = [pair(g.X, T), pair(g.PT, ni * KP)]
    for s in swaps:
        s.start()

    g.ACC[...] = jnp.zeros((T, D), f32)
    gather_steps()

    def self_forward(o, slot):
        t = shard(o)
        bias = g.VG[t].astype(f32)[0:1, LANES:]
        qkv = (dot_nt(g.X[0:T], g.SA[o, 0:m.QW]) + bias).astype(bf16)
        g.QKV[o] = qkv
        qf = qkv.astype(f32)
        outs = []
        for i in range(ni):
            r = slice(i * L, (i + 1) * L)
            qs = stack(qf[r, 0:hp], high)
            k_i = qf[r, 3 * LANES:3 * LANES + hp].astype(bf16)
            v_i = qf[r, 2 * LANES:2 * LANES + hp].astype(bf16)
            p = softmax(dot_nt(qs, k_i) * score_scale)
            g.PS[o * ni + i] = p
            outs.append(unstack(dot(p.astype(bf16), v_i), low))
        mixed = jnp.concatenate(outs, 0).astype(bf16)
        g.MX[0, o, 0:T] = mixed
        g.ACC[...] += dot(mixed, g.SO[o])

    stream(self_blocks, self_forward, after_each(gather_steps), cross_blocks)

    def out_row(j):
        return tuple(v[...].astype(f32)[j:j + 1, :] for v in (g.ob, g.gain, g.shift))

    ob, gn, sh = out_row(0)
    first, normed, inv = norm_forward(g.X[0:T].astype(f32) + g.ACC[...] + ob, gn, sh)
    g.NM[0] = normed
    g.INV[...] = jnp.broadcast_to(inv, (T, LANES))
    g.F[0:T] = first.astype(bf16)
    g.ACC[...] = jnp.zeros((T, D), f32)
    gather_steps()

    key_pos = lax.broadcasted_iota(jnp.int32, (nh * L, KP), 1)

    def cross_forward(o, slot):
        t = shard(o)
        vb = g.VG[t].astype(f32)
        cq = (dot_nt(g.F[0:T], g.SA[o, 0:hp]) + vb[0:1, 0:hp]).astype(bf16)
        g.CQ[o] = cq
        cqf = cq.astype(f32)
        kv = (dot_nt(g.PT[0:ni * KP], g.SB[slot]) + vb[1:2, 0:m.BW]).astype(bf16)
        g.KV[o] = kv
        outs = []
        for i in range(ni):
            qs = stack(cqf[i * L:(i + 1) * L], low)
            kvi = g.KV[o, i * KP:(i + 1) * KP]
            s = dot_nt(qs, kvi[:, 0:hp]) * score_scale
            s = jnp.where(key_pos < g.rows[z * ni + i], s, -1e30)
            p = softmax(s)
            g.PC[o * ni + i] = p
            outs.append(unstack(dot(p.astype(bf16), kvi[:, LANES:LANES + hp]), high))
        mixed = jnp.concatenate(outs, 0).astype(bf16)
        g.MX[1, o, 0:T] = mixed
        g.ACC[...] += dot(mixed, g.SO[o])

    stream(cross_blocks, cross_forward, after_each(gather_steps), hidden_blocks)
    ob, gn, sh = out_row(1)
    second, normed, inv = norm_forward(g.F[0:T].astype(f32) + g.ACC[...] + ob, gn, sh)
    g.NM[1] = normed
    g.INV[:, HEAD:] = jnp.broadcast_to(inv, (T, LANES - HEAD))
    g.S2[0:T] = second.astype(bf16)
    gather_steps()
    other = g.MX.at[1 - core]
    mix_swap = pltpu.make_async_remote_copy(other.at[:, pl.ds(0, T)], other.at[:, pl.ds(T, T)], g.cs.at[m.swaps - 1], g.cr.at[m.swaps - 1], device_id=(partner, z), device_id_type=MESH)
    mix_swap.start()
    swaps += [pair(g.F, T), pair(g.S2, T)]
    for s in swaps[2:4]:
        s.start()

    def hidden_forward(o, slot):
        t = shard(o)
        pre = dot(g.S2[0:T], g.SA[o]) + g.VG[t].astype(f32)[2:3, :]
        cdf = 0.5 * (1.0 + lax.erf(pre * math.sqrt(0.5)))
        g.GP[o] = cdf + pre * jnp.exp(-0.5 * pre * pre) * (1.0 / math.sqrt(2.0 * math.pi))
        g.HD[o, 0:T] = (pre * cdf).astype(bf16)

    stream(hidden_blocks, hidden_forward, after_each(gather_steps), output_blocks)
    hid_swaps = [pair(g.HD.at[o], T) for o in range(nz)]
    for s in hid_swaps:
        s.start()
    g.ACC[...] = jnp.zeros((T, D), f32)
    gather_steps()

    def output_forward(o, slot):
        g.ACC[...] += dot(g.HD[o, 0:T], g.SA[o])

    stream(output_blocks, output_forward, after_each(gather_steps), back_blocks)
    gather_steps()
    ob, gn, sh = out_row(2)
    final, normed, inv = norm_forward(g.S2[0:T].astype(f32) + g.ACC[...] + ob, gn, sh)
    g.TMP[0:T, 0:D] = final
    layer_store = pltpu.make_async_copy(g.TMP.at[pl.ds(0, T), pl.ds(0, D)], g.layer_out, g.js.at[8])
    layer_store.start()

    cot_load.wait()
    for i in range(ni):
        g.ACC[i * L:(i + 1) * L] = g.XV[i].astype(f32)
    cot = g.ACC[...]
    g.SM[...] = jnp.zeros(g.SM.shape, f32)

    def record(j, grad_in, grad_out, normed):
        g.SM[j:j + 1] = col_sum(grad_in)
        g.SM[3 + j:4 + j] = col_sum(grad_out * normed)
        g.SM[6 + j:7 + j] = col_sum(grad_out)

    third = norm_backward(cot, normed, inv, gn)
    record(2, third, cot, normed)
    g.G3[0:T] = third.astype(bf16)
    swap3 = pair(g.G3, T)
    swap3.start()

    finish_gather()
    rsem = (g.out, g.rs, g.ls)
    results = {"A": g.RA, "B": g.RB, "O": g.RO, "H": g.RH, "W": g.RW}
    chunks = []
    progress = {}
    for c, (k, h0, half, order) in enumerate(m.reduce_plan):
        recvs = {b: R[f"rv{c}_{b}"] for b in m.bits[1:3]}
        whole = m.rows[k] // 2
        chunks.append(Reduce(R[f"kp{c}"], recvs, R[f"ln{c}"], R.get(f"ex{c}"), results[k], core * whole + h0, half, order, pos, nz, m.bits, rsem, c))
    for cls in classes:
        for c in range(len(chunks) + 1):
            for what in range(3):
                progress[cls, c, what] = 0

    def half_columns(apart, count=None):
        return pl.ds(pl.multiple_of(core * apart, LANES), count or apart)

    def deal(k, t, value):
        for c, p in enumerate(m.reduce_plan):
            if p[0] == k:
                R[f"kp{c}"][t] = value[p[1]:p[1] + p[2]].astype(bf16)

    reduce_steps()

    reduce_steps()
    cols = half_columns(m.FZ // 2)
    own_part = dot_tn(g.HD[0, 0:T, cols], g.G3[0:T])
    swap3.wait_recv()
    for s in hid_swaps:
        s.wait_recv()
    deal("W", shard(jnp.int32(0)), own_part + dot_tn(g.HD[0, T:, cols], g.G3[T:]))

    def job_w(o, c):
        t = shard(o)
        deal("W", t, dot_tn(g.HD[o, :, cols], g.G3[...]))
        return c
    lax.fori_loop(1, nz, job_w, 0)
    for s in hid_swaps:
        s.wait_send()
    reduce_steps()
    g.ACC[...] = third

    def loop_send(ref, rows, kind, o):
        pltpu.make_async_remote_copy(ref.at[o, pl.ds(0, rows)], ref.at[o, pl.ds(rows, rows)], g.ds.at[kind, o], g.dr.at[kind, o], device_id=(partner, z), device_id_type=MESH).start()

    def hidden_backward(o, slot):
        t = shard(o)
        pre = (dot_nt(g.G3[0:T], g.SA[o]) * g.GP[o]).astype(bf16)
        g.DP[o, 0:T] = pre
        g.SM[pl.ds(9 + t, 1)] = col_sum(pre.astype(f32))
        loop_send(g.DP, T, 0, o)
        g.ACC[...] += dot_nt(pre, g.SH[slot])

    stream(back_blocks, hidden_backward, after_each(reduce_steps), [], cross_back)
    reduce_steps()

    def loop_wait(ref, rows, kind):
        for o in range(nz):
            cp = pltpu.make_async_remote_copy(ref.at[o, pl.ds(0, rows)], ref.at[o, pl.ds(rows, rows)], g.ds.at[kind, o], g.dr.at[kind, o], device_id=(partner, z), device_id_type=MESH)
            cp.wait()

    gn = out_row(1)[1]
    normed, inv = g.NM[1], g.INV[:, HEAD:HEAD + 1]
    grad = g.ACC[...]
    secondg = norm_backward(grad, normed, inv, gn)
    record(1, secondg, grad, normed)
    g.G12[1, 0:T] = secondg.astype(bf16)
    swap2 = pair(g.G12.at[1], T)
    swap2.start()
    reduce_steps()
    loop_wait(g.DP, T, 0)
    swaps[3].wait_recv()

    def job_h(o, c):
        t = shard(o)
        deal("H", t, dot_tn(g.S2[:, half_columns(D // 2)], g.DP[o]))
        return c
    lax.fori_loop(0, nz, job_h, 0)
    reduce_steps()

    g.ACC[...] = secondg

    def backward_unit(qs, k_i, v_i, p, ms, masks):
        grad_v = dot_tn(p.astype(bf16), ms)
        grad_p = dot_nt(ms, v_i)
        gs = (p * (grad_p - jnp.sum(p * grad_p, -1, keepdims=True))).astype(bf16)
        grad_q = unstack(dot(gs, k_i), masks) * score_scale
        grad_k = dot_tn(gs, qs) * score_scale
        return grad_q, grad_k.astype(bf16).astype(f32), grad_v.astype(bf16).astype(f32)

    def cross_backward(o, slot):
        t = shard(o)
        for b in cross_back:
            arrived(b, o)
        gm = dot_nt(g.G12[1, 0:T], g.SO[o]).astype(bf16).astype(f32)
        cqf = g.CQ[o].astype(f32)
        grads = []
        for i in range(ni):
            r = slice(i * L, (i + 1) * L)
            kvi = g.KV[o, i * KP:(i + 1) * KP]
            gq, gk, gv = backward_unit(stack(cqf[r], low), kvi[:, 0:hp], kvi[:, LANES:LANES + hp], g.PC[o * ni + i], stack(gm[r], high), low)
            grads.append(gq)
            g.DKV[o, i * KP:(i + 1) * KP] = jnp.concatenate([gk[:, 0:LANES], gk[:, LANES:] + gv[:, 0:LANES], gv[:, LANES:]], 1).astype(bf16)
        dcq = jnp.concatenate(grads, 0).astype(bf16)
        g.DCQ[o, 0:T] = dcq
        loop_send(g.DCQ, T, 1, o)
        loop_send(g.DKV, ni * KP, 2, o)
        dkv = g.DKV[o, 0:ni * KP]
        g.SM[pl.ds(9 + nz + t, 1), BW:BW + hp] = col_sum(dcq.astype(f32))
        g.SM[pl.ds(9 + nz + t, 1), 0:BW] = col_sum(dkv.astype(f32))
        g.ACC[...] += dot(dcq, g.SA[o, 0:hp])

    stream([], cross_backward, after_each(reduce_steps), [], self_blocks)
    reduce_steps()
    gn = out_row(0)[1]
    normed, inv = g.NM[0], g.INV[:, 0:1]
    grad = g.ACC[...]
    firstg = norm_backward(grad, normed, inv, gn)
    record(0, firstg, grad, normed)
    g.G12[0, 0:T] = firstg.astype(bf16)
    swap1 = pair(g.G12.at[0], T)
    swap1.start()
    reduce_steps()
    loop_wait(g.DCQ, T, 1)
    loop_wait(g.DKV, ni * KP, 2)
    swaps[1].wait_recv()

    layer_store.wait()

    def job_b(o, c):
        t = shard(o)
        g.TMP[...] = dot_tn(g.DKV[o, :, half_columns(LANES, hp)], g.PT[...])
        deal("B", t, g.TMP[pl.ds(pl.multiple_of(core * HEAD, 16), BW // 2)])
        return c
    lax.fori_loop(0, nz, job_b, 0)
    for o in range(2):
        fetch(cross_blocks[1], o, o)
    reduce_steps()

    g.ACC[...] = firstg

    def self_backward(o, slot):
        t = shard(o)
        for b in self_blocks:
            arrived(b, o)
        gm = dot_nt(g.G12[0, 0:T], g.SO[o]).astype(bf16).astype(f32)
        qf = g.QKV[o].astype(f32)
        gqs, gks, gvs = [], [], []
        for i in range(ni):
            r = slice(i * L, (i + 1) * L)
            k_i = qf[r, 3 * LANES:3 * LANES + hp].astype(bf16)
            v_i = qf[r, 2 * LANES:2 * LANES + hp].astype(bf16)
            gq, gk, gv = backward_unit(stack(qf[r, 0:hp], high), k_i, v_i, g.PS[o * ni + i], stack(gm[r], low), high)
            gqs.append(gq)
            gks.append(gk)
            gvs.append(gv)
        gq, gk, gv = (jnp.concatenate(v, 0) for v in (gqs, gks, gvs))
        dq = jnp.concatenate([gq, gv[:, 0:LANES], gv[:, LANES:] + gk[:, 0:LANES], gk[:, LANES:]], 1).astype(bf16)
        g.DQ[o, 0:T] = dq
        loop_send(g.DQ, T, 3, o)
        g.SM[pl.ds(9 + 2 * nz + t, 1), 0:m.QW] = col_sum(dq.astype(f32))
        g.ACC[...] += dot(dq, g.SA[o, 0:m.QW])

    stream([], self_backward, after_each(reduce_steps), [])
    text_store = pltpu.make_async_copy(g.ACC, g.text_grad, g.js.at[8])
    text_store.start()
    reduce_steps()
    loop_wait(g.DQ, T, 3)
    swap1.wait_recv()
    swap2.wait_recv()
    for s in swaps[0:1] + swaps[2:3] + [mix_swap]:
        s.wait_recv()

    def job_o(o, c):
        t = shard(o)
        g.TMP[:, 0:D] = dot_tn(g.MX[core, o], g.G12[core])
        deal("O", t, g.TMP[pl.ds(pl.multiple_of(core * HEAD, 16), hw), 0:D])
        return c
    lax.fori_loop(0, nz, job_o, 0)
    reduce_steps()

    def job_a(o, c):
        t = shard(o)

        @pl.when(core == 0)
        def _():
            left = dot_tn(g.DCQ[o], g.F[...])
            right = dot_tn(g.DQ[o, :, 0:hp], g.X[...])
            deal("A", t, jnp.concatenate([left[0:LANES], left[LANES:] + right[0:LANES], right[LANES:]], 0))

        @pl.when(core == 1)
        def _():
            deal("A", t, dot_tn(g.DQ[o, :, hp:], g.X[...]))
        return c
    lax.fori_loop(0, nz, job_a, 0)
    reduce_steps()

    reduce_steps()
    for part in range(nz // 2):
        for slot in range(2):
            arrived(cross_blocks[1], slot)
        for i in range(ni):
            r = pl.ds(i * KP, KP)
            total = (dot(g.DKV[2 * part, r], g.SB[0]) + dot(g.DKV[2 * part + 1, r], g.SB[1]))[0:NP]
            g.PG[:, i, :] = total if part == 0 else g.PG[:, i, :] + total
            if i == ni - 1 and part < nz // 2 - 1:
                for slot in range(2):
                    fetch(cross_blocks[1], slot, 2 * part + 2 + slot)
            if i == ni - 1 and part == nz // 2 - 1:
                patch_store = pltpu.make_async_copy(g.PG, g.patch_out, g.js.at[9])
                patch_store.start()
            if i % 2 == 1:
                reduce_steps()
    assert calls == [len(m.gather_steps[0]), len(m.reduce_steps[0])], calls
    assert all(sum(len(p) for p in m.reduce_steps[cls]) == sum(progress[cls, c, w] for c in range(len(chunks) + 1) for w in range(3)) for cls in classes)

    for cp in swaps + [swap1, swap2, swap3, mix_swap]:
        cp.wait_send()
    text_store.wait()
    patch_store.wait()
    small_store().wait()
    for cls in classes:
        @pl.when(kind == cls)
        def _():
            for c in chunks:
                c.finish(cls)


GATHER_PLAN = (("V", 0, 16, ""), ("A", 0, 256, "yxc"), ("W", 0, 512, "yc"), ("O", 0, 384, "yxc"), ("H", 0, 384, "yxc"), ("A", 256, 256, "xyc"), ("A", 512, 256,
    "yc"), ("H", 384, 384, "yxc"), ("W", 512, 256, "yc"), ("B", 0, 384, "yxc"))
GATHER_ORDER = ((0, 40, 200, 120, -1, 13, 53, 213, 133, 61, 14, 360, 221, 54, 214, 141, 134, 69, 15, 229, 222, 77, 240, 62, 373, 237, 55, 142, 149, 215, 230, 135,
    157, 70, 160, 238, 381, 374, 78, 63, 150, 253, 143, 223, 280, 158, 375, 382, 254, 261, 389, 320, 173, 269, -1, 397, 71, 231, 383, 80, 255, 293, 151,
    79, 239, 262, 174, 159, 181, 270, 175, -1, 390, 333, 263, 301, 294, 398, 271, -1, 295, 391, 182, 183, -1, 399, 341, 93, 189, -1, 309, 302, 303, 349,
    334, 197, -1, 317, 101, 94, 190, -1, 342, 335, 109, 198, 191, -1, 310, 350, 95, 199, 102, -1, 318, 311, 343, 110, -1, 319, -1, 351, 103, -1, -1, 111,
    -1, -1, -1), (0, 4, 40, 44, 200, 204, 120, 124, -1, 9, 13, 49, 53, 209, 213, 129, 133, 14, 360, 364, 57, 54, 217, 61, 214, 221, 137, 134, 369, 65,
    141, 373, 240, 62, 244, 73, 69, 222, 225, 374, 77, 233, 249, 229, 253, 160, 164, 145, 142, 237, 153, 377, 254, 169, 149, 280, 284, 173, 381, 157, 70,
    174, 230, 78, 289, 320, 324, 293, 150, 238, 382, 158, 294, 80, 84, 257, 329, 385, 333, 265, 261, -1, 393, 269, 262, 389, 177, 93, 270, -1, 397, 334,
    89, 181, 182, -1, 297, 390, -1, 301, 185, 398, -1, 302, 337, 94, 193, 189, -1, 345, 341, 197, 190, -1, 305, 349, 101, 198, -1, 313, 342, 309, 109, -1,
    317, 350, 310, 97, 318, -1, 105, -1, 102, -1, -1, 110, -1, -1, -1))
REDUCE_PLAN = (("W", 128, "xyz"), ("W", 128, "yxz"), ("W", 128, "zyx"), ("H", 128, "zyx"), ("H", 128, "xyz"), ("H", 128, "xzy"), ("B", 128, "yzx"), ("B", 64,
    "xyz"), ("O", 64, "yzx"), ("O", 64, "xyz"), ("O", 64, "zxy"), ("A", 64, "xyz"), ("A", 64, "yxz"), ("A", 64, "zxy"), ("A", 64, "yzx"), ("A", 64,
    "xyz"), ("A", 64, "xyz"))
REDUCE_ORDER = ((-1, -1, 6, 7, 0, 3, -1, -1, -1, -1, -1, -1, 12, 9, 10, 15, -1, 0, 3, -1, -1, -1, 0, 1, 12, -1, 8, 6, -1, 18, 21, 12, 13, -1, 6, 15, 16, -1, 3, 4,
    -1, -1, 2, 0, 21, 11, 9, 6, -1, 30, 31, 0, 18, 6, 19, 24, 27, 14, 12, -1, 48, 36, 0, 39, 40, 45, 33, 21, 22, 42, 9, 0, 6, 17, 15, 5, 3, -1, 51, -1, 6,
    51, 27, -1, 24, 25, 12, -1, 48, -1, 36, 32, 30, 45, 42, 43, 33, 15, 9, 3, 20, 18, 27, 28, 51, 48, 49, 12, 45, 46, 41, 39, 12, 36, 37, 33, 34, 23, 30,
    21, 15, 9, 26, 24, 18, 3, 39, 3, 51, 30, 44, 42, 15, 21, 24, 29, 27, 15, 18, 9, 42, 50, 48, 39, 30, 21, 27, 9, 24, 47, 45, 42, 21, 38, 30, 36, 18, 48,
    27, 51, 39, 30, 35, 33, 18, 24, 27, 36, 45, 24, 48, 42, 33, 39, 48, 42, 36, 45, 39, 51, 36, 33, 45, 33), (-1, -1, 6, 0, 3, -1, -1, -1, -1, -1, 7, -1,
    12, 9, 15, -1, 7, 0, 3, -1, 7, 8, -1, -1, 8, 6, 0, 12, 10, -1, 10, -1, 6, 18, 21, 10, 1, 12, 11, 15, 1, -1, 1, 13, 13, 2, 6, 3, 13, 11, 2, 0, 9, -1,
    14, 14, 12, 16, 16, -1, 6, 21, 16, 18, 4, 17, 4, 0, -1, 4, 9, 5, 12, 17, 15, 5, 3, 0, -1, 30, 31, 31, 6, 0, 31, 24, 27, 12, 21, 9, 6, -1, 48, 32, 36,
    39, 45, 19, 33, 42, 32, 30, 19, 12, 24, 27, 3, 15, -1, 51, 9, -1, 19, 51, 20, -1, 36, 40, 48, -1, 40, 20, 18, -1, 40, 22, 41, 45, 22, 22, 42, 27, 25,
    41, 39, 23, 25, 3, 23, 21, 25, 15, 33, 26, 43, 3, 30, 43, 26, 24, 9, 43, 51, 28, 28, 44, 48, 28, 9, 49, 44, 42, 49, 36, 49, 29, 45, 46, 18, 46, 21,
    50, 46, 39, 50, 48, 37, 37, 29, 37, 47, 33, 30, 47, 45, 34, 34, 34, 24, 38, 27, 38, 36, 51, 39, 18, 42, 48, 35, 30, 15, 35, 45, 33, 21, 24, 27, 39,
    36, 51, 42, 15, 21, 48, 30, 18, 48, 33, 45, 30, 24, 27, 18, 45, 36, 39, 24, 51, 27, 42, 33, 36, 39, 42, 33))


def unpack(orders, decode):
    out = []
    for order in orders:
        parts = [[]]
        for code in order:
            if code < 0:
                parts.append([])
            else:
                parts[-1].append(decode(code))
        out.append(parts)
    return out


def gather_code(code):
    return code // 40, code // 8 % 5 - 1, code // 4 % 2, code % 4


def reduce_code(code):
    return code // 3, code % 3


def plans(m):
    link = dict(zip("cxy", m.bits[:3]), z="z")
    m.gather_plan = [(k, r0, rows, tuple(link[o] for o in order)) for k, r0, rows, order in GATHER_PLAN]
    m.gather_steps = unpack(GATHER_ORDER, gather_code)
    m.reduce_plan = []
    at = {}
    for k, half, order in REDUCE_PLAN:
        h0 = at.get(k, 0)
        at[k] = h0 + half
        m.reduce_plan.append((k, h0, half, tuple(link[o] for o in order)))
    m.reduce_steps = unpack(REDUCE_ORDER, reduce_code)
    assert all(at[k] * 2 == m.rows[k] for k in at) and m.nz == 4


def run_layer(m, x, patches, rows, cot, wa, ab, wao, wq, wp, cb, wco, H, hb, W, ob, gain, shift):
    nz = m.nz
    ni, L, D = x.shape
    T = ni * L
    m.ni, m.L, m.D, m.T = ni, L, D, T
    m.NP, m.PW = patches.shape[1:]
    by_patch = jnp.swapaxes(patches, 0, 1)
    m.KP = (m.NP + 15) // 16 * 16
    hw = m.hw = D // nz
    m.nh = hw // HEAD
    m.hp = (hw + HEAD + LANES - 1) // LANES * LANES
    hp, KP, PW = m.hp, m.KP, m.PW
    m.BW, m.QW, m.FZ = 2 * hw, D - LANES, W.shape[0]
    FZ, BW = m.FZ, m.BW
    m.rows = dict(A=D, B=BW, O=2 * hw, H=D, W=FZ)
    lanes = dict(A=D, B=PW, O=D, H=FZ, W=D)
    plans(m)
    m.swaps = nz + 9
    V, sem = pltpu.VMEM, pltpu.SemaphoreType.DMA
    nc, ng = len(m.reduce_plan), len(m.gather_plan)
    nb = len(m.bits)
    sums = (9 + 3 * nz + 7) // 8 * 8
    scratch = dict(
        VG=V((nz, 16, D), bf16), X=V((2 * T, D), bf16), PT=V((2 * ni * KP, PW), bf16),
        SA=V((nz, D, D), bf16), SH=V((2, D, D), bf16), SB=V((2, BW, PW), bf16), SO=V((nz, hp, D), bf16),
        ACC=V((T, D), f32), QKV=V((nz, T, m.QW), bf16), PS=V((nz * ni, m.nh * L, L), f32), MX=V((2, nz, 2 * T, hp), bf16),
        NM=V((2, T, D), f32), INV=V((T, LANES), f32), F=V((2 * T, D), bf16), S2=V((2 * T, D), bf16),
        CQ=V((nz, T, hp), bf16), PC=V((nz * ni, m.nh * L, KP), f32),
        GP=V((nz, T, FZ), f32), HD=V((nz, 2 * T, FZ), bf16), SM=V((sums, D), f32), G3=V((2 * T, D), bf16), DP=V((nz, 2 * T, FZ), bf16),
        G12=V((2, 2 * T, D), bf16), DKV=V((nz, 2 * ni * KP, m.BW), bf16),
        TMP=V((hp, PW), f32), XV=V(x.shape, bf16), PV=V(by_patch.shape, bf16), PG=V((m.NP, ni, PW), f32), AO=V((D, D), bf16), BO=V((BW, PW), bf16), OO=V((2 * hw, D), bf16), VO=V((16, D), bf16), SR=V((nb, sums, D), f32), SZ=V((nz, sums, D), f32),
        out=sem((max(2 * nz * ng, nz * nc),)), zr=sem((ng, nz - 1)), pr=sem(((nz - 1) * sum(len(q[3]) for q in m.gather_plan),)),
        cs=sem((m.swaps,)), cr=sem((m.swaps,)), ds=sem((4, nz)), dr=sem((4, nz)),
        js=sem((14,)), sa=sem((nz,)), sh=sem((2,)), sb=sem((2,)), so=sem((nz,)),
        rs=sem((nc, 5 + nb - 3 + nz - 1 + nz // 2)), ls=sem((nc,)), ms=sem((nb + nz,)), mr=sem((nb,)), zm=sem((nz,)),
    )
    for c, (k, h0, half, order) in enumerate(m.reduce_plan):
        C = lanes[k]
        scratch[f"kp{c}"] = V((nz, half, C), bf16)
        for b in m.bits[1:3]:
            lead = nz if order.index(b) < order.index("z") else 1
            scratch[f"rv{c}_{b}"] = V((lead, op_rows(half, order, b), C), bf16)
        scratch[f"ln{c}"] = V((nz - 1 + nz // 2, op_rows(half, order, "z"), C), bf16)
        if nb > 3:
            scratch[f"ex{c}"] = V((nb - 3, half // 4, C), bf16)
    S = jax.ShapeDtypeStruct
    hbm, vm, sm = (pl.BlockSpec(memory_space=s) for s in (pl.ANY, pltpu.VMEM, pltpu.SMEM))
    outs = dict(
        layer_out=(S((T, D), f32), hbm), text_grad=(S((T, D), f32), hbm), patch_out=(S((m.NP, ni, PW), f32), hbm), small=(S((sums, D), f32), hbm),
        **{"R" + k: (S((m.rows[k], lanes[k]), bf16), hbm) for k in "ABOHW"},
        **{"G" + k: (S((nz, m.rows[k], lanes[k]), bf16), hbm) for k in "ABOHW"},
    )
    turn = lambda a: jnp.swapaxes(a, -1, -2)
    ins = dict(x=(x, hbm), patches=(by_patch, hbm), rows=(rows, sm), cot=(cot, hbm), wa=(turn(wa), hbm), ab=(ab, vm), wao=(wao, hbm), wq=(turn(wq), hbm), wp=(turn(wp), hbm),
               cb=(cb, vm), wco=(wco, hbm), H=(H, hbm), hb=(hb, vm), W=(W, hbm), ob=(ob, vm), gain=(gain, vm), shift=(shift, vm))
    m.inputs, m.outputs, m.scratch = list(ins), list(outs), list(scratch)
    res = pl.pallas_call(
        functools.partial(layer_kernel, m),
        out_shape=tuple(o[0] for o in outs.values()),
        in_specs=[i[1] for i in ins.values()],
        out_specs=tuple(o[1] for o in outs.values()),
        scratch_shapes=list(scratch.values()),
        compiler_params=pltpu.CompilerParams(collective_id=0, has_side_effects=True, vmem_limit_bytes=67043328),
        name="layer",
    )(*[i[0] for i in ins.values()])
    return dict(zip(outs, res))


finish_ins = ("RA", "RB", "RO", "RH", "RW", "layer_out", "text_grad", "patch_out", "small")
finish_outs = ("layer_out_", "text_grad_", "patch_grad", "attn", "attn_bias", "attn_out", "query", "patch", "cross_bias", "cross_out", "hidden", "hidden_bias", "output", "out_bias", "gain", "shift")


def finish_kernel(m, names, *refs):
    g = Dims()
    for k, v in zip(names, refs):
        setattr(g, k, v)
    nz, hw, ni, KP, NP = m.nz, m.hw, m.ni, m.KP, m.NP
    z = lax.axis_index("mp")
    loads = {}

    def load(name, src, dst):
        cp = pltpu.make_async_copy(src, dst, g.isem.at[len(loads)])
        cp.start()
        loads[name] = cp
    load("lo", g.layer_out, g.vL)
    load("tg", g.text_grad, g.vT)
    load("W", g.RW, g.vW)
    load("H", g.RH, g.vH)
    load("pg", g.patch_out, g.fG)
    load("B", g.RB, g.vP)
    load("O", g.RO, g.vO)
    load("A", g.RA, g.vA)
    stores = []

    def store(src, dst):
        cp = pltpu.make_async_copy(src, dst, g.osem.at[len(stores)])
        cp.start()
        stores.append(cp)

    def widen(src, dst, row0=0):
        step = HEAD

        def body(i, c):
            r = pl.multiple_of(i * step, step)
            dst[pl.ds(r, step), :] = src[pl.ds(row0 + r, step), :].astype(f32)
            return c
        lax.fori_loop(0, dst.shape[0] // step, body, 0)

    loads["lo"].wait()
    store(g.vL, g.layer_out_)
    loads["tg"].wait()
    store(g.vT, g.text_grad_)
    loads["W"].wait()
    widen(g.vW, g.fW)
    store(g.fW, g.output)
    loads["H"].wait()
    widen(g.vH, g.fH)
    store(g.fH, g.hidden)
    loads["pg"].wait()
    store(g.fG, g.patch_grad)
    loads["B"].wait()
    for j in range(2):
        widen(g.vP, g.fP.at[j], j * hw)
    store(g.fP, g.patch)
    loads["O"].wait()
    widen(g.vO, g.fO)
    store(g.fO.at[pl.ds(0, hw)], g.attn_out)
    store(g.fO.at[pl.ds(hw, hw)], g.cross_out)
    loads["A"].wait()
    widen(g.vA, g.fQ)
    for j, part in ((0, 1), (1, 3), (2, 2)):
        widen(g.vA, g.fA.at[j], part * hw)
    store(g.fQ, g.query)
    store(g.fA, g.attn)
    row = lambda k: g.small[pl.ds(9 + k * nz + z, 1), :]
    qv = row(2)[:, 0:5 * LANES]
    at = hw - LANES
    g.attn_bias[0:1] = qv[:, at:at + hw]
    g.attn_bias[1:2] = qv[:, at + hw:at + 2 * hw]
    g.cross_bias[0:1] = row(1)[:, 2 * hw:3 * hw]
    g.cross_bias[1:2] = row(1)[:, hw:2 * hw]
    g.hidden_bias[...] = row(0).reshape(m.FZ)
    g.out_bias[...] = g.small[0:3, :]
    g.gain[...] = g.small[3:6, :]
    g.shift[...] = g.small[6:9, :]
    for cp in stores:
        cp.wait()


def finish(m, r):
    nz, ni, L, D, PW, FZ, BW, KP, NP = m.nz, m.ni, m.L, m.D, m.PW, m.FZ, m.BW, m.KP, m.NP
    hw = m.hw = D // nz
    S, V, sem = jax.ShapeDtypeStruct, pltpu.VMEM, pltpu.SemaphoreType.DMA
    hbm, vm = pl.BlockSpec(memory_space=pl.ANY), pl.BlockSpec(memory_space=pltpu.VMEM)
    shapes = ((m.T, D), (m.T, D), (NP, ni, PW), (3, hw, D), (2, hw), (hw, D), (hw, D), (2, hw, PW), (2, hw), (hw, D), (D, FZ), (FZ,), (FZ, D), (3, D), (3, D), (3, D))
    small = {"attn_bias", "cross_bias", "hidden_bias", "out_bias", "gain", "shift"}
    scratch = dict(
        vW=V((FZ, D), bf16), vH=V((D, FZ), bf16), vL=V((m.T, D), f32), vT=V((m.T, D), f32),
        vP=V((BW, PW), bf16), vO=V((2 * hw, D), bf16), vA=V((D, D), bf16), fW=V((FZ, D), f32), fH=V((D, FZ), f32), fG=V((NP, ni, PW), f32),
        fP=V((2, hw, PW), f32), fO=V((2 * hw, D), f32), fQ=V((hw, D), f32), fA=V((3, hw, D), f32), isem=sem((8,)), osem=sem((11,)),
    )
    ins = [r[k] for k in finish_ins]
    return pl.pallas_call(
        functools.partial(finish_kernel, m, finish_ins + finish_outs + tuple(scratch)),
        out_shape=tuple(S(s, f32) for s in shapes),
        in_specs=[vm if k == "small" else hbm for k in finish_ins],
        out_specs=tuple(vm if k in small else hbm for k in finish_outs),
        scratch_shapes=list(scratch.values()),
        compiler_params=pltpu.CompilerParams(vmem_limit_bytes=56 << 20),
        name="finish",
    )(*ins)


def per_device(nd, nz, text_states, patch_states, patch_rows, cotangent, w_attn, attn_bias, w_attn_out, w_query, w_patch, cross_bias, w_cross_out, w_hidden, hidden_bias, w_output, out_bias, norm_gain, norm_shift):
    m = Dims()
    m.nz, m.bits = nz, tuple(range(nd.bit_length() - 1))
    r = run_layer(m, text_states, patch_states, patch_rows, cotangent, w_attn, attn_bias, w_attn_out, w_query, w_patch, cross_bias, w_cross_out, w_hidden, hidden_bias, w_output, out_bias, norm_gain, norm_shift)
    outs = list(finish(m, r))
    for k in ("attn", "query", "patch"):
        at = finish_outs.index(k)
        outs[at] = jnp.swapaxes(outs[at], -1, -2)
    for at in range(2):
        outs[at] = outs[at].reshape(text_states.shape)
    at = finish_outs.index("patch_grad")
    outs[at] = jnp.swapaxes(outs[at], 0, 1)
    return tuple(outs)


def solution(mesh):
    nd, nz = mesh.shape["dp"], mesh.shape["mp"]
    rows = P(("dp", "mp"), None, None)
    return jax.shard_map(
        functools.partial(per_device, nd, nz),
        mesh=mesh,
        in_specs=(rows, rows, P("dp"), rows, P(None, None, "mp"), P(None, "mp"), P("mp", None), P(None, "mp"), P(None, None, "mp"), P(None, "mp"), P("mp", None), P(None, "mp"), P("mp"), P("mp", None), P(), P(), P()),
        out_specs=(rows, rows, rows, P(None, None, "mp"), P(None, "mp"), P("mp", None), P(None, "mp"), P(None, None, "mp"), P(None, "mp"), P("mp", None), P(None, "mp"), P("mp"), P("mp", None), P(), P(), P()),
        check_vma=False,
    )
```
